32 devices in a mesh: seq: 4 (over z), fsdp: 8 (over y, x, core).
Axes of the slice: x: 2, y: 2, z: 4, core: 2. Of those that a mesh axis runs over, the one named last changes fastest.
Arguments:
- video: bfloat16 [8, 4096, 1152], P('fsdp', 'seq'), may hold values from -4 to 4
- context: bfloat16 [8, 120, 1152], P('fsdp'), may hold values from -4 to 4
- modulation: float32 [8, 1, 6, 1152], P('fsdp'), may hold values from -0.6 to 0.6
- adapter_index: int32 [8], P('fsdp'), may hold values from 0 to 7
- cotangent: bfloat16 [8, 4096, 1152], P('fsdp', 'seq'), may hold values from -6 to 6
- qkv_weights: bfloat16 [1, 9, 1152, 1152], P(None, None, 'fsdp'), may hold values from -0.1875 to 0.1875
- out_weights: bfloat16 [1, 3, 1152, 1152], P(None, None, 'fsdp'), may hold values from -0.375 to 0.375
- ffn_up: bfloat16 [1, 1152, 4608], P(None, 'fsdp'), may hold values from -0.1875 to 0.1875
- ffn_down: bfloat16 [1, 4608, 1152], P(None, 'fsdp'), may hold values from -0.09375 to 0.09375
- adapt_wide: bfloat16 [1, 26, 8, 16, 1152], P(None, None, None, None, 'fsdp'), may hold values from -0.375 to 0.375
- adapt_ff: bfloat16 [1, 2, 8, 16, 4608], P(None, None, None, None, 'fsdp'), may hold values from -0.1875 to 0.1875
Outputs:
- output: bfloat16 [8, 4096, 1152], P('fsdp', 'seq')
- input_grad: bfloat16 [8, 4096, 1152], P('fsdp', 'seq')
- adapt_wide_grad: float32 [1, 26, 8, 16, 1152], P(None, None, None, None, 'fsdp')
- adapt_ff_grad: float32 [1, 2, 8, 16, 4608], P(None, None, None, None, 'fsdp')
The draws below stay inside these ranges and needn't reach their ends.
Inputs may be any that keep to these rules, and one draw needn't show every extreme that they name: `adapter_index`: each clip's adapter.
All inputs are finite; a program needn't handle non-finite values.
Results may differ from the reference program's by a relative error of at most 0.022.
Values may be sent and summed in bfloat16 or wider, within the bound.
No kernel may reach another device: no remote copies, remote signals or barrier semaphores. Data moves between devices by JAX's collectives and lax.ppermute only.
A program may use at most 448 MiB of HBM per device.

```python
import jax
import jax.numpy as jnp
from jax import lax

D = 1152
HEADS = 16
HEAD_DIM = 72
FF = 4608
CTX = 120
RANK = 16
ADAPTERS = 8
FRAMES = 16
SPATIAL = 256
LAYERS = 1
CLIPS = 8


def draw_video(key, part):
    own_key = jax.random.fold_in(key, 101)
    shape = (CLIPS, FRAMES * SPATIAL, D)
    values = jnp.clip(jax.random.normal(own_key, shape, jnp.float32), -4.0, 4.0)
    return values.astype(jnp.bfloat16)


def draw_context(key, part):
    own_key = jax.random.fold_in(key, 202)
    shape = (CLIPS, CTX, D)
    values = jnp.clip(jax.random.normal(own_key, shape, jnp.float32), -4.0, 4.0)
    return values.astype(jnp.bfloat16)


def draw_modulation(key, part):
    own_key = jax.random.fold_in(key, 303)
    shape = (CLIPS, LAYERS, 6, D)
    values = jnp.clip(0.25 * jax.random.normal(own_key, shape, jnp.float32), -0.6, 0.6)
    return values


def with_ends(array, key, low, top_value):
    place = [jax.random.randint(jax.random.fold_in(key, axis), (), 0, length) for axis, length in enumerate(array.shape)]
    longest = array.shape.index(max(array.shape))
    beside = place[:longest] + [(place[longest] + 1) % array.shape[longest]] + place[longest + 1:]
    return array.at[tuple(place)].set(low).at[tuple(beside)].set(top_value)


def block_levels(rng, shape, split, smallest, high):
    factor_of, own = 1.0, jax.random.fold_in(rng, 6)
    for axis_at, blocks in split:
        draws = jnp.exp(jax.random.uniform(jax.random.fold_in(own, axis_at), (blocks,), jnp.float32, smallest / len(split), high / len(split)))
        factor_of = factor_of * jnp.repeat(draws, shape[axis_at] // blocks).reshape([-1 if axis == axis_at else 1 for axis in range(len(shape))])
    return factor_of


def bell_draw(key, shape, deviation, reach, pieces=(), held_as=jnp.bfloat16):
    entries = jax.random.normal(key, shape, jnp.float32) * deviation
    if len(pieces) > 0:
        entries = block_levels(key, shape, pieces, -0.22, 0.18) * entries
    return jnp.clip(entries, min=-reach, max=reach).astype(held_as)


def setup_inputs(seed: int = 0) -> dict:
    arg_keys = jax.random.split(jax.random.key(seed), 12)
    video = draw_video(jax.random.fold_in(arg_keys[11], 71), 0)
    context = draw_context(jax.random.fold_in(arg_keys[11], 71), 0)
    modulation = draw_modulation(jax.random.fold_in(arg_keys[11], 71), 0)
    adapter_index = with_ends(jax.random.randint(arg_keys[3], (CLIPS,), 0, ADAPTERS), jax.random.fold_in(arg_keys[3], 1), 0, ADAPTERS - 1).astype(jnp.int32)
    cotangent = bell_draw(arg_keys[4], (CLIPS, FRAMES * SPATIAL, D), 1.0, 6.0, ((0, 8), (1, 4)))
    qkv_weights = bell_draw(arg_keys[5], (LAYERS, 9, D, D), D ** -0.5, 0.1875, ((2, 8),))
    out_weights = bell_draw(arg_keys[6], (LAYERS, 3, D, D), (D // 4) ** -0.5, 0.375, ((2, 8),))
    ffn_up = bell_draw(arg_keys[7], (LAYERS, D, FF), D ** -0.5, 0.1875, ((1, 8),))
    ffn_down = bell_draw(arg_keys[8], (LAYERS, FF, D), FF ** -0.5, 0.09375, ((1, 8),))
    adapt_wide = bell_draw(arg_keys[9], (LAYERS, 26, ADAPTERS, RANK, D), (D // 4) ** -0.5, 0.375, ((4, 8),))
    adapt_ff = bell_draw(arg_keys[10], (LAYERS, 2, ADAPTERS, RANK, FF), (FF // 4) ** -0.5, 0.1875, ((4, 8),))
    return {"video": video, "context": context, "modulation": modulation, "adapter_index": adapter_index, "cotangent": cotangent, "qkv_weights": qkv_weights, "out_weights": out_weights, "ffn_up": ffn_up, "ffn_down": ffn_down, "adapt_wide": adapt_wide, "adapt_ff": adapt_ff}


HIGHEST = lax.Precision.HIGHEST

@jax.custom_vjp
def low(v):
    return lax.optimization_barrier(v.astype(jnp.bfloat16)).astype(jnp.float32)

@jax.custom_vjp
def low_back(v):
    return v

def low_keep(v):
    return (low(v), None)

def low_pass(kept, grad):
    return (grad,)

def back_keep(v):
    return (v, None)

def back_low(kept, grad):
    return (low(grad),)
low.defvjp(low_keep, low_pass)
low_back.defvjp(back_keep, back_low)

def both_round(values_in):
    return low_back(low(values_in))

def matmul(left, right):
    return jnp.dot(left, right, precision=HIGHEST)

def layer_norm(stream):
    average = lax.optimization_barrier(jnp.mean(stream, -1, keepdims=True))
    centred = stream - average
    return centred * lax.rsqrt(lax.optimization_barrier(jnp.mean(centred * centred, -1, keepdims=True)) + 1e-06)

def attention(queries, keys_in, values):
    scaling = HEAD_DIM ** (-0.5)
    scores = low_back(jnp.einsum('gqhe,gkhe->ghqk', queries, keys_in, precision=HIGHEST) * scaling)
    probabilities = jax.nn.softmax(scores, axis=-1)
    return both_round(jnp.einsum('ghqk,gkhe->gqhe', low(probabilities), values, precision=HIGHEST))

def token_project(inputs, weight, down_map, up_map):
    rank_term = both_round(matmul(inputs, down_map.T))
    return matmul(inputs, weight) + matmul(rank_term, up_map)

def context_project(inputs, weight, down_map, up_map):
    rank_term = low(matmul(inputs, down_map.T))
    return matmul(inputs, weight) + matmul(rank_term, up_map)

def layer_forward(stream, context_in, modulators, qkv_w, out_w, up_w, down_w, wide_sel, narrow_sel):
    length = stream.shape[0]

    def weight_of(number):
        if number % 4 == 3:
            return out_w[number // 4]
        return qkv_w[3 * (number // 4) + number % 4]

    def project_number(inputs, number):
        return token_project(inputs, weight_of(number), wide_sel[2 * number], wide_sel[2 * number + 1])
    normed = low(layer_norm(stream) * (1.0 + modulators[1]) + modulators[0])
    spatial = [both_round(project_number(normed, number)).reshape(FRAMES, SPATIAL, HEADS, HEAD_DIM) for number in range(3)]
    attended = attention(spatial[0], spatial[1], spatial[2]).reshape(length, D)
    stream = stream + modulators[2] * low_back(project_number(attended, 3))
    inputs = low(stream)
    temporal = [both_round(project_number(inputs, 4 + number)).reshape(FRAMES, SPATIAL, HEADS, HEAD_DIM).transpose(1, 0, 2, 3) for number in range(3)]
    attended = attention(temporal[0], temporal[1], temporal[2]).transpose(1, 0, 2, 3).reshape(length, D)
    stream = stream + modulators[2] * low_back(project_number(attended, 7))
    inputs = low(stream)
    queries = both_round(project_number(inputs, 8)).reshape(1, length, HEADS, HEAD_DIM)
    keys_in = low(context_project(context_in, qkv_w[7], wide_sel[18], wide_sel[19])).reshape(1, CTX, HEADS, HEAD_DIM)
    values = low(context_project(context_in, qkv_w[8], wide_sel[20], wide_sel[21])).reshape(1, CTX, HEADS, HEAD_DIM)
    attended = attention(queries, keys_in, values).reshape(length, D)
    stream = stream + low_back(project_number(attended, 11))
    normed = low(layer_norm(stream) * (1.0 + modulators[4]) + modulators[3])
    hidden = low_back(token_project(normed, up_w, wide_sel[24], narrow_sel[0]))
    activated = low(jax.nn.gelu(hidden, approximate=True))
    return stream + modulators[5] * low_back(token_project(activated, down_w, narrow_sel[1], wide_sel[25]))

def reference(video, context, modulation, adapter_index, cotangent, qkv_weights, out_weights, ffn_up, ffn_down, adapt_wide, adapt_ff):
    qkv_full = qkv_weights.astype(jnp.float32)
    out_full = out_weights.astype(jnp.float32)
    up_full = ffn_up.astype(jnp.float32)
    down_full = ffn_down.astype(jnp.float32)
    wide_all = adapt_wide.astype(jnp.float32)
    narrow_all = adapt_ff.astype(jnp.float32)

    def clip_step(running, clip_items):
        clip_video, clip_context, clip_mod, clip_index, clip_cot = clip_items
        context_in = clip_context.astype(jnp.float32)

        def forward(stream, wide_tables, narrow_tables):
            for layer_num in range(LAYERS):
                wide_sel = jnp.take(wide_tables[layer_num], clip_index, axis=1)
                narrow_sel = jnp.take(narrow_tables[layer_num], clip_index, axis=1)
                stream = layer_forward(stream, context_in, clip_mod[layer_num], qkv_full[layer_num], out_full[layer_num], up_full[layer_num], down_full[layer_num], wide_sel, narrow_sel)
            return stream
        result, pullback = jax.vjp(forward, clip_video.astype(jnp.float32), wide_all, narrow_all)
        grad_in, grad_wide, grad_narrow = pullback(clip_cot.astype(jnp.float32))
        return ((running[0] + grad_wide, running[1] + grad_narrow), (result.astype(jnp.bfloat16), grad_in.astype(jnp.bfloat16)))
    zero_sums = (jnp.zeros(adapt_wide.shape, jnp.float32), jnp.zeros(adapt_ff.shape, jnp.float32))
    totals, per_clip = lax.scan(clip_step, zero_sums, (video, context, modulation, adapter_index, cotangent))
    return (per_clip[0], per_clip[1], totals[0], totals[1])
```

```python
import math

import jax
import jax.numpy as jnp
from jax import lax
from jax.experimental import pallas as pl
from jax.experimental.pallas import tpu as pltpu
from jax.sharding import PartitionSpec as P

HEAD_DIM = 72
HEADS = 16
FRAMES = 16
SPATIAL = 256
RANK = 16
ROWS = 256
PAIRS = HEADS // 2
PAD = 128
SCALE = HEAD_DIM ** (-0.5)
EXP_SCALE = SCALE * math.log2(math.e)
HIGHEST = lax.Precision.HIGHEST
F32 = jnp.float32
BF16 = jnp.bfloat16
VMEM_LIMIT = 60 * 1024 * 1024


def nn(left, right):
    return lax.dot_general(left, right, (((1,), (0,)), ((), ())), preferred_element_type=F32)


def nt(left, right):
    return lax.dot_general(left, right, (((1,), (1,)), ((), ())), preferred_element_type=F32)


def tn(left, right):
    return lax.dot_general(left, right, (((0,), (0,)), ((), ())), preferred_element_type=F32)


def window(pair):
    return slice(128 * pair, 128 * pair + 256)


def normalize(stream):
    average = jnp.mean(stream, -1, keepdims=True)
    centred = stream - average
    inverse = lax.rsqrt(jnp.mean(centred * centred, -1, keepdims=True) + 1e-06)
    return centred * inverse, inverse


def normalize_back(normal, inverse, grad):
    mean_grad = jnp.mean(grad, -1, keepdims=True)
    mean_both = jnp.mean(grad * normal, -1, keepdims=True)
    return inverse * (grad - mean_grad - normal * mean_both)


def spread_rank(ad_ref, base, number):
    rows = ad_ref[base + 2 * number + 1]
    nothing = jnp.zeros_like(rows)
    return jnp.concatenate([rows if i == number else nothing for i in range(3)], 0)


def three_downs(ad_ref, base):
    return jnp.concatenate([ad_ref[base], ad_ref[base + 2], ad_ref[base + 4]], 0)


class Loads:
    def __init__(self, entries, sems):
        self.first = pl.program_id(0) == 0
        self.entries = entries
        self.sems = sems

    def copy(self, index):
        source, target = self.entries[index]
        return pltpu.make_async_copy(source, target, self.sems.at[index])

    def start(self):
        @pl.when(self.first)
        def _():
            for index in range(len(self.entries)):
                self.copy(index).start()

    def ready(self, index):
        @pl.when(self.first)
        def _():
            self.copy(index).wait()


def head_masks():
    lane = jnp.arange(256)[None, :]
    begin = jnp.array([16 * (h // 2) + HEAD_DIM * (h % 2) for h in range(HEADS)])[:, None]
    return ((lane >= begin) & (lane < begin + HEAD_DIM)).astype(BF16)


def same_place(shape):
    rows = lax.broadcasted_iota(jnp.int32, shape, 0)
    cols = lax.broadcasted_iota(jnp.int32, shape, 1)
    return jnp.where(rows % 16 == cols % 16, 0.0, -1e30).astype(F32)


def attend(q_ref, k_ref, v_ref, mask_ref, bias, put_out, stat_ref):
    carried = None
    for pair in range(PAIRS):
        win = window(pair)
        q_win, k_win, v_win = q_ref[:, win], k_ref[:, win], v_ref[:, win]
        out = None
        for head in (2 * pair, 2 * pair + 1):
            mask = mask_ref[head : head + 1, :]
            scores = nt(k_win * mask, q_win) * EXP_SCALE
            if bias is not None:
                scores = scores + bias[...]
            top = jnp.max(scores, 0, keepdims=True)
            grown = jnp.exp2(scores - top)
            total = jnp.sum(grown, 0, keepdims=True)
            stat_ref[head : head + 1, :] = top + jnp.log2(total)
            weights = (grown * (1.0 / total)).astype(BF16)
            part = tn(weights, v_win * mask)
            out = part if out is None else out + part
        low = out[:, :128]
        put_out(pair, low if carried is None else low + carried)
        carried = out[:, 128:]
    put_out(PAIRS, carried)


def attend_back(q_ref, k_ref, v_ref, do_ref, mask_ref, bias, stat_ref, put):
    carried = None
    for pair in range(PAIRS):
        win = window(pair)
        q_win, k_win, v_win, do_win = q_ref[:, win], k_ref[:, win], v_ref[:, win], do_ref[:, win]
        grads = None
        for head in (2 * pair, 2 * pair + 1):
            mask = mask_ref[head : head + 1, :]
            k_own = k_win * mask
            scores = nt(k_own, q_win) * EXP_SCALE
            if bias is not None:
                scores = scores + bias[...]
            probs = jnp.exp2(scores - stat_ref[head : head + 1, :])
            grad_probs = nt(v_win * mask, do_win)
            inner = jnp.sum(probs * grad_probs, 0, keepdims=True)
            grad_scores = (probs * (grad_probs - inner)).astype(BF16)
            parts = (
                tn(grad_scores, k_own),
                nn(grad_scores, q_win * mask),
                nn(probs.astype(BF16), do_win * mask),
            )
            grads = parts if grads is None else tuple(a + b for a, b in zip(grads, parts))
        lows = tuple(g[:, :128] for g in grads)
        if carried is not None:
            lows = tuple(a + b for a, b in zip(lows, carried))
        put(pair, lows)
        carried = tuple(g[:, 128:] for g in grads)
    put(PAIRS, carried)


def tile(index):
    return slice(128 * index, 128 * index + 128)


def three_projections(inputs, ad_ref, base, weights, loads, first_load, outs, rank_ref):
    ranks = nt(inputs, three_downs(ad_ref, base)).astype(BF16)
    rank_ref[...] = ranks
    for number in range(3):
        loads.ready(first_load + number)
        total = nn(inputs, weights[first_load + number]) + nn(
            ranks, spread_rank(ad_ref, base, number)
        )
        outs[number][...] = total.astype(BF16)


def one_projection(inputs, ad_ref, base, weight_ref, rank_ref):
    ranks = nt(inputs, ad_ref[base]).astype(BF16)
    rank_ref[...] = ranks
    return nn(inputs, weight_ref[...]) + nn(ranks, ad_ref[base + 1])


def one_back(grad, kept, ranks, ad_ref, base, weight_ref, grad_ref, at):
    grad_rank = nt(grad, ad_ref[base + 1]).astype(BF16)
    grad_ref[at] += tn(grad_rank, kept)
    grad_ref[at + 1] += tn(ranks, grad)
    return nt(grad, weight_ref[...]) + nn(grad_rank, ad_ref[base])


def three_back(grads, inputs, ranks, ad_ref, base, weights, loads, first_load, grad_ref, at):
    grad_ranks = None
    total = None
    for number in range(3):
        grad = grads[number][...]
        part = nt(grad, spread_rank(ad_ref, base, number))
        grad_ranks = part if grad_ranks is None else grad_ranks + part
        ups = tn(ranks, grad)
        grad_ref[at + 2 * number + 1] += ups[RANK * number : RANK * (number + 1)]
        loads.ready(first_load + number)
        part = nt(grad, weights[first_load + number])
        total = part if total is None else total + part
    grad_ranks = grad_ranks.astype(BF16)
    downs = tn(grad_ranks, inputs)
    for number in range(3):
        grad_ref[at + 2 * number] += downs[RANK * number : RANK * (number + 1)]
    return total + nn(grad_ranks, three_downs(ad_ref, base))


def spatial_forward(
    x_ref, mod_ref, mask_ref, ad_ref, w_hbm, x1_ref, q_ref, k_ref, v_ref, o_ref, stat_ref, rq_ref, ro_ref, w_ref, sems
):
    loads = Loads([(w_hbm.at[i], w_ref.at[i]) for i in range(4)], sems)
    loads.start()
    stream = x_ref[0].astype(F32)
    normal, _ = normalize(stream)
    inputs = (normal * (1.0 + mod_ref[1:2, :]) + mod_ref[0:1, :]).astype(BF16)
    q, k, v, o = q_ref.at[0], k_ref.at[0], v_ref.at[0], o_ref.at[0]
    three_projections(inputs, ad_ref, 0, w_ref, loads, 0, (q, k, v), rq_ref.at[0])

    def put_out(index, value):
        o[:, tile(index)] = value.astype(BF16)

    attend(q, k, v, mask_ref, None, put_out, stat_ref.at[0])
    loads.ready(3)
    branch = one_projection(o[...], ad_ref, 6, w_ref.at[3], ro_ref.at[0])
    result = (stream + mod_ref[2:3, :] * branch).astype(BF16)
    x1_ref[...] = result.reshape(x1_ref.shape)


def temporal_cross_forward(
    x_ref, ctx_ref, mod_ref, mask_ref, ad_ref, wt_hbm, wc_hbm,
    q_ref, k_ref, v_ref, o_ref, stat_ref, rq_ref, ro_ref,
    u2_ref, qc_ref, oc_ref, statc_ref, rqc_ref, roc_ref, kp_ref, vp_ref, rk_ref, rv_ref, x3_ref,
    w_ref, bias_ref, q_s, k_s, v_s, o_s, sems,
):
    first = pl.program_id(0) == 0
    loads = Loads(
        [(wt_hbm.at[i], w_ref.at[i]) for i in range(4)]
        + [(wc_hbm.at[i], w_ref.at[4 + i]) for i in range(4)],
        sems,
    )
    loads.start()

    @pl.when(first)
    def _():
        bias_ref[...] = same_place(bias_ref.shape)

    loaded = x_ref[...].reshape(ROWS, x_ref.shape[2])
    stream = loaded.astype(F32)
    three_projections(loaded, ad_ref, 8, w_ref, loads, 0, (q_s, k_s, v_s), rq_ref.at[0])
    q_ref[...] = q_s[...].reshape(q_ref.shape)
    k_ref[...] = k_s[...].reshape(k_ref.shape)
    v_ref[...] = v_s[...].reshape(v_ref.shape)

    def put_out(index, value):
        o_s[:, tile(index)] = value.astype(BF16)

    attend(q_s, k_s, v_s, mask_ref, bias_ref, put_out, stat_ref.at[0])
    o_ref[...] = o_s[...].reshape(o_ref.shape)
    loads.ready(3)
    branch = one_projection(o_s[...], ad_ref, 14, w_ref.at[3], ro_ref.at[0])
    stream = stream + mod_ref[2:3, :] * branch
    inputs = stream.astype(BF16)
    u2_ref[...] = inputs.reshape(u2_ref.shape)
    loads.ready(4)
    queries = one_projection(inputs, ad_ref, 16, w_ref.at[4], rqc_ref.at[0])
    q_s[...] = queries.astype(BF16)
    qc_ref[...] = q_s[...].reshape(qc_ref.shape)
    loads.ready(5)
    loads.ready(6)

    @pl.when(first)
    def _():
        for base, at, rank_ref, pair_ref in ((18, 5, rk_ref, kp_ref), (20, 6, rv_ref, vp_ref)):
            made = one_projection(ctx_ref[...], ad_ref, base, w_ref.at[at], rank_ref).astype(BF16)
            k_s[:PAD, :] = made
            for pair in range(PAIRS):
                piece = k_s[:PAD, window(pair)]
                pair_ref[pair, :PAD, :] = piece * mask_ref[2 * pair : 2 * pair + 1, :]
                pair_ref[pair, PAD:, :] = piece * mask_ref[2 * pair + 1 : 2 * pair + 2, :]

    carried = None
    count = rk_ref.shape[0] - (PAD - 120)
    for pair in range(PAIRS):
        scores = nt(kp_ref[pair], q_s[:, window(pair)]) * EXP_SCALE
        pieces = []
        for sub in range(2):
            own = scores[PAD * sub : PAD * sub + count]
            top = jnp.max(own, 0, keepdims=True)
            grown = jnp.exp2(own - top)
            total = jnp.sum(grown, 0, keepdims=True)
            statc_ref[0, 2 * pair + sub : 2 * pair + sub + 1, :] = top + jnp.log2(total)
            pieces += [grown * (1.0 / total), jnp.zeros((PAD - count, ROWS), F32)]
        weights = jnp.concatenate(pieces, 0).astype(BF16)
        out = tn(weights, vp_ref[pair])
        low = out[:, :128]
        put_out(pair, low if carried is None else low + carried)
        carried = out[:, 128:]
    put_out(PAIRS, carried)
    oc_ref[...] = o_s[...].reshape(oc_ref.shape)
    loads.ready(7)
    stream = stream + one_projection(o_s[...], ad_ref, 22, w_ref.at[7], roc_ref.at[0])
    x3_ref[...] = stream.reshape(x3_ref.shape)


def gelu_both(hidden):
    root = math.sqrt(2.0 / math.pi)
    square = hidden * hidden
    inner = root * (hidden + 0.044715 * (square * hidden))
    bent = jnp.tanh(inner)
    half = 0.5 * (1.0 + bent)
    slope = half + 0.5 * hidden * (1.0 - bent * bent) * (root * (1.0 + 3.0 * 0.044715 * square))
    return hidden * half, slope


def feed_forward(
    x3_ref, cot_ref, mod_ref, ad_ref, ff_ref, up_hbm, down_hbm,
    x4_ref, g3_ref, gw_ref, gf_ref, up_ref, down_ref, sems,
):
    width = x3_ref.shape[1]
    chunks = down_ref.shape[0]
    loads = Loads(
        [(up_hbm.at[:, pl.ds(c * width, width)], up_ref.at[c]) for c in range(chunks)]
        + [(down_hbm.at[pl.ds(c * width, width), :], down_ref.at[c]) for c in range(chunks)],
        sems,
    )
    loads.start()

    @pl.when(pl.program_id(0) == 0)
    def _():
        gw_ref[...] = jnp.zeros_like(gw_ref)
        gf_ref[...] = jnp.zeros_like(gf_ref)

    stream = x3_ref[...]
    normal, inverse = normalize(stream)
    inputs = (normal * (1.0 + mod_ref[4:5, :]) + mod_ref[3:4, :]).astype(BF16)
    cot = cot_ref[...].astype(F32)
    grad_branch = (mod_ref[5:6, :] * cot).astype(BF16)
    rank_up = nt(inputs, ad_ref[0]).astype(BF16)
    grad_rank_down = nt(grad_branch, ad_ref[1]).astype(BF16)
    branch = None
    rank_down = None
    grad_in = None
    grad_rank_up = None

    def add(old, new):
        return new if old is None else old + new

    for c in range(chunks):
        cols = slice(c * width, c * width + width)
        loads.ready(c)
        hidden = nn(inputs, up_ref[c]) + nn(rank_up, ff_ref[0, :, cols])
        active, slope = gelu_both(hidden)
        active = active.astype(BF16)
        loads.ready(chunks + c)
        grad_active = nt(grad_branch, down_ref[c]) + nn(grad_rank_down, ff_ref[1, :, cols])
        grad_hidden = (slope * grad_active).astype(BF16)
        branch = add(branch, nn(active, down_ref[c]))
        rank_down = add(rank_down, nt(active, ff_ref[1, :, cols]))
        grad_in = add(grad_in, nt(grad_hidden, up_ref[c]))
        grad_rank_up = add(grad_rank_up, nt(grad_hidden, ff_ref[0, :, cols]))
        gf_ref[0, :, cols] += tn(rank_up, grad_hidden)
        gf_ref[1, :, cols] += tn(grad_rank_down, active)
    rank_down = rank_down.astype(BF16)
    grad_rank_up = grad_rank_up.astype(BF16)
    branch = branch + nn(rank_down, ad_ref[1])
    x4_ref[...] = (stream + mod_ref[5:6, :] * branch).astype(BF16)
    grad_in = grad_in + nn(grad_rank_up, ad_ref[0])
    gw_ref[0] += tn(grad_rank_up, inputs)
    gw_ref[1] += tn(rank_down, grad_branch)
    g3_ref[...] = cot + normalize_back(normal, inverse, grad_in * (1.0 + mod_ref[4:5, :]))


def cross_temporal_backward(
    g3_ref, u1_ref, q_ref, k_ref, v_ref, o_ref, stat_ref, rq_ref, ro_ref,
    u2_ref, qc_ref, oc_ref, statc_ref, rqc_ref, roc_ref, kp_ref, vp_ref, rk_ref, rv_ref,
    ctx_ref, mod_ref, mask_ref, ad_ref, wt_hbm, wc_hbm,
    g1_ref, gw_ref,
    w_ref, bias_ref, dk_acc, dv_acc, q_s, k_s, v_s, do_s, dq_s, dk_s, dv_s, ctx_s, sems,
):
    step = pl.program_id(0)
    first = step == 0
    loads = Loads(
        [(wc_hbm.at[3], w_ref.at[0]), (wc_hbm.at[0], w_ref.at[1]), (wt_hbm.at[3], w_ref.at[2])]
        + [(wt_hbm.at[i], w_ref.at[3 + i]) for i in range(3)],
        sems,
    )
    loads.start()

    @pl.when(first)
    def _():
        bias_ref[...] = same_place(bias_ref.shape)
        gw_ref[...] = jnp.zeros_like(gw_ref)
        dk_acc[...] = jnp.zeros_like(dk_acc)
        dv_acc[...] = jnp.zeros_like(dv_acc)

    def rows(ref):
        return ref[...].reshape(ROWS, ref.shape[2])

    grad = rows(g3_ref)
    loads.ready(0)
    do_s[...] = one_back(
        grad.astype(BF16), rows(oc_ref), roc_ref[0], ad_ref, 22, w_ref.at[0], gw_ref, 14
    ).astype(BF16)
    q_s[...] = rows(qc_ref)
    count = 120
    carried = None
    for pair in range(PAIRS):
        win = window(pair)
        q_win, do_win = q_s[:, win], do_s[:, win]
        scores = nt(kp_ref[pair], q_win) * EXP_SCALE
        grad_probs = nt(vp_ref[pair], do_win)
        all_probs, all_grads = [], []
        nothing = jnp.zeros((PAD - count, ROWS), F32)
        for sub in range(2):
            span = slice(PAD * sub, PAD * sub + count)
            row = 2 * pair + sub
            probs = jnp.exp2(scores[span] - statc_ref[0, row : row + 1, :])
            own = grad_probs[span]
            inner = jnp.sum(probs * own, 0, keepdims=True)
            all_probs += [probs, nothing]
            all_grads += [probs * (own - inner), nothing]
        probs = jnp.concatenate(all_probs, 0).astype(BF16)
        grad_scores = jnp.concatenate(all_grads, 0).astype(BF16)
        dk_acc[pair] += nn(grad_scores, q_win)
        dv_acc[pair] += nn(probs, do_win)
        out = tn(grad_scores, kp_ref[pair])
        low = out[:, :128]
        dq_s[:, tile(pair)] = ((low if carried is None else low + carried) * SCALE).astype(BF16)
        carried = out[:, 128:]
    dq_s[:, tile(PAIRS)] = (carried * SCALE).astype(BF16)
    loads.ready(1)
    grad = grad + one_back(
        dq_s[...], rows(u2_ref), rqc_ref[0], ad_ref, 16, w_ref.at[1], gw_ref, 8
    )
    loads.ready(2)
    do_s[...] = one_back(
        (mod_ref[2:3, :] * grad).astype(BF16), rows(o_ref), ro_ref[0], ad_ref, 14, w_ref.at[2], gw_ref, 6
    ).astype(BF16)
    q_s[...] = rows(q_ref)
    k_s[...] = rows(k_ref)
    v_s[...] = rows(v_ref)

    def put(index, values):
        dq_s[:, tile(index)] = (values[0] * SCALE).astype(BF16)
        dk_s[:, tile(index)] = (values[1] * SCALE).astype(BF16)
        dv_s[:, tile(index)] = values[2].astype(BF16)

    attend_back(q_s, k_s, v_s, do_s, mask_ref, bias_ref, stat_ref.at[0], put)
    grad = grad + three_back(
        (dq_s, dk_s, dv_s), rows(u1_ref), rq_ref[0], ad_ref, 8, w_ref, loads, 3, gw_ref, 0
    )
    g1_ref[...] = grad.astype(BF16).reshape(g1_ref.shape)

    @pl.when(step == pl.num_programs(0) - 1)
    def _():
        context = ctx_ref[...].astype(F32)
        for acc, factor, rank_ref, base, at in (
            (dk_acc, SCALE, rk_ref, 18, 10),
            (dv_acc, 1.0, rv_ref, 20, 12),
        ):
            held = None
            for pair in range(PAIRS):
                whole = acc[pair]
                out = whole[:PAD] * mask_ref[2 * pair : 2 * pair + 1, :].astype(F32)
                out = out + whole[PAD:] * mask_ref[2 * pair + 1 : 2 * pair + 2, :].astype(F32)
                out = out * factor
                low = out[:, :128]
                ctx_s[:, tile(pair)] = low if held is None else low + held
                held = out[:, 128:]
            ctx_s[:, tile(PAIRS)] = held
            grad_kv = ctx_s[...]
            grad_rank = lax.dot_general(
                grad_kv, ad_ref[base + 1].astype(F32), (((1,), (1,)), ((), ())),
                precision=HIGHEST, preferred_element_type=F32,
            )
            gw_ref[at] = lax.dot_general(
                grad_rank, context, (((0,), (0,)), ((), ())),
                precision=HIGHEST, preferred_element_type=F32,
            )
            gw_ref[at + 1] = lax.dot_general(
                rank_ref[...].astype(F32), grad_kv, (((0,), (0,)), ((), ())),
                precision=HIGHEST, preferred_element_type=F32,
            )


def spatial_backward(
    g1_ref, x_ref, q_ref, k_ref, v_ref, o_ref, stat_ref, rq_ref, ro_ref, mod_ref, mask_ref, ad_ref, w_hbm,
    g0_ref, gw_ref, w_ref, do_s, dq_s, dk_s, dv_s, sems,
):
    loads = Loads(
        [(w_hbm.at[3], w_ref.at[0])] + [(w_hbm.at[i], w_ref.at[1 + i]) for i in range(3)], sems
    )
    loads.start()

    @pl.when(pl.program_id(0) == 0)
    def _():
        gw_ref[...] = jnp.zeros_like(gw_ref)

    grad = g1_ref[...].reshape(ROWS, g1_ref.shape[3]).astype(F32)
    loads.ready(0)
    do_s[...] = one_back(
        (mod_ref[2:3, :] * grad).astype(BF16), o_ref[0], ro_ref[0], ad_ref, 6, w_ref.at[0], gw_ref, 6
    ).astype(BF16)

    def put(index, values):
        dq_s[:, tile(index)] = (values[0] * SCALE).astype(BF16)
        dk_s[:, tile(index)] = (values[1] * SCALE).astype(BF16)
        dv_s[:, tile(index)] = values[2].astype(BF16)

    attend_back(
        q_ref.at[0], k_ref.at[0], v_ref.at[0], do_s, mask_ref, None, stat_ref.at[0], put
    )
    normal, inverse = normalize(x_ref[0].astype(F32))
    inputs = (normal * (1.0 + mod_ref[1:2, :]) + mod_ref[0:1, :]).astype(BF16)
    grad_in = three_back(
        (dq_s, dk_s, dv_s), inputs, rq_ref[0], ad_ref, 0, w_ref, loads, 1, gw_ref, 0
    )
    grad = grad + normalize_back(normal, inverse, grad_in * (1.0 + mod_ref[1:2, :]))
    g0_ref[0] = grad.astype(BF16)


def whole_block(array):
    zeros = (0,) * array.ndim
    return pl.BlockSpec(array.shape, lambda i: zeros)


def anywhere():
    return pl.BlockSpec(memory_space=pl.ANY)


def like(shape, dtype):
    return jax.ShapeDtypeStruct(shape, dtype)


PARAMS = pltpu.CompilerParams(
    dimension_semantics=("arbitrary",), vmem_limit_bytes=VMEM_LIMIT
)


def cost(flops, read):
    return pl.CostEstimate(flops=flops, bytes_accessed=read, transcendentals=flops // 4096)


def run_spatial_forward(video, mods, masks, wide, w_s, parts):
    frames, rows, d = video.shape
    places = rows // parts
    by_frame = lambda i: (i, 0, 0)
    row_block = pl.BlockSpec((1, rows, d), by_frame)
    return pl.pallas_call(
        spatial_forward,
        grid=(frames,),
        in_specs=[row_block, whole_block(mods), whole_block(masks), whole_block(wide), anywhere()],
        out_specs=[
            pl.BlockSpec((parts, 1, places, d), lambda i: (0, i, 0, 0)),
            row_block,
            row_block,
            row_block,
            row_block,
            pl.BlockSpec((1, HEADS, rows), by_frame),
            pl.BlockSpec((1, rows, 3 * RANK), by_frame),
            pl.BlockSpec((1, rows, RANK), by_frame),
        ],
        out_shape=[like((parts, frames, places, d), BF16)]
        + [like(video.shape, BF16)] * 4
        + [
            like((frames, HEADS, rows), F32),
            like((frames, rows, 3 * RANK), BF16),
            like((frames, rows, RANK), BF16),
        ],
        scratch_shapes=[pltpu.VMEM((4, d, d), BF16), pltpu.SemaphoreType.DMA((4,))],
        compiler_params=PARAMS,
        cost_estimate=cost(10 * frames * rows * d * d, 30_000_000),
        name="spatial_forward",
    )(video, mods, masks, wide, w_s)


def run_temporal_cross_forward(x1, context, mods, masks, wide, w_t, w_c):
    frames, places, d = x1.shape
    groups = places * frames // ROWS
    across = pl.BlockSpec((frames, ROWS // frames, d), lambda i: (0, i, 0))
    by_group = lambda i: (i, 0, 0)
    stat = pl.BlockSpec((1, HEADS, ROWS), by_group)
    three = pl.BlockSpec((1, ROWS, 3 * RANK), by_group)
    one = pl.BlockSpec((1, ROWS, RANK), by_group)
    full = lambda *shape: pl.BlockSpec(shape, lambda i: (0,) * len(shape))
    act = like(x1.shape, BF16)
    stat_shape = like((groups, HEADS, ROWS), F32)
    one_shape = like((groups, ROWS, RANK), BF16)
    return pl.pallas_call(
        temporal_cross_forward,
        grid=(groups,),
        in_specs=[across, whole_block(context), whole_block(mods), whole_block(masks), whole_block(wide), anywhere(), anywhere()],
        out_specs=[across] * 4 + [stat, three, one] + [across] * 3 + [stat, one, one]
        + [full(PAIRS, 2 * PAD, 256)] * 2 + [full(PAD, RANK)] * 2 + [across],
        out_shape=[act] * 4 + [stat_shape, like((groups, ROWS, 3 * RANK), BF16), one_shape]
        + [act] * 3 + [stat_shape, one_shape, one_shape]
        + [like((PAIRS, 2 * PAD, 256), BF16)] * 2 + [like((PAD, RANK), BF16)] * 2
        + [like(x1.shape, F32)],
        scratch_shapes=[pltpu.VMEM((8, d, d), BF16), pltpu.VMEM((ROWS, ROWS), F32)]
        + [pltpu.VMEM((ROWS, d), BF16)] * 4
        + [pltpu.SemaphoreType.DMA((8,))],
        compiler_params=PARAMS,
        cost_estimate=cost(14 * places * frames * d * d, 50_000_000),
        name="temporal_cross_forward",
    )(x1, context, mods, masks, wide, w_t, w_c)


def run_feed_forward(x3, cot, mods, wide_ff, narrow, up, down):
    tokens, d = x3.shape
    hidden = up.shape[1]
    chunks = hidden // d
    rows = pl.BlockSpec((ROWS, d), lambda i: (i, 0))
    return pl.pallas_call(
        feed_forward,
        grid=(tokens // ROWS,),
        in_specs=[rows, rows, whole_block(mods), whole_block(wide_ff), whole_block(narrow), anywhere(), anywhere()],
        out_specs=[
            rows,
            rows,
            pl.BlockSpec((2, RANK, d), lambda i: (0, 0, 0)),
            pl.BlockSpec((2, RANK, hidden), lambda i: (0, 0, 0)),
        ],
        out_shape=[
            like((tokens, d), BF16),
            like((tokens, d), F32),
            like((2, RANK, d), F32),
            like((2, RANK, hidden), F32),
        ],
        scratch_shapes=[
            pltpu.VMEM((chunks, d, d), BF16),
            pltpu.VMEM((chunks, d, d), BF16),
            pltpu.SemaphoreType.DMA((2 * chunks,)),
        ],
        compiler_params=PARAMS,
        cost_estimate=cost(8 * tokens * d * hidden, 50_000_000),
        name="feed_forward",
    )(x3, cot, mods, wide_ff, narrow, up, down)


def run_cross_temporal_backward(g3, u1, saved, context, mods, masks, wide, w_t, w_c):
    frames, places, d = u1.shape
    groups = places * frames // ROWS
    across = pl.BlockSpec((frames, ROWS // frames, d), lambda i: (0, i, 0))
    by_group = lambda i: (i, 0, 0)
    stat = pl.BlockSpec((1, HEADS, ROWS), by_group)
    three = pl.BlockSpec((1, ROWS, 3 * RANK), by_group)
    one = pl.BlockSpec((1, ROWS, RANK), by_group)
    kp, vp, rk, rv = saved[13:17]
    return pl.pallas_call(
        cross_temporal_backward,
        grid=(groups,),
        in_specs=[across, across] + [across] * 4 + [stat, three, one] + [across] * 3 + [stat, one, one]
        + [whole_block(kp), whole_block(vp), whole_block(rk), whole_block(rv)]
        + [whole_block(context), whole_block(mods), whole_block(masks), whole_block(wide), anywhere(), anywhere()],
        out_specs=[across, pl.BlockSpec((16, RANK, d), lambda i: (0, 0, 0))],
        out_shape=[like(u1.shape, BF16), like((16, RANK, d), F32)],
        scratch_shapes=[
            pltpu.VMEM((6, d, d), BF16),
            pltpu.VMEM((ROWS, ROWS), F32),
            pltpu.VMEM((PAIRS, 2 * PAD, 256), F32),
            pltpu.VMEM((PAIRS, 2 * PAD, 256), F32),
        ]
        + [pltpu.VMEM((ROWS, d), BF16)] * 7
        + [pltpu.VMEM((PAD, d), F32), pltpu.SemaphoreType.DMA((6,))],
        compiler_params=PARAMS,
        cost_estimate=cost(14 * places * frames * d * d, 50_000_000),
        name="cross_temporal_backward",
    )(g3, u1, *saved[:17], context, mods, masks, wide, w_t, w_c)


def run_spatial_backward(g1, video, saved, mods, masks, wide, w_s):
    frames, rows, d = video.shape
    parts, _, places, _ = g1.shape
    by_frame = lambda i: (i, 0, 0)
    row_block = pl.BlockSpec((1, rows, d), by_frame)
    return pl.pallas_call(
        spatial_backward,
        grid=(frames,),
        in_specs=[pl.BlockSpec((parts, 1, places, d), lambda i: (0, i, 0, 0))]
        + [row_block] * 5
        + [
            pl.BlockSpec((1, HEADS, rows), by_frame),
            pl.BlockSpec((1, rows, 3 * RANK), by_frame),
            pl.BlockSpec((1, rows, RANK), by_frame),
            whole_block(mods),
            whole_block(masks),
            whole_block(wide),
            anywhere(),
        ],
        out_specs=[row_block, pl.BlockSpec((8, RANK, d), lambda i: (0, 0, 0))],
        out_shape=[like(video.shape, BF16), like((8, RANK, d), F32)],
        scratch_shapes=[pltpu.VMEM((4, d, d), BF16)]
        + [pltpu.VMEM((ROWS, d), BF16)] * 4
        + [pltpu.SemaphoreType.DMA((4,))],
        compiler_params=PARAMS,
        cost_estimate=cost(10 * frames * rows * d * d, 30_000_000),
        name="spatial_backward",
    )(g1, video, *saved, mods, masks, wide, w_s)


def exchange(array):
    return lax.all_to_all(array, "seq", split_axis=0, concat_axis=0, tiled=True)


def exchange_clips(array):
    return lax.all_to_all(array, "fsdp", split_axis=0, concat_axis=0, tiled=True)


def fetch_adapters(choice, adapt_wide, adapt_ff):
    clips = choice.shape[0]
    narrow_cols, cols = adapt_ff.shape[-1], adapt_wide.shape[-1]
    times = narrow_cols // cols
    narrow = adapt_ff.reshape(adapt_ff.shape[:-1] + (times, cols))
    narrow = jnp.moveaxis(narrow, 3, 1).reshape(2 * times, *adapt_wide.shape[1:])
    table = jnp.concatenate([adapt_wide, narrow], 0)
    picked = jnp.sum(
        choice[:, None, :, None, None] * table[None].astype(F32), axis=2
    ).astype(BF16)
    got = exchange_clips(picked)
    count = adapt_wide.shape[0]
    wide = jnp.moveaxis(got[:, :count], 0, 2).reshape(count, RANK, clips * cols)
    narrow = got[:, count:].reshape(clips, 2, times, RANK, cols)
    narrow = narrow.transpose(1, 3, 0, 2, 4).reshape(2, RANK, clips * narrow_cols)
    return wide, narrow


def collect_grads(choice, wide, narrow):
    clips = choice.shape[0]
    count, _, d = wide.shape
    cols = d // clips
    times = narrow.shape[-1] // d
    wide = jnp.moveaxis(wide.astype(BF16).reshape(count, RANK, clips, cols), 2, 0)
    narrow = narrow.astype(BF16).reshape(2, RANK, clips, times, cols)
    narrow = narrow.transpose(2, 0, 3, 1, 4).reshape(clips, 2 * times, RANK, cols)
    got = exchange_clips(jnp.concatenate([wide, narrow], 1))
    table = jnp.sum(
        choice[:, None, :, None, None] * got[:, :, None].astype(F32), axis=0
    )
    total = lax.psum(table.astype(BF16), "seq").astype(F32)
    wide_out = total[:count]
    narrow_out = total[count:].reshape(2, times, -1, RANK, cols)
    narrow_out = jnp.moveaxis(narrow_out, 1, 3).reshape(2, -1, RANK, times * cols)
    return wide_out, narrow_out


def on_device(
    video,
    context,
    modulation,
    adapter_index,
    cotangent,
    qkv_weights,
    out_weights,
    ffn_up,
    ffn_down,
    adapt_wide,
    adapt_ff,
):
    parts = lax.axis_size("seq")
    clips = lax.axis_size("fsdp")
    d = video.shape[-1]
    places = SPATIAL // parts
    frames = FRAMES // parts
    mods = modulation[0, 0]
    masks = head_masks()
    ctx = jnp.pad(context[0], ((0, PAD - context.shape[1]), (0, 0)))

    def gather(array, axis):
        return lax.all_gather(array, "fsdp", axis=axis, tiled=True)

    all_index = exchange_clips(jnp.broadcast_to(adapter_index, (clips,)))
    choice = (all_index[:, None] == jnp.arange(adapt_wide.shape[2])[None, :]).astype(F32)
    wide, narrow = fetch_adapters(choice, adapt_wide[0], adapt_ff[0])
    quads = [
        gather(jnp.concatenate([qkv_weights[0, 3 * j : 3 * j + 3], out_weights[0, j : j + 1]], 0), 1)
        for j in range(3)
    ]
    down = gather(ffn_down[0], 0)
    up = gather(ffn_up[0], 0)

    cot = cotangent.reshape(frames, parts, places, d).transpose(1, 0, 2, 3)
    cot = exchange(cot).reshape(FRAMES * places, d)
    frames_in = video.reshape(frames, SPATIAL, d)
    x1, *kept_s = run_spatial_forward(frames_in, mods, masks, wide, quads[0], parts)
    u1 = exchange(x1).reshape(FRAMES, places, d)
    *kept_t, x3 = run_temporal_cross_forward(u1, ctx, mods, masks, wide, quads[1], quads[2])
    x4, g3, grads_f, narrow_grads = run_feed_forward(
        x3.reshape(FRAMES * places, d), cot, mods, wide[24:26], narrow, up, down
    )
    output = exchange(x4.reshape(parts, frames, places, d))
    output = output.transpose(1, 0, 2, 3).reshape(video.shape)
    g1, grads_t = run_cross_temporal_backward(
        g3.reshape(FRAMES, places, d), u1, kept_t, ctx, mods, masks, wide, quads[1], quads[2]
    )
    g1 = exchange(g1.reshape(parts, frames, places, d))
    g0, grads_s = run_spatial_backward(g1, frames_in, kept_s, mods, masks, wide, quads[0])
    wide_grads = jnp.concatenate([grads_s, grads_t, grads_f], 0)
    wide_out, narrow_out = collect_grads(choice, wide_grads, narrow_grads)
    return (output, g0.reshape(video.shape), wide_out[None], narrow_out[None])


def solution(mesh):
    return jax.shard_map(
        on_device,
        mesh=mesh,
        in_specs=(
            P("fsdp", "seq", None),
            P("fsdp", None, None),
            P("fsdp", None, None, None),
            P("fsdp"),
            P("fsdp", "seq", None),
            P(None, None, "fsdp", None),
            P(None, None, "fsdp", None),
            P(None, "fsdp", None),
            P(None, "fsdp", None),
            P(None, None, None, None, "fsdp"),
            P(None, None, None, None, "fsdp"),
        ),
        out_specs=(
            P("fsdp", "seq", None),
            P("fsdp", "seq", None),
            P(None, None, None, None, "fsdp"),
            P(None, None, None, None, "fsdp"),
        ),
        check_vma=False,
    )
```

```python
import math

import jax
import jax.numpy as jnp
from jax import lax
from jax.experimental import pallas as pl
from jax.experimental.pallas import tpu as pltpu
from jax.sharding import PartitionSpec as P

HEAD_DIM = 72
HEADS = 16
FRAMES = 16
SPATIAL = 256
RANK = 16
ROWS = 256
PAIRS = HEADS // 2
PAD = 128
SCALE = HEAD_DIM ** (-0.5)
EXP_SCALE = SCALE * math.log2(math.e)
HIGHEST = lax.Precision.HIGHEST
F32 = jnp.float32
BF16 = jnp.bfloat16
VMEM_LIMIT = 60 * 1024 * 1024


def nn(left, right):
    return lax.dot_general(left, right, (((1,), (0,)), ((), ())), preferred_element_type=F32)


def nt(left, right):
    return lax.dot_general(left, right, (((1,), (1,)), ((), ())), preferred_element_type=F32)


def tn(left, right):
    return lax.dot_general(left, right, (((0,), (0,)), ((), ())), preferred_element_type=F32)


def window(pair):
    return slice(128 * pair, 128 * pair + 256)


def normalize(stream):
    average = jnp.mean(stream, -1, keepdims=True)
    centred = stream - average
    inverse = lax.rsqrt(jnp.mean(centred * centred, -1, keepdims=True) + 1e-06)
    return centred * inverse, inverse


def normalize_back(normal, inverse, grad):
    mean_grad = jnp.mean(grad, -1, keepdims=True)
    mean_both = jnp.mean(grad * normal, -1, keepdims=True)
    return inverse * (grad - mean_grad - normal * mean_both)


def up_rows(ad_ref, number, slot, width):
    rows = ad_ref[2 * number + 1]
    before = jnp.zeros((RANK * slot, width), BF16)
    after = jnp.zeros((PAD - RANK * (slot + 1), width), BF16)
    return jnp.concatenate(([before] if slot else []) + [rows, after], 0)


def three_downs(ad_ref, number):
    return jnp.concatenate([ad_ref[2 * (number + i)] for i in range(3)], 0)


class Loads:
    def __init__(self, entries, sems):
        self.first = pl.program_id(0) == 0
        self.entries = entries
        self.sems = sems

    def copy(self, index):
        source, target = self.entries[index]
        return pltpu.make_async_copy(source, target, self.sems.at[index])

    def start(self):
        @pl.when(self.first)
        def _():
            for index in range(len(self.entries)):
                self.copy(index).start()

    def ready(self, index):
        @pl.when(self.first)
        def _():
            self.copy(index).wait()


def head_masks():
    lane = jnp.arange(256)[None, :]
    begin = jnp.array([16 * (h // 2) + HEAD_DIM * (h % 2) for h in range(HEADS)])[:, None]
    return ((lane >= begin) & (lane < begin + HEAD_DIM)).astype(BF16)


def same_place(shape):
    rows = lax.broadcasted_iota(jnp.int32, shape, 0)
    cols = lax.broadcasted_iota(jnp.int32, shape, 1)
    return jnp.where(rows % 16 == cols % 16, 0.0, -1e30).astype(F32)


def attend(q_ref, k_ref, v_ref, mask_ref, bias, put_out, stat_ref):
    carried = None
    for pair in range(PAIRS):
        win = window(pair)
        q_win, k_win, v_win = q_ref[:, win], k_ref[:, win], v_ref[:, win]
        out = None
        for head in (2 * pair, 2 * pair + 1):
            mask = mask_ref[head : head + 1, :]
            scores = nt(k_win * mask, q_win) * EXP_SCALE
            if bias is not None:
                scores = scores + bias[...]
            top = jnp.max(scores, 0, keepdims=True)
            grown = jnp.exp2(scores - top)
            total = jnp.sum(grown, 0, keepdims=True)
            stat_ref[head : head + 1, :] = top + jnp.log2(total)
            weights = (grown * (1.0 / total)).astype(BF16)
            part = tn(weights, v_win * mask)
            out = part if out is None else out + part
        low = out[:, :128]
        put_out(pair, low if carried is None else low + carried)
        carried = out[:, 128:]
    put_out(PAIRS, carried)


def attend_back(q_ref, k_ref, v_ref, do_ref, mask_ref, bias, stat_ref, put):
    carried = None
    for pair in range(PAIRS):
        win = window(pair)
        q_win, k_win, v_win, do_win = q_ref[:, win], k_ref[:, win], v_ref[:, win], do_ref[:, win]
        grads = None
        for head in (2 * pair, 2 * pair + 1):
            mask = mask_ref[head : head + 1, :]
            k_own = k_win * mask
            scores = nt(k_own, q_win) * EXP_SCALE
            if bias is not None:
                scores = scores + bias[...]
            probs = jnp.exp2(scores - stat_ref[head : head + 1, :])
            grad_probs = nt(v_win * mask, do_win)
            inner = jnp.sum(probs * grad_probs, 0, keepdims=True)
            grad_scores = (probs * (grad_probs - inner)).astype(BF16)
            parts = (
                tn(grad_scores, k_own),
                nn(grad_scores, q_win * mask),
                nn(probs.astype(BF16), do_win * mask),
            )
            grads = parts if grads is None else tuple(a + b for a, b in zip(grads, parts))
        lows = tuple(g[:, :128] for g in grads)
        if carried is not None:
            lows = tuple(a + b for a, b in zip(lows, carried))
        put(pair, lows)
        carried = tuple(g[:, 128:] for g in grads)
    put(PAIRS, carried)


def tile(index):
    return slice(128 * index, 128 * index + 128)


def three_projections(lhs_ref, ad_ref, number, weights, loads, first_load, outs, rank_ref):
    width = weights.shape[2]
    ranks = nt(lhs_ref[:, :width], three_downs(ad_ref, number)).astype(BF16)
    rank_ref[...] = ranks
    lhs_ref[:, width : width + 3 * RANK] = ranks
    for i in range(3):
        loads.ready(first_load + i)
        outs[i][...] = nn(lhs_ref[...], weights[first_load + i]).astype(BF16)


def one_projection(lhs_ref, ad_ref, number, weight_ref, rank_ref):
    width = weight_ref.shape[1]
    ranks = nt(lhs_ref[:, :width], ad_ref[2 * number]).astype(BF16)
    rank_ref[...] = ranks
    lhs_ref[:, width : width + RANK] = ranks
    return nn(lhs_ref[...], weight_ref[...])


def block_rows(index):
    return slice(RANK * index, RANK * (index + 1))


def one_back(grad, kept, ranks, ad_ref, number, weight_ref, grad_ref, at):
    width = weight_ref.shape[1]
    both = nt(grad, weight_ref[...])
    grad_rank = both[:, width : width + RANK].astype(BF16)
    grad_ref[block_rows(at), :] += tn(grad_rank, kept)
    grad_ref[block_rows(at + 1), :] += tn(ranks, grad)
    return both[:, :width] + nn(grad_rank, ad_ref[2 * number])


def three_back(grads, inputs, ranks, ad_ref, number, weights, loads, first_load, grad_ref, at):
    width = weights.shape[2]
    both = None
    for i in range(3):
        grad = grads[i][...]
        ups = tn(ranks, grad)
        grad_ref[block_rows(at + 2 * i + 1), :] += ups[block_rows(i)]
        loads.ready(first_load + i)
        part = nt(grad, weights[first_load + i])
        both = part if both is None else both + part
    grad_ranks = both[:, width : width + 3 * RANK].astype(BF16)
    downs = tn(grad_ranks, inputs)
    for i in range(3):
        grad_ref[block_rows(at + 2 * i), :] += downs[block_rows(i)]
    return both[:, :width] + nn(grad_ranks, three_downs(ad_ref, number))


def spatial_forward(
    x_ref, mod_ref, mask_ref, ad_ref, w_hbm, x1_ref, q_ref, k_ref, v_ref, o_ref, stat_ref, rq_ref, ro_ref,
    w_ref, lhs_ref, sems,
):
    width = x_ref.shape[2]
    loads = Loads([(w_hbm.at[i], w_ref.at[i, pl.ds(0, width), :]) for i in range(4)], sems)
    loads.start()

    @pl.when(loads.first)
    def _():
        lhs_ref[:, width:] = jnp.zeros((ROWS, PAD), BF16)
        for i in range(4):
            w_ref[i, width:, :] = up_rows(ad_ref, i, i % 3, width)

    stream = x_ref[0].astype(F32)
    normal, _ = normalize(stream)
    lhs_ref[:, :width] = (normal * (1.0 + mod_ref[1:2, :]) + mod_ref[0:1, :]).astype(BF16)
    q, k, v = q_ref.at[0], k_ref.at[0], v_ref.at[0]
    three_projections(lhs_ref, ad_ref, 0, w_ref, loads, 0, (q, k, v), rq_ref.at[0])

    def put_out(index, value):
        value = value.astype(BF16)
        o_ref[0, :, tile(index)] = value
        lhs_ref[:, tile(index)] = value

    attend(q, k, v, mask_ref, None, put_out, stat_ref.at[0])
    loads.ready(3)
    branch = one_projection(lhs_ref, ad_ref, 3, w_ref.at[3], ro_ref.at[0])
    result = (stream + mod_ref[2:3, :] * branch).astype(BF16)
    x1_ref[...] = result.reshape(x1_ref.shape)


def temporal_cross_forward(
    x_ref, ctx_ref, mod_ref, mask_ref, ad_ref, w_hbm,
    q_ref, k_ref, v_ref, o_ref, stat_ref, rq_ref, ro_ref,
    u2_ref, qc_ref, oc_ref, statc_ref, rqc_ref, roc_ref, kp_ref, vp_ref, rk_ref, rv_ref, x3_ref,
    w_ref, bias_ref, lhs_ref, q_s, k_s, v_s, o_s, sems,
):
    width = x_ref.shape[2]
    first = pl.program_id(0) == 0
    loads = Loads([(w_hbm.at[i], w_ref.at[i, pl.ds(0, width), :]) for i in range(8)], sems)
    loads.start()

    @pl.when(first)
    def _():
        bias_ref[...] = same_place(bias_ref.shape)
        lhs_ref[:, width:] = jnp.zeros((ROWS, PAD), BF16)
        for i in range(8):
            w_ref[i, width:, :] = up_rows(ad_ref, 4 + i, i if i < 3 else 0, width)

    loaded = x_ref[...].reshape(ROWS, width)
    stream = loaded.astype(F32)
    lhs_ref[:, :width] = loaded
    three_projections(lhs_ref, ad_ref, 4, w_ref, loads, 0, (q_s, k_s, v_s), rq_ref.at[0])
    q_ref[...] = q_s[...].reshape(q_ref.shape)
    k_ref[...] = k_s[...].reshape(k_ref.shape)
    v_ref[...] = v_s[...].reshape(v_ref.shape)

    def put_out(index, value):
        o_s[:, tile(index)] = value.astype(BF16)

    attend(q_s, k_s, v_s, mask_ref, bias_ref, put_out, stat_ref.at[0])
    lhs_ref[:, :width] = o_s[...]
    o_ref[...] = o_s[...].reshape(o_ref.shape)
    loads.ready(3)
    branch = one_projection(lhs_ref, ad_ref, 7, w_ref.at[3], ro_ref.at[0])
    stream = stream + mod_ref[2:3, :] * branch
    inputs = stream.astype(BF16)
    u2_ref[...] = inputs.reshape(u2_ref.shape)
    lhs_ref[:, :width] = inputs
    loads.ready(4)
    q_s[...] = one_projection(lhs_ref, ad_ref, 8, w_ref.at[4], rqc_ref.at[0]).astype(BF16)
    qc_ref[...] = q_s[...].reshape(qc_ref.shape)
    loads.ready(5)
    loads.ready(6)

    @pl.when(first)
    def _():
        for number, at, rank_ref, pair_ref in ((9, 5, rk_ref, kp_ref), (10, 6, rv_ref, vp_ref)):
            ranks = nt(ctx_ref[...], ad_ref[2 * number]).astype(BF16)
            rank_ref[...] = ranks
            made = nn(ctx_ref[...], w_ref[at, :width, :]) + nn(ranks, ad_ref[2 * number + 1])
            k_s[:PAD, :] = made.astype(BF16)
            for pair in range(PAIRS):
                piece = k_s[:PAD, window(pair)]
                pair_ref[pair, :PAD, :] = piece * mask_ref[2 * pair : 2 * pair + 1, :]
                pair_ref[pair, PAD:, :] = piece * mask_ref[2 * pair + 1 : 2 * pair + 2, :]

    carried = None
    count = 120
    for pair in range(PAIRS):
        scores = nt(kp_ref[pair], q_s[:, window(pair)]) * EXP_SCALE
        pieces = []
        for sub in range(2):
            own = scores[PAD * sub : PAD * sub + count]
            top = jnp.max(own, 0, keepdims=True)
            grown = jnp.exp2(own - top)
            total = jnp.sum(grown, 0, keepdims=True)
            statc_ref[0, 2 * pair + sub : 2 * pair + sub + 1, :] = top + jnp.log2(total)
            pieces += [grown * (1.0 / total), jnp.zeros((PAD - count, ROWS), F32)]
        weights = jnp.concatenate(pieces, 0).astype(BF16)
        out = tn(weights, vp_ref[pair])
        low = out[:, :128]
        put_out(pair, low if carried is None else low + carried)
        carried = out[:, 128:]
    put_out(PAIRS, carried)
    lhs_ref[:, :width] = o_s[...]
    oc_ref[...] = o_s[...].reshape(oc_ref.shape)
    loads.ready(7)
    stream = stream + one_projection(lhs_ref, ad_ref, 11, w_ref.at[7], roc_ref.at[0])
    x3_ref[...] = stream.reshape(x3_ref.shape)


def gelu_both(hidden):
    root = math.sqrt(2.0 / math.pi)
    square = hidden * hidden
    inner = root * (hidden + 0.044715 * (square * hidden))
    bent = jnp.tanh(inner)
    half = 0.5 * (1.0 + bent)
    slope = half + 0.5 * hidden * (1.0 - bent * bent) * (root * (1.0 + 3.0 * 0.044715 * square))
    return hidden * half, slope


def transposed_map(rows):
    wide = jnp.concatenate([rows.astype(F32), jnp.zeros((PAD - RANK, rows.shape[1]), F32)], 0)
    return wide.T.astype(BF16)


def down_loads(down_hbm, down_ref, first):
    chunks, width, _ = down_ref.shape
    return [(down_hbm.at[first + c], down_ref.at[c, :, pl.ds(0, width)]) for c in range(chunks)]


def feed_forward(
    x3_ref, cot_ref, mod_ref, ad_ref, w_hbm,
    act_ref, g3_ref, gd_ref, gu_ref, up_ref, down_ref, lhs_ref, dlhs_ref, sems,
):
    width = x3_ref.shape[1]
    chunks = down_ref.shape[0]
    loads = Loads(
        [(w_hbm.at[c], up_ref.at[c, pl.ds(0, width), :]) for c in range(chunks)]
        + down_loads(w_hbm, down_ref, chunks),
        sems,
    )
    loads.start()

    @pl.when(loads.first)
    def _():
        gd_ref[...] = jnp.zeros_like(gd_ref)
        gu_ref[...] = jnp.zeros_like(gu_ref)
        lhs_ref[:, width:] = jnp.zeros((ROWS, PAD), BF16)
        dlhs_ref[:, width:] = jnp.zeros((ROWS, PAD), BF16)
        for c in range(chunks):
            rows = ad_ref[2 + c]
            up_ref[c, width:, :] = jnp.concatenate([rows, jnp.zeros((PAD - RANK, width), BF16)], 0)
            down_ref[c, :, width:] = transposed_map(ad_ref[2 + chunks + c])

    normal, inverse = normalize(x3_ref[...])
    inputs = (normal * (1.0 + mod_ref[4:5, :]) + mod_ref[3:4, :]).astype(BF16)
    cot = cot_ref[...].astype(F32)
    grad_branch = (mod_ref[5:6, :] * cot).astype(BF16)
    rank_up = nt(inputs, ad_ref[0]).astype(BF16)
    lhs_ref[:, :width] = inputs
    lhs_ref[:, width : width + RANK] = rank_up
    dlhs_ref[:, :width] = grad_branch
    dlhs_ref[:, width : width + RANK] = nt(grad_branch, ad_ref[1]).astype(BF16)
    both = None
    for c in range(chunks):
        loads.ready(c)
        hidden = nn(lhs_ref[...], up_ref[c])
        active, slope = gelu_both(hidden)
        act_ref[:, c * width : (c + 1) * width] = active.astype(BF16)
        loads.ready(chunks + c)
        grad_active = nt(dlhs_ref[...], down_ref[c])
        grad_hidden = (slope * grad_active).astype(BF16)
        part = nt(grad_hidden, up_ref[c])
        both = part if both is None else both + part
        gu_ref[block_rows(c), :] += tn(rank_up, grad_hidden)
    grad_rank = both[:, width : width + RANK].astype(BF16)
    grad_in = both[:, :width] + nn(grad_rank, ad_ref[0])
    gd_ref[...] += tn(grad_rank, lhs_ref[:, :width])
    g3_ref[...] = cot + normalize_back(normal, inverse, grad_in * (1.0 + mod_ref[4:5, :]))


def feed_forward_out(
    act_ref, x3_ref, cot_ref, mod_ref, ad_ref, w_hbm, x4_ref, gu_ref, gd_ref, down_ref, sems
):
    width = x3_ref.shape[1]
    chunks = down_ref.shape[0]
    loads = Loads(down_loads(w_hbm, down_ref, chunks), sems)
    loads.start()

    @pl.when(loads.first)
    def _():
        gu_ref[...] = jnp.zeros_like(gu_ref)
        gd_ref[...] = jnp.zeros_like(gd_ref)
        for c in range(chunks):
            down_ref[c, :, width:] = transposed_map(ad_ref[2 + chunks + c])

    grad_branch = (mod_ref[5:6, :] * cot_ref[...].astype(F32)).astype(BF16)
    grad_rank = nt(grad_branch, ad_ref[1]).astype(BF16)
    both = None
    for c in range(chunks):
        active = act_ref[:, c * width : (c + 1) * width]
        loads.ready(c)
        part = nn(active, down_ref[c])
        both = part if both is None else both + part
        gd_ref[block_rows(c), :] += tn(grad_rank, active)
    ranks = both[:, width : width + RANK].astype(BF16)
    branch = both[:, :width] + nn(ranks, ad_ref[1])
    gu_ref[...] += tn(ranks, grad_branch)
    x4_ref[...] = (x3_ref[...] + mod_ref[5:6, :] * branch).astype(BF16)


def cross_temporal_backward(
    continued, g3_ref, u1_ref, q_ref, k_ref, v_ref, o_ref, stat_ref, rq_ref, ro_ref,
    u2_ref, qc_ref, oc_ref, statc_ref, rqc_ref, roc_ref, kp_ref, vp_ref, rk_ref, rv_ref,
    ctx_ref, mod_ref, mask_ref, ad_ref, w_hbm, *rest,
):
    before_ref = None
    if continued:
        before_ref, *rest = rest
    (
        g1_ref, gw_ref, w_ref, bias_ref, dk_acc, dv_acc, q_s, k_s, v_s, do_s, dq_s, dk_s, dv_s, ctx_s, sems,
    ) = rest
    width = u1_ref.shape[2]
    step = pl.program_id(0)
    first = step == 0
    order = (7, 4, 3, 0, 1, 2)
    loads = Loads(
        [(w_hbm.at[n], w_ref.at[i, pl.ds(0, width), :]) for i, n in enumerate(order)], sems
    )
    loads.start()

    @pl.when(first)
    def _():
        bias_ref[...] = same_place(bias_ref.shape)
        gw_ref[...] = before_ref[...] if continued else jnp.zeros_like(gw_ref)
        dk_acc[...] = jnp.zeros_like(dk_acc)
        dv_acc[...] = jnp.zeros_like(dv_acc)
        for i, n in enumerate(order):
            w_ref[i, width:, :] = up_rows(ad_ref, 4 + n, n if n < 3 else 0, width)

    def rows(ref):
        return ref[...].reshape(ROWS, ref.shape[2])

    grad = rows(g3_ref)
    loads.ready(0)
    do_s[...] = one_back(
        grad.astype(BF16), rows(oc_ref), roc_ref[0], ad_ref, 11, w_ref.at[0], gw_ref, 14
    ).astype(BF16)
    q_s[...] = rows(qc_ref)
    count = 120
    carried = None
    for pair in range(PAIRS):
        win = window(pair)
        q_win, do_win = q_s[:, win], do_s[:, win]
        scores = nt(kp_ref[pair], q_win) * EXP_SCALE
        grad_probs = nt(vp_ref[pair], do_win)
        all_probs, all_grads = [], []
        nothing = jnp.zeros((PAD - count, ROWS), F32)
        for sub in range(2):
            span = slice(PAD * sub, PAD * sub + count)
            row = 2 * pair + sub
            probs = jnp.exp2(scores[span] - statc_ref[0, row : row + 1, :])
            own = grad_probs[span]
            inner = jnp.sum(probs * own, 0, keepdims=True)
            all_probs += [probs, nothing]
            all_grads += [probs * (own - inner), nothing]
        probs = jnp.concatenate(all_probs, 0).astype(BF16)
        grad_scores = jnp.concatenate(all_grads, 0).astype(BF16)
        dk_acc[pair] += nn(grad_scores, q_win)
        dv_acc[pair] += nn(probs, do_win)
        out = tn(grad_scores, kp_ref[pair])
        low = out[:, :128]
        dq_s[:, tile(pair)] = ((low if carried is None else low + carried) * SCALE).astype(BF16)
        carried = out[:, 128:]
    dq_s[:, tile(PAIRS)] = (carried * SCALE).astype(BF16)
    loads.ready(1)
    grad = grad + one_back(
        dq_s[...], rows(u2_ref), rqc_ref[0], ad_ref, 8, w_ref.at[1], gw_ref, 8
    )
    loads.ready(2)
    do_s[...] = one_back(
        (mod_ref[2:3, :] * grad).astype(BF16), rows(o_ref), ro_ref[0], ad_ref, 7, w_ref.at[2], gw_ref, 6
    ).astype(BF16)
    q_s[...] = rows(q_ref)
    k_s[...] = rows(k_ref)
    v_s[...] = rows(v_ref)

    def put(index, values):
        dq_s[:, tile(index)] = (values[0] * SCALE).astype(BF16)
        dk_s[:, tile(index)] = (values[1] * SCALE).astype(BF16)
        dv_s[:, tile(index)] = values[2].astype(BF16)

    attend_back(q_s, k_s, v_s, do_s, mask_ref, bias_ref, stat_ref.at[0], put)
    grad = grad + three_back(
        (dq_s, dk_s, dv_s), rows(u1_ref), rq_ref[0], ad_ref, 4, w_ref, loads, 3, gw_ref, 0
    )
    g1_ref[...] = grad.astype(BF16).reshape(g1_ref.shape)

    @pl.when(step == pl.num_programs(0) - 1)
    def _():
        context = ctx_ref[...].astype(F32)
        for acc, factor, rank_ref, number, at in (
            (dk_acc, SCALE, rk_ref, 9, 10),
            (dv_acc, 1.0, rv_ref, 10, 12),
        ):
            held = None
            for pair in range(PAIRS):
                whole = acc[pair]
                out = whole[:PAD] * mask_ref[2 * pair : 2 * pair + 1, :].astype(F32)
                out = out + whole[PAD:] * mask_ref[2 * pair + 1 : 2 * pair + 2, :].astype(F32)
                out = out * factor
                low = out[:, :128]
                ctx_s[:, tile(pair)] = low if held is None else low + held
                held = out[:, 128:]
            ctx_s[:, tile(PAIRS)] = held
            grad_kv = ctx_s[...]
            grad_rank = lax.dot_general(
                grad_kv, ad_ref[2 * number + 1].astype(F32), (((1,), (1,)), ((), ())),
                precision=HIGHEST, preferred_element_type=F32,
            )
            gw_ref[block_rows(at), :] += lax.dot_general(
                grad_rank, context, (((0,), (0,)), ((), ())),
                precision=HIGHEST, preferred_element_type=F32,
            )
            gw_ref[block_rows(at + 1), :] += lax.dot_general(
                rank_ref[...].astype(F32), grad_kv, (((0,), (0,)), ((), ())),
                precision=HIGHEST, preferred_element_type=F32,
            )


def pack_columns(table_ref, packed_ref, clips):
    parts = packed_ref.shape[0] // clips
    _, share, cols = packed_ref.shape
    for f in range(clips):
        for s in range(parts):
            piece = table_ref[share * s : share * (s + 1), cols * f : cols * (f + 1)]
            packed_ref[f * parts + s] = piece.astype(BF16)


def spatial_backward(
    halves, clips, *refs,
):
    g1_refs, refs = refs[:halves], refs[halves:]
    (
        x_ref, q_ref, k_ref, v_ref, o_ref, stat_ref, rq_ref, ro_ref, mod_ref, mask_ref, ad_ref, w_hbm,
        g0_ref, packed_ref, w_ref, gw_ref, do_s, dq_s, dk_s, dv_s, sems,
    ) = refs
    width = x_ref.shape[2]
    order = (3, 0, 1, 2)
    loads = Loads(
        [(w_hbm.at[n], w_ref.at[i, pl.ds(0, width), :]) for i, n in enumerate(order)], sems
    )
    loads.start()

    @pl.when(loads.first)
    def _():
        gw_ref[...] = jnp.zeros_like(gw_ref)
        for i, n in enumerate(order):
            w_ref[i, width:, :] = up_rows(ad_ref, n, n % 3, width)

    parts = g1_refs[0].shape[0]
    pieces = [ref[s, 0] for s in range(parts) for ref in g1_refs]
    grad = jnp.concatenate(pieces, 0).astype(F32)
    loads.ready(0)
    do_s[...] = one_back(
        (mod_ref[2:3, :] * grad).astype(BF16), o_ref[0], ro_ref[0], ad_ref, 3, w_ref.at[0], gw_ref, 6
    ).astype(BF16)

    def put(index, values):
        dq_s[:, tile(index)] = (values[0] * SCALE).astype(BF16)
        dk_s[:, tile(index)] = (values[1] * SCALE).astype(BF16)
        dv_s[:, tile(index)] = values[2].astype(BF16)

    attend_back(
        q_ref.at[0], k_ref.at[0], v_ref.at[0], do_s, mask_ref, None, stat_ref.at[0], put
    )
    normal, inverse = normalize(x_ref[0].astype(F32))
    inputs = (normal * (1.0 + mod_ref[1:2, :]) + mod_ref[0:1, :]).astype(BF16)
    grad_in = three_back(
        (dq_s, dk_s, dv_s), inputs, rq_ref[0], ad_ref, 0, w_ref, loads, 1, gw_ref, 0
    )
    grad = grad + normalize_back(normal, inverse, grad_in * (1.0 + mod_ref[1:2, :]))
    g0_ref[0] = grad.astype(BF16)

    @pl.when(pl.program_id(0) == pl.num_programs(0) - 1)
    def _():
        pack_columns(gw_ref, packed_ref, clips)


def pack_early(clips, *refs):
    *sources, packed_ref, table_ref = refs
    at = 0
    for ref in sources:
        table_ref[at : at + ref.shape[0], :] = ref[...]
        at += ref.shape[0]
    table_ref[at:, :] = jnp.zeros((table_ref.shape[0] - at, table_ref.shape[1]), F32)
    pack_columns(table_ref, packed_ref, clips)


def combine(index_ref, got_ref, out_ref, acc_ref):
    clips = index_ref.shape[0]
    parts = got_ref.shape[0] // clips
    acc_ref[...] = jnp.zeros_like(acc_ref)

    def step(f, carry):
        total = got_ref[f * parts].astype(F32)
        for s in range(1, parts):
            total = total + got_ref[f * parts + s].astype(F32)
        acc_ref[index_ref[f]] += total
        return carry

    lax.fori_loop(0, clips, step, 0)
    table = acc_ref[...].astype(BF16)
    for s in range(parts):
        out_ref[s] = table


def whole_block(array):
    zeros = (0,) * array.ndim
    return pl.BlockSpec(array.shape, lambda i: zeros)


def anywhere():
    return pl.BlockSpec(memory_space=pl.ANY)


def like(shape, dtype):
    return jax.ShapeDtypeStruct(shape, dtype)


PARAMS = pltpu.CompilerParams(
    dimension_semantics=("arbitrary",), vmem_limit_bytes=VMEM_LIMIT
)


def cost(flops, read):
    return pl.CostEstimate(flops=flops, bytes_accessed=read, transcendentals=flops // 4096)


def run_spatial_forward(video, mods, masks, wide, w_s, parts):
    frames, rows, d = video.shape
    places = rows // parts
    by_frame = lambda i: (i, 0, 0)
    row_block = pl.BlockSpec((1, rows, d), by_frame)
    return pl.pallas_call(
        spatial_forward,
        grid=(frames,),
        in_specs=[row_block, whole_block(mods), whole_block(masks), whole_block(wide), anywhere()],
        out_specs=[
            pl.BlockSpec((parts, 1, places, d), lambda i: (0, i, 0, 0)),
            row_block,
            row_block,
            row_block,
            row_block,
            pl.BlockSpec((1, HEADS, rows), by_frame),
            pl.BlockSpec((1, rows, 3 * RANK), by_frame),
            pl.BlockSpec((1, rows, RANK), by_frame),
        ],
        out_shape=[like((parts, frames, places, d), BF16)]
        + [like(video.shape, BF16)] * 4
        + [
            like((frames, HEADS, rows), F32),
            like((frames, rows, 3 * RANK), BF16),
            like((frames, rows, RANK), BF16),
        ],
        scratch_shapes=[
            pltpu.VMEM((4, d + PAD, d), BF16),
            pltpu.VMEM((ROWS, d + PAD), BF16),
            pltpu.SemaphoreType.DMA((4,)),
        ],
        compiler_params=PARAMS,
        cost_estimate=cost(10 * frames * rows * d * d, 30_000_000),
        name="spatial_forward",
    )(video, mods, masks, wide, w_s)


def run_temporal_cross_forward(x1, context, mods, masks, wide, w_tc):
    frames, places, d = x1.shape
    groups = places * frames // ROWS
    across = pl.BlockSpec((frames, ROWS // frames, d), lambda i: (0, i, 0))
    by_group = lambda i: (i, 0, 0)
    stat = pl.BlockSpec((1, HEADS, ROWS), by_group)
    three = pl.BlockSpec((1, ROWS, 3 * RANK), by_group)
    one = pl.BlockSpec((1, ROWS, RANK), by_group)
    full = lambda *shape: pl.BlockSpec(shape, lambda i: (0,) * len(shape))
    act = like(x1.shape, BF16)
    stat_shape = like((groups, HEADS, ROWS), F32)
    one_shape = like((groups, ROWS, RANK), BF16)
    return pl.pallas_call(
        temporal_cross_forward,
        grid=(groups,),
        in_specs=[across, whole_block(context), whole_block(mods), whole_block(masks), whole_block(wide), anywhere()],
        out_specs=[across] * 4 + [stat, three, one] + [across] * 3 + [stat, one, one]
        + [full(PAIRS, 2 * PAD, 256)] * 2 + [full(PAD, RANK)] * 2 + [across],
        out_shape=[act] * 4 + [stat_shape, like((groups, ROWS, 3 * RANK), BF16), one_shape]
        + [act] * 3 + [stat_shape, one_shape, one_shape]
        + [like((PAIRS, 2 * PAD, 256), BF16)] * 2 + [like((PAD, RANK), BF16)] * 2
        + [like(x1.shape, F32)],
        scratch_shapes=[pltpu.VMEM((8, d + PAD, d), BF16), pltpu.VMEM((ROWS, ROWS), F32)]
        + [pltpu.VMEM((ROWS, d + PAD), BF16)]
        + [pltpu.VMEM((ROWS, d), BF16)] * 4
        + [pltpu.SemaphoreType.DMA((8,))],
        compiler_params=PARAMS,
        cost_estimate=cost(14 * places * frames * d * d, 50_000_000),
        name="temporal_cross_forward",
    )(x1, context, mods, masks, wide, w_tc)


def run_feed_forward(x3, cot, mods, maps, w_f):
    tokens, d = x3.shape
    chunks = w_f.shape[0] // 2
    rows = pl.BlockSpec((ROWS, d), lambda i: (i, 0))
    fixed = lambda n: pl.BlockSpec((n * RANK, d), lambda i: (0, 0))
    return pl.pallas_call(
        feed_forward,
        grid=(tokens // ROWS,),
        in_specs=[rows, rows, whole_block(mods), whole_block(maps), anywhere()],
        out_specs=[pl.BlockSpec((ROWS, chunks * d), lambda i: (i, 0)), rows, fixed(1), fixed(chunks)],
        out_shape=[
            like((tokens, chunks * d), BF16),
            like((tokens, d), F32),
            like((RANK, d), F32),
            like((chunks * RANK, d), F32),
        ],
        scratch_shapes=[
            pltpu.VMEM((chunks, d + PAD, d), BF16),
            pltpu.VMEM((chunks, d, d + PAD), BF16),
            pltpu.VMEM((ROWS, d + PAD), BF16),
            pltpu.VMEM((ROWS, d + PAD), BF16),
            pltpu.SemaphoreType.DMA((2 * chunks,)),
        ],
        compiler_params=PARAMS,
        cost_estimate=cost(6 * tokens * d * d * chunks, 50_000_000),
        name="feed_forward",
    )(x3, cot, mods, maps, w_f)


def run_feed_forward_out(active, x3, cot, mods, maps, w_f):
    tokens, d = x3.shape
    chunks = w_f.shape[0] // 2
    rows = pl.BlockSpec((ROWS, d), lambda i: (i, 0))
    fixed = lambda n: pl.BlockSpec((n * RANK, d), lambda i: (0, 0))
    return pl.pallas_call(
        feed_forward_out,
        grid=(tokens // ROWS,),
        in_specs=[
            pl.BlockSpec((ROWS, chunks * d), lambda i: (i, 0)),
            rows,
            rows,
            whole_block(mods),
            whole_block(maps),
            anywhere(),
        ],
        out_specs=[rows, fixed(1), fixed(chunks)],
        out_shape=[
            like((tokens, d), BF16),
            like((RANK, d), F32),
            like((chunks * RANK, d), F32),
        ],
        scratch_shapes=[pltpu.VMEM((chunks, d, d + PAD), BF16), pltpu.SemaphoreType.DMA((chunks,))],
        compiler_params=PARAMS,
        cost_estimate=cost(2 * tokens * d * d * chunks, 30_000_000),
        name="feed_forward_out",
    )(active, x3, cot, mods, maps, w_f)


def run_cross_temporal_backward(g3, u1, saved, context, mods, masks, wide, w_tc, half, halves, before):
    frames, places, d = u1.shape
    groups = places * frames // ROWS // halves
    start = half * groups
    across = pl.BlockSpec((frames, ROWS // frames, d), lambda i: (0, i + start, 0))
    by_group = lambda i: (i + start, 0, 0)
    stat = pl.BlockSpec((1, HEADS, ROWS), by_group)
    three = pl.BlockSpec((1, ROWS, 3 * RANK), by_group)
    one = pl.BlockSpec((1, ROWS, RANK), by_group)
    kp, vp, rk, rv = saved[13:17]
    grads = pl.BlockSpec((16 * RANK, d), lambda i: (0, 0))
    extra = [] if before is None else [before]

    def body(*refs):
        cross_temporal_backward(before is not None, *refs)

    return pl.pallas_call(
        body,
        grid=(groups,),
        in_specs=[across, across] + [across] * 4 + [stat, three, one] + [across] * 3 + [stat, one, one]
        + [whole_block(kp), whole_block(vp), whole_block(rk), whole_block(rv)]
        + [whole_block(context), whole_block(mods), whole_block(masks), whole_block(wide), anywhere()]
        + [grads] * len(extra),
        out_specs=[pl.BlockSpec((frames, ROWS // frames, d), lambda i: (0, i, 0)), grads],
        out_shape=[like((frames, places // halves, d), BF16), like((16 * RANK, d), F32)],
        scratch_shapes=[
            pltpu.VMEM((6, d + PAD, d), BF16),
            pltpu.VMEM((ROWS, ROWS), F32),
            pltpu.VMEM((PAIRS, 2 * PAD, 256), F32),
            pltpu.VMEM((PAIRS, 2 * PAD, 256), F32),
        ]
        + [pltpu.VMEM((ROWS, d), BF16)] * 7
        + [pltpu.VMEM((PAD, d), F32), pltpu.SemaphoreType.DMA((6,))],
        compiler_params=PARAMS,
        cost_estimate=cost(14 * places // halves * frames * d * d, 30_000_000),
        name="cross_temporal_backward",
    )(g3, u1, *saved[:17], context, mods, masks, wide, w_tc, *extra)


def run_spatial_backward(g1_halves, video, saved, mods, masks, wide, w_s, clips):
    frames, rows, d = video.shape
    parts = g1_halves[0].shape[0]
    by_frame = lambda i: (i, 0, 0)
    row_block = pl.BlockSpec((1, rows, d), by_frame)
    packed = (clips * parts, 8 * RANK // parts, d // clips)

    def body(*refs):
        spatial_backward(len(g1_halves), clips, *refs)

    return pl.pallas_call(
        body,
        grid=(frames,),
        in_specs=[
            pl.BlockSpec((parts, 1, g.shape[2], d), lambda i: (0, i, 0, 0)) for g in g1_halves
        ]
        + [row_block] * 5
        + [
            pl.BlockSpec((1, HEADS, rows), by_frame),
            pl.BlockSpec((1, rows, 3 * RANK), by_frame),
            pl.BlockSpec((1, rows, RANK), by_frame),
            whole_block(mods),
            whole_block(masks),
            whole_block(wide),
            anywhere(),
        ],
        out_specs=[row_block, pl.BlockSpec(packed, lambda i: (0, 0, 0))],
        out_shape=[like(video.shape, BF16), like(packed, BF16)],
        scratch_shapes=[pltpu.VMEM((4, d + PAD, d), BF16), pltpu.VMEM((8 * RANK, d), F32)]
        + [pltpu.VMEM((ROWS, d), BF16)] * 4
        + [pltpu.SemaphoreType.DMA((4,))],
        compiler_params=PARAMS,
        cost_estimate=cost(10 * frames * rows * d * d, 30_000_000),
        name="spatial_backward",
    )(*g1_halves, video, *saved, mods, masks, wide, w_s)


EARLY_BLOCKS = 28


def run_pack_early(sources, clips, parts):
    d = sources[0].shape[1]
    packed = (clips * parts, EARLY_BLOCKS * RANK // parts, d // clips)

    def body(*refs):
        pack_early(clips, *refs)

    return pl.pallas_call(
        body,
        out_shape=like(packed, BF16),
        scratch_shapes=[pltpu.VMEM((EARLY_BLOCKS * RANK, d), F32)],
        compiler_params=pltpu.CompilerParams(vmem_limit_bytes=VMEM_LIMIT),
        name="pack_early",
    )(*sources)


def run_combine(all_index, got, adapters):
    clips = all_index.shape[0]
    parts = got.shape[0] // clips
    _, share, cols = got.shape
    return pl.pallas_call(
        combine,
        in_specs=[pl.BlockSpec(memory_space=pltpu.SMEM), pl.BlockSpec(memory_space=pltpu.VMEM)],
        out_specs=pl.BlockSpec(memory_space=pltpu.VMEM),
        out_shape=like((parts, adapters, share, cols), BF16),
        scratch_shapes=[pltpu.VMEM((adapters, share, cols), F32)],
        compiler_params=pltpu.CompilerParams(vmem_limit_bytes=VMEM_LIMIT),
        name="combine",
    )(all_index, got)


def exchange(array, axes="seq"):
    return lax.all_to_all(array, axes, split_axis=0, concat_axis=0, tiled=True)


def fetch_adapters(choice, adapt_wide, adapt_ff):
    cols = adapt_wide.shape[-1]
    times = adapt_ff.shape[-1] // cols
    narrow = adapt_ff.reshape(adapt_ff.shape[:-1] + (times, cols))
    narrow = jnp.moveaxis(narrow, 3, 1).reshape(2 * times, *adapt_wide.shape[1:])
    table = jnp.concatenate([adapt_wide, narrow], 0)
    picked = jnp.sum(
        choice[:, None, :, None, None] * table[None].astype(F32), axis=2
    ).astype(BF16)
    got = exchange(picked, "fsdp")
    return jnp.moveaxis(got, 0, 2).reshape(table.shape[0], RANK, -1)


def reduce_grads(packed, all_index, adapters):
    got = exchange(packed, ("fsdp", "seq"))
    return run_combine(all_index, got, adapters)


def spread_grads(quarter):
    whole = exchange(quarter)
    parts, adapters, share, cols = whole.shape
    table = whole.transpose(1, 0, 2, 3).reshape(adapters, -1, RANK, cols)
    return table.transpose(1, 0, 2, 3).astype(F32)


def hidden_order(up, down, clips):
    rows, hidden = up.shape
    width = down.shape[1]
    times = hidden // width
    cols = width // clips
    up = up.reshape(rows, clips, times, cols).transpose(2, 0, 1, 3).reshape(times, rows, width)
    return jnp.concatenate([up, down.reshape(times, cols, width)], 0)


def on_device(
    video,
    context,
    modulation,
    adapter_index,
    cotangent,
    qkv_weights,
    out_weights,
    ffn_up,
    ffn_down,
    adapt_wide,
    adapt_ff,
):
    parts = lax.axis_size("seq")
    clips = lax.axis_size("fsdp")
    d = video.shape[-1]
    adapters = adapt_wide.shape[2]
    places = SPATIAL // parts
    frames = FRAMES // parts
    mods = modulation[0, 0]
    masks = head_masks()
    ctx = jnp.pad(context[0], ((0, PAD - context.shape[1]), (0, 0)))

    def gather(array):
        return lax.all_gather(array, "fsdp", axis=1, tiled=True)

    def attention_weights(j):
        return [qkv_weights[0, 3 * j : 3 * j + 3], out_weights[0, j : j + 1]]

    w_s = gather(jnp.concatenate(attention_weights(0), 0))
    all_index = exchange(jnp.broadcast_to(adapter_index, (clips,)), "fsdp")
    choice = (all_index[:, None] == jnp.arange(adapters)[None, :]).astype(F32)
    wide = fetch_adapters(choice, adapt_wide[0], adapt_ff[0])
    w_tc = gather(jnp.concatenate(attention_weights(1) + attention_weights(2), 0))
    w_f = gather(hidden_order(ffn_up[0], ffn_down[0], clips))
    maps_f = wide[24:]

    cot = cotangent.reshape(frames, parts, places, d).transpose(1, 0, 2, 3)
    cot = exchange(cot).reshape(FRAMES * places, d)
    frames_in = video.reshape(frames, SPATIAL, d)
    x1, *kept_s = run_spatial_forward(frames_in, mods, masks, wide, w_s, parts)
    u1 = exchange(x1).reshape(FRAMES, places, d)
    *kept_t, x3 = run_temporal_cross_forward(u1, ctx, mods, masks, wide, w_tc)
    x3 = x3.reshape(FRAMES * places, d)
    active, g3, grad_a24, grad_b24 = run_feed_forward(x3, cot, mods, maps_f, w_f)
    g3 = g3.reshape(FRAMES, places, d)
    groups = FRAMES * places // ROWS
    halves = 2 if groups % 2 == 0 else 1
    g1_halves, grads_t = [], None
    for half in range(halves):
        g1, grads_t = run_cross_temporal_backward(
            g3, u1, kept_t, ctx, mods, masks, wide, w_tc, half, halves, grads_t
        )
        g1_halves.append(exchange(g1.reshape(parts, frames, places // halves, d)))
    x4, grad_b25, grad_down = run_feed_forward_out(active, x3, cot, mods, maps_f, w_f)
    packed = run_pack_early([grads_t, grad_a24, grad_b25, grad_b24, grad_down], clips, parts)
    early = reduce_grads(packed, all_index, adapters)
    output = exchange(x4.reshape(parts, frames, places, d))
    early, *g1_halves = lax.optimization_barrier((early, *g1_halves))
    g0, packed = run_spatial_backward(g1_halves, frames_in, kept_s, mods, masks, wide, w_s, clips)
    early = spread_grads(early)
    late = spread_grads(reduce_grads(packed, all_index, adapters))
    output = output.transpose(1, 0, 2, 3).reshape(video.shape)
    wide_out = jnp.concatenate([late, early[:18]], 0)
    times = adapt_ff.shape[-1] // adapt_wide.shape[-1]
    narrow_out = early[18 : 18 + 2 * times].reshape(2, times, adapters, RANK, -1)
    narrow_out = jnp.moveaxis(narrow_out, 1, 3).reshape(2, adapters, RANK, -1)
    return (output, g0.reshape(video.shape), wide_out[None], narrow_out[None])


def solution(mesh):
    return jax.shard_map(
        on_device,
        mesh=mesh,
        in_specs=(
            P("fsdp", "seq", None),
            P("fsdp", None, None),
            P("fsdp", None, None, None),
            P("fsdp"),
            P("fsdp", "seq", None),
            P(None, None, "fsdp", None),
            P(None, None, "fsdp", None),
            P(None, "fsdp", None),
            P(None, "fsdp", None),
            P(None, None, None, None, "fsdp"),
            P(None, None, None, None, "fsdp"),
        ),
        out_specs=(
            P("fsdp", "seq", None),
            P("fsdp", "seq", None),
            P(None, None, None, None, "fsdp"),
            P(None, None, None, None, "fsdp"),
        ),
        check_vma=False,
    )
```

```python
import math

import jax
import jax.numpy as jnp
from jax import lax
from jax.experimental import pallas as pl
from jax.experimental.pallas import tpu as pltpu
from jax.sharding import PartitionSpec as P

HEAD_DIM = 72
HEADS = 16
FRAMES = 16
SPATIAL = 256
RANK = 16
ROWS = 256
PAIRS = HEADS // 2
PAD = 128
SCALE = HEAD_DIM ** (-0.5)
EXP_SCALE = SCALE * math.log2(math.e)
LN2 = math.log(2.0)
HIGHEST = lax.Precision.HIGHEST
F32 = jnp.float32
BF16 = jnp.bfloat16
VMEM_LIMIT = 60 * 1024 * 1024


def nn(left, right):
    return lax.dot_general(left, right, (((1,), (0,)), ((), ())), preferred_element_type=F32)


def nt(left, right):
    return lax.dot_general(left, right, (((1,), (1,)), ((), ())), preferred_element_type=F32)


def tn(left, right):
    return lax.dot_general(left, right, (((0,), (0,)), ((), ())), preferred_element_type=F32)


def window(pair):
    return slice(128 * pair, 128 * pair + 256)


def normalize(stream):
    average = jnp.mean(stream, -1, keepdims=True)
    centred = stream - average
    inverse = lax.rsqrt(jnp.mean(centred * centred, -1, keepdims=True) + 1e-06)
    return centred * inverse, inverse


def normalize_back(normal, inverse, grad):
    mean_grad = jnp.mean(grad, -1, keepdims=True)
    mean_both = jnp.mean(grad * normal, -1, keepdims=True)
    return inverse * (grad - mean_grad - normal * mean_both)


def up_rows(ad_ref, number, slot, width):
    rows = ad_ref[2 * number + 1]
    before = jnp.zeros((RANK * slot, width), BF16)
    after = jnp.zeros((PAD - RANK * (slot + 1), width), BF16)
    return jnp.concatenate(([before] if slot else []) + [rows, after], 0)


def three_downs(ad_ref, number):
    return jnp.concatenate([ad_ref[2 * (number + i)] for i in range(3)], 0)


class Loads:
    def __init__(self, entries, sems):
        self.first = pl.program_id(0) == 0
        self.entries = entries
        self.sems = sems

    def copy(self, index):
        source, target = self.entries[index]
        return pltpu.make_async_copy(source, target, self.sems.at[index])

    def start(self):
        @pl.when(self.first)
        def _():
            for index in range(len(self.entries)):
                self.copy(index).start()

    def ready(self, index):
        @pl.when(self.first)
        def _():
            self.copy(index).wait()


def head_masks():
    lane = jnp.arange(256)[None, :]
    begin = jnp.array([16 * (h // 2) + HEAD_DIM * (h % 2) for h in range(HEADS)])[:, None]
    return ((lane >= begin) & (lane < begin + HEAD_DIM)).astype(BF16)


def same_place(shape):
    rows = lax.broadcasted_iota(jnp.int32, shape, 0)
    cols = lax.broadcasted_iota(jnp.int32, shape, 1)
    return jnp.where(rows % 16 == cols % 16, 0.0, -1e30).astype(F32)


def attend(q_ref, k_ref, v_ref, mask_ref, bias, put_out, stat_ref):
    carried = None
    for pair in range(PAIRS):
        win = window(pair)
        q_win, k_win, v_win = q_ref[:, win], k_ref[:, win], v_ref[:, win]
        all_weights, all_values = [], []
        for head in (2 * pair, 2 * pair + 1):
            mask = mask_ref[head : head + 1, :]
            scores = nt(k_win * mask, q_win)
            if bias is not None:
                scores = scores + bias[...]
            top = jnp.max(scores, 0, keepdims=True)
            grown = jnp.exp2(scores - top)
            total = jnp.sum(grown, 0, keepdims=True)
            stat_ref[head : head + 1, :] = top + jnp.log2(total)
            all_weights.append((grown * (1.0 / total)).astype(BF16))
            all_values.append(v_win * mask)
        out = tn(jnp.concatenate(all_weights, 0), jnp.concatenate(all_values, 0))
        low = out[:, :128]
        put_out(pair, low if carried is None else low + carried)
        carried = out[:, 128:]
    put_out(PAIRS, carried)


def attend_back(q_ref, k_ref, v_ref, do_ref, mask_ref, bias, stat_ref, put):
    carried = None
    for pair in range(PAIRS):
        win = window(pair)
        q_win, k_win, v_win, do_win = q_ref[:, win], k_ref[:, win], v_ref[:, win], do_ref[:, win]
        all_grads, all_probs, keys, queries, outs = [], [], [], [], []
        for head in (2 * pair, 2 * pair + 1):
            mask = mask_ref[head : head + 1, :]
            k_own = k_win * mask
            scores = nt(k_own, q_win)
            if bias is not None:
                scores = scores + bias[...]
            probs = jnp.exp2(scores - stat_ref[head : head + 1, :])
            grad_probs = nt(v_win * mask, do_win)
            inner = jnp.sum(probs * grad_probs, 0, keepdims=True)
            all_grads.append((probs * (grad_probs - inner)).astype(BF16))
            all_probs.append(probs.astype(BF16))
            keys.append(k_own)
            queries.append(q_win * mask)
            outs.append(do_win * mask)
        grads = (
            tn(jnp.concatenate(all_grads, 0), jnp.concatenate(keys, 0)),
            nn(jnp.concatenate(all_grads, 1), jnp.concatenate(queries, 0)),
            nn(jnp.concatenate(all_probs, 1), jnp.concatenate(outs, 0)),
        )
        lows = tuple(g[:, :128] for g in grads)
        if carried is not None:
            lows = tuple(a + b for a, b in zip(lows, carried))
        put(pair, lows)
        carried = tuple(g[:, 128:] for g in grads)
    put(PAIRS, carried)


def tile(index):
    return slice(128 * index, 128 * index + 128)


def three_projections(lhs_ref, ad_ref, number, weights, loads, first_load, outs, rank_ref):
    width = weights.shape[2]
    ranks = nt(lhs_ref[:, :width], three_downs(ad_ref, number)).astype(BF16)
    rank_ref[...] = ranks
    lhs_ref[:, width : width + 3 * RANK] = ranks
    for i in range(3):
        loads.ready(first_load + i)
        total = nn(lhs_ref[...], weights[first_load + i])
        outs[i][...] = (total * EXP_SCALE if i == 0 else total).astype(BF16)


def one_projection(lhs_ref, ad_ref, number, weight_ref, rank_ref):
    width = weight_ref.shape[1]
    ranks = nt(lhs_ref[:, :width], ad_ref[2 * number]).astype(BF16)
    rank_ref[...] = ranks
    lhs_ref[:, width : width + RANK] = ranks
    return nn(lhs_ref[...], weight_ref[...])


def block_rows(index):
    return slice(RANK * index, RANK * (index + 1))


def one_back(grad, kept, ranks, ad_ref, number, weight_ref, grad_ref, at):
    width = weight_ref.shape[1]
    both = nt(grad, weight_ref[...])
    grad_rank = both[:, width : width + RANK].astype(BF16)
    grad_ref[block_rows(at), :] += tn(grad_rank, kept)
    grad_ref[block_rows(at + 1), :] += tn(ranks, grad)
    return both[:, :width] + nn(grad_rank, ad_ref[2 * number])


def three_back(grads, inputs, ranks, ad_ref, number, weights, loads, first_load, grad_ref, at):
    width = weights.shape[2]
    both = None
    for i in range(3):
        grad = grads[i][...]
        ups = tn(ranks, grad)
        grad_ref[block_rows(at + 2 * i + 1), :] += ups[block_rows(i)]
        loads.ready(first_load + i)
        part = nt(grad, weights[first_load + i])
        both = part if both is None else both + part
    grad_ranks = both[:, width : width + 3 * RANK].astype(BF16)
    downs = tn(grad_ranks, inputs)
    for i in range(3):
        grad_ref[block_rows(at + 2 * i), :] += downs[block_rows(i)]
    return both[:, :width] + nn(grad_ranks, three_downs(ad_ref, number))


def spatial_forward(
    x_ref, mod_ref, mask_ref, ad_ref, w_hbm, x1_ref, q_ref, k_ref, v_ref, o_ref, stat_ref, rq_ref, ro_ref,
    w_ref, lhs_ref, sems,
):
    width = x_ref.shape[2]
    loads = Loads([(w_hbm.at[i], w_ref.at[i, pl.ds(0, width), :]) for i in range(4)], sems)
    loads.start()

    @pl.when(loads.first)
    def _():
        lhs_ref[:, width:] = jnp.zeros((ROWS, PAD), BF16)
        for i in range(4):
            w_ref[i, width:, :] = up_rows(ad_ref, i, i % 3, width)

    stream = x_ref[0].astype(F32)
    normal, _ = normalize(stream)
    lhs_ref[:, :width] = (normal * (1.0 + mod_ref[1:2, :]) + mod_ref[0:1, :]).astype(BF16)
    q, k, v = q_ref.at[0], k_ref.at[0], v_ref.at[0]
    three_projections(lhs_ref, ad_ref, 0, w_ref, loads, 0, (q, k, v), rq_ref.at[0])

    def put_out(index, value):
        value = value.astype(BF16)
        o_ref[0, :, tile(index)] = value
        lhs_ref[:, tile(index)] = value

    attend(q, k, v, mask_ref, None, put_out, stat_ref.at[0])
    loads.ready(3)
    branch = one_projection(lhs_ref, ad_ref, 3, w_ref.at[3], ro_ref.at[0])
    result = (stream + mod_ref[2:3, :] * branch).astype(BF16)
    x1_ref[...] = result.reshape(x1_ref.shape)


def temporal_cross_forward(
    x_ref, ctx_ref, mod_ref, mask_ref, ad_ref, wt_hbm, wc_hbm,
    q_ref, k_ref, v_ref, o_ref, stat_ref, rq_ref, ro_ref,
    u2_ref, qc_ref, oc_ref, statc_ref, rqc_ref, roc_ref, kp_ref, vp_ref, rk_ref, rv_ref, x3_ref,
    w_ref, bias_ref, lhs_ref, q_s, k_s, v_s, o_s, sems,
):
    width = x_ref.shape[2]
    first = pl.program_id(0) == 0
    sources = [wt_hbm.at[i] for i in range(4)] + [wc_hbm.at[i] for i in range(4)]
    loads = Loads([(w, w_ref.at[i, pl.ds(0, width), :]) for i, w in enumerate(sources)], sems)
    loads.start()

    @pl.when(first)
    def _():
        bias_ref[...] = same_place(bias_ref.shape)
        lhs_ref[:, width:] = jnp.zeros((ROWS, PAD), BF16)
        for i in range(8):
            w_ref[i, width:, :] = up_rows(ad_ref, 4 + i, i if i < 3 else 0, width)

    loaded = x_ref[...].reshape(ROWS, width)
    stream = loaded.astype(F32)
    lhs_ref[:, :width] = loaded
    three_projections(lhs_ref, ad_ref, 4, w_ref, loads, 0, (q_s, k_s, v_s), rq_ref.at[0])
    q_ref[...] = q_s[...].reshape(q_ref.shape)
    k_ref[...] = k_s[...].reshape(k_ref.shape)
    v_ref[...] = v_s[...].reshape(v_ref.shape)

    def put_out(index, value):
        o_s[:, tile(index)] = value.astype(BF16)

    attend(q_s, k_s, v_s, mask_ref, bias_ref, put_out, stat_ref.at[0])
    lhs_ref[:, :width] = o_s[...]
    o_ref[...] = o_s[...].reshape(o_ref.shape)
    loads.ready(3)
    branch = one_projection(lhs_ref, ad_ref, 7, w_ref.at[3], ro_ref.at[0])
    stream = stream + mod_ref[2:3, :] * branch
    inputs = stream.astype(BF16)
    u2_ref[...] = inputs.reshape(u2_ref.shape)
    lhs_ref[:, :width] = inputs
    loads.ready(4)
    queries = one_projection(lhs_ref, ad_ref, 8, w_ref.at[4], rqc_ref.at[0])
    q_s[...] = (queries * EXP_SCALE).astype(BF16)
    qc_ref[...] = q_s[...].reshape(qc_ref.shape)
    loads.ready(5)
    loads.ready(6)

    @pl.when(first)
    def _():
        for number, at, rank_ref, pair_ref in ((9, 5, rk_ref, kp_ref), (10, 6, rv_ref, vp_ref)):
            ranks = nt(ctx_ref[...], ad_ref[2 * number]).astype(BF16)
            rank_ref[...] = ranks
            made = nn(ctx_ref[...], w_ref[at, :width, :]) + nn(ranks, ad_ref[2 * number + 1])
            k_s[:PAD, :] = made.astype(BF16)
            for pair in range(PAIRS):
                piece = k_s[:PAD, window(pair)]
                pair_ref[pair, :PAD, :] = piece * mask_ref[2 * pair : 2 * pair + 1, :]
                pair_ref[pair, PAD:, :] = piece * mask_ref[2 * pair + 1 : 2 * pair + 2, :]

    carried = None
    count = 120
    for pair in range(PAIRS):
        scores = nt(kp_ref[pair], q_s[:, window(pair)])
        pieces = []
        for sub in range(2):
            own = scores[PAD * sub : PAD * sub + count]
            top = jnp.max(own, 0, keepdims=True)
            grown = jnp.exp2(own - top)
            total = jnp.sum(grown, 0, keepdims=True)
            statc_ref[0, 2 * pair + sub : 2 * pair + sub + 1, :] = top + jnp.log2(total)
            pieces += [grown * (1.0 / total), jnp.zeros((PAD - count, ROWS), F32)]
        weights = jnp.concatenate(pieces, 0).astype(BF16)
        out = tn(weights, vp_ref[pair])
        low = out[:, :128]
        put_out(pair, low if carried is None else low + carried)
        carried = out[:, 128:]
    put_out(PAIRS, carried)
    lhs_ref[:, :width] = o_s[...]
    oc_ref[...] = o_s[...].reshape(oc_ref.shape)
    loads.ready(7)
    stream = stream + one_projection(lhs_ref, ad_ref, 11, w_ref.at[7], roc_ref.at[0])
    x3_ref[...] = stream.reshape(x3_ref.shape)


def gelu_both(hidden):
    root = math.sqrt(2.0 / math.pi)
    square = hidden * hidden
    inner = root * (hidden + 0.044715 * (square * hidden))
    bent = jnp.tanh(inner)
    half = 0.5 * (1.0 + bent)
    slope = half + 0.5 * hidden * (1.0 - bent * bent) * (root * (1.0 + 3.0 * 0.044715 * square))
    return hidden * half, slope


def transposed_map(rows):
    nothing = jnp.zeros((PAD - rows.shape[0], rows.shape[1]), F32)
    wide = jnp.concatenate([rows.astype(F32), nothing], 0)
    return wide.T.astype(BF16)


def down_loads(core_ref, mine_hbm, other_hbm, down_ref, width):
    half = width // 2
    entries = []
    for c in range(down_ref.shape[0] // width):
        for source, core in ((mine_hbm, core_ref[0]), (other_hbm, 1 - core_ref[0])):
            start = pl.multiple_of(c * width + core * half, 16)
            entries.append((source.at[c], down_ref.at[pl.ds(start, half), pl.ds(0, width)]))
    return entries


def fill_down_maps(ad_ref, down_ref, width):
    chunks = down_ref.shape[0] // width
    for c in range(chunks):
        rows = slice(c * width, (c + 1) * width)
        down_ref[rows, width:] = transposed_map(ad_ref[2 + chunks + c])


def feed_forward_grad(
    core_ref, cot_ref, mod_ref, ad_ref, mine_hbm, other_hbm, grad_ref, down_ref, lhs_ref, sems
):
    width = cot_ref.shape[1]
    entries = down_loads(core_ref, mine_hbm, other_hbm, down_ref, width)
    loads = Loads(entries, sems)
    loads.start()

    @pl.when(loads.first)
    def _():
        lhs_ref[:, width:] = jnp.zeros((ROWS, PAD), BF16)
        fill_down_maps(ad_ref, down_ref, width)

    branch = (mod_ref[5:6, :] * cot_ref[...].astype(F32)).astype(BF16)
    lhs_ref[:, :width] = branch
    lhs_ref[:, width : width + RANK] = nt(branch, ad_ref[1]).astype(BF16)
    for i in range(len(entries)):
        loads.ready(i)
    for cols in hidden_chunks(down_ref.shape[0]):
        grad_ref[:, cols] = nt(lhs_ref[...], down_ref[cols, :]).astype(BF16)


def hidden_chunks(hidden):
    return [slice(at, at + 1536) for at in range(0, hidden, 1536)]


def feed_forward(
    x3_ref, cot_ref, grad_ref, mod_ref, ad_ref, w_hbm,
    act_ref, g3_ref, gd_ref, gu_ref, up_ref, lhs_ref, dh_ref, sems,
):
    width = x3_ref.shape[1]
    hidden_size = up_ref.shape[1]
    chunks = hidden_size // width
    loads = Loads(
        [
            (w_hbm.at[c], up_ref.at[pl.ds(0, width), pl.ds(c * width, width)])
            for c in range(chunks)
        ],
        sems,
    )
    loads.start()

    @pl.when(loads.first)
    def _():
        gd_ref[...] = jnp.zeros_like(gd_ref)
        gu_ref[...] = jnp.zeros_like(gu_ref)
        lhs_ref[:, width:] = jnp.zeros((ROWS, PAD), BF16)
        up_ref[width + RANK :, :] = jnp.zeros((PAD - RANK, hidden_size), BF16)
        for c in range(chunks):
            up_ref[width : width + RANK, c * width : (c + 1) * width] = ad_ref[2 + c]

    normal, inverse = normalize(x3_ref[...])
    inputs = (normal * (1.0 + mod_ref[4:5, :]) + mod_ref[3:4, :]).astype(BF16)
    rank_up = nt(inputs, ad_ref[0]).astype(BF16)
    lhs_ref[:, :width] = inputs
    lhs_ref[:, width : width + RANK] = rank_up
    for c in range(chunks):
        loads.ready(c)
    for cols in hidden_chunks(hidden_size):
        active, slope = gelu_both(nn(lhs_ref[...], up_ref[:, cols]))
        act_ref[:, cols] = active.astype(BF16)
        dh_ref[:, cols] = (slope * grad_ref[:, cols].astype(F32)).astype(BF16)
    both = nt(dh_ref[...], up_ref[...])
    gu_ref[...] += tn(rank_up, dh_ref[...])
    grad_rank = both[:, width : width + RANK].astype(BF16)
    grad_in = both[:, :width] + nn(grad_rank, ad_ref[0])
    gd_ref[...] += tn(grad_rank, lhs_ref[:, :width])
    grad_in = normalize_back(normal, inverse, grad_in * (1.0 + mod_ref[4:5, :]))
    g3_ref[...] = cot_ref[...].astype(F32) + grad_in


def feed_forward_out(
    core_ref, act_ref, x3_ref, cot_ref, mod_ref, ad_ref, mine_hbm, other_hbm,
    x4_ref, gu_ref, gd_ref, down_ref, sems,
):
    width = x3_ref.shape[1]
    entries = down_loads(core_ref, mine_hbm, other_hbm, down_ref, width)
    loads = Loads(entries, sems)
    loads.start()

    @pl.when(loads.first)
    def _():
        gu_ref[...] = jnp.zeros_like(gu_ref)
        gd_ref[...] = jnp.zeros_like(gd_ref)
        fill_down_maps(ad_ref, down_ref, width)

    grad_branch = (mod_ref[5:6, :] * cot_ref[...].astype(F32)).astype(BF16)
    gd_ref[...] += tn(nt(grad_branch, ad_ref[1]).astype(BF16), act_ref[...])
    for i in range(len(entries)):
        loads.ready(i)
    both = nn(act_ref[...], down_ref[...])
    ranks = both[:, width : width + RANK].astype(BF16)
    branch = both[:, :width] + nn(ranks, ad_ref[1])
    gu_ref[...] += tn(ranks, grad_branch)
    x4_ref[...] = (x3_ref[...] + mod_ref[5:6, :] * branch).astype(BF16)


def cross_temporal_backward(
    g3_ref, u1_ref, q_ref, k_ref, v_ref, o_ref, stat_ref, rq_ref, ro_ref,
    u2_ref, qc_ref, oc_ref, statc_ref, rqc_ref, roc_ref, kp_ref, vp_ref,
    mod_ref, mask_ref, ad_ref, wt_hbm, wc_hbm,
    g1_ref, gw_ref, dk_acc, dv_acc, w_ref, bias_ref, q_s, k_s, v_s, do_s, dq_s, dk_s, dv_s, sems,
):
    width = u1_ref.shape[2]
    first = pl.program_id(0) == 0
    order = (7, 4, 3, 0, 1, 2)
    sources = [wc_hbm.at[n - 4] if n >= 4 else wt_hbm.at[n] for n in order]
    loads = Loads([(w, w_ref.at[i, pl.ds(0, width), :]) for i, w in enumerate(sources)], sems)
    loads.start()

    @pl.when(first)
    def _():
        bias_ref[...] = same_place(bias_ref.shape)
        gw_ref[...] = jnp.zeros_like(gw_ref)
        dk_acc[...] = jnp.zeros_like(dk_acc)
        dv_acc[...] = jnp.zeros_like(dv_acc)
        for i, n in enumerate(order):
            w_ref[i, width:, :] = up_rows(ad_ref, 4 + n, n if n < 3 else 0, width)

    def rows(ref):
        return ref[...].reshape(ROWS, ref.shape[2])

    grad = rows(g3_ref)
    loads.ready(0)
    do_s[...] = one_back(
        grad.astype(BF16), rows(oc_ref), roc_ref[0], ad_ref, 11, w_ref.at[0], gw_ref, 14
    ).astype(BF16)
    q_s[...] = rows(qc_ref)
    count = 120
    carried = None
    for pair in range(PAIRS):
        win = window(pair)
        q_win, do_win = q_s[:, win], do_s[:, win]
        scores = nt(kp_ref[pair], q_win)
        grad_probs = nt(vp_ref[pair], do_win)
        all_probs, all_grads = [], []
        nothing = jnp.zeros((PAD - count, ROWS), F32)
        for sub in range(2):
            span = slice(PAD * sub, PAD * sub + count)
            row = 2 * pair + sub
            probs = jnp.exp2(scores[span] - statc_ref[0, row : row + 1, :])
            own = grad_probs[span]
            inner = jnp.sum(probs * own, 0, keepdims=True)
            all_probs += [probs, nothing]
            all_grads += [probs * (own - inner), nothing]
        probs = jnp.concatenate(all_probs, 0).astype(BF16)
        grad_scores = jnp.concatenate(all_grads, 0).astype(BF16)
        dk_acc[pair] += nn(grad_scores, q_win)
        dv_acc[pair] += nn(probs, do_win)
        out = tn(grad_scores, kp_ref[pair])
        low = out[:, :128]
        dq_s[:, tile(pair)] = ((low if carried is None else low + carried) * SCALE).astype(BF16)
        carried = out[:, 128:]
    dq_s[:, tile(PAIRS)] = (carried * SCALE).astype(BF16)
    loads.ready(1)
    grad = grad + one_back(
        dq_s[...], rows(u2_ref), rqc_ref[0], ad_ref, 8, w_ref.at[1], gw_ref, 8
    )
    loads.ready(2)
    do_s[...] = one_back(
        (mod_ref[2:3, :] * grad).astype(BF16), rows(o_ref), ro_ref[0], ad_ref, 7, w_ref.at[2], gw_ref, 6
    ).astype(BF16)
    q_s[...] = rows(q_ref)
    k_s[...] = rows(k_ref)
    v_s[...] = rows(v_ref)

    def put(index, values):
        dq_s[:, tile(index)] = (values[0] * SCALE).astype(BF16)
        dk_s[:, tile(index)] = (values[1] * LN2).astype(BF16)
        dv_s[:, tile(index)] = values[2].astype(BF16)

    attend_back(q_s, k_s, v_s, do_s, mask_ref, bias_ref, stat_ref.at[0], put)
    grad = grad + three_back(
        (dq_s, dk_s, dv_s), rows(u1_ref), rq_ref[0], ad_ref, 4, w_ref, loads, 3, gw_ref, 0
    )
    g1_ref[...] = grad.astype(BF16).reshape(g1_ref.shape)


def pack_columns(table_ref, packed_ref, clips):
    parts = packed_ref.shape[0] // clips
    _, share, cols = packed_ref.shape
    for f in range(clips):
        for s in range(parts):
            piece = table_ref[share * s : share * (s + 1), cols * f : cols * (f + 1)]
            packed_ref[f * parts + s] = piece.astype(BF16)


def stacked(g1_refs):
    parts = g1_refs[0].shape[0]
    pieces = [ref[s, 0] for s in range(parts) for ref in g1_refs]
    return jnp.concatenate(pieces, 0).astype(F32)


def spatial_backward(halves, clips, *refs):
    g1_refs, refs = refs[:halves], refs[halves:]
    (
        x_ref, q_ref, k_ref, v_ref, o_ref, stat_ref, rq_ref, ro_ref, mod_ref, mask_ref, ad_ref, w_hbm,
        down_ref, up_ref, d_ref, packed_ref, w_ref, gw_ref, do_s, sems,
    ) = refs
    width = x_ref.shape[2]
    loads = Loads([(w_hbm.at[3], w_ref.at[pl.ds(0, width), :])], sems)
    loads.start()

    @pl.when(loads.first)
    def _():
        gw_ref[...] = jnp.zeros_like(gw_ref)
        w_ref[width:, :] = up_rows(ad_ref, 3, 0, width)

    grad = stacked(g1_refs)
    loads.ready(0)
    do_s[...] = one_back(
        (mod_ref[2:3, :] * grad).astype(BF16), o_ref[0], ro_ref[0], ad_ref, 3, w_ref, gw_ref, 6
    ).astype(BF16)

    def put(index, values):
        for i, factor in enumerate((SCALE, LN2, 1.0)):
            value = values[i] if factor == 1.0 else values[i] * factor
            d_ref[0, :, width * i + 128 * index : width * i + 128 * index + 128] = value.astype(BF16)

    attend_back(
        q_ref.at[0], k_ref.at[0], v_ref.at[0], do_s, mask_ref, None, stat_ref.at[0], put
    )
    ranks = rq_ref[0]
    grad_ranks = None
    for i in range(3):
        grad = d_ref[0, :, width * i : width * (i + 1)]
        gw_ref[block_rows(2 * i + 1), :] += tn(ranks, grad)[block_rows(i)]
        part = nt(grad, up_rows(ad_ref, i, i, width))
        grad_ranks = part if grad_ranks is None else grad_ranks + part
    d_ref[0, :, 3 * width :] = grad_ranks.astype(BF16)
    normal, _ = normalize(x_ref[0].astype(F32))
    inputs = (normal * (1.0 + mod_ref[1:2, :]) + mod_ref[0:1, :]).astype(BF16)
    downs = tn(d_ref[0, :, 3 * width :], inputs)
    for i in range(3):
        gw_ref[block_rows(2 * i), :] += downs[block_rows(i)]

    @pl.when(pl.program_id(0) == pl.num_programs(0) - 1)
    def _():
        at = 8 * RANK
        gw_ref[at : at + RANK, :] = down_ref[...]
        gw_ref[at + RANK : at + RANK + up_ref.shape[0], :] = up_ref[...]
        pack_columns(gw_ref, packed_ref, clips)


def spatial_input_grad(halves, *refs):
    g1_refs, refs = refs[:halves], refs[halves:]
    x_ref, d_ref, mod_ref, ad_ref, w_hbm, g0_ref, w_ref, sems = refs
    width = x_ref.shape[2]
    loads = Loads(
        [(w_hbm.at[i], w_ref.at[:, pl.ds(i * width, width)]) for i in range(3)], sems
    )
    loads.start()

    @pl.when(loads.first)
    def _():
        w_ref[:, 3 * width :] = transposed_map(three_downs(ad_ref, 0))

    normal, inverse = normalize(x_ref[0].astype(F32))
    grad = stacked(g1_refs)
    for i in range(3):
        loads.ready(i)
    grad_in = nt(d_ref[0], w_ref[...])
    grad = grad + normalize_back(normal, inverse, grad_in * (1.0 + mod_ref[1:2, :]))
    g0_ref[0] = grad.astype(BF16)


def pack_early(clips, halves, *refs):
    gw_refs, refs = refs[:halves], refs[halves:]
    dk_refs, refs = refs[:halves], refs[halves:]
    dv_refs, refs = refs[:halves], refs[halves:]
    down_ref, up_ref, rk_ref, rv_ref, ctx_ref, mask_ref, ad_ref, packed_ref, table_ref, ctx_s = refs

    def added(each):
        total = each[0]
        for value in each[1:]:
            total = total + value
        return total

    at = gw_refs[0].shape[0]
    table_ref[:at, :] = added([ref[...] for ref in gw_refs])
    table_ref[at : at + RANK, :] = down_ref[...]
    at += RANK
    table_ref[at : at + up_ref.shape[0], :] = up_ref[...]
    at += up_ref.shape[0]
    table_ref[at:, :] = jnp.zeros((table_ref.shape[0] - at, table_ref.shape[1]), F32)
    context = ctx_ref[...].astype(F32)
    for accs, factor, rank_ref, number, at in (
        (dk_refs, LN2, rk_ref, 9, 10),
        (dv_refs, 1.0, rv_ref, 10, 12),
    ):
        held = None
        for pair in range(PAIRS):
            whole = added([ref[pair] for ref in accs]) * factor
            out = whole[:PAD] * mask_ref[2 * pair : 2 * pair + 1, :].astype(F32)
            out = out + whole[PAD:] * mask_ref[2 * pair + 1 : 2 * pair + 2, :].astype(F32)
            low = out[:, :128]
            ctx_s[:, tile(pair)] = low if held is None else low + held
            held = out[:, 128:]
        ctx_s[:, tile(PAIRS)] = held
        grad_kv = ctx_s[...]
        grad_rank = lax.dot_general(
            grad_kv, ad_ref[2 * number + 1].astype(F32), (((1,), (1,)), ((), ())),
            precision=HIGHEST, preferred_element_type=F32,
        )
        table_ref[block_rows(at), :] = lax.dot_general(
            grad_rank, context, (((0,), (0,)), ((), ())),
            precision=HIGHEST, preferred_element_type=F32,
        )
        table_ref[block_rows(at + 1), :] = lax.dot_general(
            rank_ref[...].astype(F32), grad_kv, (((0,), (0,)), ((), ())),
            precision=HIGHEST, preferred_element_type=F32,
        )
    pack_columns(table_ref, packed_ref, clips)


def assemble(early_ref, late_ref, wide_ref, narrow_ref):
    adapters = wide_ref.shape[1]
    times = narrow_ref.shape[3] // wide_ref.shape[3]

    def block(ref, index, a):
        each = ref.shape[2] // RANK
        return ref[index // each, a, block_rows(index % each), :].astype(F32)

    for a in range(adapters):
        for i in range(8):
            wide_ref[i, a] = block(late_ref, i, a)
        for i in range(17):
            wide_ref[8 + i, a] = block(early_ref, i, a)
        wide_ref[25, a] = block(late_ref, 8, a)
        for n, (ref, at) in enumerate(((early_ref, 17), (late_ref, 9))):
            narrow_ref[n, a] = jnp.concatenate([block(ref, at + j, a) for j in range(times)], 1)


def combine(index_ref, got_ref, out_ref, acc_ref):
    clips = index_ref.shape[0]
    parts = got_ref.shape[0] // clips
    acc_ref[...] = jnp.zeros_like(acc_ref)

    def step(f, carry):
        total = got_ref[f * parts].astype(F32)
        for s in range(1, parts):
            total = total + got_ref[f * parts + s].astype(F32)
        acc_ref[index_ref[f]] += total
        return carry

    lax.fori_loop(0, clips, step, 0)
    table = acc_ref[...].astype(BF16)
    for s in range(parts):
        out_ref[s] = table


def tail_groups(cols):
    tail = cols - PAD
    return PAD // tail if 0 < tail < PAD and PAD % tail == 0 else 0


def pick(index_ref, wide_ref, narrow_ref, out_ref):
    clips = index_ref.shape[0]
    count, _, _, cols = wide_ref.shape
    times = narrow_ref.shape[3] // cols
    group = tail_groups(cols)
    total = count + 2 * times

    def step(f, carry):
        a = index_ref[f]
        blocks = [wide_ref[k, a] for k in range(count)]
        for p in range(2):
            rows = narrow_ref[p, a]
            blocks += [rows[:, cols * j : cols * (j + 1)] for j in range(times)]
        if not group:
            for k, rows in enumerate(blocks):
                out_ref[f, block_rows(k), :] = rows
            return carry
        for k, rows in enumerate(blocks):
            out_ref[f, block_rows(k), :] = rows[:, :PAD]
        for k in range(0, total, group):
            tails = [rows[:, PAD:] for rows in blocks[k : k + group]]
            missing = group - len(tails)
            if missing:
                tails.append(jnp.zeros((RANK, missing * (cols - PAD)), BF16))
            out_ref[f, block_rows(total + k // group), :] = jnp.concatenate(tails, 1)
        return carry

    lax.fori_loop(0, clips, step, 0)


def unpick(count, cols, got_ref, out_ref):
    clips = got_ref.shape[0]
    group = tail_groups(cols)
    for k in range(count):
        pieces = []
        for f in range(clips):
            pieces.append(got_ref[f, block_rows(k), :])
            if group:
                at = (k % group) * (cols - PAD)
                tails = got_ref[f, block_rows(count + k // group), :]
                pieces.append(tails[:, at : at + cols - PAD])
        out_ref[k] = jnp.concatenate(pieces, 1)


def whole_block(array):
    zeros = (0,) * array.ndim
    return pl.BlockSpec(array.shape, lambda i: zeros, pipeline_mode=pl.Buffered(1))


def anywhere():
    return pl.BlockSpec(memory_space=pl.ANY)


def like(shape, dtype):
    return jax.ShapeDtypeStruct(shape, dtype)


PARAMS = pltpu.CompilerParams(
    dimension_semantics=("arbitrary",), vmem_limit_bytes=VMEM_LIMIT
)


def cost(flops, read):
    return pl.CostEstimate(flops=flops, bytes_accessed=read, transcendentals=flops // 4096)


def run_spatial_forward(video, mods, masks, wide, w_s, parts):
    frames, rows, d = video.shape
    places = rows // parts
    by_frame = lambda i: (i, 0, 0)
    row_block = pl.BlockSpec((1, rows, d), by_frame)
    return pl.pallas_call(
        spatial_forward,
        grid=(frames,),
        in_specs=[row_block, whole_block(mods), whole_block(masks), whole_block(wide), anywhere()],
        out_specs=[
            pl.BlockSpec((parts, 1, places, d), lambda i: (0, i, 0, 0)),
            row_block,
            row_block,
            row_block,
            row_block,
            pl.BlockSpec((1, HEADS, rows), by_frame),
            pl.BlockSpec((1, rows, 3 * RANK), by_frame),
            pl.BlockSpec((1, rows, RANK), by_frame),
        ],
        out_shape=[like((parts, frames, places, d), BF16)]
        + [like(video.shape, BF16)] * 4
        + [
            like((frames, HEADS, rows), F32),
            like((frames, rows, 3 * RANK), BF16),
            like((frames, rows, RANK), BF16),
        ],
        scratch_shapes=[
            pltpu.VMEM((4, d + PAD, d), BF16),
            pltpu.VMEM((ROWS, d + PAD), BF16),
            pltpu.SemaphoreType.DMA((4,)),
        ],
        compiler_params=PARAMS,
        cost_estimate=cost(10 * frames * rows * d * d, 30_000_000),
        name="spatial_forward",
    )(video, mods, masks, wide, w_s)


def run_temporal_cross_forward(x1, context, mods, masks, wide, w_t, w_c):
    frames, places, d = x1.shape
    groups = places * frames // ROWS
    across = pl.BlockSpec((frames, ROWS // frames, d), lambda i: (0, i, 0))
    by_group = lambda i: (i, 0, 0)
    stat = pl.BlockSpec((1, HEADS, ROWS), by_group)
    three = pl.BlockSpec((1, ROWS, 3 * RANK), by_group)
    one = pl.BlockSpec((1, ROWS, RANK), by_group)
    full = lambda *shape: pl.BlockSpec(shape, lambda i: (0,) * len(shape))
    act = like(x1.shape, BF16)
    stat_shape = like((groups, HEADS, ROWS), F32)
    one_shape = like((groups, ROWS, RANK), BF16)
    return pl.pallas_call(
        temporal_cross_forward,
        grid=(groups,),
        in_specs=[across, whole_block(context), whole_block(mods), whole_block(masks), whole_block(wide), anywhere(), anywhere()],
        out_specs=[across] * 4 + [stat, three, one] + [across] * 3 + [stat, one, one]
        + [full(PAIRS, 2 * PAD, 256)] * 2 + [full(PAD, RANK)] * 2 + [across],
        out_shape=[act] * 4 + [stat_shape, like((groups, ROWS, 3 * RANK), BF16), one_shape]
        + [act] * 3 + [stat_shape, one_shape, one_shape]
        + [like((PAIRS, 2 * PAD, 256), BF16)] * 2 + [like((PAD, RANK), BF16)] * 2
        + [like(x1.shape, F32)],
        scratch_shapes=[pltpu.VMEM((8, d + PAD, d), BF16), pltpu.VMEM((ROWS, ROWS), F32)]
        + [pltpu.VMEM((ROWS, d + PAD), BF16)]
        + [pltpu.VMEM((ROWS, d), BF16)] * 4
        + [pltpu.SemaphoreType.DMA((8,))],
        compiler_params=PARAMS,
        cost_estimate=cost(14 * places * frames * d * d, 50_000_000),
        name="temporal_cross_forward",
    )(x1, context, mods, masks, wide, w_t, w_c)


def in_smem():
    return pl.BlockSpec(memory_space=pltpu.SMEM)


def run_feed_forward_grad(cot, mods, maps, down):
    tokens, d = cot.shape
    core, mine, other = down
    hidden = mine.shape[0] * d
    return pl.pallas_call(
        feed_forward_grad,
        grid=(tokens // ROWS,),
        in_specs=[in_smem(), pl.BlockSpec((ROWS, d), lambda i: (i, 0)), whole_block(mods), whole_block(maps), anywhere(), anywhere()],
        out_specs=pl.BlockSpec((ROWS, hidden), lambda i: (i, 0)),
        out_shape=like((tokens, hidden), BF16),
        scratch_shapes=[
            pltpu.VMEM((hidden, d + PAD), BF16),
            pltpu.VMEM((ROWS, d + PAD), BF16),
            pltpu.SemaphoreType.DMA((2 * mine.shape[0],)),
        ],
        compiler_params=PARAMS,
        cost_estimate=cost(2 * tokens * d * hidden, 30_000_000),
        name="feed_forward_grad",
    )(core, cot, mods, maps, mine, other)


def run_feed_forward(x3, cot, grad_active, mods, maps, up):
    tokens, d = x3.shape
    chunks = up.shape[0]
    rows = pl.BlockSpec((ROWS, d), lambda i: (i, 0))
    wide_rows = pl.BlockSpec((ROWS, chunks * d), lambda i: (i, 0))
    return pl.pallas_call(
        feed_forward,
        grid=(tokens // ROWS,),
        in_specs=[rows, rows, wide_rows, whole_block(mods), whole_block(maps), anywhere()],
        out_specs=[
            wide_rows,
            rows,
            pl.BlockSpec((RANK, d), lambda i: (0, 0)),
            pl.BlockSpec((RANK, chunks * d), lambda i: (0, 0)),
        ],
        out_shape=[
            like((tokens, chunks * d), BF16),
            like((tokens, d), F32),
            like((RANK, d), F32),
            like((RANK, chunks * d), F32),
        ],
        scratch_shapes=[
            pltpu.VMEM((d + PAD, chunks * d), BF16),
            pltpu.VMEM((ROWS, d + PAD), BF16),
            pltpu.VMEM((ROWS, chunks * d), BF16),
            pltpu.SemaphoreType.DMA((chunks,)),
        ],
        compiler_params=PARAMS,
        cost_estimate=cost(4 * tokens * d * d * chunks, 50_000_000),
        name="feed_forward",
    )(x3, cot, grad_active, mods, maps, up)


def run_feed_forward_out(active, x3, cot, mods, maps, down):
    tokens, d = x3.shape
    core, mine, other = down
    hidden = active.shape[1]
    rows = pl.BlockSpec((ROWS, d), lambda i: (i, 0))
    return pl.pallas_call(
        feed_forward_out,
        grid=(tokens // ROWS,),
        in_specs=[
            in_smem(),
            pl.BlockSpec((ROWS, hidden), lambda i: (i, 0)),
            rows,
            rows,
            whole_block(mods),
            whole_block(maps),
            anywhere(),
            anywhere(),
        ],
        out_specs=[
            rows,
            pl.BlockSpec((RANK, d), lambda i: (0, 0)),
            pl.BlockSpec((RANK, hidden), lambda i: (0, 0)),
        ],
        out_shape=[
            like((tokens, d), BF16),
            like((RANK, d), F32),
            like((RANK, hidden), F32),
        ],
        scratch_shapes=[
            pltpu.VMEM((hidden, d + PAD), BF16),
            pltpu.SemaphoreType.DMA((2 * mine.shape[0],)),
        ],
        compiler_params=PARAMS,
        cost_estimate=cost(2 * tokens * d * hidden, 30_000_000),
        name="feed_forward_out",
    )(core, active, x3, cot, mods, maps, mine, other)


def run_cross_temporal_backward(g3, u1, saved, mods, masks, wide, w_t, w_c, half, halves):
    frames, places, d = u1.shape
    groups = places * frames // ROWS // halves
    start = half * groups
    across = pl.BlockSpec((frames, ROWS // frames, d), lambda i: (0, i + start, 0))
    by_group = lambda i: (i + start, 0, 0)
    stat = pl.BlockSpec((1, HEADS, ROWS), by_group)
    three = pl.BlockSpec((1, ROWS, 3 * RANK), by_group)
    one = pl.BlockSpec((1, ROWS, RANK), by_group)
    kp, vp = saved[13:15]
    pair_sums = pl.BlockSpec((PAIRS, 2 * PAD, 256), lambda i: (0, 0, 0))
    return pl.pallas_call(
        cross_temporal_backward,
        grid=(groups,),
        in_specs=[across, across] + [across] * 4 + [stat, three, one] + [across] * 3 + [stat, one, one]
        + [whole_block(kp), whole_block(vp)]
        + [whole_block(mods), whole_block(masks), whole_block(wide), anywhere(), anywhere()],
        out_specs=[
            pl.BlockSpec((frames, ROWS // frames, d), lambda i: (0, i, 0)),
            pl.BlockSpec((16 * RANK, d), lambda i: (0, 0)),
            pair_sums,
            pair_sums,
        ],
        out_shape=[like((frames, places // halves, d), BF16), like((16 * RANK, d), F32)]
        + [like((PAIRS, 2 * PAD, 256), F32)] * 2,
        scratch_shapes=[
            pltpu.VMEM((6, d + PAD, d), BF16),
            pltpu.VMEM((ROWS, ROWS), F32),
        ]
        + [pltpu.VMEM((ROWS, d), BF16)] * 7
        + [pltpu.SemaphoreType.DMA((6,))],
        compiler_params=PARAMS,
        cost_estimate=cost(14 * places // halves * frames * d * d, 30_000_000),
        name="cross_temporal_backward",
    )(g3, u1, *saved[:15], mods, masks, wide, w_t, w_c)


LATE_BLOCKS = 16
EARLY_BLOCKS = 24


def run_spatial_backward(g1_halves, video, saved, mods, masks, wide, w_s, late_down, late_up, clips):
    frames, rows, d = video.shape
    parts = g1_halves[0].shape[0]
    by_frame = lambda i: (i, 0, 0)
    row_block = pl.BlockSpec((1, rows, d), by_frame)
    packed = (clips * parts, LATE_BLOCKS * RANK // parts, d // clips)

    def body(*refs):
        spatial_backward(len(g1_halves), clips, *refs)

    return pl.pallas_call(
        body,
        grid=(frames,),
        in_specs=[
            pl.BlockSpec((parts, 1, g.shape[2], d), lambda i: (0, i, 0, 0)) for g in g1_halves
        ]
        + [row_block] * 5
        + [
            pl.BlockSpec((1, HEADS, rows), by_frame),
            pl.BlockSpec((1, rows, 3 * RANK), by_frame),
            pl.BlockSpec((1, rows, RANK), by_frame),
            whole_block(mods),
            whole_block(masks),
            whole_block(wide),
            anywhere(),
            whole_block(late_down),
            whole_block(late_up),
        ],
        out_specs=[
            pl.BlockSpec((1, rows, 3 * d + PAD), by_frame),
            pl.BlockSpec(packed, lambda i: (0, 0, 0)),
        ],
        out_shape=[like((frames, rows, 3 * d + PAD), BF16), like(packed, BF16)],
        scratch_shapes=[pltpu.VMEM((d + PAD, d), BF16), pltpu.VMEM((LATE_BLOCKS * RANK, d), F32)]
        + [pltpu.VMEM((ROWS, d), BF16), pltpu.SemaphoreType.DMA((1,))],
        compiler_params=PARAMS,
        cost_estimate=cost(6 * frames * rows * d * d, 30_000_000),
        name="spatial_backward",
    )(*g1_halves, video, *saved, mods, masks, wide, w_s, late_down, late_up)


def run_spatial_input_grad(g1_halves, video, grads, mods, wide, w_s):
    frames, rows, d = video.shape
    parts = g1_halves[0].shape[0]
    by_frame = lambda i: (i, 0, 0)
    row_block = pl.BlockSpec((1, rows, d), by_frame)

    def body(*refs):
        spatial_input_grad(len(g1_halves), *refs)

    return pl.pallas_call(
        body,
        grid=(frames,),
        in_specs=[
            pl.BlockSpec((parts, 1, g.shape[2], d), lambda i: (0, i, 0, 0)) for g in g1_halves
        ]
        + [
            row_block,
            pl.BlockSpec((1, rows, grads.shape[2]), by_frame),
            whole_block(mods),
            whole_block(wide),
            anywhere(),
        ],
        out_specs=row_block,
        out_shape=like(video.shape, BF16),
        scratch_shapes=[pltpu.VMEM((d, 3 * d + PAD), BF16), pltpu.SemaphoreType.DMA((3,))],
        compiler_params=PARAMS,
        cost_estimate=cost(6 * frames * rows * d * d, 20_000_000),
        name="spatial_input_grad",
    )(*g1_halves, video, grads, mods, wide, w_s)


PLAIN = pltpu.CompilerParams(vmem_limit_bytes=VMEM_LIMIT)


def in_vmem():
    return pl.BlockSpec(memory_space=pltpu.VMEM)


def run_pack_early(gw, dk, dv, sources, clips, parts):
    d = gw[0].shape[1]
    packed = (clips * parts, EARLY_BLOCKS * RANK // parts, d // clips)

    def body(*refs):
        pack_early(clips, len(gw), *refs)

    return pl.pallas_call(
        body,
        out_shape=like(packed, BF16),
        scratch_shapes=[pltpu.VMEM((EARLY_BLOCKS * RANK, d), F32), pltpu.VMEM((PAD, d), F32)],
        compiler_params=PLAIN,
        name="pack_early",
    )(*gw, *dk, *dv, *sources)


def run_assemble(early, late, wide_shape, narrow_shape):
    return pl.pallas_call(
        assemble,
        in_specs=[in_vmem()] * 2,
        out_specs=[in_vmem()] * 2,
        out_shape=[like(wide_shape, F32), like(narrow_shape, F32)],
        compiler_params=PLAIN,
        name="assemble",
    )(early, late)


def run_pick(all_index, wide, narrow):
    count, _, _, cols = wide.shape
    blocks = count + 2 * (narrow.shape[3] // cols)
    group = tail_groups(cols)
    shape = (blocks * RANK, cols)
    if group:
        shape = ((blocks + -(-blocks // group)) * RANK, PAD)
    return pl.pallas_call(
        pick,
        in_specs=[in_smem(), in_vmem(), in_vmem()],
        out_specs=in_vmem(),
        out_shape=like((all_index.shape[0], *shape), BF16),
        compiler_params=PLAIN,
        name="pick",
    )(all_index, wide, narrow)


def run_unpick(got, blocks, cols):
    def body(*refs):
        unpick(blocks, cols, *refs)

    return pl.pallas_call(
        body,
        in_specs=[in_vmem()],
        out_specs=in_vmem(),
        out_shape=like((blocks, RANK, got.shape[0] * cols), BF16),
        compiler_params=PLAIN,
        name="unpick",
    )(got)


def run_combine(all_index, got, adapters):
    clips = all_index.shape[0]
    parts = got.shape[0] // clips
    _, share, cols = got.shape
    return pl.pallas_call(
        combine,
        in_specs=[pl.BlockSpec(memory_space=pltpu.SMEM), pl.BlockSpec(memory_space=pltpu.VMEM)],
        out_specs=pl.BlockSpec(memory_space=pltpu.VMEM),
        out_shape=like((parts, adapters, share, cols), BF16),
        scratch_shapes=[pltpu.VMEM((adapters, share, cols), F32)],
        compiler_params=pltpu.CompilerParams(vmem_limit_bytes=VMEM_LIMIT),
        name="combine",
    )(all_index, got)


def exchange(array, axes="seq"):
    return lax.all_to_all(array, axes, split_axis=0, concat_axis=0, tiled=True)


def reduce_grads(packed, all_index, adapters):
    got = exchange(packed, ("fsdp", "seq"))
    return run_combine(all_index, got, adapters)


def up_chunks(up, clips, times):
    rows, hidden = up.shape
    cols = hidden // (clips * times)
    return up.reshape(rows, clips, times, cols).transpose(2, 0, 1, 3).reshape(times, rows, -1)


def gather(array):
    return lax.all_gather(array, "fsdp", axis=1, tiled=True)


def fetch_down(down, clips, parts, times, d):
    quarters = down.reshape(times, -1, d)
    half = d // 2
    if times != parts or clips % 2:
        whole = gather(quarters)
        return jnp.zeros((1,), jnp.int32), whole[:, :half], whole[:, half:]
    own = gather(lax.dynamic_slice_in_dim(quarters, lax.axis_index("seq"), 1, 0))[0]
    core = lax.axis_index("fsdp") % 2
    piece = lax.dynamic_slice_in_dim(own, core * half, half, 0)
    mine = exchange(jnp.broadcast_to(piece[None], (parts, half, d)))
    other = lax.ppermute(mine, "fsdp", [(i, i ^ 1) for i in range(clips)])
    return core.astype(jnp.int32)[None], mine, other


def on_device(
    video,
    context,
    modulation,
    adapter_index,
    cotangent,
    qkv_weights,
    out_weights,
    ffn_up,
    ffn_down,
    adapt_wide,
    adapt_ff,
):
    parts = lax.axis_size("seq")
    clips = lax.axis_size("fsdp")
    d = video.shape[-1]
    count, adapters, _, cols = adapt_wide.shape[1:]
    times = adapt_ff.shape[-1] // cols
    places = SPATIAL // parts
    frames = FRAMES // parts
    mods = modulation[0, 0]
    masks = head_masks()
    ctx = jnp.pad(context[0], ((0, PAD - context.shape[1]), (0, 0)))

    def attention_weights(j):
        return gather(
            jnp.concatenate([qkv_weights[0, 3 * j : 3 * j + 3], out_weights[0, j : j + 1]], 0)
        )

    all_index = exchange(jnp.broadcast_to(adapter_index, (clips,)), "fsdp")
    down = fetch_down(ffn_down[0], clips, parts, times, d)
    w_s = attention_weights(0)
    picked = run_pick(all_index, adapt_wide[0], adapt_ff[0])
    wide = run_unpick(exchange(picked, "fsdp"), count + 2 * times, cols)
    w_t = attention_weights(1)
    w_c = attention_weights(2)
    ffn_up, _ = lax.optimization_barrier((ffn_up, picked))
    up = gather(up_chunks(ffn_up[0], clips, times))
    maps_f = wide[24:]

    cot = cotangent.reshape(frames, parts, places, d).transpose(1, 0, 2, 3)
    cot = exchange(cot).reshape(FRAMES * places, d)
    frames_in = video.reshape(frames, SPATIAL, d)
    x1, *kept_s = run_spatial_forward(frames_in, mods, masks, wide, w_s, parts)
    u1 = exchange(x1).reshape(FRAMES, places, d)
    grad_active = run_feed_forward_grad(cot, mods, maps_f, down)
    *kept_t, x3 = run_temporal_cross_forward(u1, ctx, mods, masks, wide, w_t, w_c)
    x3 = x3.reshape(FRAMES * places, d)
    active, g3, grad_a24, grad_b24 = run_feed_forward(x3, cot, grad_active, mods, maps_f, up)
    g3 = g3.reshape(FRAMES, places, d)
    groups = FRAMES * places // ROWS
    halves = 2 if groups % 2 == 0 else 1
    g1_halves, gw, dk, dv = [], [], [], []
    for half in range(halves):
        g1, *sums = run_cross_temporal_backward(
            g3, u1, kept_t, mods, masks, wide, w_t, w_c, half, halves
        )
        for kept, value in zip((gw, dk, dv), sums):
            kept.append(value)
        g1_halves.append(exchange(g1.reshape(parts, frames, places // halves, d)))

    def as_blocks(rows):
        return rows.reshape(RANK, times, d).transpose(1, 0, 2).reshape(times * RANK, d)

    sources = [grad_a24, as_blocks(grad_b24), kept_t[15], kept_t[16], ctx, masks, wide]
    packed = run_pack_early(gw, dk, dv, sources, clips, parts)
    active, packed = lax.optimization_barrier((active, packed))
    x4, grad_b25, grad_down = run_feed_forward_out(active, x3, cot, mods, maps_f, down)
    early = reduce_grads(packed, all_index, adapters)
    output = exchange(x4.reshape(parts, frames, places, d))
    early, *g1_halves = lax.optimization_barrier((early, *g1_halves))
    grads, packed = run_spatial_backward(
        g1_halves, frames_in, kept_s, mods, masks, wide, w_s, grad_b25, as_blocks(grad_down), clips
    )
    early = exchange(early)
    g0 = run_spatial_input_grad(g1_halves, frames_in, grads, mods, wide, w_s)
    late = reduce_grads(packed, all_index, adapters)
    late, early, output = lax.optimization_barrier((late, early, output))
    wide_out, narrow_out = run_assemble(
        early, exchange(late), adapt_wide.shape[1:], adapt_ff.shape[1:]
    )
    output = output.transpose(1, 0, 2, 3).reshape(video.shape)
    return (output, g0.reshape(video.shape), wide_out[None], narrow_out[None])


def solution(mesh):
    return jax.shard_map(
        on_device,
        mesh=mesh,
        in_specs=(
            P("fsdp", "seq", None),
            P("fsdp", None, None),
            P("fsdp", None, None, None),
            P("fsdp"),
            P("fsdp", "seq", None),
            P(None, None, "fsdp", None),
            P(None, None, "fsdp", None),
            P(None, "fsdp", None),
            P(None, "fsdp", None),
            P(None, None, None, None, "fsdp"),
            P(None, None, None, None, "fsdp"),
        ),
        out_specs=(
            P("fsdp", "seq", None),
            P("fsdp", "seq", None),
            P(None, None, None, None, "fsdp"),
            P(None, None, None, None, "fsdp"),
        ),
        check_vma=False,
    )
```

```python
import math

import jax
import jax.numpy as jnp
from jax import lax
from jax.experimental import pallas as pl
from jax.experimental.pallas import tpu as pltpu
from jax.sharding import PartitionSpec as P

HEAD_DIM = 72
HEADS = 16
FRAMES = 16
SPATIAL = 256
RANK = 16
ROWS = 256
PAIRS = HEADS // 2
PAD = 128
SCALE = HEAD_DIM ** (-0.5)
EXP_SCALE = SCALE * math.log2(math.e)
LN2 = math.log(2.0)
HIGHEST = lax.Precision.HIGHEST
F32 = jnp.float32
BF16 = jnp.bfloat16
VMEM_LIMIT = 60 * 1024 * 1024


def nn(left, right):
    return lax.dot_general(left, right, (((1,), (0,)), ((), ())), preferred_element_type=F32)


def nt(left, right):
    return lax.dot_general(left, right, (((1,), (1,)), ((), ())), preferred_element_type=F32)


def tn(left, right):
    return lax.dot_general(left, right, (((0,), (0,)), ((), ())), preferred_element_type=F32)


def window(pair):
    return slice(128 * pair, 128 * pair + 256)


def normalize(stream):
    average = jnp.mean(stream, -1, keepdims=True)
    centred = stream - average
    inverse = lax.rsqrt(jnp.mean(centred * centred, -1, keepdims=True) + 1e-06)
    return centred * inverse, inverse


def normalize_back(normal, inverse, grad):
    mean_grad = jnp.mean(grad, -1, keepdims=True)
    mean_both = jnp.mean(grad * normal, -1, keepdims=True)
    return inverse * (grad - mean_grad - normal * mean_both)


def up_rows(ad_ref, number, slot, width):
    rows = ad_ref[2 * number + 1]
    before = jnp.zeros((RANK * slot, width), BF16)
    after = jnp.zeros((PAD - RANK * (slot + 1), width), BF16)
    return jnp.concatenate(([before] if slot else []) + [rows, after], 0)


def three_downs(ad_ref, number):
    return jnp.concatenate([ad_ref[2 * (number + i)] for i in range(3)], 0)


class Loads:
    def __init__(self, entries, sems):
        self.first = pl.program_id(0) == 0
        self.entries = entries
        self.sems = sems

    def copy(self, index):
        source, target = self.entries[index]
        return pltpu.make_async_copy(source, target, self.sems.at[index])

    def start(self):
        @pl.when(self.first)
        def _():
            for index in range(len(self.entries)):
                self.copy(index).start()

    def ready(self, index):
        @pl.when(self.first)
        def _():
            self.copy(index).wait()


def head_masks():
    lane = jnp.arange(256)[None, :]
    begin = jnp.array([16 * (h // 2) + HEAD_DIM * (h % 2) for h in range(HEADS)])[:, None]
    return ((lane >= begin) & (lane < begin + HEAD_DIM)).astype(BF16)


def same_place(shape):
    rows = lax.broadcasted_iota(jnp.int32, shape, 0)
    cols = lax.broadcasted_iota(jnp.int32, shape, 1)
    return jnp.where(rows % 16 == cols % 16, 0.0, -1e30).astype(F32)


def attend(q_ref, k_ref, v_ref, mask_ref, bias, put_out, stat_ref):
    carried = None
    for pair in range(PAIRS):
        win = window(pair)
        q_win, k_win, v_win = q_ref[:, win], k_ref[:, win], v_ref[:, win]
        all_weights, all_values = [], []
        for head in (2 * pair, 2 * pair + 1):
            mask = mask_ref[head : head + 1, :]
            scores = nt(k_win * mask, q_win)
            if bias is not None:
                scores = scores + bias[...]
            top = jnp.max(scores, 0, keepdims=True)
            grown = jnp.exp2(scores - top)
            total = jnp.sum(grown, 0, keepdims=True)
            stat_ref[head : head + 1, :] = top + jnp.log2(total)
            all_weights.append((grown * (1.0 / total)).astype(BF16))
            all_values.append(v_win * mask)
        out = tn(jnp.concatenate(all_weights, 0), jnp.concatenate(all_values, 0))
        low = out[:, :128]
        put_out(pair, low if carried is None else low + carried)
        carried = out[:, 128:]
    put_out(PAIRS, carried)


def attend_back(q_ref, k_ref, v_ref, do_ref, mask_ref, bias, stat_ref, put):
    carried = None
    for pair in range(PAIRS):
        win = window(pair)
        q_win, k_win, v_win, do_win = q_ref[:, win], k_ref[:, win], v_ref[:, win], do_ref[:, win]
        all_grads, all_probs, keys, queries, outs = [], [], [], [], []
        for head in (2 * pair, 2 * pair + 1):
            mask = mask_ref[head : head + 1, :]
            k_own = k_win * mask
            scores = nt(k_own, q_win)
            if bias is not None:
                scores = scores + bias[...]
            probs = jnp.exp2(scores - stat_ref[head : head + 1, :])
            grad_probs = nt(v_win * mask, do_win)
            inner = jnp.sum(probs * grad_probs, 0, keepdims=True)
            all_grads.append((probs * (grad_probs - inner)).astype(BF16))
            all_probs.append(probs.astype(BF16))
            keys.append(k_own)
            queries.append(q_win * mask)
            outs.append(do_win * mask)
        grads = (
            tn(jnp.concatenate(all_grads, 0), jnp.concatenate(keys, 0)),
            nn(jnp.concatenate(all_grads, 1), jnp.concatenate(queries, 0)),
            nn(jnp.concatenate(all_probs, 1), jnp.concatenate(outs, 0)),
        )
        lows = tuple(g[:, :128] for g in grads)
        if carried is not None:
            lows = tuple(a + b for a, b in zip(lows, carried))
        put(pair, lows)
        carried = tuple(g[:, 128:] for g in grads)
    put(PAIRS, carried)


def tile(index):
    return slice(128 * index, 128 * index + 128)


def three_projections(lhs_ref, ad_ref, number, weights, loads, first_load, outs, rank_ref):
    width = weights.shape[2]
    ranks = nt(lhs_ref[:, :width], three_downs(ad_ref, number)).astype(BF16)
    rank_ref[...] = ranks
    lhs_ref[:, width : width + 3 * RANK] = ranks
    for i in range(3):
        loads.ready(first_load + i)
        total = nn(lhs_ref[...], weights[first_load + i])
        outs[i][...] = (total * EXP_SCALE if i == 0 else total).astype(BF16)


def one_projection(lhs_ref, ad_ref, number, weight_ref, rank_ref):
    width = weight_ref.shape[1]
    ranks = nt(lhs_ref[:, :width], ad_ref[2 * number]).astype(BF16)
    rank_ref[...] = ranks
    lhs_ref[:, width : width + RANK] = ranks
    return nn(lhs_ref[...], weight_ref[...])


def block_rows(index):
    return slice(RANK * index, RANK * (index + 1))


def one_back(grad, kept, ranks, ad_ref, number, weight_ref, grad_ref, at):
    width = weight_ref.shape[1]
    both = nt(grad, weight_ref[...])
    grad_rank = both[:, width : width + RANK].astype(BF16)
    grad_ref[block_rows(at), :] += tn(grad_rank, kept)
    grad_ref[block_rows(at + 1), :] += tn(ranks, grad)
    return both[:, :width] + nn(grad_rank, ad_ref[2 * number])


def three_back(grads, inputs, ranks, ad_ref, number, weights, loads, first_load, grad_ref, at):
    width = weights.shape[2]
    both = None
    for i in range(3):
        grad = grads[i][...]
        ups = tn(ranks, grad)
        grad_ref[block_rows(at + 2 * i + 1), :] += ups[block_rows(i)]
        loads.ready(first_load + i)
        part = nt(grad, weights[first_load + i])
        both = part if both is None else both + part
    grad_ranks = both[:, width : width + 3 * RANK].astype(BF16)
    downs = tn(grad_ranks, inputs)
    for i in range(3):
        grad_ref[block_rows(at + 2 * i), :] += downs[block_rows(i)]
    return both[:, :width] + nn(grad_ranks, three_downs(ad_ref, number))


def place_of(seq_ref, k, parts, places):
    return pl.multiple_of(lax.rem(seq_ref[0] + k, parts) * places, 16)


def spatial_forward(seq_ref, x_ref, mod_ref, mask_ref, ad_ref, w_hbm, *refs):
    x1_refs = refs[:-11]
    q_ref, k_ref, v_ref, o_ref, stat_ref, rq_ref, ro_ref, w_ref, lhs_ref, x1_s, sems = refs[-11:]
    width = x_ref.shape[2]
    loads = Loads([(w_hbm.at[i], w_ref.at[i, pl.ds(0, width), :]) for i in range(4)], sems)
    loads.start()

    @pl.when(loads.first)
    def _():
        lhs_ref[:, width:] = jnp.zeros((ROWS, PAD), BF16)
        for i in range(4):
            w_ref[i, width:, :] = up_rows(ad_ref, i, i % 3, width)

    stream = x_ref[0].astype(F32)
    normal, _ = normalize(stream)
    lhs_ref[:, :width] = (normal * (1.0 + mod_ref[1:2, :]) + mod_ref[0:1, :]).astype(BF16)
    q, k, v = q_ref.at[0], k_ref.at[0], v_ref.at[0]
    three_projections(lhs_ref, ad_ref, 0, w_ref, loads, 0, (q, k, v), rq_ref.at[0])

    def put_out(index, value):
        value = value.astype(BF16)
        o_ref[0, :, tile(index)] = value
        lhs_ref[:, tile(index)] = value

    attend(q, k, v, mask_ref, None, put_out, stat_ref.at[0])
    loads.ready(3)
    branch = one_projection(lhs_ref, ad_ref, 3, w_ref.at[3], ro_ref.at[0])
    x1_s[...] = (stream + mod_ref[2:3, :] * branch).astype(BF16)
    places = x1_refs[0].shape[1]
    for k, ref in enumerate(x1_refs):
        ref[0] = x1_s[pl.ds(place_of(seq_ref, k, len(x1_refs), places), places), :]


def rows_of(refs):
    pieces = [ref[...].reshape(-1, ref.shape[2]) for ref in refs]
    return pieces[0] if len(pieces) == 1 else jnp.concatenate(pieces, 0)


def temporal_cross_forward(parts, *refs):
    _temporal_cross_forward(refs[:parts], *refs[parts:])


def _temporal_cross_forward(
    x_refs, ctx_ref, mod_ref, mask_ref, ad_ref, wt_hbm, wc_hbm,
    q_ref, k_ref, v_ref, o_ref, stat_ref, rq_ref, ro_ref,
    u2_ref, qc_ref, oc_ref, statc_ref, rqc_ref, roc_ref, kp_ref, vp_ref, rk_ref, rv_ref, x3_ref,
    w_ref, bias_ref, lhs_ref, q_s, k_s, v_s, o_s, sems,
):
    width = x_refs[0].shape[2]
    first = pl.program_id(0) == 0
    sources = [wt_hbm.at[i] for i in range(4)] + [wc_hbm.at[i] for i in range(4)]
    loads = Loads([(w, w_ref.at[i, pl.ds(0, width), :]) for i, w in enumerate(sources)], sems)
    loads.start()

    @pl.when(first)
    def _():
        bias_ref[...] = same_place(bias_ref.shape)
        lhs_ref[:, width:] = jnp.zeros((ROWS, PAD), BF16)
        for i in range(8):
            w_ref[i, width:, :] = up_rows(ad_ref, 4 + i, i if i < 3 else 0, width)

    loaded = rows_of(x_refs)
    stream = loaded.astype(F32)
    lhs_ref[:, :width] = loaded
    three_projections(lhs_ref, ad_ref, 4, w_ref, loads, 0, (q_s, k_s, v_s), rq_ref.at[0])
    q_ref[...] = q_s[...].reshape(q_ref.shape)
    k_ref[...] = k_s[...].reshape(k_ref.shape)
    v_ref[...] = v_s[...].reshape(v_ref.shape)

    def put_out(index, value):
        o_s[:, tile(index)] = value.astype(BF16)

    attend(q_s, k_s, v_s, mask_ref, bias_ref, put_out, stat_ref.at[0])
    lhs_ref[:, :width] = o_s[...]
    o_ref[...] = o_s[...].reshape(o_ref.shape)
    loads.ready(3)
    branch = one_projection(lhs_ref, ad_ref, 7, w_ref.at[3], ro_ref.at[0])
    stream = stream + mod_ref[2:3, :] * branch
    inputs = stream.astype(BF16)
    u2_ref[...] = inputs.reshape(u2_ref.shape)
    lhs_ref[:, :width] = inputs
    loads.ready(4)
    queries = one_projection(lhs_ref, ad_ref, 8, w_ref.at[4], rqc_ref.at[0])
    q_s[...] = (queries * EXP_SCALE).astype(BF16)
    qc_ref[...] = q_s[...].reshape(qc_ref.shape)
    loads.ready(5)
    loads.ready(6)

    @pl.when(first)
    def _():
        for number, at, rank_ref, pair_ref in ((9, 5, rk_ref, kp_ref), (10, 6, rv_ref, vp_ref)):
            ranks = nt(ctx_ref[...], ad_ref[2 * number]).astype(BF16)
            rank_ref[...] = ranks
            made = nn(ctx_ref[...], w_ref[at, :width, :]) + nn(ranks, ad_ref[2 * number + 1])
            k_s[:PAD, :] = made.astype(BF16)
            for pair in range(PAIRS):
                piece = k_s[:PAD, window(pair)]
                pair_ref[pair, :PAD, :] = piece * mask_ref[2 * pair : 2 * pair + 1, :]
                pair_ref[pair, PAD:, :] = piece * mask_ref[2 * pair + 1 : 2 * pair + 2, :]

    carried = None
    count = 120
    for pair in range(PAIRS):
        scores = nt(kp_ref[pair], q_s[:, window(pair)])
        pieces = []
        for sub in range(2):
            own = scores[PAD * sub : PAD * sub + count]
            top = jnp.max(own, 0, keepdims=True)
            grown = jnp.exp2(own - top)
            total = jnp.sum(grown, 0, keepdims=True)
            statc_ref[0, 2 * pair + sub : 2 * pair + sub + 1, :] = top + jnp.log2(total)
            pieces += [grown * (1.0 / total), jnp.zeros((PAD - count, ROWS), F32)]
        weights = jnp.concatenate(pieces, 0).astype(BF16)
        out = tn(weights, vp_ref[pair])
        low = out[:, :128]
        put_out(pair, low if carried is None else low + carried)
        carried = out[:, 128:]
    put_out(PAIRS, carried)
    lhs_ref[:, :width] = o_s[...]
    oc_ref[...] = o_s[...].reshape(oc_ref.shape)
    loads.ready(7)
    stream = stream + one_projection(lhs_ref, ad_ref, 11, w_ref.at[7], roc_ref.at[0])
    x3_ref[...] = stream.reshape(x3_ref.shape)


def gelu_both(hidden):
    root = math.sqrt(2.0 / math.pi)
    square = hidden * hidden
    inner = root * (hidden + 0.044715 * (square * hidden))
    bent = jnp.tanh(inner)
    half = 0.5 * (1.0 + bent)
    slope = half + 0.5 * hidden * (1.0 - bent * bent) * (root * (1.0 + 3.0 * 0.044715 * square))
    return hidden * half, slope


def transposed_map(rows):
    nothing = jnp.zeros((PAD - rows.shape[0], rows.shape[1]), F32)
    wide = jnp.concatenate([rows.astype(F32), nothing], 0)
    return wide.T.astype(BF16)


def down_loads(order_ref, pieces, down_ref, width):
    half = width // 2
    count = len(pieces) // 2
    core = order_ref[count]
    entries = []
    for k in range(count):
        for source, side in ((pieces[k], core), (pieces[count + k], 1 - core)):
            start = pl.multiple_of(order_ref[k] * width + side * half, 16)
            entries.append((source, down_ref.at[pl.ds(start, half), pl.ds(0, width)]))
    return entries


def fill_down_maps(ad_ref, down_ref, width):
    chunks = down_ref.shape[0] // width
    for c in range(chunks):
        rows = slice(c * width, (c + 1) * width)
        down_ref[rows, width:] = transposed_map(ad_ref[2 + chunks + c])


def feed_forward_grad(count, order_ref, cot_ref, mod_ref, ad_ref, *refs):
    pieces = refs[:count]
    grad_ref, down_ref, lhs_ref, sems = refs[count:]
    width = cot_ref.shape[1]
    entries = down_loads(order_ref, pieces, down_ref, width)
    loads = Loads(entries, sems)
    loads.start()

    @pl.when(loads.first)
    def _():
        lhs_ref[:, width:] = jnp.zeros((ROWS, PAD), BF16)
        fill_down_maps(ad_ref, down_ref, width)

    branch = (mod_ref[5:6, :] * cot_ref[...].astype(F32)).astype(BF16)
    lhs_ref[:, :width] = branch
    lhs_ref[:, width : width + RANK] = nt(branch, ad_ref[1]).astype(BF16)
    for i in range(len(entries)):
        loads.ready(i)
    for cols in hidden_chunks(down_ref.shape[0]):
        grad_ref[:, cols] = nt(lhs_ref[...], down_ref[cols, :]).astype(BF16)


def hidden_chunks(hidden):
    return [slice(at, at + 1536) for at in range(0, hidden, 1536)]


def feed_forward(
    x3_ref, cot_ref, grad_ref, mod_ref, ad_ref, w_hbm,
    act_ref, g3_ref, gd_ref, gu_ref, up_ref, lhs_ref, dh_ref, sems,
):
    width = x3_ref.shape[1]
    hidden_size = up_ref.shape[1]
    chunks = hidden_size // width
    loads = Loads(
        [
            (w_hbm.at[c], up_ref.at[pl.ds(0, width), pl.ds(c * width, width)])
            for c in range(chunks)
        ],
        sems,
    )
    loads.start()

    @pl.when(loads.first)
    def _():
        gd_ref[...] = jnp.zeros_like(gd_ref)
        gu_ref[...] = jnp.zeros_like(gu_ref)
        lhs_ref[:, width:] = jnp.zeros((ROWS, PAD), BF16)
        up_ref[width + RANK :, :] = jnp.zeros((PAD - RANK, hidden_size), BF16)
        for c in range(chunks):
            up_ref[width : width + RANK, c * width : (c + 1) * width] = ad_ref[2 + c]

    normal, inverse = normalize(x3_ref[...])
    inputs = (normal * (1.0 + mod_ref[4:5, :]) + mod_ref[3:4, :]).astype(BF16)
    rank_up = nt(inputs, ad_ref[0]).astype(BF16)
    lhs_ref[:, :width] = inputs
    lhs_ref[:, width : width + RANK] = rank_up
    for c in range(chunks):
        loads.ready(c)
    for cols in hidden_chunks(hidden_size):
        active, slope = gelu_both(nn(lhs_ref[...], up_ref[:, cols]))
        act_ref[:, cols] = active.astype(BF16)
        dh_ref[:, cols] = (slope * grad_ref[:, cols].astype(F32)).astype(BF16)
    both = nt(dh_ref[...], up_ref[...])
    gu_ref[...] += tn(rank_up, dh_ref[...])
    grad_rank = both[:, width : width + RANK].astype(BF16)
    grad_in = both[:, :width] + nn(grad_rank, ad_ref[0])
    gd_ref[...] += tn(grad_rank, lhs_ref[:, :width])
    grad_in = normalize_back(normal, inverse, grad_in * (1.0 + mod_ref[4:5, :]))
    g3_ref[...] = cot_ref[...].astype(F32) + grad_in


def feed_forward_out(count, order_ref, act_ref, x3_ref, cot_ref, mod_ref, ad_ref, *refs):
    pieces, refs = refs[:count], refs[count:]
    x4_refs = refs[:-4]
    gu_ref, gd_ref, down_ref, sems = refs[-4:]
    width = x3_ref.shape[1]
    step = pl.program_id(0)
    entries = down_loads(order_ref, pieces, down_ref, width)
    loads = Loads(entries, sems)
    loads.start()

    @pl.when(loads.first)
    def _():
        gu_ref[...] = jnp.zeros_like(gu_ref)
        gd_ref[...] = jnp.zeros_like(gd_ref)
        fill_down_maps(ad_ref, down_ref, width)

    grad_branch = (mod_ref[5:6, :] * cot_ref[...].astype(F32)).astype(BF16)
    gd_ref[...] += tn(nt(grad_branch, ad_ref[1]).astype(BF16), act_ref[...])
    for i in range(len(entries)):
        loads.ready(i)
    both = nn(act_ref[...], down_ref[...])
    ranks = both[:, width : width + RANK].astype(BF16)
    branch = both[:, :width] + nn(ranks, ad_ref[1])
    gu_ref[...] += tn(ranks, grad_branch)
    result = (x3_ref[...] + mod_ref[5:6, :] * branch).astype(BF16)
    share = x4_refs[0].shape[0]
    for k, ref in enumerate(x4_refs):
        at = k * share

        @pl.when(step == at // ROWS)
        def _():
            ref[...] = result[at % ROWS : at % ROWS + share]


def cross_temporal_backward(parts, *refs):
    outs = len(refs) - parts - 13
    _cross_temporal_backward(refs[:parts], refs[outs : outs + parts], *refs[parts:outs], *refs[outs + parts :])


def _cross_temporal_backward(
    u1_refs, g1_refs, g3_ref, q_ref, k_ref, v_ref, o_ref, stat_ref, rq_ref, ro_ref,
    u2_ref, qc_ref, oc_ref, statc_ref, rqc_ref, roc_ref, kp_ref, vp_ref,
    mod_ref, mask_ref, ad_ref, wt_hbm, wc_hbm,
    gw_ref, dk_acc, dv_acc, w_ref, bias_ref, q_s, k_s, v_s, do_s, dq_s, dk_s, dv_s, sems,
):
    width = u1_refs[0].shape[2]
    first = pl.program_id(0) == 0
    order = (7, 4, 3, 0, 1, 2)
    sources = [wc_hbm.at[n - 4] if n >= 4 else wt_hbm.at[n] for n in order]
    loads = Loads([(w, w_ref.at[i, pl.ds(0, width), :]) for i, w in enumerate(sources)], sems)
    loads.start()

    @pl.when(first)
    def _():
        bias_ref[...] = same_place(bias_ref.shape)
        gw_ref[...] = jnp.zeros_like(gw_ref)
        dk_acc[...] = jnp.zeros_like(dk_acc)
        dv_acc[...] = jnp.zeros_like(dv_acc)
        for i, n in enumerate(order):
            w_ref[i, width:, :] = up_rows(ad_ref, 4 + n, n if n < 3 else 0, width)

    def rows(ref):
        return ref[...].reshape(ROWS, ref.shape[2])

    grad = rows(g3_ref)
    loads.ready(0)
    do_s[...] = one_back(
        grad.astype(BF16), rows(oc_ref), roc_ref[0], ad_ref, 11, w_ref.at[0], gw_ref, 14
    ).astype(BF16)
    q_s[...] = rows(qc_ref)
    count = 120
    carried = None
    for pair in range(PAIRS):
        win = window(pair)
        q_win, do_win = q_s[:, win], do_s[:, win]
        scores = nt(kp_ref[pair], q_win)
        grad_probs = nt(vp_ref[pair], do_win)
        all_probs, all_grads = [], []
        nothing = jnp.zeros((PAD - count, ROWS), F32)
        for sub in range(2):
            span = slice(PAD * sub, PAD * sub + count)
            row = 2 * pair + sub
            probs = jnp.exp2(scores[span] - statc_ref[0, row : row + 1, :])
            own = grad_probs[span]
            inner = jnp.sum(probs * own, 0, keepdims=True)
            all_probs += [probs, nothing]
            all_grads += [probs * (own - inner), nothing]
        probs = jnp.concatenate(all_probs, 0).astype(BF16)
        grad_scores = jnp.concatenate(all_grads, 0).astype(BF16)
        dk_acc[pair] += nn(grad_scores, q_win)
        dv_acc[pair] += nn(probs, do_win)
        out = tn(grad_scores, kp_ref[pair])
        low = out[:, :128]
        dq_s[:, tile(pair)] = ((low if carried is None else low + carried) * SCALE).astype(BF16)
        carried = out[:, 128:]
    dq_s[:, tile(PAIRS)] = (carried * SCALE).astype(BF16)
    loads.ready(1)
    grad = grad + one_back(
        dq_s[...], rows(u2_ref), rqc_ref[0], ad_ref, 8, w_ref.at[1], gw_ref, 8
    )
    loads.ready(2)
    do_s[...] = one_back(
        (mod_ref[2:3, :] * grad).astype(BF16), rows(o_ref), ro_ref[0], ad_ref, 7, w_ref.at[2], gw_ref, 6
    ).astype(BF16)
    q_s[...] = rows(q_ref)
    k_s[...] = rows(k_ref)
    v_s[...] = rows(v_ref)

    def put(index, values):
        dq_s[:, tile(index)] = (values[0] * SCALE).astype(BF16)
        dk_s[:, tile(index)] = (values[1] * LN2).astype(BF16)
        dv_s[:, tile(index)] = values[2].astype(BF16)

    attend_back(q_s, k_s, v_s, do_s, mask_ref, bias_ref, stat_ref.at[0], put)
    grad = grad + three_back(
        (dq_s, dk_s, dv_s), rows_of(u1_refs), rq_ref[0], ad_ref, 4, w_ref, loads, 3, gw_ref, 0
    )
    grad = grad.astype(BF16)
    share = ROWS // len(g1_refs)
    for k, ref in enumerate(g1_refs):
        ref[...] = grad[share * k : share * (k + 1)].reshape(ref.shape)


def tail_groups(cols):
    tail = cols - PAD
    return PAD // tail if 0 < tail < PAD and PAD % tail == 0 else 0


def packed_rows(blocks, cols):
    group = tail_groups(cols)
    if not group:
        return blocks * RANK, cols
    return (blocks + -(-blocks // group)) * RANK, PAD


def put_blocks(blocks, put):
    cols = blocks[0].shape[1]
    group = tail_groups(cols)
    for k, rows in enumerate(blocks):
        put(k, rows[:, :PAD] if group else rows)
    for k in range(0, len(blocks), group) if group else ():
        tails = [rows[:, PAD:] for rows in blocks[k : k + group]]
        missing = group - len(tails)
        if missing:
            tails.append(jnp.zeros((RANK, missing * (cols - PAD)), blocks[0].dtype))
        put(len(blocks) + k // group, jnp.concatenate(tails, 1))


def get_block(get, index, count, cols):
    group = tail_groups(cols)
    if not group:
        return get(index)
    at = (index % group) * (cols - PAD)
    return jnp.concatenate([get(index), get(count + index // group)[:, at : at + cols - PAD]], 1)


def pack_columns(table_ref, packed_ref, clips):
    parts = packed_ref.shape[0] // clips
    share = table_ref.shape[0] // parts
    cols = table_ref.shape[1] // clips
    for f in range(clips):
        for s in range(parts):
            piece = table_ref[share * s : share * (s + 1), cols * f : cols * (f + 1)].astype(BF16)
            blocks = [piece[block_rows(k)] for k in range(share // RANK)]

            def put(k, rows):
                packed_ref[f * parts + s, block_rows(k), :] = rows

            put_blocks(blocks, put)


def stacked(seq_ref, g1_refs, halves, whole_ref):
    parts = len(g1_refs) // halves
    part = g1_refs[0].shape[1]
    for half in range(halves):
        for k in range(parts):
            start = place_of(seq_ref, k, parts, part * halves) + half * part
            whole_ref[pl.ds(pl.multiple_of(start, 16), part), :] = g1_refs[half * parts + k][0]
    return whole_ref[...].astype(F32)


def spatial_backward(pieces, halves, clips, seq_ref, *refs):
    g1_refs, refs = refs[:pieces], refs[pieces:]
    (
        x_ref, q_ref, k_ref, v_ref, o_ref, stat_ref, rq_ref, ro_ref, mod_ref, mask_ref, ad_ref, w_hbm,
        down_ref, up_ref, d_ref, packed_ref, w_ref, gw_ref, do_s, sems,
    ) = refs
    width = x_ref.shape[2]
    loads = Loads([(w_hbm.at[3], w_ref.at[pl.ds(0, width), :])], sems)
    loads.start()

    @pl.when(loads.first)
    def _():
        gw_ref[...] = jnp.zeros_like(gw_ref)
        w_ref[width:, :] = up_rows(ad_ref, 3, 0, width)

    grad = stacked(seq_ref, g1_refs, halves, do_s)
    loads.ready(0)
    do_s[...] = one_back(
        (mod_ref[2:3, :] * grad).astype(BF16), o_ref[0], ro_ref[0], ad_ref, 3, w_ref, gw_ref, 6
    ).astype(BF16)

    def put(index, values):
        for i, factor in enumerate((SCALE, LN2, 1.0)):
            value = values[i] if factor == 1.0 else values[i] * factor
            d_ref[0, :, width * i + 128 * index : width * i + 128 * index + 128] = value.astype(BF16)

    attend_back(
        q_ref.at[0], k_ref.at[0], v_ref.at[0], do_s, mask_ref, None, stat_ref.at[0], put
    )
    ranks = rq_ref[0]
    grad_ranks = None
    for i in range(3):
        grad = d_ref[0, :, width * i : width * (i + 1)]
        gw_ref[block_rows(2 * i + 1), :] += tn(ranks, grad)[block_rows(i)]
        part = nt(grad, up_rows(ad_ref, i, i, width))
        grad_ranks = part if grad_ranks is None else grad_ranks + part
    d_ref[0, :, 3 * width :] = grad_ranks.astype(BF16)
    normal, _ = normalize(x_ref[0].astype(F32))
    inputs = (normal * (1.0 + mod_ref[1:2, :]) + mod_ref[0:1, :]).astype(BF16)
    downs = tn(d_ref[0, :, 3 * width :], inputs)
    for i in range(3):
        gw_ref[block_rows(2 * i), :] += downs[block_rows(i)]

    @pl.when(pl.program_id(0) == pl.num_programs(0) - 1)
    def _():
        at = 8 * RANK
        gw_ref[at : at + RANK, :] = down_ref[...]
        gw_ref[at + RANK : at + RANK + up_ref.shape[0], :] = up_ref[...]
        pack_columns(gw_ref, packed_ref, clips)


def spatial_input_grad(pieces, halves, seq_ref, *refs):
    g1_refs, refs = refs[:pieces], refs[pieces:]
    x_ref, d_ref, mod_ref, ad_ref, w_hbm, g0_ref, w_ref, whole_s, sems = refs
    width = x_ref.shape[2]
    loads = Loads(
        [(w_hbm.at[i], w_ref.at[:, pl.ds(i * width, width)]) for i in range(3)], sems
    )
    loads.start()

    @pl.when(loads.first)
    def _():
        w_ref[:, 3 * width :] = transposed_map(three_downs(ad_ref, 0))

    normal, inverse = normalize(x_ref[0].astype(F32))
    grad = stacked(seq_ref, g1_refs, halves, whole_s)
    for i in range(3):
        loads.ready(i)
    grad_in = nt(d_ref[0], w_ref[...])
    grad = grad + normalize_back(normal, inverse, grad_in * (1.0 + mod_ref[1:2, :]))
    g0_ref[0] = grad.astype(BF16)


def put_in_place(seq_ref, *refs):
    *pieces, out_ref = refs
    places = pieces[0].shape[1]
    for k, ref in enumerate(pieces):
        out_ref[0, pl.ds(place_of(seq_ref, k, len(pieces), places), places), :] = ref[0]


def pack_early(clips, halves, *refs):
    gw_refs, refs = refs[:halves], refs[halves:]
    dk_refs, refs = refs[:halves], refs[halves:]
    dv_refs, refs = refs[:halves], refs[halves:]
    down_ref, up_ref, rk_ref, rv_ref, ctx_ref, mask_ref, ad_ref, packed_ref, table_ref, ctx_s = refs

    def added(each):
        total = each[0]
        for value in each[1:]:
            total = total + value
        return total

    at = gw_refs[0].shape[0]
    table_ref[:at, :] = added([ref[...] for ref in gw_refs])
    table_ref[at : at + RANK, :] = down_ref[...]
    at += RANK
    table_ref[at : at + up_ref.shape[0], :] = up_ref[...]
    at += up_ref.shape[0]
    table_ref[at:, :] = jnp.zeros((table_ref.shape[0] - at, table_ref.shape[1]), F32)
    context = ctx_ref[...].astype(F32)
    for accs, factor, rank_ref, number, at in (
        (dk_refs, LN2, rk_ref, 9, 10),
        (dv_refs, 1.0, rv_ref, 10, 12),
    ):
        held = None
        for pair in range(PAIRS):
            whole = added([ref[pair] for ref in accs]) * factor
            out = whole[:PAD] * mask_ref[2 * pair : 2 * pair + 1, :].astype(F32)
            out = out + whole[PAD:] * mask_ref[2 * pair + 1 : 2 * pair + 2, :].astype(F32)
            low = out[:, :128]
            ctx_s[:, tile(pair)] = low if held is None else low + held
            held = out[:, 128:]
        ctx_s[:, tile(PAIRS)] = held
        grad_kv = ctx_s[...]
        grad_rank = lax.dot_general(
            grad_kv, ad_ref[2 * number + 1].astype(F32), (((1,), (1,)), ((), ())),
            precision=HIGHEST, preferred_element_type=F32,
        )
        table_ref[block_rows(at), :] = lax.dot_general(
            grad_rank, context, (((0,), (0,)), ((), ())),
            precision=HIGHEST, preferred_element_type=F32,
        )
        table_ref[block_rows(at + 1), :] = lax.dot_general(
            rank_ref[...].astype(F32), grad_kv, (((0,), (0,)), ((), ())),
            precision=HIGHEST, preferred_element_type=F32,
        )
    pack_columns(table_ref, packed_ref, clips)


def assemble(early_ref, late_ref, wide_ref, narrow_ref):
    _, adapters, _, cols = wide_ref.shape
    times = narrow_ref.shape[3] // cols

    def block(ref, total, index, a):
        each = total // ref.shape[0]

        def get(k):
            return ref[index // each, a, block_rows(k), :].astype(F32)

        return get_block(get, index % each, each, cols)

    for a in range(adapters):
        for i in range(8):
            wide_ref[i, a] = block(late_ref, LATE_BLOCKS, i, a)
        for i in range(17):
            wide_ref[8 + i, a] = block(early_ref, EARLY_BLOCKS, i, a)
        wide_ref[25, a] = block(late_ref, LATE_BLOCKS, 8, a)
        narrow_ref[0, a] = jnp.concatenate(
            [block(early_ref, EARLY_BLOCKS, 17 + j, a) for j in range(times)], 1
        )
        narrow_ref[1, a] = jnp.concatenate(
            [block(late_ref, LATE_BLOCKS, 9 + j, a) for j in range(times)], 1
        )


def combine(index_ref, got_ref, out_ref, acc_ref):
    clips = index_ref.shape[0]
    parts = got_ref.shape[0] // clips
    acc_ref[...] = jnp.zeros_like(acc_ref)

    def step(f, carry):
        total = got_ref[f * parts].astype(F32)
        for s in range(1, parts):
            total = total + got_ref[f * parts + s].astype(F32)
        acc_ref[index_ref[f]] += total
        return carry

    lax.fori_loop(0, clips, step, 0)
    table = acc_ref[...].astype(BF16)
    for s in range(parts):
        out_ref[s] = table


def pick(index_ref, wide_ref, narrow_ref, out_ref):
    count, _, _, cols = wide_ref.shape
    times = narrow_ref.shape[3] // cols

    def step(f, carry):
        a = index_ref[f]
        blocks = [wide_ref[k, a] for k in range(count)]
        for p in range(2):
            rows = narrow_ref[p, a]
            blocks += [rows[:, cols * j : cols * (j + 1)] for j in range(times)]

        def put(k, rows):
            out_ref[f, block_rows(k), :] = rows

        put_blocks(blocks, put)
        return carry

    lax.fori_loop(0, index_ref.shape[0], step, 0)


def unpick(count, cols, got_ref, out_ref):
    for k in range(count):
        pieces = []
        for f in range(got_ref.shape[0]):

            def get(index):
                return got_ref[f, block_rows(index), :]

            pieces.append(get_block(get, k, count, cols))
        out_ref[k] = jnp.concatenate(pieces, 1)


def whole_block(array):
    zeros = (0,) * array.ndim
    return pl.BlockSpec(array.shape, lambda i: zeros, pipeline_mode=pl.Buffered(1))


def anywhere():
    return pl.BlockSpec(memory_space=pl.ANY)


def like(shape, dtype):
    return jax.ShapeDtypeStruct(shape, dtype)


PARAMS = pltpu.CompilerParams(
    dimension_semantics=("arbitrary",), vmem_limit_bytes=VMEM_LIMIT
)


def cost(flops, read):
    return pl.CostEstimate(flops=flops, bytes_accessed=read, transcendentals=flops // 4096)


def run_spatial_forward(seq, video, mods, masks, wide, w_s, parts):
    frames, rows, d = video.shape
    places = rows // parts
    by_frame = lambda i: (i, 0, 0)
    row_block = pl.BlockSpec((1, rows, d), by_frame)
    return pl.pallas_call(
        spatial_forward,
        grid=(frames,),
        in_specs=[in_smem(), row_block, whole_block(mods), whole_block(masks), whole_block(wide), anywhere()],
        out_specs=[pl.BlockSpec((1, places, d), by_frame)] * parts
        + [
            row_block,
            row_block,
            row_block,
            row_block,
            pl.BlockSpec((1, HEADS, rows), by_frame),
            pl.BlockSpec((1, rows, 3 * RANK), by_frame),
            pl.BlockSpec((1, rows, RANK), by_frame),
        ],
        out_shape=[like((frames, places, d), BF16)] * parts
        + [like(video.shape, BF16)] * 4
        + [
            like((frames, HEADS, rows), F32),
            like((frames, rows, 3 * RANK), BF16),
            like((frames, rows, RANK), BF16),
        ],
        scratch_shapes=[
            pltpu.VMEM((4, d + PAD, d), BF16),
            pltpu.VMEM((ROWS, d + PAD), BF16),
            pltpu.VMEM((ROWS, d), BF16),
            pltpu.SemaphoreType.DMA((4,)),
        ],
        compiler_params=PARAMS,
        cost_estimate=cost(10 * frames * rows * d * d, 30_000_000),
        name="spatial_forward",
    )(seq, video, mods, masks, wide, w_s)


def run_temporal_cross_forward(x1, context, mods, masks, wide, w_t, w_c):
    parts = len(x1)
    own_frames, places, d = x1[0].shape
    frames = own_frames * parts
    groups = places * frames // ROWS
    each = ROWS // frames
    across = pl.BlockSpec((frames, each, d), lambda i: (0, i, 0))
    by_group = lambda i: (i, 0, 0)
    stat = pl.BlockSpec((1, HEADS, ROWS), by_group)
    three = pl.BlockSpec((1, ROWS, 3 * RANK), by_group)
    one = pl.BlockSpec((1, ROWS, RANK), by_group)
    full = lambda *shape: pl.BlockSpec(shape, lambda i: (0,) * len(shape))
    act = like((frames, places, d), BF16)

    def body(*refs):
        temporal_cross_forward(parts, *refs)

    stat_shape = like((groups, HEADS, ROWS), F32)
    one_shape = like((groups, ROWS, RANK), BF16)
    return pl.pallas_call(
        body,
        grid=(groups,),
        in_specs=[pl.BlockSpec((own_frames, each, d), lambda i: (0, i, 0))] * parts
        + [whole_block(context), whole_block(mods), whole_block(masks), whole_block(wide), anywhere(), anywhere()],
        out_specs=[across] * 4 + [stat, three, one] + [across] * 3 + [stat, one, one]
        + [full(PAIRS, 2 * PAD, 256)] * 2 + [full(PAD, RANK)] * 2 + [across],
        out_shape=[act] * 4 + [stat_shape, like((groups, ROWS, 3 * RANK), BF16), one_shape]
        + [act] * 3 + [stat_shape, one_shape, one_shape]
        + [like((PAIRS, 2 * PAD, 256), BF16)] * 2 + [like((PAD, RANK), BF16)] * 2
        + [like((frames, places, d), F32)],
        scratch_shapes=[pltpu.VMEM((8, d + PAD, d), BF16), pltpu.VMEM((ROWS, ROWS), F32)]
        + [pltpu.VMEM((ROWS, d + PAD), BF16)]
        + [pltpu.VMEM((ROWS, d), BF16)] * 4
        + [pltpu.SemaphoreType.DMA((8,))],
        compiler_params=PARAMS,
        cost_estimate=cost(14 * places * frames * d * d, 50_000_000),
        name="temporal_cross_forward",
    )(*x1, context, mods, masks, wide, w_t, w_c)


def in_smem():
    return pl.BlockSpec(memory_space=pltpu.SMEM)


def run_feed_forward_grad(cot, mods, maps, down):
    tokens, d = cot.shape
    order, *pieces = down
    hidden = len(pieces) // 2 * d

    def body(*refs):
        feed_forward_grad(len(pieces), *refs)

    return pl.pallas_call(
        body,
        grid=(tokens // ROWS,),
        in_specs=[in_smem(), pl.BlockSpec((ROWS, d), lambda i: (i, 0)), whole_block(mods), whole_block(maps)]
        + [anywhere()] * len(pieces),
        out_specs=pl.BlockSpec((ROWS, hidden), lambda i: (i, 0)),
        out_shape=like((tokens, hidden), BF16),
        scratch_shapes=[
            pltpu.VMEM((hidden, d + PAD), BF16),
            pltpu.VMEM((ROWS, d + PAD), BF16),
            pltpu.SemaphoreType.DMA((len(pieces),)),
        ],
        compiler_params=PARAMS,
        cost_estimate=cost(2 * tokens * d * hidden, 30_000_000),
        name="feed_forward_grad",
    )(order, cot, mods, maps, *pieces)


def run_feed_forward(x3, cot, grad_active, mods, maps, up):
    tokens, d = x3.shape
    chunks = up.shape[0]
    rows = pl.BlockSpec((ROWS, d), lambda i: (i, 0))
    wide_rows = pl.BlockSpec((ROWS, chunks * d), lambda i: (i, 0))
    return pl.pallas_call(
        feed_forward,
        grid=(tokens // ROWS,),
        in_specs=[rows, rows, wide_rows, whole_block(mods), whole_block(maps), anywhere()],
        out_specs=[
            wide_rows,
            rows,
            pl.BlockSpec((RANK, d), lambda i: (0, 0)),
            pl.BlockSpec((RANK, chunks * d), lambda i: (0, 0)),
        ],
        out_shape=[
            like((tokens, chunks * d), BF16),
            like((tokens, d), F32),
            like((RANK, d), F32),
            like((RANK, chunks * d), F32),
        ],
        scratch_shapes=[
            pltpu.VMEM((d + PAD, chunks * d), BF16),
            pltpu.VMEM((ROWS, d + PAD), BF16),
            pltpu.VMEM((ROWS, chunks * d), BF16),
            pltpu.SemaphoreType.DMA((chunks,)),
        ],
        compiler_params=PARAMS,
        cost_estimate=cost(4 * tokens * d * d * chunks, 50_000_000),
        name="feed_forward",
    )(x3, cot, grad_active, mods, maps, up)


def run_feed_forward_out(active, x3, cot, mods, maps, down, parts):
    tokens, d = x3.shape
    order, *pieces = down
    hidden = active.shape[1]
    share = tokens // parts

    def body(*refs):
        feed_forward_out(len(pieces), *refs)

    rows = pl.BlockSpec((ROWS, d), lambda i: (i, 0))
    return pl.pallas_call(
        body,
        grid=(tokens // ROWS,),
        in_specs=[
            in_smem(),
            pl.BlockSpec((ROWS, hidden), lambda i: (i, 0)),
            rows,
            rows,
            whole_block(mods),
            whole_block(maps),
        ]
        + [anywhere()] * len(pieces),
        out_specs=[pl.BlockSpec((share, d), lambda i: (0, 0))] * parts
        + [
            pl.BlockSpec((RANK, d), lambda i: (0, 0)),
            pl.BlockSpec((RANK, hidden), lambda i: (0, 0)),
        ],
        out_shape=[like((share, d), BF16)] * parts
        + [
            like((RANK, d), F32),
            like((RANK, hidden), F32),
        ],
        scratch_shapes=[
            pltpu.VMEM((hidden, d + PAD), BF16),
            pltpu.SemaphoreType.DMA((len(pieces),)),
        ],
        compiler_params=PARAMS,
        cost_estimate=cost(2 * tokens * d * hidden, 30_000_000),
        name="feed_forward_out",
    )(order, active, x3, cot, mods, maps, *pieces)


def run_cross_temporal_backward(g3, u1, saved, mods, masks, wide, w_t, w_c, half, halves):
    parts = len(u1)
    own_frames, places, d = u1[0].shape
    frames = own_frames * parts
    each = ROWS // frames
    groups = places * frames // ROWS // halves
    start = half * groups
    across = pl.BlockSpec((frames, ROWS // frames, d), lambda i: (0, i + start, 0))
    by_group = lambda i: (i + start, 0, 0)
    stat = pl.BlockSpec((1, HEADS, ROWS), by_group)
    three = pl.BlockSpec((1, ROWS, 3 * RANK), by_group)
    one = pl.BlockSpec((1, ROWS, RANK), by_group)
    kp, vp = saved[13:15]
    pair_sums = pl.BlockSpec((PAIRS, 2 * PAD, 256), lambda i: (0, 0, 0))

    def body(*refs):
        cross_temporal_backward(parts, *refs)

    return pl.pallas_call(
        body,
        grid=(groups,),
        in_specs=[pl.BlockSpec((own_frames, each, d), lambda i: (0, i + start, 0))] * parts
        + [across] + [across] * 4 + [stat, three, one] + [across] * 3 + [stat, one, one]
        + [whole_block(kp), whole_block(vp)]
        + [whole_block(mods), whole_block(masks), whole_block(wide), anywhere(), anywhere()],
        out_specs=[pl.BlockSpec((own_frames, each, d), lambda i: (0, i, 0))] * parts
        + [
            pl.BlockSpec((16 * RANK, d), lambda i: (0, 0)),
            pair_sums,
            pair_sums,
        ],
        out_shape=[like((own_frames, places // halves, d), BF16)] * parts
        + [like((16 * RANK, d), F32)]
        + [like((PAIRS, 2 * PAD, 256), F32)] * 2,
        scratch_shapes=[
            pltpu.VMEM((6, d + PAD, d), BF16),
            pltpu.VMEM((ROWS, ROWS), F32),
        ]
        + [pltpu.VMEM((ROWS, d), BF16)] * 7
        + [pltpu.SemaphoreType.DMA((6,))],
        compiler_params=PARAMS,
        cost_estimate=cost(14 * places // halves * frames * d * d, 30_000_000),
        name="cross_temporal_backward",
    )(*u1, g3, *saved[:15], mods, masks, wide, w_t, w_c)


LATE_BLOCKS = 16
EARLY_BLOCKS = 24


def run_spatial_backward(seq, g1, halves, video, saved, mods, masks, wide, w_s, late_down, late_up, clips):
    frames, rows, d = video.shape
    parts = len(g1) // halves
    by_frame = lambda i: (i, 0, 0)
    row_block = pl.BlockSpec((1, rows, d), by_frame)
    packed = (clips * parts, *packed_rows(LATE_BLOCKS // parts, d // clips))

    def body(*refs):
        spatial_backward(len(g1), halves, clips, *refs)

    return pl.pallas_call(
        body,
        grid=(frames,),
        in_specs=[in_smem()] + [pl.BlockSpec((1, g.shape[1], d), by_frame) for g in g1]
        + [row_block] * 5
        + [
            pl.BlockSpec((1, HEADS, rows), by_frame),
            pl.BlockSpec((1, rows, 3 * RANK), by_frame),
            pl.BlockSpec((1, rows, RANK), by_frame),
            whole_block(mods),
            whole_block(masks),
            whole_block(wide),
            anywhere(),
            whole_block(late_down),
            whole_block(late_up),
        ],
        out_specs=[
            pl.BlockSpec((1, rows, 3 * d + PAD), by_frame),
            pl.BlockSpec(packed, lambda i: (0, 0, 0)),
        ],
        out_shape=[like((frames, rows, 3 * d + PAD), BF16), like(packed, BF16)],
        scratch_shapes=[pltpu.VMEM((d + PAD, d), BF16), pltpu.VMEM((LATE_BLOCKS * RANK, d), F32)]
        + [pltpu.VMEM((ROWS, d), BF16), pltpu.SemaphoreType.DMA((1,))],
        compiler_params=PARAMS,
        cost_estimate=cost(6 * frames * rows * d * d, 30_000_000),
        name="spatial_backward",
    )(seq, *g1, video, *saved, mods, masks, wide, w_s, late_down, late_up)


def run_spatial_input_grad(seq, g1, halves, video, grads, mods, wide, w_s):
    frames, rows, d = video.shape
    by_frame = lambda i: (i, 0, 0)
    row_block = pl.BlockSpec((1, rows, d), by_frame)

    def body(*refs):
        spatial_input_grad(len(g1), halves, *refs)

    return pl.pallas_call(
        body,
        grid=(frames,),
        in_specs=[in_smem()] + [pl.BlockSpec((1, g.shape[1], d), by_frame) for g in g1]
        + [
            row_block,
            pl.BlockSpec((1, rows, grads.shape[2]), by_frame),
            whole_block(mods),
            whole_block(wide),
            anywhere(),
        ],
        out_specs=row_block,
        out_shape=like(video.shape, BF16),
        scratch_shapes=[
            pltpu.VMEM((d, 3 * d + PAD), BF16),
            pltpu.VMEM((ROWS, d), BF16),
            pltpu.SemaphoreType.DMA((3,)),
        ],
        compiler_params=PARAMS,
        cost_estimate=cost(6 * frames * rows * d * d, 20_000_000),
        name="spatial_input_grad",
    )(seq, *g1, video, grads, mods, wide, w_s)


def run_put_in_place(seq, pieces):
    frames, places, d = pieces[0].shape
    by_frame = lambda i: (i, 0, 0)
    rows = places * len(pieces)
    return pl.pallas_call(
        put_in_place,
        grid=(frames,),
        in_specs=[in_smem()] + [pl.BlockSpec((1, places, d), by_frame)] * len(pieces),
        out_specs=pl.BlockSpec((1, rows, d), by_frame),
        out_shape=like((frames, rows, d), BF16),
        compiler_params=PARAMS,
        cost_estimate=cost(0, 4 * frames * rows * d),
        name="put_in_place",
    )(seq, *pieces)


PLAIN = pltpu.CompilerParams(vmem_limit_bytes=VMEM_LIMIT)


def in_vmem():
    return pl.BlockSpec(memory_space=pltpu.VMEM)


def run_pack_early(gw, dk, dv, sources, clips, parts):
    d = gw[0].shape[1]
    packed = (clips * parts, *packed_rows(EARLY_BLOCKS // parts, d // clips))

    def body(*refs):
        pack_early(clips, len(gw), *refs)

    return pl.pallas_call(
        body,
        out_shape=like(packed, BF16),
        scratch_shapes=[pltpu.VMEM((EARLY_BLOCKS * RANK, d), F32), pltpu.VMEM((PAD, d), F32)],
        compiler_params=PLAIN,
        cost_estimate=cost(50000000, 8000000),
        name="pack_early",
    )(*gw, *dk, *dv, *sources)


def run_assemble(early, late, wide_shape, narrow_shape):
    return pl.pallas_call(
        assemble,
        in_specs=[in_vmem()] * 2,
        out_specs=[in_vmem()] * 2,
        out_shape=[like(wide_shape, F32), like(narrow_shape, F32)],
        compiler_params=PLAIN,
        cost_estimate=cost(0, 6000000),
        name="assemble",
    )(early, late)


def run_pick(all_index, wide, narrow):
    count, _, _, cols = wide.shape
    shape = packed_rows(count + 2 * (narrow.shape[3] // cols), cols)
    return pl.pallas_call(
        pick,
        in_specs=[in_smem(), in_vmem(), in_vmem()],
        out_specs=in_vmem(),
        out_shape=like((all_index.shape[0], *shape), BF16),
        compiler_params=PLAIN,
        cost_estimate=cost(0, 3000000),
        name="pick",
    )(all_index, wide, narrow)


def run_unpick(got, blocks, cols):
    def body(*refs):
        unpick(blocks, cols, *refs)

    return pl.pallas_call(
        body,
        in_specs=[in_vmem()],
        out_specs=in_vmem(),
        out_shape=like((blocks, RANK, got.shape[0] * cols), BF16),
        compiler_params=PLAIN,
        cost_estimate=cost(0, 2500000),
        name="unpick",
    )(got)


def run_combine(all_index, got, adapters):
    clips = all_index.shape[0]
    parts = got.shape[0] // clips
    _, share, cols = got.shape
    return pl.pallas_call(
        combine,
        in_specs=[pl.BlockSpec(memory_space=pltpu.SMEM), pl.BlockSpec(memory_space=pltpu.VMEM)],
        out_specs=pl.BlockSpec(memory_space=pltpu.VMEM),
        out_shape=like((parts, adapters, share, cols), BF16),
        scratch_shapes=[pltpu.VMEM((adapters, share, cols), F32)],
        compiler_params=pltpu.CompilerParams(vmem_limit_bytes=VMEM_LIMIT),
        cost_estimate=cost(0, 1000000),
        name="combine",
    )(all_index, got)


def exchange(array, axes="seq"):
    return lax.all_to_all(array, axes, split_axis=0, concat_axis=0, tiled=True)


def reduce_grads(packed, all_index, adapters):
    got = exchange(packed, ("fsdp", "seq"))
    return run_combine(all_index, got, adapters)


def up_chunks(up, clips, times):
    rows, hidden = up.shape
    cols = hidden // (clips * times)
    return up.reshape(rows, clips, times, cols).transpose(2, 0, 1, 3).reshape(times, rows, -1)


def gather(array):
    return lax.all_gather(array, "fsdp", axis=1, tiled=True)


def send(array, axis, shift):
    size = lax.axis_size(axis)
    return lax.ppermute(array, axis, [(i, (i + shift) % size) for i in range(size)])


def to_places(pieces):
    return [pieces[0]] + [send(pieces[k], "seq", k) for k in range(1, len(pieces))]


def to_frames(pieces):
    return [pieces[0]] + [send(pieces[k], "seq", -k) for k in range(1, len(pieces))]


def fetch_spatial_and_down(spatial, down, clips, parts, times, d):
    quarters = down.reshape(times, -1, d)
    half = d // 2
    if times != parts or clips % 2:
        whole = gather(quarters)
        pieces = [whole[i, side * half : (side + 1) * half] for side in range(2) for i in range(times)]
        return gather(spatial), [jnp.arange(times + 1, dtype=jnp.int32) % times, *pieces]
    seq = lax.axis_index("seq")
    core = lax.axis_index("fsdp") % 2
    own = lax.dynamic_slice_in_dim(quarters, seq, 1, 0)
    got = gather(jnp.concatenate([spatial, own], 0))
    first = lax.dynamic_slice(got, (times, core * half, 0), (1, half, d))[0]
    other = lax.dynamic_slice(got, (times, (1 - core) * half, 0), (1, half, d))[0]
    mine = [first] + [send(first, "seq", k) for k in range(1, parts)]
    swap = [(i, i ^ 1) for i in range(clips)]
    others = [other] + [lax.ppermute(piece, "fsdp", swap) for piece in mine[1:]]
    order = jnp.concatenate([(seq - jnp.arange(parts)) % parts, core[None]]).astype(jnp.int32)
    return got, [order, *mine, *others]


def on_device(
    video,
    context,
    modulation,
    adapter_index,
    cotangent,
    qkv_weights,
    out_weights,
    ffn_up,
    ffn_down,
    adapt_wide,
    adapt_ff,
):
    parts = lax.axis_size("seq")
    clips = lax.axis_size("fsdp")
    d = video.shape[-1]
    count, adapters, _, cols = adapt_wide.shape[1:]
    times = adapt_ff.shape[-1] // cols
    places = SPATIAL // parts
    frames = FRAMES // parts
    mods = modulation[0, 0]
    masks = head_masks()
    ctx = jnp.pad(context[0], ((0, PAD - context.shape[1]), (0, 0)))

    def attention_weights(j):
        return jnp.concatenate([qkv_weights[0, 3 * j : 3 * j + 3], out_weights[0, j : j + 1]], 0)

    seq = lax.axis_index("seq").astype(jnp.int32)[None]
    all_index = exchange(jnp.broadcast_to(adapter_index, (clips,)), "fsdp")
    w_s, down = fetch_spatial_and_down(
        attention_weights(0), ffn_down[0], clips, parts, times, d
    )
    picked = run_pick(all_index, adapt_wide[0], adapt_ff[0])
    wide = run_unpick(exchange(picked, "fsdp"), count + 2 * times, cols)
    w_t = gather(attention_weights(1))
    w_c = gather(attention_weights(2))
    ffn_up, _ = lax.optimization_barrier((ffn_up, picked))
    up = gather(up_chunks(ffn_up[0], clips, times))
    maps_f = wide[24:]

    cot = cotangent.reshape(frames, SPATIAL, d)
    cot = to_places(
        [
            lax.dynamic_slice_in_dim(cot, (seq[0] + k) % parts * places, places, 1)
            for k in range(parts)
        ]
    )
    cot = jnp.concatenate(cot, 0).reshape(FRAMES * places, d)
    frames_in = video.reshape(frames, SPATIAL, d)
    made = run_spatial_forward(seq, frames_in, mods, masks, wide, w_s, parts)
    u1, kept_s = to_places(made[:parts]), made[parts:]
    grad_active = run_feed_forward_grad(cot, mods, maps_f, down)
    *kept_t, x3 = run_temporal_cross_forward(u1, ctx, mods, masks, wide, w_t, w_c)
    x3 = x3.reshape(FRAMES * places, d)
    active, g3, grad_a24, grad_b24 = run_feed_forward(x3, cot, grad_active, mods, maps_f, up)
    g3 = g3.reshape(FRAMES, places, d)
    groups = FRAMES * places // ROWS
    halves = 2 if groups % 2 == 0 else 1
    g1, gw, dk, dv = [], [], [], []
    for half in range(halves):
        *pieces, gw_half, dk_half, dv_half = run_cross_temporal_backward(
            g3, u1, kept_t, mods, masks, wide, w_t, w_c, half, halves
        )
        gw.append(gw_half)
        dk.append(dk_half)
        dv.append(dv_half)
        g1.append(to_frames(pieces))

    def as_blocks(rows):
        return rows.reshape(RANK, times, d).transpose(1, 0, 2).reshape(times * RANK, d)

    sources = [grad_a24, as_blocks(grad_b24), kept_t[15], kept_t[16], ctx, masks, wide]
    packed = run_pack_early(gw, dk, dv, sources, clips, parts)
    active, packed, *g1[0] = lax.optimization_barrier((active, packed, *g1[0]))
    *x4, grad_b25, grad_down = run_feed_forward_out(active, x3, cot, mods, maps_f, down, parts)
    early = reduce_grads(packed, all_index, adapters)
    output = to_frames([piece.reshape(frames, places, d) for piece in x4])
    g1 = [piece for pieces in g1 for piece in pieces]
    early, *g1 = lax.optimization_barrier((early, *g1))
    grads, packed = run_spatial_backward(
        seq, g1, halves, frames_in, kept_s, mods, masks, wide, w_s, grad_b25, as_blocks(grad_down), clips
    )
    early = exchange(early)
    packed, early, *output = lax.optimization_barrier((packed, early, *output))
    g0 = run_spatial_input_grad(seq, g1, halves, frames_in, grads, mods, wide, w_s)
    late = reduce_grads(packed, all_index, adapters)
    wide_out, narrow_out = run_assemble(
        early, exchange(late), adapt_wide.shape[1:], adapt_ff.shape[1:]
    )
    output = run_put_in_place(seq, output).reshape(video.shape)
    return (output, g0.reshape(video.shape), wide_out[None], narrow_out[None])


def solution(mesh):
    return jax.shard_map(
        on_device,
        mesh=mesh,
        in_specs=(
            P("fsdp", "seq", None),
            P("fsdp", None, None),
            P("fsdp", None, None, None),
            P("fsdp"),
            P("fsdp", "seq", None),
            P(None, None, "fsdp", None),
            P(None, None, "fsdp", None),
            P(None, "fsdp", None),
            P(None, "fsdp", None),
            P(None, None, None, None, "fsdp"),
            P(None, None, None, None, "fsdp"),
        ),
        out_specs=(
            P("fsdp", "seq", None),
            P("fsdp", "seq", None),
            P(None, None, None, None, "fsdp"),
            P(None, None, None, None, "fsdp"),
        ),
        check_vma=False,
    )
```

```python
import math

import jax
import jax.numpy as jnp
from jax import lax
from jax.experimental import pallas as pl
from jax.experimental.pallas import tpu as pltpu
from jax.sharding import PartitionSpec as P

HEAD_DIM = 72
HEADS = 16
FRAMES = 16
SPATIAL = 256
RANK = 16
ROWS = 256
PAIRS = HEADS // 2
PAD = 128
SCALE = HEAD_DIM ** (-0.5)
EXP_SCALE = SCALE * math.log2(math.e)
LN2 = math.log(2.0)
HIGHEST = lax.Precision.HIGHEST
F32 = jnp.float32
BF16 = jnp.bfloat16
VMEM_LIMIT = 60 * 1024 * 1024


def nn(left, right):
    return lax.dot_general(left, right, (((1,), (0,)), ((), ())), preferred_element_type=F32)


def nt(left, right):
    return lax.dot_general(left, right, (((1,), (1,)), ((), ())), preferred_element_type=F32)


def tn(left, right):
    return lax.dot_general(left, right, (((0,), (0,)), ((), ())), preferred_element_type=F32)


def window(pair):
    return slice(128 * pair, 128 * pair + 256)


def normalize(stream):
    average = jnp.mean(stream, -1, keepdims=True)
    centred = stream - average
    inverse = lax.rsqrt(jnp.mean(centred * centred, -1, keepdims=True) + 1e-06)
    return centred * inverse, inverse


def normalize_back(normal, inverse, grad):
    mean_grad = jnp.mean(grad, -1, keepdims=True)
    mean_both = jnp.mean(grad * normal, -1, keepdims=True)
    return inverse * (grad - mean_grad - normal * mean_both)


def up_rows(ad_ref, number, slot, width):
    rows = ad_ref[2 * number + 1]
    before = jnp.zeros((RANK * slot, width), BF16)
    after = jnp.zeros((PAD - RANK * (slot + 1), width), BF16)
    return jnp.concatenate(([before] if slot else []) + [rows, after], 0)


def three_downs(ad_ref, number):
    return jnp.concatenate([ad_ref[2 * (number + i)] for i in range(3)], 0)


class Loads:
    def __init__(self, entries, sems):
        self.first = pl.program_id(0) == 0
        self.entries = entries
        self.sems = sems

    def copy(self, index):
        source, target = self.entries[index]
        return pltpu.make_async_copy(source, target, self.sems.at[index])

    def start(self):
        @pl.when(self.first)
        def _():
            for index in range(len(self.entries)):
                self.copy(index).start()

    def ready(self, index):
        @pl.when(self.first)
        def _():
            self.copy(index).wait()


def head_masks():
    lane = jnp.arange(256)[None, :]
    begin = jnp.array([16 * (h // 2) + HEAD_DIM * (h % 2) for h in range(HEADS)])[:, None]
    return ((lane >= begin) & (lane < begin + HEAD_DIM)).astype(BF16)


def same_place(shape):
    rows = lax.broadcasted_iota(jnp.int32, shape, 0)
    cols = lax.broadcasted_iota(jnp.int32, shape, 1)
    return jnp.where(rows % 16 == cols % 16, 0.0, -1e30).astype(F32)


def attend(q_ref, k_ref, v_ref, mask_ref, bias, put_out, stat_ref):
    carried = None
    for pair in range(PAIRS):
        win = window(pair)
        q_win, k_win, v_win = q_ref[:, win], k_ref[:, win], v_ref[:, win]
        all_weights, all_values = [], []
        for head in (2 * pair, 2 * pair + 1):
            mask = mask_ref[head : head + 1, :]
            scores = nt(k_win * mask, q_win)
            if bias is not None:
                scores = scores + bias[...]
            top = jnp.max(scores, 0, keepdims=True)
            grown = jnp.exp2(scores - top)
            total = jnp.sum(grown, 0, keepdims=True)
            stat_ref[head : head + 1, :] = top + jnp.log2(total)
            all_weights.append((grown * (1.0 / total)).astype(BF16))
            all_values.append(v_win * mask)
        out = tn(jnp.concatenate(all_weights, 0), jnp.concatenate(all_values, 0))
        low = out[:, :128]
        put_out(pair, low if carried is None else low + carried)
        carried = out[:, 128:]
    put_out(PAIRS, carried)


def attend_back(q_ref, k_ref, v_ref, do_ref, mask_ref, bias, stat_ref, put):
    carried = None
    for pair in range(PAIRS):
        win = window(pair)
        q_win, k_win, v_win, do_win = q_ref[:, win], k_ref[:, win], v_ref[:, win], do_ref[:, win]
        all_grads, all_probs, keys, queries, outs = [], [], [], [], []
        for head in (2 * pair, 2 * pair + 1):
            mask = mask_ref[head : head + 1, :]
            k_own = k_win * mask
            scores = nt(k_own, q_win)
            if bias is not None:
                scores = scores + bias[...]
            probs = jnp.exp2(scores - stat_ref[head : head + 1, :])
            grad_probs = nt(v_win * mask, do_win)
            inner = jnp.sum(probs * grad_probs, 0, keepdims=True)
            all_grads.append((probs * (grad_probs - inner)).astype(BF16))
            all_probs.append(probs.astype(BF16))
            keys.append(k_own)
            queries.append(q_win * mask)
            outs.append(do_win * mask)
        grads = (
            tn(jnp.concatenate(all_grads, 0), jnp.concatenate(keys, 0)),
            nn(jnp.concatenate(all_grads, 1), jnp.concatenate(queries, 0)),
            nn(jnp.concatenate(all_probs, 1), jnp.concatenate(outs, 0)),
        )
        lows = tuple(g[:, :128] for g in grads)
        if carried is not None:
            lows = tuple(a + b for a, b in zip(lows, carried))
        put(pair, lows)
        carried = tuple(g[:, 128:] for g in grads)
    put(PAIRS, carried)


def tile(index):
    return slice(128 * index, 128 * index + 128)


def three_projections(lhs_ref, ad_ref, number, weights, loads, first_load, outs, rank_ref):
    width = weights.shape[2]
    ranks = nt(lhs_ref[:, :width], three_downs(ad_ref, number)).astype(BF16)
    rank_ref[...] = ranks
    lhs_ref[:, width : width + 3 * RANK] = ranks
    for i in range(3):
        loads.ready(first_load + i)
        total = nn(lhs_ref[...], weights[first_load + i])
        outs[i][...] = (total * EXP_SCALE if i == 0 else total).astype(BF16)


def one_projection(lhs_ref, ad_ref, number, weight_ref, rank_ref):
    width = weight_ref.shape[1]
    ranks = nt(lhs_ref[:, :width], ad_ref[2 * number]).astype(BF16)
    rank_ref[...] = ranks
    lhs_ref[:, width : width + RANK] = ranks
    return nn(lhs_ref[...], weight_ref[...])


def block_rows(index):
    return slice(RANK * index, RANK * (index + 1))


def one_back(grad, kept, ranks, ad_ref, number, weight_ref, grad_ref, at):
    width = weight_ref.shape[1]
    both = nt(grad, weight_ref[...])
    grad_rank = both[:, width : width + RANK].astype(BF16)
    grad_ref[block_rows(at), :] += tn(grad_rank, kept)
    grad_ref[block_rows(at + 1), :] += tn(ranks, grad)
    return both[:, :width] + nn(grad_rank, ad_ref[2 * number])


def three_back(grads, inputs, ranks, ad_ref, number, weights, loads, first_load, grad_ref, at):
    width = weights.shape[2]
    both = None
    for i in range(3):
        grad = grads[i][...]
        ups = tn(ranks, grad)
        grad_ref[block_rows(at + 2 * i + 1), :] += ups[block_rows(i)]
        loads.ready(first_load + i)
        part = nt(grad, weights[first_load + i])
        both = part if both is None else both + part
    grad_ranks = both[:, width : width + 3 * RANK].astype(BF16)
    downs = tn(grad_ranks, inputs)
    for i in range(3):
        grad_ref[block_rows(at + 2 * i), :] += downs[block_rows(i)]
    return both[:, :width] + nn(grad_ranks, three_downs(ad_ref, number))


def place_of(seq_ref, k, parts, places):
    return pl.multiple_of(lax.rem(seq_ref[0] + k, parts) * places, 16)


def spatial_forward(seq_ref, x_ref, mod_ref, mask_ref, ad_ref, w_hbm, *refs):
    x1_refs = refs[:-11]
    q_ref, k_ref, v_ref, o_ref, stat_ref, rq_ref, ro_ref, w_ref, lhs_ref, x1_s, sems = refs[-11:]
    width = x_ref.shape[2]
    loads = Loads([(w_hbm.at[i], w_ref.at[i, pl.ds(0, width), :]) for i in range(4)], sems)
    loads.start()

    @pl.when(loads.first)
    def _():
        lhs_ref[:, width:] = jnp.zeros((ROWS, PAD), BF16)
        for i in range(4):
            w_ref[i, width:, :] = up_rows(ad_ref, i, i % 3, width)

    stream = x_ref[0].astype(F32)
    normal, _ = normalize(stream)
    lhs_ref[:, :width] = (normal * (1.0 + mod_ref[1:2, :]) + mod_ref[0:1, :]).astype(BF16)
    q, k, v = q_ref.at[0], k_ref.at[0], v_ref.at[0]
    three_projections(lhs_ref, ad_ref, 0, w_ref, loads, 0, (q, k, v), rq_ref.at[0])

    def put_out(index, value):
        value = value.astype(BF16)
        o_ref[0, :, tile(index)] = value
        lhs_ref[:, tile(index)] = value

    attend(q, k, v, mask_ref, None, put_out, stat_ref.at[0])
    loads.ready(3)
    branch = one_projection(lhs_ref, ad_ref, 3, w_ref.at[3], ro_ref.at[0])
    x1_s[...] = (stream + mod_ref[2:3, :] * branch).astype(BF16)
    places = x1_refs[0].shape[1]
    for k, ref in enumerate(x1_refs):
        ref[0] = x1_s[pl.ds(place_of(seq_ref, k, len(x1_refs), places), places), :]


def rows_of(refs):
    pieces = [ref[...].reshape(-1, ref.shape[2]) for ref in refs]
    return pieces[0] if len(pieces) == 1 else jnp.concatenate(pieces, 0)


def temporal_cross_forward(parts, *refs):
    _temporal_cross_forward(refs[:parts], *refs[parts:])


def _temporal_cross_forward(
    x_refs, ctx_ref, mod_ref, mask_ref, ad_ref, wt_hbm, wc_hbm,
    q_ref, k_ref, v_ref, o_ref, stat_ref, rq_ref, ro_ref,
    u2_ref, qc_ref, oc_ref, statc_ref, rqc_ref, roc_ref, kp_ref, vp_ref, rk_ref, rv_ref, x3_ref,
    w_ref, bias_ref, lhs_ref, q_s, k_s, v_s, o_s, sems,
):
    width = x_refs[0].shape[2]
    first = pl.program_id(0) == 0
    sources = [wt_hbm.at[i] for i in range(4)] + [wc_hbm.at[i] for i in range(4)]
    loads = Loads([(w, w_ref.at[i, pl.ds(0, width), :]) for i, w in enumerate(sources)], sems)
    loads.start()

    @pl.when(first)
    def _():
        bias_ref[...] = same_place(bias_ref.shape)
        lhs_ref[:, width:] = jnp.zeros((ROWS, PAD), BF16)
        for i in range(8):
            w_ref[i, width:, :] = up_rows(ad_ref, 4 + i, i if i < 3 else 0, width)

    loaded = rows_of(x_refs)
    stream = loaded.astype(F32)
    lhs_ref[:, :width] = loaded
    three_projections(lhs_ref, ad_ref, 4, w_ref, loads, 0, (q_s, k_s, v_s), rq_ref.at[0])
    q_ref[...] = q_s[...].reshape(q_ref.shape)
    k_ref[...] = k_s[...].reshape(k_ref.shape)
    v_ref[...] = v_s[...].reshape(v_ref.shape)

    def put_out(index, value):
        o_s[:, tile(index)] = value.astype(BF16)

    attend(q_s, k_s, v_s, mask_ref, bias_ref, put_out, stat_ref.at[0])
    lhs_ref[:, :width] = o_s[...]
    o_ref[...] = o_s[...].reshape(o_ref.shape)
    loads.ready(3)
    branch = one_projection(lhs_ref, ad_ref, 7, w_ref.at[3], ro_ref.at[0])
    stream = stream + mod_ref[2:3, :] * branch
    inputs = stream.astype(BF16)
    u2_ref[...] = inputs.reshape(u2_ref.shape)
    lhs_ref[:, :width] = inputs
    loads.ready(4)
    queries = one_projection(lhs_ref, ad_ref, 8, w_ref.at[4], rqc_ref.at[0])
    q_s[...] = (queries * EXP_SCALE).astype(BF16)
    qc_ref[...] = q_s[...].reshape(qc_ref.shape)
    loads.ready(5)
    loads.ready(6)

    @pl.when(first)
    def _():
        for number, at, rank_ref, pair_ref in ((9, 5, rk_ref, kp_ref), (10, 6, rv_ref, vp_ref)):
            ranks = nt(ctx_ref[...], ad_ref[2 * number]).astype(BF16)
            rank_ref[...] = ranks
            made = nn(ctx_ref[...], w_ref[at, :width, :]) + nn(ranks, ad_ref[2 * number + 1])
            k_s[:PAD, :] = made.astype(BF16)
            for pair in range(PAIRS):
                piece = k_s[:PAD, window(pair)]
                pair_ref[pair, :PAD, :] = piece * mask_ref[2 * pair : 2 * pair + 1, :]
                pair_ref[pair, PAD:, :] = piece * mask_ref[2 * pair + 1 : 2 * pair + 2, :]

    carried = None
    count = 120
    for pair in range(PAIRS):
        scores = nt(kp_ref[pair], q_s[:, window(pair)])
        pieces = []
        for sub in range(2):
            own = scores[PAD * sub : PAD * sub + count]
            top = jnp.max(own, 0, keepdims=True)
            grown = jnp.exp2(own - top)
            total = jnp.sum(grown, 0, keepdims=True)
            statc_ref[0, 2 * pair + sub : 2 * pair + sub + 1, :] = top + jnp.log2(total)
            pieces += [grown * (1.0 / total), jnp.zeros((PAD - count, ROWS), F32)]
        weights = jnp.concatenate(pieces, 0).astype(BF16)
        out = tn(weights, vp_ref[pair])
        low = out[:, :128]
        put_out(pair, low if carried is None else low + carried)
        carried = out[:, 128:]
    put_out(PAIRS, carried)
    lhs_ref[:, :width] = o_s[...]
    oc_ref[...] = o_s[...].reshape(oc_ref.shape)
    loads.ready(7)
    stream = stream + one_projection(lhs_ref, ad_ref, 11, w_ref.at[7], roc_ref.at[0])
    x3_ref[...] = stream.reshape(x3_ref.shape)


def gelu_both(hidden):
    root = math.sqrt(2.0 / math.pi)
    square = hidden * hidden
    inner = root * (hidden + 0.044715 * (square * hidden))
    bent = jnp.tanh(inner)
    half = 0.5 * (1.0 + bent)
    slope = half + 0.5 * hidden * (1.0 - bent * bent) * (root * (1.0 + 3.0 * 0.044715 * square))
    return hidden * half, slope


def transposed_map(rows):
    nothing = jnp.zeros((PAD - rows.shape[0], rows.shape[1]), F32)
    wide = jnp.concatenate([rows.astype(F32), nothing], 0)
    return wide.T.astype(BF16)


def down_loads(order_ref, pieces, down_ref, width):
    half = width // 2
    count = len(pieces) // 2
    core = order_ref[count]
    entries = []
    for k in range(count):
        for source, side in ((pieces[k], core), (pieces[count + k], 1 - core)):
            start = pl.multiple_of(order_ref[k] * width + side * half, 16)
            entries.append((source, down_ref.at[pl.ds(start, half), pl.ds(0, width)]))
    return entries


def fill_down_maps(ad_ref, down_ref, width):
    chunks = down_ref.shape[0] // width
    for c in range(chunks):
        rows = slice(c * width, (c + 1) * width)
        down_ref[rows, width:] = transposed_map(ad_ref[2 + chunks + c])


def feed_forward_grad(count, order_ref, cot_ref, mod_ref, ad_ref, *refs):
    pieces = refs[:count]
    grad_ref, down_ref, lhs_ref, sems = refs[count:]
    width = cot_ref.shape[1]
    entries = down_loads(order_ref, pieces, down_ref, width)
    loads = Loads(entries, sems)
    loads.start()

    @pl.when(loads.first)
    def _():
        lhs_ref[:, width:] = jnp.zeros((ROWS, PAD), BF16)
        fill_down_maps(ad_ref, down_ref, width)

    branch = (mod_ref[5:6, :] * cot_ref[...].astype(F32)).astype(BF16)
    lhs_ref[:, :width] = branch
    lhs_ref[:, width : width + RANK] = nt(branch, ad_ref[1]).astype(BF16)
    for i in range(len(entries)):
        loads.ready(i)
    for cols in hidden_chunks(down_ref.shape[0]):
        grad_ref[:, cols] = nt(lhs_ref[...], down_ref[cols, :]).astype(BF16)


def hidden_chunks(hidden):
    return [slice(at, at + 1536) for at in range(0, hidden, 1536)]


def feed_forward(
    x3_ref, cot_ref, grad_ref, mod_ref, ad_ref, w_hbm,
    act_ref, g3_ref, gd_ref, gu_ref, up_ref, lhs_ref, dh_ref, sems,
):
    width = x3_ref.shape[1]
    hidden_size = up_ref.shape[1]
    chunks = hidden_size // width
    loads = Loads(
        [
            (w_hbm.at[c], up_ref.at[pl.ds(0, width), pl.ds(c * width, width)])
            for c in range(chunks)
        ],
        sems,
    )
    loads.start()

    @pl.when(loads.first)
    def _():
        gd_ref[...] = jnp.zeros_like(gd_ref)
        gu_ref[...] = jnp.zeros_like(gu_ref)
        lhs_ref[:, width:] = jnp.zeros((ROWS, PAD), BF16)
        up_ref[width + RANK :, :] = jnp.zeros((PAD - RANK, hidden_size), BF16)
        for c in range(chunks):
            up_ref[width : width + RANK, c * width : (c + 1) * width] = ad_ref[2 + c]

    normal, inverse = normalize(x3_ref[...])
    inputs = (normal * (1.0 + mod_ref[4:5, :]) + mod_ref[3:4, :]).astype(BF16)
    rank_up = nt(inputs, ad_ref[0]).astype(BF16)
    lhs_ref[:, :width] = inputs
    lhs_ref[:, width : width + RANK] = rank_up
    for c in range(chunks):
        loads.ready(c)
    for cols in hidden_chunks(hidden_size):
        active, slope = gelu_both(nn(lhs_ref[...], up_ref[:, cols]))
        act_ref[:, cols] = active.astype(BF16)
        dh_ref[:, cols] = (slope * grad_ref[:, cols].astype(F32)).astype(BF16)
    both = nt(dh_ref[...], up_ref[...])
    gu_ref[...] += tn(rank_up, dh_ref[...])
    grad_rank = both[:, width : width + RANK].astype(BF16)
    grad_in = both[:, :width] + nn(grad_rank, ad_ref[0])
    gd_ref[...] += tn(grad_rank, lhs_ref[:, :width])
    grad_in = normalize_back(normal, inverse, grad_in * (1.0 + mod_ref[4:5, :]))
    g3_ref[...] = cot_ref[...].astype(F32) + grad_in


def feed_forward_out(count, order_ref, act_ref, x3_ref, cot_ref, mod_ref, ad_ref, *refs):
    pieces, refs = refs[:count], refs[count:]
    x4_refs = refs[:-4]
    gu_ref, gd_ref, down_ref, sems = refs[-4:]
    width = x3_ref.shape[1]
    step = pl.program_id(0)
    entries = down_loads(order_ref, pieces, down_ref, width)
    loads = Loads(entries, sems)
    loads.start()

    @pl.when(loads.first)
    def _():
        gu_ref[...] = jnp.zeros_like(gu_ref)
        gd_ref[...] = jnp.zeros_like(gd_ref)
        fill_down_maps(ad_ref, down_ref, width)

    grad_branch = (mod_ref[5:6, :] * cot_ref[...].astype(F32)).astype(BF16)
    gd_ref[...] += tn(nt(grad_branch, ad_ref[1]).astype(BF16), act_ref[...])
    for i in range(len(entries)):
        loads.ready(i)
    both = nn(act_ref[...], down_ref[...])
    ranks = both[:, width : width + RANK].astype(BF16)
    branch = both[:, :width] + nn(ranks, ad_ref[1])
    gu_ref[...] += tn(ranks, grad_branch)
    result = (x3_ref[...] + mod_ref[5:6, :] * branch).astype(BF16)
    share = x4_refs[0].shape[0]
    for k, ref in enumerate(x4_refs):
        at = k * share

        @pl.when(step == at // ROWS)
        def _():
            ref[...] = result[at % ROWS : at % ROWS + share]


def cross_temporal_backward(parts, *refs):
    outs = len(refs) - parts - 13
    _cross_temporal_backward(refs[:parts], refs[outs : outs + parts], *refs[parts:outs], *refs[outs + parts :])


def _cross_temporal_backward(
    u1_refs, g1_refs, g3_ref, q_ref, k_ref, v_ref, o_ref, stat_ref, rq_ref, ro_ref,
    u2_ref, qc_ref, oc_ref, statc_ref, rqc_ref, roc_ref, kp_ref, vp_ref,
    mod_ref, mask_ref, ad_ref, wt_hbm, wc_hbm,
    gw_ref, dk_acc, dv_acc, w_ref, bias_ref, q_s, k_s, v_s, do_s, dq_s, dk_s, dv_s, sems,
):
    width = u1_refs[0].shape[2]
    first = pl.program_id(0) == 0
    order = (7, 4, 3, 0, 1, 2)
    sources = [wc_hbm.at[n - 4] if n >= 4 else wt_hbm.at[n] for n in order]
    loads = Loads([(w, w_ref.at[i, pl.ds(0, width), :]) for i, w in enumerate(sources)], sems)
    loads.start()

    @pl.when(first)
    def _():
        bias_ref[...] = same_place(bias_ref.shape)
        gw_ref[...] = jnp.zeros_like(gw_ref)
        dk_acc[...] = jnp.zeros_like(dk_acc)
        dv_acc[...] = jnp.zeros_like(dv_acc)
        for i, n in enumerate(order):
            w_ref[i, width:, :] = up_rows(ad_ref, 4 + n, n if n < 3 else 0, width)

    def rows(ref):
        return ref[...].reshape(ROWS, ref.shape[2])

    grad = rows(g3_ref)
    loads.ready(0)
    do_s[...] = one_back(
        grad.astype(BF16), rows(oc_ref), roc_ref[0], ad_ref, 11, w_ref.at[0], gw_ref, 14
    ).astype(BF16)
    q_s[...] = rows(qc_ref)
    count = 120
    carried = None
    for pair in range(PAIRS):
        win = window(pair)
        q_win, do_win = q_s[:, win], do_s[:, win]
        scores = nt(kp_ref[pair], q_win)
        grad_probs = nt(vp_ref[pair], do_win)
        all_probs, all_grads = [], []
        nothing = jnp.zeros((PAD - count, ROWS), F32)
        for sub in range(2):
            span = slice(PAD * sub, PAD * sub + count)
            row = 2 * pair + sub
            probs = jnp.exp2(scores[span] - statc_ref[0, row : row + 1, :])
            own = grad_probs[span]
            inner = jnp.sum(probs * own, 0, keepdims=True)
            all_probs += [probs, nothing]
            all_grads += [probs * (own - inner), nothing]
        probs = jnp.concatenate(all_probs, 0).astype(BF16)
        grad_scores = jnp.concatenate(all_grads, 0).astype(BF16)
        dk_acc[pair] += nn(grad_scores, q_win)
        dv_acc[pair] += nn(probs, do_win)
        out = tn(grad_scores, kp_ref[pair])
        low = out[:, :128]
        dq_s[:, tile(pair)] = ((low if carried is None else low + carried) * SCALE).astype(BF16)
        carried = out[:, 128:]
    dq_s[:, tile(PAIRS)] = (carried * SCALE).astype(BF16)
    loads.ready(1)
    grad = grad + one_back(
        dq_s[...], rows(u2_ref), rqc_ref[0], ad_ref, 8, w_ref.at[1], gw_ref, 8
    )
    loads.ready(2)
    do_s[...] = one_back(
        (mod_ref[2:3, :] * grad).astype(BF16), rows(o_ref), ro_ref[0], ad_ref, 7, w_ref.at[2], gw_ref, 6
    ).astype(BF16)
    q_s[...] = rows(q_ref)
    k_s[...] = rows(k_ref)
    v_s[...] = rows(v_ref)

    def put(index, values):
        dq_s[:, tile(index)] = (values[0] * SCALE).astype(BF16)
        dk_s[:, tile(index)] = (values[1] * LN2).astype(BF16)
        dv_s[:, tile(index)] = values[2].astype(BF16)

    attend_back(q_s, k_s, v_s, do_s, mask_ref, bias_ref, stat_ref.at[0], put)
    grad = grad + three_back(
        (dq_s, dk_s, dv_s), rows_of(u1_refs), rq_ref[0], ad_ref, 4, w_ref, loads, 3, gw_ref, 0
    )
    grad = grad.astype(BF16)
    share = ROWS // len(g1_refs)
    for k, ref in enumerate(g1_refs):
        ref[...] = grad[share * k : share * (k + 1)].reshape(ref.shape)


def tail_groups(cols):
    tail = cols - PAD
    return PAD // tail if 0 < tail < PAD and PAD % tail == 0 else 0


def packed_rows(blocks, cols):
    group = tail_groups(cols)
    if not group:
        return blocks * RANK, cols
    return (blocks + -(-blocks // group)) * RANK, PAD


def put_blocks(blocks, put):
    cols = blocks[0].shape[1]
    group = tail_groups(cols)
    for k, rows in enumerate(blocks):
        put(k, rows[:, :PAD] if group else rows)
    for k in range(0, len(blocks), group) if group else ():
        tails = [rows[:, PAD:] for rows in blocks[k : k + group]]
        missing = group - len(tails)
        if missing:
            tails.append(jnp.zeros((RANK, missing * (cols - PAD)), blocks[0].dtype))
        put(len(blocks) + k // group, jnp.concatenate(tails, 1))


def get_block(get, index, count, cols):
    group = tail_groups(cols)
    if not group:
        return get(index)
    at = (index % group) * (cols - PAD)
    return jnp.concatenate([get(index), get(count + index // group)[:, at : at + cols - PAD]], 1)


def pack_columns(table_ref, packed_ref, clips):
    parts = packed_ref.shape[0] // clips
    share = table_ref.shape[0] // parts
    cols = table_ref.shape[1] // clips
    for f in range(clips):
        for s in range(parts):
            piece = table_ref[share * s : share * (s + 1), cols * f : cols * (f + 1)].astype(BF16)
            blocks = [piece[block_rows(k)] for k in range(share // RANK)]

            def put(k, rows):
                packed_ref[f * parts + s, block_rows(k), :] = rows

            put_blocks(blocks, put)


def stacked(seq_ref, g1_refs, halves, whole_ref):
    parts = len(g1_refs) // halves
    part = g1_refs[0].shape[1]
    for half in range(halves):
        for k in range(parts):
            start = place_of(seq_ref, k, parts, part * halves) + half * part
            whole_ref[pl.ds(pl.multiple_of(start, 16), part), :] = g1_refs[half * parts + k][0]
    return whole_ref[...].astype(F32)


def spatial_backward(pieces, halves, clips, seq_ref, *refs):
    g1_refs, refs = refs[:pieces], refs[pieces:]
    (
        x_ref, q_ref, k_ref, v_ref, o_ref, stat_ref, rq_ref, ro_ref, mod_ref, mask_ref, ad_ref, w_hbm,
        down_ref, up_ref, d_ref, packed_ref, w_ref, gw_ref, do_s, sems,
    ) = refs
    width = x_ref.shape[2]
    loads = Loads([(w_hbm.at[3], w_ref.at[pl.ds(0, width), :])], sems)
    loads.start()

    @pl.when(loads.first)
    def _():
        gw_ref[...] = jnp.zeros_like(gw_ref)
        w_ref[width:, :] = up_rows(ad_ref, 3, 0, width)

    grad = stacked(seq_ref, g1_refs, halves, do_s)
    loads.ready(0)
    do_s[...] = one_back(
        (mod_ref[2:3, :] * grad).astype(BF16), o_ref[0], ro_ref[0], ad_ref, 3, w_ref, gw_ref, 6
    ).astype(BF16)

    def put(index, values):
        for i, factor in enumerate((SCALE, LN2, 1.0)):
            value = values[i] if factor == 1.0 else values[i] * factor
            d_ref[0, :, width * i + 128 * index : width * i + 128 * index + 128] = value.astype(BF16)

    attend_back(
        q_ref.at[0], k_ref.at[0], v_ref.at[0], do_s, mask_ref, None, stat_ref.at[0], put
    )
    ranks = rq_ref[0]
    grad_ranks = None
    for i in range(3):
        grad = d_ref[0, :, width * i : width * (i + 1)]
        gw_ref[block_rows(2 * i + 1), :] += tn(ranks, grad)[block_rows(i)]
        part = nt(grad, up_rows(ad_ref, i, i, width))
        grad_ranks = part if grad_ranks is None else grad_ranks + part
    d_ref[0, :, 3 * width :] = grad_ranks.astype(BF16)
    normal, _ = normalize(x_ref[0].astype(F32))
    inputs = (normal * (1.0 + mod_ref[1:2, :]) + mod_ref[0:1, :]).astype(BF16)
    downs = tn(d_ref[0, :, 3 * width :], inputs)
    for i in range(3):
        gw_ref[block_rows(2 * i), :] += downs[block_rows(i)]

    @pl.when(pl.program_id(0) == pl.num_programs(0) - 1)
    def _():
        at = 8 * RANK
        gw_ref[at : at + RANK, :] = down_ref[...]
        gw_ref[at + RANK : at + RANK + up_ref.shape[0], :] = up_ref[...]
        pack_columns(gw_ref, packed_ref, clips)


def spatial_input_grad(pieces, halves, seq_ref, *refs):
    g1_refs, refs = refs[:pieces], refs[pieces:]
    x_ref, d_ref, mod_ref, ad_ref, w_hbm, g0_ref, w_ref, whole_s, sems = refs
    width = x_ref.shape[2]
    loads = Loads(
        [(w_hbm.at[i], w_ref.at[:, pl.ds(i * width, width)]) for i in range(3)], sems
    )
    loads.start()

    @pl.when(loads.first)
    def _():
        w_ref[:, 3 * width :] = transposed_map(three_downs(ad_ref, 0))

    normal, inverse = normalize(x_ref[0].astype(F32))
    grad = stacked(seq_ref, g1_refs, halves, whole_s)
    for i in range(3):
        loads.ready(i)
    grad_in = nt(d_ref[0], w_ref[...])
    grad = grad + normalize_back(normal, inverse, grad_in * (1.0 + mod_ref[1:2, :]))
    g0_ref[0] = grad.astype(BF16)


def put_in_place(seq_ref, *refs):
    *pieces, out_ref = refs
    places = pieces[0].shape[1]
    for k, ref in enumerate(pieces):
        out_ref[0, pl.ds(place_of(seq_ref, k, len(pieces), places), places), :] = ref[0]


def pack_early(clips, halves, *refs):
    gw_refs, refs = refs[:halves], refs[halves:]
    dk_refs, refs = refs[:halves], refs[halves:]
    dv_refs, refs = refs[:halves], refs[halves:]
    down_ref, up_ref, rk_ref, rv_ref, ctx_ref, mask_ref, ad_ref, packed_ref, table_ref, ctx_s = refs

    def added(each):
        total = each[0]
        for value in each[1:]:
            total = total + value
        return total

    at = gw_refs[0].shape[0]
    table_ref[:at, :] = added([ref[...] for ref in gw_refs])
    table_ref[at : at + RANK, :] = down_ref[...]
    at += RANK
    table_ref[at : at + up_ref.shape[0], :] = up_ref[...]
    at += up_ref.shape[0]
    table_ref[at:, :] = jnp.zeros((table_ref.shape[0] - at, table_ref.shape[1]), F32)
    context = ctx_ref[...].astype(F32)
    for accs, factor, rank_ref, number, at in (
        (dk_refs, LN2, rk_ref, 9, 10),
        (dv_refs, 1.0, rv_ref, 10, 12),
    ):
        held = None
        for pair in range(PAIRS):
            whole = added([ref[pair] for ref in accs]) * factor
            out = whole[:PAD] * mask_ref[2 * pair : 2 * pair + 1, :].astype(F32)
            out = out + whole[PAD:] * mask_ref[2 * pair + 1 : 2 * pair + 2, :].astype(F32)
            low = out[:, :128]
            ctx_s[:, tile(pair)] = low if held is None else low + held
            held = out[:, 128:]
        ctx_s[:, tile(PAIRS)] = held
        grad_kv = ctx_s[...]
        grad_rank = lax.dot_general(
            grad_kv, ad_ref[2 * number + 1].astype(F32), (((1,), (1,)), ((), ())),
            precision=HIGHEST, preferred_element_type=F32,
        )
        table_ref[block_rows(at), :] = lax.dot_general(
            grad_rank, context, (((0,), (0,)), ((), ())),
            precision=HIGHEST, preferred_element_type=F32,
        )
        table_ref[block_rows(at + 1), :] = lax.dot_general(
            rank_ref[...].astype(F32), grad_kv, (((0,), (0,)), ((), ())),
            precision=HIGHEST, preferred_element_type=F32,
        )
    pack_columns(table_ref, packed_ref, clips)


def assemble(early_ref, late_ref, wide_ref, narrow_ref):
    _, adapters, _, cols = wide_ref.shape
    times = narrow_ref.shape[3] // cols

    def block(ref, total, index, a):
        each = total // ref.shape[0]

        def get(k):
            return ref[index // each, a, block_rows(k), :].astype(F32)

        return get_block(get, index % each, each, cols)

    for a in range(adapters):
        for i in range(8):
            wide_ref[i, a] = block(late_ref, LATE_BLOCKS, i, a)
        for i in range(17):
            wide_ref[8 + i, a] = block(early_ref, EARLY_BLOCKS, i, a)
        wide_ref[25, a] = block(late_ref, LATE_BLOCKS, 8, a)
        narrow_ref[0, a] = jnp.concatenate(
            [block(early_ref, EARLY_BLOCKS, 17 + j, a) for j in range(times)], 1
        )
        narrow_ref[1, a] = jnp.concatenate(
            [block(late_ref, LATE_BLOCKS, 9 + j, a) for j in range(times)], 1
        )


def combine(index_ref, got_ref, out_ref, acc_ref):
    clips = index_ref.shape[0]
    parts = got_ref.shape[0] // clips
    acc_ref[...] = jnp.zeros_like(acc_ref)

    def step(f, carry):
        total = got_ref[f * parts].astype(F32)
        for s in range(1, parts):
            total = total + got_ref[f * parts + s].astype(F32)
        acc_ref[index_ref[f]] += total
        return carry

    lax.fori_loop(0, clips, step, 0)
    table = acc_ref[...].astype(BF16)
    for s in range(parts):
        out_ref[s] = table


def pick(index_ref, wide_ref, narrow_ref, out_ref):
    count, _, _, cols = wide_ref.shape
    times = narrow_ref.shape[3] // cols

    def step(f, carry):
        a = index_ref[f]
        blocks = [wide_ref[k, a] for k in range(count)]
        for p in range(2):
            rows = narrow_ref[p, a]
            blocks += [rows[:, cols * j : cols * (j + 1)] for j in range(times)]

        def put(k, rows):
            out_ref[f, block_rows(k), :] = rows

        put_blocks(blocks, put)
        return carry

    lax.fori_loop(0, index_ref.shape[0], step, 0)


def unpick(count, cols, got_ref, out_ref):
    for k in range(count):
        pieces = []
        for f in range(got_ref.shape[0]):

            def get(index):
                return got_ref[f, block_rows(index), :]

            pieces.append(get_block(get, k, count, cols))
        out_ref[k] = jnp.concatenate(pieces, 1)


def whole_block(array):
    zeros = (0,) * array.ndim
    return pl.BlockSpec(array.shape, lambda i: zeros, pipeline_mode=pl.Buffered(1))


def anywhere():
    return pl.BlockSpec(memory_space=pl.ANY)


def like(shape, dtype):
    return jax.ShapeDtypeStruct(shape, dtype)


PARAMS = pltpu.CompilerParams(
    dimension_semantics=("arbitrary",), vmem_limit_bytes=VMEM_LIMIT
)


def cost(flops, read):
    return pl.CostEstimate(flops=flops, bytes_accessed=read, transcendentals=flops // 4096)


def run_spatial_forward(seq, video, mods, masks, wide, w_s, parts):
    frames, rows, d = video.shape
    places = rows // parts
    by_frame = lambda i: (i, 0, 0)
    row_block = pl.BlockSpec((1, rows, d), by_frame)
    return pl.pallas_call(
        spatial_forward,
        grid=(frames,),
        in_specs=[in_smem(), row_block, whole_block(mods), whole_block(masks), whole_block(wide), anywhere()],
        out_specs=[pl.BlockSpec((1, places, d), by_frame)] * parts
        + [
            row_block,
            row_block,
            row_block,
            row_block,
            pl.BlockSpec((1, HEADS, rows), by_frame),
            pl.BlockSpec((1, rows, 3 * RANK), by_frame),
            pl.BlockSpec((1, rows, RANK), by_frame),
        ],
        out_shape=[like((frames, places, d), BF16)] * parts
        + [like(video.shape, BF16)] * 4
        + [
            like((frames, HEADS, rows), F32),
            like((frames, rows, 3 * RANK), BF16),
            like((frames, rows, RANK), BF16),
        ],
        scratch_shapes=[
            pltpu.VMEM((4, d + PAD, d), BF16),
            pltpu.VMEM((ROWS, d + PAD), BF16),
            pltpu.VMEM((ROWS, d), BF16),
            pltpu.SemaphoreType.DMA((4,)),
        ],
        compiler_params=PARAMS,
        cost_estimate=cost(10 * frames * rows * d * d, 30_000_000),
        name="spatial_forward",
    )(seq, video, mods, masks, wide, w_s)


def run_temporal_cross_forward(x1, context, mods, masks, wide, w_t, w_c):
    parts = len(x1)
    own_frames, places, d = x1[0].shape
    frames = own_frames * parts
    groups = places * frames // ROWS
    each = ROWS // frames
    across = pl.BlockSpec((frames, each, d), lambda i: (0, i, 0))
    by_group = lambda i: (i, 0, 0)
    stat = pl.BlockSpec((1, HEADS, ROWS), by_group)
    three = pl.BlockSpec((1, ROWS, 3 * RANK), by_group)
    one = pl.BlockSpec((1, ROWS, RANK), by_group)
    full = lambda *shape: pl.BlockSpec(shape, lambda i: (0,) * len(shape))
    act = like((frames, places, d), BF16)

    def body(*refs):
        temporal_cross_forward(parts, *refs)

    stat_shape = like((groups, HEADS, ROWS), F32)
    one_shape = like((groups, ROWS, RANK), BF16)
    return pl.pallas_call(
        body,
        grid=(groups,),
        in_specs=[pl.BlockSpec((own_frames, each, d), lambda i: (0, i, 0))] * parts
        + [whole_block(context), whole_block(mods), whole_block(masks), whole_block(wide), anywhere(), anywhere()],
        out_specs=[across] * 4 + [stat, three, one] + [across] * 3 + [stat, one, one]
        + [full(PAIRS, 2 * PAD, 256)] * 2 + [full(PAD, RANK)] * 2 + [across],
        out_shape=[act] * 4 + [stat_shape, like((groups, ROWS, 3 * RANK), BF16), one_shape]
        + [act] * 3 + [stat_shape, one_shape, one_shape]
        + [like((PAIRS, 2 * PAD, 256), BF16)] * 2 + [like((PAD, RANK), BF16)] * 2
        + [like((frames, places, d), F32)],
        scratch_shapes=[pltpu.VMEM((8, d + PAD, d), BF16), pltpu.VMEM((ROWS, ROWS), F32)]
        + [pltpu.VMEM((ROWS, d + PAD), BF16)]
        + [pltpu.VMEM((ROWS, d), BF16)] * 4
        + [pltpu.SemaphoreType.DMA((8,))],
        compiler_params=PARAMS,
        cost_estimate=cost(14 * places * frames * d * d, 50_000_000),
        name="temporal_cross_forward",
    )(*x1, context, mods, masks, wide, w_t, w_c)


def in_smem():
    return pl.BlockSpec(memory_space=pltpu.SMEM)


def run_feed_forward_grad(cot, mods, maps, down):
    tokens, d = cot.shape
    order, *pieces = down
    hidden = len(pieces) // 2 * d

    def body(*refs):
        feed_forward_grad(len(pieces), *refs)

    return pl.pallas_call(
        body,
        grid=(tokens // ROWS,),
        in_specs=[in_smem(), pl.BlockSpec((ROWS, d), lambda i: (i, 0)), whole_block(mods), whole_block(maps)]
        + [anywhere()] * len(pieces),
        out_specs=pl.BlockSpec((ROWS, hidden), lambda i: (i, 0)),
        out_shape=like((tokens, hidden), BF16),
        scratch_shapes=[
            pltpu.VMEM((hidden, d + PAD), BF16),
            pltpu.VMEM((ROWS, d + PAD), BF16),
            pltpu.SemaphoreType.DMA((len(pieces),)),
        ],
        compiler_params=PARAMS,
        cost_estimate=cost(2 * tokens * d * hidden, 30_000_000),
        name="feed_forward_grad",
    )(order, cot, mods, maps, *pieces)


def run_feed_forward(x3, cot, grad_active, mods, maps, up):
    tokens, d = x3.shape
    chunks = up.shape[0]
    rows = pl.BlockSpec((ROWS, d), lambda i: (i, 0))
    wide_rows = pl.BlockSpec((ROWS, chunks * d), lambda i: (i, 0))
    return pl.pallas_call(
        feed_forward,
        grid=(tokens // ROWS,),
        in_specs=[rows, rows, wide_rows, whole_block(mods), whole_block(maps), anywhere()],
        out_specs=[
            wide_rows,
            rows,
            pl.BlockSpec((RANK, d), lambda i: (0, 0)),
            pl.BlockSpec((RANK, chunks * d), lambda i: (0, 0)),
        ],
        out_shape=[
            like((tokens, chunks * d), BF16),
            like((tokens, d), F32),
            like((RANK, d), F32),
            like((RANK, chunks * d), F32),
        ],
        scratch_shapes=[
            pltpu.VMEM((d + PAD, chunks * d), BF16),
            pltpu.VMEM((ROWS, d + PAD), BF16),
            pltpu.VMEM((ROWS, chunks * d), BF16),
            pltpu.SemaphoreType.DMA((chunks,)),
        ],
        compiler_params=PARAMS,
        cost_estimate=cost(4 * tokens * d * d * chunks, 50_000_000),
        name="feed_forward",
    )(x3, cot, grad_active, mods, maps, up)


def run_feed_forward_out(active, x3, cot, mods, maps, down, parts):
    tokens, d = x3.shape
    order, *pieces = down
    hidden = active.shape[1]
    share = tokens // parts

    def body(*refs):
        feed_forward_out(len(pieces), *refs)

    rows = pl.BlockSpec((ROWS, d), lambda i: (i, 0))
    return pl.pallas_call(
        body,
        grid=(tokens // ROWS,),
        in_specs=[
            in_smem(),
            pl.BlockSpec((ROWS, hidden), lambda i: (i, 0)),
            rows,
            rows,
            whole_block(mods),
            whole_block(maps),
        ]
        + [anywhere()] * len(pieces),
        out_specs=[pl.BlockSpec((share, d), lambda i: (0, 0))] * parts
        + [
            pl.BlockSpec((RANK, d), lambda i: (0, 0)),
            pl.BlockSpec((RANK, hidden), lambda i: (0, 0)),
        ],
        out_shape=[like((share, d), BF16)] * parts
        + [
            like((RANK, d), F32),
            like((RANK, hidden), F32),
        ],
        scratch_shapes=[
            pltpu.VMEM((hidden, d + PAD), BF16),
            pltpu.SemaphoreType.DMA((len(pieces),)),
        ],
        compiler_params=PARAMS,
        cost_estimate=cost(2 * tokens * d * hidden, 30_000_000),
        name="feed_forward_out",
    )(order, active, x3, cot, mods, maps, *pieces)


def run_cross_temporal_backward(g3, u1, saved, mods, masks, wide, w_t, w_c, half, halves):
    parts = len(u1)
    own_frames, places, d = u1[0].shape
    frames = own_frames * parts
    each = ROWS // frames
    groups = places * frames // ROWS // halves
    start = half * groups
    across = pl.BlockSpec((frames, ROWS // frames, d), lambda i: (0, i + start, 0))
    by_group = lambda i: (i + start, 0, 0)
    stat = pl.BlockSpec((1, HEADS, ROWS), by_group)
    three = pl.BlockSpec((1, ROWS, 3 * RANK), by_group)
    one = pl.BlockSpec((1, ROWS, RANK), by_group)
    kp, vp = saved[13:15]
    pair_sums = pl.BlockSpec((PAIRS, 2 * PAD, 256), lambda i: (0, 0, 0))

    def body(*refs):
        cross_temporal_backward(parts, *refs)

    return pl.pallas_call(
        body,
        grid=(groups,),
        in_specs=[pl.BlockSpec((own_frames, each, d), lambda i: (0, i + start, 0))] * parts
        + [across] + [across] * 4 + [stat, three, one] + [across] * 3 + [stat, one, one]
        + [whole_block(kp), whole_block(vp)]
        + [whole_block(mods), whole_block(masks), whole_block(wide), anywhere(), anywhere()],
        out_specs=[pl.BlockSpec((own_frames, each, d), lambda i: (0, i, 0))] * parts
        + [
            pl.BlockSpec((16 * RANK, d), lambda i: (0, 0)),
            pair_sums,
            pair_sums,
        ],
        out_shape=[like((own_frames, places // halves, d), BF16)] * parts
        + [like((16 * RANK, d), F32)]
        + [like((PAIRS, 2 * PAD, 256), F32)] * 2,
        scratch_shapes=[
            pltpu.VMEM((6, d + PAD, d), BF16),
            pltpu.VMEM((ROWS, ROWS), F32),
        ]
        + [pltpu.VMEM((ROWS, d), BF16)] * 7
        + [pltpu.SemaphoreType.DMA((6,))],
        compiler_params=PARAMS,
        cost_estimate=cost(14 * places // halves * frames * d * d, 30_000_000),
        name="cross_temporal_backward",
    )(*u1, g3, *saved[:15], mods, masks, wide, w_t, w_c)


LATE_BLOCKS = 16
EARLY_BLOCKS = 24


def run_spatial_backward(seq, g1, halves, video, saved, mods, masks, wide, w_s, late_down, late_up, clips):
    frames, rows, d = video.shape
    parts = len(g1) // halves
    by_frame = lambda i: (i, 0, 0)
    row_block = pl.BlockSpec((1, rows, d), by_frame)
    packed = (clips * parts, *packed_rows(LATE_BLOCKS // parts, d // clips))

    def body(*refs):
        spatial_backward(len(g1), halves, clips, *refs)

    return pl.pallas_call(
        body,
        grid=(frames,),
        in_specs=[in_smem()] + [pl.BlockSpec((1, g.shape[1], d), by_frame) for g in g1]
        + [row_block] * 5
        + [
            pl.BlockSpec((1, HEADS, rows), by_frame),
            pl.BlockSpec((1, rows, 3 * RANK), by_frame),
            pl.BlockSpec((1, rows, RANK), by_frame),
            whole_block(mods),
            whole_block(masks),
            whole_block(wide),
            anywhere(),
            whole_block(late_down),
            whole_block(late_up),
        ],
        out_specs=[
            pl.BlockSpec((1, rows, 3 * d + PAD), by_frame),
            pl.BlockSpec(packed, lambda i: (0, 0, 0)),
        ],
        out_shape=[like((frames, rows, 3 * d + PAD), BF16), like(packed, BF16)],
        scratch_shapes=[pltpu.VMEM((d + PAD, d), BF16), pltpu.VMEM((LATE_BLOCKS * RANK, d), F32)]
        + [pltpu.VMEM((ROWS, d), BF16), pltpu.SemaphoreType.DMA((1,))],
        compiler_params=PARAMS,
        cost_estimate=cost(6 * frames * rows * d * d, 30_000_000),
        name="spatial_backward",
    )(seq, *g1, video, *saved, mods, masks, wide, w_s, late_down, late_up)


def run_spatial_input_grad(seq, g1, halves, video, grads, mods, wide, w_s):
    frames, rows, d = video.shape
    by_frame = lambda i: (i, 0, 0)
    row_block = pl.BlockSpec((1, rows, d), by_frame)

    def body(*refs):
        spatial_input_grad(len(g1), halves, *refs)

    return pl.pallas_call(
        body,
        grid=(frames,),
        in_specs=[in_smem()] + [pl.BlockSpec((1, g.shape[1], d), by_frame) for g in g1]
        + [
            row_block,
            pl.BlockSpec((1, rows, grads.shape[2]), by_frame),
            whole_block(mods),
            whole_block(wide),
            anywhere(),
        ],
        out_specs=row_block,
        out_shape=like(video.shape, BF16),
        scratch_shapes=[
            pltpu.VMEM((d, 3 * d + PAD), BF16),
            pltpu.VMEM((ROWS, d), BF16),
            pltpu.SemaphoreType.DMA((3,)),
        ],
        compiler_params=PARAMS,
        cost_estimate=cost(6 * frames * rows * d * d, 20_000_000),
        name="spatial_input_grad",
    )(seq, *g1, video, grads, mods, wide, w_s)


def run_put_in_place(seq, pieces):
    frames, places, d = pieces[0].shape
    by_frame = lambda i: (i, 0, 0)
    rows = places * len(pieces)
    return pl.pallas_call(
        put_in_place,
        grid=(frames,),
        in_specs=[in_smem()] + [pl.BlockSpec((1, places, d), by_frame)] * len(pieces),
        out_specs=pl.BlockSpec((1, rows, d), by_frame),
        out_shape=like((frames, rows, d), BF16),
        compiler_params=PARAMS,
        cost_estimate=cost(0, 4 * frames * rows * d),
        name="put_in_place",
    )(seq, *pieces)


PLAIN = pltpu.CompilerParams(vmem_limit_bytes=VMEM_LIMIT)


def in_vmem():
    return pl.BlockSpec(memory_space=pltpu.VMEM)


def run_pack_early(gw, dk, dv, sources, clips, parts):
    d = gw[0].shape[1]
    packed = (clips * parts, *packed_rows(EARLY_BLOCKS // parts, d // clips))

    def body(*refs):
        pack_early(clips, len(gw), *refs)

    return pl.pallas_call(
        body,
        out_shape=like(packed, BF16),
        scratch_shapes=[pltpu.VMEM((EARLY_BLOCKS * RANK, d), F32), pltpu.VMEM((PAD, d), F32)],
        compiler_params=PLAIN,
        cost_estimate=cost(50000000, 8000000),
        name="pack_early",
    )(*gw, *dk, *dv, *sources)


def run_assemble(early, late, wide_shape, narrow_shape):
    return pl.pallas_call(
        assemble,
        in_specs=[in_vmem()] * 2,
        out_specs=[in_vmem()] * 2,
        out_shape=[like(wide_shape, F32), like(narrow_shape, F32)],
        compiler_params=PLAIN,
        cost_estimate=cost(0, 6000000),
        name="assemble",
    )(early, late)


def run_pick(all_index, wide, narrow):
    count, _, _, cols = wide.shape
    shape = packed_rows(count + 2 * (narrow.shape[3] // cols), cols)
    return pl.pallas_call(
        pick,
        in_specs=[in_smem(), in_vmem(), in_vmem()],
        out_specs=in_vmem(),
        out_shape=like((all_index.shape[0], *shape), BF16),
        compiler_params=PLAIN,
        cost_estimate=cost(0, 3000000),
        name="pick",
    )(all_index, wide, narrow)


def run_unpick(got, blocks, cols):
    def body(*refs):
        unpick(blocks, cols, *refs)

    return pl.pallas_call(
        body,
        in_specs=[in_vmem()],
        out_specs=in_vmem(),
        out_shape=like((blocks, RANK, got.shape[0] * cols), BF16),
        compiler_params=PLAIN,
        cost_estimate=cost(0, 2500000),
        name="unpick",
    )(got)


def run_combine(all_index, got, adapters):
    clips = all_index.shape[0]
    parts = got.shape[0] // clips
    _, share, cols = got.shape
    return pl.pallas_call(
        combine,
        in_specs=[pl.BlockSpec(memory_space=pltpu.SMEM), pl.BlockSpec(memory_space=pltpu.VMEM)],
        out_specs=pl.BlockSpec(memory_space=pltpu.VMEM),
        out_shape=like((parts, adapters, share, cols), BF16),
        scratch_shapes=[pltpu.VMEM((adapters, share, cols), F32)],
        compiler_params=pltpu.CompilerParams(vmem_limit_bytes=VMEM_LIMIT),
        cost_estimate=cost(0, 1000000),
        name="combine",
    )(all_index, got)


def exchange(array, axes="seq"):
    return lax.all_to_all(array, axes, split_axis=0, concat_axis=0, tiled=True)


def up_chunks(up, clips, times):
    rows, hidden = up.shape
    cols = hidden // (clips * times)
    return up.reshape(rows, clips, times, cols).transpose(2, 0, 1, 3).reshape(times, rows, -1)


def gather(array):
    return lax.all_gather(array, "fsdp", axis=1, tiled=True)


def send(array, axis, shift):
    size = lax.axis_size(axis)
    return lax.ppermute(array, axis, [(i, (i + shift) % size) for i in range(size)])


def to_places(pieces):
    return [pieces[0]] + [send(pieces[k], "seq", k) for k in range(1, len(pieces))]


def to_frames(pieces):
    return [pieces[0]] + [send(pieces[k], "seq", -k) for k in range(1, len(pieces))]


def gather_spatial_and_down(spatial, down, parts, times, clips, d):
    quarters = down.reshape(times, -1, d)
    if times != parts or clips % 2:
        return gather(spatial), None
    own = lax.dynamic_slice_in_dim(quarters, lax.axis_index("seq"), 1, 0)
    got = gather(jnp.concatenate([spatial, own], 0))
    half = d // 2
    core = lax.axis_index("fsdp") % 2
    first = lax.dynamic_slice(got, (times, core * half, 0), (1, half, d))[0]
    other = lax.dynamic_slice(got, (times, (1 - core) * half, 0), (1, half, d))[0]
    return got, (first, other, send(first, "seq", 1))


def spread_down(started, down, arrived, parts, times, clips, d):
    half = d // 2
    if started is None:
        whole = gather(down.reshape(times, -1, d))
        return [whole[i, side * half : (side + 1) * half] for side in range(2) for i in range(times)], arrived
    first, other, second = started
    later, second, *arrived = lax.optimization_barrier((first, second, *arrived))
    mine = [first, second] + [send(later, "seq", k) for k in range(2, parts)]
    return mine + [other], arrived


def swap_down(pieces, after, parts, times, clips):
    if len(pieces) == 2 * times:
        return [jnp.arange(times + 1, dtype=jnp.int32) % times, *pieces], after
    *mine, other = pieces
    after, *mine = lax.optimization_barrier((after, *mine))
    swap = [(i, i ^ 1) for i in range(clips)]
    others = [other] + [lax.ppermute(piece, "fsdp", swap) for piece in mine[1:]]
    seq = lax.axis_index("seq")
    core = lax.axis_index("fsdp") % 2
    order = jnp.concatenate([(seq - jnp.arange(parts)) % parts, core[None]]).astype(jnp.int32)
    return [order, *mine, *others], after


def on_device(
    video,
    context,
    modulation,
    adapter_index,
    cotangent,
    qkv_weights,
    out_weights,
    ffn_up,
    ffn_down,
    adapt_wide,
    adapt_ff,
):
    parts = lax.axis_size("seq")
    clips = lax.axis_size("fsdp")
    d = video.shape[-1]
    count, adapters, _, cols = adapt_wide.shape[1:]
    times = adapt_ff.shape[-1] // cols
    places = SPATIAL // parts
    frames = FRAMES // parts
    mods = modulation[0, 0]
    masks = head_masks()
    ctx = jnp.pad(context[0], ((0, PAD - context.shape[1]), (0, 0)))

    def attention_weights(j):
        return jnp.concatenate([qkv_weights[0, 3 * j : 3 * j + 3], out_weights[0, j : j + 1]], 0)

    seq = lax.axis_index("seq").astype(jnp.int32)[None]
    all_index = exchange(jnp.broadcast_to(adapter_index, (clips,)), "fsdp")
    w_s, started = gather_spatial_and_down(
        attention_weights(0), ffn_down[0], parts, times, clips, d
    )
    picked = run_pick(all_index, adapt_wide[0], adapt_ff[0])
    wide = run_unpick(exchange(picked, "fsdp"), count + 2 * times, cols)
    w_t = gather(attention_weights(1))
    w_c = gather(attention_weights(2))
    ffn_up, _ = lax.optimization_barrier((ffn_up, picked))
    up = gather(up_chunks(ffn_up[0], clips, times))
    maps_f = wide[24:]

    cot = cotangent.reshape(frames, SPATIAL, d)
    cot = to_places(
        [
            lax.dynamic_slice_in_dim(cot, (seq[0] + k) % parts * places, places, 1)
            for k in range(parts)
        ]
    )
    frames_in, *cot = lax.optimization_barrier((video.reshape(frames, SPATIAL, d), *cot))
    cot = jnp.concatenate(cot, 0).reshape(FRAMES * places, d)
    made = run_spatial_forward(seq, frames_in, mods, masks, wide, w_s, parts)
    u1, kept_s = to_places(made[:parts]), made[parts:]
    pieces, u1 = spread_down(started, ffn_down[0], u1, parts, times, clips, d)
    *kept_t, x3 = run_temporal_cross_forward(u1, ctx, mods, masks, wide, w_t, w_c)
    down, x3 = swap_down(pieces, x3.reshape(FRAMES * places, d), parts, times, clips)
    grad_active = run_feed_forward_grad(cot, mods, maps_f, down)
    active, g3, grad_a24, grad_b24 = run_feed_forward(x3, cot, grad_active, mods, maps_f, up)
    g3 = g3.reshape(FRAMES, places, d)
    groups = FRAMES * places // ROWS
    halves = 2 if groups % 2 == 0 else 1
    g1, gw, dk, dv = [], [], [], []
    for half in range(halves):
        *pieces, gw_half, dk_half, dv_half = run_cross_temporal_backward(
            g3, u1, kept_t, mods, masks, wide, w_t, w_c, half, halves
        )
        gw.append(gw_half)
        dk.append(dk_half)
        dv.append(dv_half)
        g1.append(to_frames(pieces))

    def as_blocks(rows):
        return rows.reshape(RANK, times, d).transpose(1, 0, 2).reshape(times * RANK, d)

    sources = [grad_a24, as_blocks(grad_b24), kept_t[15], kept_t[16], ctx, masks, wide]
    packed = run_pack_early(gw, dk, dv, sources, clips, parts)
    active, packed, *g1[0] = lax.optimization_barrier((active, packed, *g1[0]))
    *x4, grad_b25, grad_down = run_feed_forward_out(active, x3, cot, mods, maps_f, down, parts)
    early, *x4 = lax.optimization_barrier((exchange(packed, ("fsdp", "seq")), *x4))
    early = run_combine(all_index, early, adapters)
    output = to_frames([piece.reshape(frames, places, d) for piece in x4])
    g1 = [piece for pieces in g1 for piece in pieces]
    early, *g1 = lax.optimization_barrier((early, *g1))
    grads, packed = run_spatial_backward(
        seq, g1, halves, frames_in, kept_s, mods, masks, wide, w_s, grad_b25, as_blocks(grad_down), clips
    )
    early = exchange(early)
    packed, early, *output = lax.optimization_barrier((packed, early, *output))
    g0 = run_spatial_input_grad(seq, g1, halves, frames_in, grads, mods, wide, w_s)
    late = run_combine(all_index, exchange(packed, ("fsdp", "seq")), adapters)
    wide_out, narrow_out = run_assemble(
        early, exchange(late), adapt_wide.shape[1:], adapt_ff.shape[1:]
    )
    output = run_put_in_place(seq, output).reshape(video.shape)
    return (output, g0.reshape(video.shape), wide_out[None], narrow_out[None])


def solution(mesh):
    return jax.shard_map(
        on_device,
        mesh=mesh,
        in_specs=(
            P("fsdp", "seq", None),
            P("fsdp", None, None),
            P("fsdp", None, None, None),
            P("fsdp"),
            P("fsdp", "seq", None),
            P(None, None, "fsdp", None),
            P(None, None, "fsdp", None),
            P(None, "fsdp", None),
            P(None, "fsdp", None),
            P(None, None, None, None, "fsdp"),
            P(None, None, None, None, "fsdp"),
        ),
        out_specs=(
            P("fsdp", "seq", None),
            P("fsdp", "seq", None),
            P(None, None, None, None, "fsdp"),
            P(None, None, None, None, "fsdp"),
        ),
        check_vma=False,
    )
```

```python
import math

import jax
import jax.numpy as jnp
from jax import lax
from jax.experimental import pallas as pl
from jax.experimental.pallas import tpu as pltpu
from jax.sharding import PartitionSpec as P

HEAD_DIM = 72
HEADS = 16
FRAMES = 16
SPATIAL = 256
RANK = 16
ROWS = 256
PAIRS = HEADS // 2
PAD = 128
SCALE = HEAD_DIM ** (-0.5)
EXP_SCALE = SCALE * math.log2(math.e)
LN2 = math.log(2.0)
HIGHEST = lax.Precision.HIGHEST
F32 = jnp.float32
BF16 = jnp.bfloat16
VMEM_LIMIT = 60 * 1024 * 1024


def nn(left, right):
    return lax.dot_general(left, right, (((1,), (0,)), ((), ())), preferred_element_type=F32)


def nt(left, right):
    return lax.dot_general(left, right, (((1,), (1,)), ((), ())), preferred_element_type=F32)


def tn(left, right):
    return lax.dot_general(left, right, (((0,), (0,)), ((), ())), preferred_element_type=F32)


def window(pair):
    return slice(128 * pair, 128 * pair + 256)


def normalize(stream):
    average = jnp.mean(stream, -1, keepdims=True)
    centred = stream - average
    inverse = lax.rsqrt(jnp.mean(centred * centred, -1, keepdims=True) + 1e-06)
    return centred * inverse, inverse


def normalize_back(normal, inverse, grad):
    mean_grad = jnp.mean(grad, -1, keepdims=True)
    mean_both = jnp.mean(grad * normal, -1, keepdims=True)
    return inverse * (grad - mean_grad - normal * mean_both)


def up_rows(ad_ref, number, slot, width):
    rows = ad_ref[2 * number + 1]
    before = jnp.zeros((RANK * slot, width), BF16)
    after = jnp.zeros((PAD - RANK * (slot + 1), width), BF16)
    return jnp.concatenate(([before] if slot else []) + [rows, after], 0)


def three_downs(ad_ref, number):
    return jnp.concatenate([ad_ref[2 * (number + i)] for i in range(3)], 0)


class Loads:
    def __init__(self, entries, sems):
        self.first = pl.program_id(0) == 0
        self.entries = entries
        self.sems = sems

    def copy(self, index):
        source, target = self.entries[index]
        return pltpu.make_async_copy(source, target, self.sems.at[index])

    def start(self):
        @pl.when(self.first)
        def _():
            for index in range(len(self.entries)):
                self.copy(index).start()

    def ready(self, index):
        @pl.when(self.first)
        def _():
            self.copy(index).wait()


def head_masks():
    lane = jnp.arange(256)[None, :]
    begin = jnp.array([16 * (h // 2) + HEAD_DIM * (h % 2) for h in range(HEADS)])[:, None]
    return ((lane >= begin) & (lane < begin + HEAD_DIM)).astype(BF16)


def same_place(shape):
    rows = lax.broadcasted_iota(jnp.int32, shape, 0)
    cols = lax.broadcasted_iota(jnp.int32, shape, 1)
    return jnp.where(rows % 16 == cols % 16, 0.0, -1e30).astype(F32)


def attend(q_ref, k_ref, v_ref, mask_ref, bias, put_out, stat_ref):
    carried = None
    for pair in range(PAIRS):
        win = window(pair)
        q_win, k_win, v_win = q_ref[:, win], k_ref[:, win], v_ref[:, win]
        all_weights, all_values = [], []
        for head in (2 * pair, 2 * pair + 1):
            mask = mask_ref[head : head + 1, :]
            scores = nt(k_win * mask, q_win)
            if bias is not None:
                scores = scores + bias[...]
            top = jnp.max(scores, 0, keepdims=True)
            grown = jnp.exp2(scores - top)
            total = jnp.sum(grown, 0, keepdims=True)
            stat_ref[head : head + 1, :] = top + jnp.log2(total)
            all_weights.append((grown * (1.0 / total)).astype(BF16))
            all_values.append(v_win * mask)
        out = tn(jnp.concatenate(all_weights, 0), jnp.concatenate(all_values, 0))
        low = out[:, :128]
        put_out(pair, low if carried is None else low + carried)
        carried = out[:, 128:]
    put_out(PAIRS, carried)


def attend_back(q_ref, k_ref, v_ref, do_ref, mask_ref, bias, stat_ref, put):
    carried = None
    for pair in range(PAIRS):
        win = window(pair)
        q_win, k_win, v_win, do_win = q_ref[:, win], k_ref[:, win], v_ref[:, win], do_ref[:, win]
        all_grads, all_probs, keys, queries, outs = [], [], [], [], []
        for head in (2 * pair, 2 * pair + 1):
            mask = mask_ref[head : head + 1, :]
            k_own = k_win * mask
            scores = nt(k_own, q_win)
            if bias is not None:
                scores = scores + bias[...]
            probs = jnp.exp2(scores - stat_ref[head : head + 1, :])
            grad_probs = nt(v_win * mask, do_win)
            inner = jnp.sum(probs * grad_probs, 0, keepdims=True)
            all_grads.append((probs * (grad_probs - inner)).astype(BF16))
            all_probs.append(probs.astype(BF16))
            keys.append(k_own)
            queries.append(q_win * mask)
            outs.append(do_win * mask)
        grads = (
            tn(jnp.concatenate(all_grads, 0), jnp.concatenate(keys, 0)),
            nn(jnp.concatenate(all_grads, 1), jnp.concatenate(queries, 0)),
            nn(jnp.concatenate(all_probs, 1), jnp.concatenate(outs, 0)),
        )
        lows = tuple(g[:, :128] for g in grads)
        if carried is not None:
            lows = tuple(a + b for a, b in zip(lows, carried))
        put(pair, lows)
        carried = tuple(g[:, 128:] for g in grads)
    put(PAIRS, carried)


def tile(index):
    return slice(128 * index, 128 * index + 128)


def three_projections(lhs_ref, ad_ref, number, weights, loads, first_load, outs, rank_ref):
    width = weights.shape[2]
    ranks = nt(lhs_ref[:, :width], three_downs(ad_ref, number)).astype(BF16)
    rank_ref[...] = ranks
    lhs_ref[:, width : width + 3 * RANK] = ranks
    for i in range(3):
        loads.ready(first_load + i)
        total = nn(lhs_ref[...], weights[first_load + i])
        outs[i][...] = (total * EXP_SCALE if i == 0 else total).astype(BF16)


def one_projection(lhs_ref, ad_ref, number, weight_ref, rank_ref):
    width = weight_ref.shape[1]
    ranks = nt(lhs_ref[:, :width], ad_ref[2 * number]).astype(BF16)
    rank_ref[...] = ranks
    lhs_ref[:, width : width + RANK] = ranks
    return nn(lhs_ref[...], weight_ref[...])


def block_rows(index):
    return slice(RANK * index, RANK * (index + 1))


def one_back(grad, kept, ranks, ad_ref, number, weight_ref, grad_ref, at):
    width = weight_ref.shape[1]
    both = nt(grad, weight_ref[...])
    grad_rank = both[:, width : width + RANK].astype(BF16)
    grad_ref[block_rows(at), :] += tn(grad_rank, kept)
    grad_ref[block_rows(at + 1), :] += tn(ranks, grad)
    return both[:, :width] + nn(grad_rank, ad_ref[2 * number])


def three_back(grads, inputs, ranks, ad_ref, number, weights, loads, first_load, grad_ref, at):
    width = weights.shape[2]
    both = None
    for i in range(3):
        grad = grads[i][...]
        ups = tn(ranks, grad)
        grad_ref[block_rows(at + 2 * i + 1), :] += ups[block_rows(i)]
        loads.ready(first_load + i)
        part = nt(grad, weights[first_load + i])
        both = part if both is None else both + part
    grad_ranks = both[:, width : width + 3 * RANK].astype(BF16)
    downs = tn(grad_ranks, inputs)
    for i in range(3):
        grad_ref[block_rows(at + 2 * i), :] += downs[block_rows(i)]
    return both[:, :width] + nn(grad_ranks, three_downs(ad_ref, number))


def place_of(seq_ref, k, parts, places):
    return pl.multiple_of(lax.rem(seq_ref[0] + k, parts) * places, 16)


def spatial_forward(seq_ref, x_ref, mod_ref, mask_ref, ad_ref, w_hbm, *refs):
    x1_refs = refs[:-11]
    q_ref, k_ref, v_ref, o_ref, stat_ref, rq_ref, ro_ref, w_ref, lhs_ref, x1_s, sems = refs[-11:]
    width = x_ref.shape[2]
    loads = Loads([(w_hbm.at[i], w_ref.at[i, pl.ds(0, width), :]) for i in range(4)], sems)
    loads.start()

    @pl.when(loads.first)
    def _():
        lhs_ref[:, width:] = jnp.zeros((ROWS, PAD), BF16)
        for i in range(4):
            w_ref[i, width:, :] = up_rows(ad_ref, i, i % 3, width)

    stream = x_ref[0].astype(F32)
    normal, _ = normalize(stream)
    lhs_ref[:, :width] = (normal * (1.0 + mod_ref[1:2, :]) + mod_ref[0:1, :]).astype(BF16)
    q, k, v = q_ref.at[0], k_ref.at[0], v_ref.at[0]
    three_projections(lhs_ref, ad_ref, 0, w_ref, loads, 0, (q, k, v), rq_ref.at[0])

    def put_out(index, value):
        value = value.astype(BF16)
        o_ref[0, :, tile(index)] = value
        lhs_ref[:, tile(index)] = value

    attend(q, k, v, mask_ref, None, put_out, stat_ref.at[0])
    loads.ready(3)
    branch = one_projection(lhs_ref, ad_ref, 3, w_ref.at[3], ro_ref.at[0])
    x1_s[...] = (stream + mod_ref[2:3, :] * branch).astype(BF16)
    places = x1_refs[0].shape[1]
    for k, ref in enumerate(x1_refs):
        ref[0] = x1_s[pl.ds(place_of(seq_ref, k, len(x1_refs), places), places), :]


def rows_of(refs):
    pieces = [ref[...].reshape(-1, ref.shape[2]) for ref in refs]
    return pieces[0] if len(pieces) == 1 else jnp.concatenate(pieces, 0)


def temporal_forward(parts, *refs):
    x_refs, refs = refs[:parts], refs[parts:]
    (
        mod_ref, mask_ref, ad_ref, w_hbm,
        q_ref, k_ref, v_ref, o_ref, stat_ref, rq_ref, ro_ref, u2_ref, x2_ref,
        w_ref, bias_ref, lhs_ref, q_s, k_s, v_s, sems,
    ) = refs
    width = x_refs[0].shape[2]
    loads = Loads([(w_hbm.at[i], w_ref.at[i, pl.ds(0, width), :]) for i in range(4)], sems)
    loads.start()

    @pl.when(loads.first)
    def _():
        bias_ref[...] = same_place(bias_ref.shape)
        lhs_ref[:, width:] = jnp.zeros((ROWS, PAD), BF16)
        for i in range(4):
            w_ref[i, width:, :] = up_rows(ad_ref, 4 + i, i % 3, width)

    loaded = rows_of(x_refs)
    lhs_ref[:, :width] = loaded
    three_projections(lhs_ref, ad_ref, 4, w_ref, loads, 0, (q_s, k_s, v_s), rq_ref.at[0])
    q_ref[...] = q_s[...].reshape(q_ref.shape)
    k_ref[...] = k_s[...].reshape(k_ref.shape)
    v_ref[...] = v_s[...].reshape(v_ref.shape)

    def put_out(index, value):
        lhs_ref[:, tile(index)] = value.astype(BF16)

    attend(q_s, k_s, v_s, mask_ref, bias_ref, put_out, stat_ref.at[0])
    o_ref[...] = lhs_ref[:, :width].reshape(o_ref.shape)
    loads.ready(3)
    branch = one_projection(lhs_ref, ad_ref, 7, w_ref.at[3], ro_ref.at[0])
    stream = loaded.astype(F32) + mod_ref[2:3, :] * branch
    u2_ref[...] = stream.astype(BF16).reshape(u2_ref.shape)
    x2_ref[...] = stream.reshape(x2_ref.shape)


def cross_forward(
    x_ref, ctx_ref, mask_ref, ad_ref, w_hbm,
    q_ref, o_ref, stat_ref, rq_ref, ro_ref, kp_ref, vp_ref, rk_ref, rv_ref, x3_ref,
    w_ref, lhs_ref, q_s, k_s, sems,
):
    width = x_ref.shape[2]
    loads = Loads([(w_hbm.at[i], w_ref.at[i, pl.ds(0, width), :]) for i in range(4)], sems)
    loads.start()

    @pl.when(loads.first)
    def _():
        lhs_ref[:, width:] = jnp.zeros((ROWS, PAD), BF16)
        for i in (0, 3):
            w_ref[i, width:, :] = up_rows(ad_ref, 8 + i, 0, width)

    stream = x_ref[...].reshape(ROWS, width)
    lhs_ref[:, :width] = stream.astype(BF16)
    loads.ready(0)
    queries = one_projection(lhs_ref, ad_ref, 8, w_ref.at[0], rq_ref.at[0])
    q_s[...] = (queries * EXP_SCALE).astype(BF16)
    q_ref[...] = q_s[...].reshape(q_ref.shape)
    loads.ready(1)
    loads.ready(2)

    @pl.when(loads.first)
    def _():
        for number, at, rank_ref, pair_ref in ((9, 1, rk_ref, kp_ref), (10, 2, rv_ref, vp_ref)):
            ranks = nt(ctx_ref[...], ad_ref[2 * number]).astype(BF16)
            rank_ref[...] = ranks
            made = nn(ctx_ref[...], w_ref[at, :width, :]) + nn(ranks, ad_ref[2 * number + 1])
            k_s[...] = made.astype(BF16)
            for pair in range(PAIRS):
                piece = k_s[:, window(pair)]
                pair_ref[pair, :PAD, :] = piece * mask_ref[2 * pair : 2 * pair + 1, :]
                pair_ref[pair, PAD:, :] = piece * mask_ref[2 * pair + 1 : 2 * pair + 2, :]

    carried = None
    count = 120
    for pair in range(PAIRS):
        scores = nt(kp_ref[pair], q_s[:, window(pair)])
        pieces = []
        for sub in range(2):
            own = scores[PAD * sub : PAD * sub + count]
            top = jnp.max(own, 0, keepdims=True)
            grown = jnp.exp2(own - top)
            total = jnp.sum(grown, 0, keepdims=True)
            stat_ref[0, 2 * pair + sub : 2 * pair + sub + 1, :] = top + jnp.log2(total)
            pieces += [grown * (1.0 / total), jnp.zeros((PAD - count, ROWS), F32)]
        weights = jnp.concatenate(pieces, 0).astype(BF16)
        out = tn(weights, vp_ref[pair])
        low = out[:, :128]
        lhs_ref[:, tile(pair)] = (low if carried is None else low + carried).astype(BF16)
        carried = out[:, 128:]
    lhs_ref[:, tile(PAIRS)] = carried.astype(BF16)
    o_ref[...] = lhs_ref[:, :width].reshape(o_ref.shape)
    loads.ready(3)
    stream = stream + one_projection(lhs_ref, ad_ref, 11, w_ref.at[3], ro_ref.at[0])
    x3_ref[...] = stream.reshape(x3_ref.shape)


def gelu_both(hidden):
    root = math.sqrt(2.0 / math.pi)
    square = hidden * hidden
    inner = root * (hidden + 0.044715 * (square * hidden))
    bent = jnp.tanh(inner)
    half = 0.5 * (1.0 + bent)
    slope = half + 0.5 * hidden * (1.0 - bent * bent) * (root * (1.0 + 3.0 * 0.044715 * square))
    return hidden * half, slope


def transposed_map(rows):
    nothing = jnp.zeros((PAD - rows.shape[0], rows.shape[1]), F32)
    wide = jnp.concatenate([rows.astype(F32), nothing], 0)
    return wide.T.astype(BF16)


def down_loads(order_ref, pieces, down_ref, width):
    half = width // 2
    count = len(pieces) // 2
    core = order_ref[count]
    entries = []
    for k in range(count):
        for source, side in ((pieces[k], core), (pieces[count + k], 1 - core)):
            start = pl.multiple_of(order_ref[k] * width + side * half, 16)
            entries.append((source, down_ref.at[pl.ds(start, half), pl.ds(0, width)]))
    return entries


def fill_down_maps(ad_ref, down_ref, width):
    chunks = down_ref.shape[0] // width
    for c in range(chunks):
        rows = slice(c * width, (c + 1) * width)
        down_ref[rows, width:] = transposed_map(ad_ref[2 + chunks + c])


def feed_forward_grad(count, order_ref, cot_ref, mod_ref, ad_ref, *refs):
    pieces = refs[:count]
    grad_ref, down_ref, lhs_ref, sems = refs[count:]
    width = cot_ref.shape[1]
    half = width // 2
    chunks = count // 2
    core = order_ref[chunks]
    entries = []
    for k in range(chunks):
        for source, side in ((pieces[k], core), (pieces[chunks + k], 1 - core)):
            start = pl.multiple_of(k * width + side * half, 16)
            entries.append((source, down_ref.at[pl.ds(start, half), pl.ds(0, width)]))
    loads = Loads(entries, sems)
    loads.start()

    @pl.when(loads.first)
    def _():
        lhs_ref[:, width:] = jnp.zeros((ROWS, PAD), BF16)
        for k in range(chunks):
            rows = slice(k * width, (k + 1) * width)
            down_ref[rows, width:] = transposed_map(ad_ref[2 + (ad_ref.shape[0] - 2) // 2 + order_ref[k]])

    branch = (mod_ref[5:6, :] * cot_ref[...].astype(F32)).astype(BF16)
    lhs_ref[:, :width] = branch
    lhs_ref[:, width : width + RANK] = nt(branch, ad_ref[1]).astype(BF16)
    for i in range(len(entries)):
        loads.ready(i)
    for k in range(chunks):
        rows = slice(k * width, (k + 1) * width)
        grad_ref[k] = nt(lhs_ref[...], down_ref[rows, :]).astype(BF16)


def hidden_chunks(hidden):
    return [slice(at, at + 1536) for at in range(0, hidden, 1536)]


def feed_forward(groups, count, order_ref, x3_ref, cot_ref, *refs):
    grad_refs, pieces, refs = refs[:groups], refs[groups : groups + count], refs[groups + count :]
    (
        mod_ref, ad_ref, w_hbm, act_ref, g3_ref, gd_ref, gu_ref, up_ref, lhs_ref, dh_ref, sems, *rest
    ) = refs
    width = x3_ref.shape[1]
    hidden_size = up_ref.shape[1]
    chunks = hidden_size // width
    late = count // 2
    core = order_ref[chunks]
    entries = [
        (w_hbm.at[c], up_ref.at[pl.ds(0, width), pl.ds(c * width, width)]) for c in range(chunks)
    ]
    if late:
        down_ref, dlhs_ref = rest
        half = width // 2
        for k in range(late):
            for source, side in ((pieces[k], core), (pieces[late + k], 1 - core)):
                start = pl.multiple_of(k * width + side * half, 16)
                entries.append((source, down_ref.at[pl.ds(start, half), pl.ds(0, width)]))
    loads = Loads(entries, sems)
    loads.start()

    @pl.when(loads.first)
    def _():
        gd_ref[...] = jnp.zeros_like(gd_ref)
        gu_ref[...] = jnp.zeros_like(gu_ref)
        lhs_ref[:, width:] = jnp.zeros((ROWS, PAD), BF16)
        up_ref[width + RANK :, :] = jnp.zeros((PAD - RANK, hidden_size), BF16)
        for c in range(chunks):
            up_ref[width : width + RANK, c * width : (c + 1) * width] = ad_ref[2 + c]
        for k in range(late):
            rows = slice(k * width, (k + 1) * width)
            at = order_ref[chunks - late + k]
            down_ref[rows, width:] = transposed_map(ad_ref[2 + chunks + at])
        if late:
            dlhs_ref[:, width:] = jnp.zeros((ROWS, PAD), BF16)

    normal, inverse = normalize(x3_ref[...])
    inputs = (normal * (1.0 + mod_ref[4:5, :]) + mod_ref[3:4, :]).astype(BF16)
    rank_up = nt(inputs, ad_ref[0]).astype(BF16)
    lhs_ref[:, :width] = inputs
    lhs_ref[:, width : width + RANK] = rank_up
    at = 0
    for grad_ref in grad_refs:
        for k in range(grad_ref.shape[0]):
            start = pl.multiple_of(order_ref[at] * width, 128)
            dh_ref[:, pl.ds(start, width)] = grad_ref[k]
            at += 1
    if late:
        branch = (mod_ref[5:6, :] * cot_ref[...].astype(F32)).astype(BF16)
        dlhs_ref[:, :width] = branch
        dlhs_ref[:, width : width + RANK] = nt(branch, ad_ref[1]).astype(BF16)
    for i in range(len(entries)):
        loads.ready(i)
    for k in range(late):
        start = pl.multiple_of(order_ref[at + k] * width, 128)
        rows = slice(k * width, (k + 1) * width)
        dh_ref[:, pl.ds(start, width)] = nt(dlhs_ref[...], down_ref[rows, :]).astype(BF16)
    for cols in hidden_chunks(hidden_size):
        active, slope = gelu_both(nn(lhs_ref[...], up_ref[:, cols]))
        act_ref[:, cols] = active.astype(BF16)
        dh_ref[:, cols] = (slope * dh_ref[:, cols].astype(F32)).astype(BF16)
    both = nt(dh_ref[...], up_ref[...])
    gu_ref[...] += tn(rank_up, dh_ref[...])
    grad_rank = both[:, width : width + RANK].astype(BF16)
    grad_in = both[:, :width] + nn(grad_rank, ad_ref[0])
    gd_ref[...] += tn(grad_rank, lhs_ref[:, :width])
    grad_in = normalize_back(normal, inverse, grad_in * (1.0 + mod_ref[4:5, :]))
    g3_ref[...] = cot_ref[...].astype(F32) + grad_in


def feed_forward_out(count, order_ref, act_ref, x3_ref, cot_ref, mod_ref, ad_ref, *refs):
    pieces, refs = refs[:count], refs[count:]
    x4_refs = refs[:-4]
    gu_ref, gd_ref, down_ref, sems = refs[-4:]
    width = x3_ref.shape[1]
    step = pl.program_id(0)
    entries = down_loads(order_ref, pieces, down_ref, width)
    loads = Loads(entries, sems)
    loads.start()

    @pl.when(loads.first)
    def _():
        gu_ref[...] = jnp.zeros_like(gu_ref)
        gd_ref[...] = jnp.zeros_like(gd_ref)
        fill_down_maps(ad_ref, down_ref, width)

    share = x4_refs[0].shape[0]
    grad_branch = (mod_ref[5:6, :] * cot_ref[...].astype(F32)).astype(BF16)
    gd_ref[...] += tn(nt(grad_branch, ad_ref[1]).astype(BF16), act_ref[...])
    for i in range(len(entries)):
        loads.ready(i)
    both = nn(act_ref[...], down_ref[...])
    ranks = both[:, width : width + RANK].astype(BF16)
    branch = both[:, :width] + nn(ranks, ad_ref[1])
    gu_ref[...] += tn(ranks, grad_branch)
    result = (x3_ref[...] + mod_ref[5:6, :] * branch).astype(BF16)
    for k, ref in enumerate(x4_refs):
        at = k * share

        @pl.when(step == at // ROWS)
        def _():
            ref[...] = result[at % ROWS : at % ROWS + share]


def cross_temporal_backward(parts, *refs):
    outs = len(refs) - parts - 13
    _cross_temporal_backward(refs[:parts], refs[outs : outs + parts], *refs[parts:outs], *refs[outs + parts :])


def _cross_temporal_backward(
    u1_refs, g1_refs, g3_ref, q_ref, k_ref, v_ref, o_ref, stat_ref, rq_ref, ro_ref,
    u2_ref, qc_ref, oc_ref, statc_ref, rqc_ref, roc_ref, kp_ref, vp_ref,
    mod_ref, mask_ref, ad_ref, wt_hbm, wc_hbm,
    gw_ref, dk_acc, dv_acc, w_ref, bias_ref, q_s, k_s, v_s, do_s, dq_s, dk_s, dv_s, sems,
):
    width = u1_refs[0].shape[2]
    first = pl.program_id(0) == 0
    order = (7, 4, 3, 0, 1, 2)
    sources = [wc_hbm.at[n - 4] if n >= 4 else wt_hbm.at[n] for n in order]
    loads = Loads([(w, w_ref.at[i, pl.ds(0, width), :]) for i, w in enumerate(sources)], sems)
    loads.start()

    @pl.when(first)
    def _():
        bias_ref[...] = same_place(bias_ref.shape)
        gw_ref[...] = jnp.zeros_like(gw_ref)
        dk_acc[...] = jnp.zeros_like(dk_acc)
        dv_acc[...] = jnp.zeros_like(dv_acc)
        for i, n in enumerate(order):
            w_ref[i, width:, :] = up_rows(ad_ref, 4 + n, n if n < 3 else 0, width)

    def rows(ref):
        return ref[...].reshape(ROWS, ref.shape[2])

    grad = rows(g3_ref)
    loads.ready(0)
    do_s[...] = one_back(
        grad.astype(BF16), rows(oc_ref), roc_ref[0], ad_ref, 11, w_ref.at[0], gw_ref, 14
    ).astype(BF16)
    q_s[...] = rows(qc_ref)
    count = 120
    carried = None
    for pair in range(PAIRS):
        win = window(pair)
        q_win, do_win = q_s[:, win], do_s[:, win]
        scores = nt(kp_ref[pair], q_win)
        grad_probs = nt(vp_ref[pair], do_win)
        all_probs, all_grads = [], []
        nothing = jnp.zeros((PAD - count, ROWS), F32)
        for sub in range(2):
            span = slice(PAD * sub, PAD * sub + count)
            row = 2 * pair + sub
            probs = jnp.exp2(scores[span] - statc_ref[0, row : row + 1, :])
            own = grad_probs[span]
            inner = jnp.sum(probs * own, 0, keepdims=True)
            all_probs += [probs, nothing]
            all_grads += [probs * (own - inner), nothing]
        probs = jnp.concatenate(all_probs, 0).astype(BF16)
        grad_scores = jnp.concatenate(all_grads, 0).astype(BF16)
        dk_acc[pair] += nn(grad_scores, q_win)
        dv_acc[pair] += nn(probs, do_win)
        out = tn(grad_scores, kp_ref[pair])
        low = out[:, :128]
        dq_s[:, tile(pair)] = ((low if carried is None else low + carried) * SCALE).astype(BF16)
        carried = out[:, 128:]
    dq_s[:, tile(PAIRS)] = (carried * SCALE).astype(BF16)
    loads.ready(1)
    grad = grad + one_back(
        dq_s[...], rows(u2_ref), rqc_ref[0], ad_ref, 8, w_ref.at[1], gw_ref, 8
    )
    loads.ready(2)
    do_s[...] = one_back(
        (mod_ref[2:3, :] * grad).astype(BF16), rows(o_ref), ro_ref[0], ad_ref, 7, w_ref.at[2], gw_ref, 6
    ).astype(BF16)
    q_s[...] = rows(q_ref)
    k_s[...] = rows(k_ref)
    v_s[...] = rows(v_ref)

    def put(index, values):
        dq_s[:, tile(index)] = (values[0] * SCALE).astype(BF16)
        dk_s[:, tile(index)] = (values[1] * LN2).astype(BF16)
        dv_s[:, tile(index)] = values[2].astype(BF16)

    attend_back(q_s, k_s, v_s, do_s, mask_ref, bias_ref, stat_ref.at[0], put)
    grad = grad + three_back(
        (dq_s, dk_s, dv_s), rows_of(u1_refs), rq_ref[0], ad_ref, 4, w_ref, loads, 3, gw_ref, 0
    )
    grad = grad.astype(BF16)
    share = ROWS // len(g1_refs)
    for k, ref in enumerate(g1_refs):
        ref[...] = grad[share * k : share * (k + 1)].reshape(ref.shape)


def tail_groups(cols):
    tail = cols - PAD
    return PAD // tail if 0 < tail < PAD and PAD % tail == 0 else 0


def packed_rows(blocks, cols):
    group = tail_groups(cols)
    if not group:
        return blocks * RANK, cols
    return (blocks + -(-blocks // group)) * RANK, PAD


def put_blocks(blocks, put):
    cols = blocks[0].shape[1]
    group = tail_groups(cols)
    for k, rows in enumerate(blocks):
        put(k, rows[:, :PAD] if group else rows)
    for k in range(0, len(blocks), group) if group else ():
        tails = [rows[:, PAD:] for rows in blocks[k : k + group]]
        missing = group - len(tails)
        if missing:
            tails.append(jnp.zeros((RANK, missing * (cols - PAD)), blocks[0].dtype))
        put(len(blocks) + k // group, jnp.concatenate(tails, 1))


def get_block(get, index, count, cols):
    group = tail_groups(cols)
    if not group:
        return get(index)
    at = (index % group) * (cols - PAD)
    return jnp.concatenate([get(index), get(count + index // group)[:, at : at + cols - PAD]], 1)


def pack_columns(table_ref, packed_ref, clips):
    parts = packed_ref.shape[0] // clips
    share = table_ref.shape[0] // parts
    cols = table_ref.shape[1] // clips
    for f in range(clips):
        for s in range(parts):
            piece = table_ref[share * s : share * (s + 1), cols * f : cols * (f + 1)].astype(BF16)
            blocks = [piece[block_rows(k)] for k in range(share // RANK)]

            def put(k, rows):
                packed_ref[f * parts + s, block_rows(k), :] = rows

            put_blocks(blocks, put)


def stacked(seq_ref, g1_refs, shares, whole_ref):
    parts = len(g1_refs) // shares
    places = whole_ref.shape[0] // parts
    at = 0
    for share in range(shares):
        refs = g1_refs[share * parts : (share + 1) * parts]
        size = refs[0].shape[1]
        for k, ref in enumerate(refs):
            start = pl.multiple_of(place_of(seq_ref, k, parts, places) + at, 16)
            whole_ref[pl.ds(start, size), :] = ref[0]
        at += size
    return whole_ref[...].astype(F32)


def spatial_backward(pieces, halves, clips, continued, last, seq_ref, *refs):
    g1_refs, refs = refs[:pieces], refs[pieces:]
    if continued:
        (_, before_ref), refs = refs[:2], refs[2:]
    (
        x_ref, q_ref, k_ref, v_ref, o_ref, stat_ref, rq_ref, ro_ref, mod_ref, mask_ref, ad_ref, w_hbm,
        d_ref, sums_ref, w_ref, gw_ref, do_s, sems,
    ) = refs
    width = x_ref.shape[2]
    loads = Loads([(w_hbm.at[3], w_ref.at[pl.ds(0, width), :])], sems)
    loads.start()

    @pl.when(loads.first)
    def _():
        gw_ref[...] = before_ref[...] if continued else jnp.zeros_like(gw_ref)
        w_ref[width:, :] = up_rows(ad_ref, 3, 0, width)

    grad = stacked(seq_ref, g1_refs, halves, do_s)
    loads.ready(0)
    do_s[...] = one_back(
        (mod_ref[2:3, :] * grad).astype(BF16), o_ref[0], ro_ref[0], ad_ref, 3, w_ref, gw_ref, 6
    ).astype(BF16)

    def put(index, values):
        for i, factor in enumerate((SCALE, LN2, 1.0)):
            value = values[i] if factor == 1.0 else values[i] * factor
            d_ref[0, :, width * i + 128 * index : width * i + 128 * index + 128] = value.astype(BF16)

    attend_back(
        q_ref.at[0], k_ref.at[0], v_ref.at[0], do_s, mask_ref, None, stat_ref.at[0], put
    )
    ranks = rq_ref[0]
    grad_ranks = None
    for i in range(3):
        grad = d_ref[0, :, width * i : width * (i + 1)]
        gw_ref[block_rows(2 * i + 1), :] += tn(ranks, grad)[block_rows(i)]
        part = nt(grad, up_rows(ad_ref, i, i, width))
        grad_ranks = part if grad_ranks is None else grad_ranks + part
    d_ref[0, :, 3 * width :] = grad_ranks.astype(BF16)
    normal, _ = normalize(x_ref[0].astype(F32))
    inputs = (normal * (1.0 + mod_ref[1:2, :]) + mod_ref[0:1, :]).astype(BF16)
    downs = tn(d_ref[0, :, 3 * width :], inputs)
    for i in range(3):
        gw_ref[block_rows(2 * i), :] += downs[block_rows(i)]

    @pl.when(pl.program_id(0) == pl.num_programs(0) - 1)
    def _():
        if last:
            pack_columns(gw_ref, sums_ref, clips)
        else:
            sums_ref[...] = gw_ref[...]


def spatial_input_grad(pieces, halves, seq_ref, *refs):
    g1_refs, refs = refs[:pieces], refs[pieces:]
    x_ref, d_ref, mod_ref, ad_ref, w_hbm, g0_ref, w_ref, whole_s, sems = refs
    width = x_ref.shape[2]
    loads = Loads(
        [(w_hbm.at[i], w_ref.at[:, pl.ds(i * width, width)]) for i in range(3)], sems
    )
    loads.start()

    @pl.when(loads.first)
    def _():
        w_ref[:, 3 * width :] = transposed_map(three_downs(ad_ref, 0))

    normal, inverse = normalize(x_ref[0].astype(F32))
    grad = stacked(seq_ref, g1_refs, halves, whole_s)
    for i in range(3):
        loads.ready(i)
    grad_in = nt(d_ref[0], w_ref[...])
    grad = grad + normalize_back(normal, inverse, grad_in * (1.0 + mod_ref[1:2, :]))
    g0_ref[0] = grad.astype(BF16)


def put_in_place(seq_ref, *refs):
    *pieces, out_ref = refs
    places = pieces[0].shape[1]
    for k, ref in enumerate(pieces):
        out_ref[0, pl.ds(place_of(seq_ref, k, len(pieces), places), places), :] = ref[0]


def pack_early(clips, shares, *refs):
    gw_refs, refs = refs[:shares], refs[shares:]
    dk_refs, refs = refs[:shares], refs[shares:]
    dv_refs, refs = refs[:shares], refs[shares:]
    *others, rk_ref, rv_ref, ctx_ref, mask_ref, ad_ref, packed_ref, table_ref, ctx_s = refs

    def added(each):
        total = each[0]
        for value in each[1:]:
            total = total + value
        return total

    at = gw_refs[0].shape[0]
    table_ref[:at, :] = added([ref[...] for ref in gw_refs])
    width = table_ref.shape[1]
    for ref in others:
        for k in range(ref.shape[1] // width):
            table_ref[at : at + RANK, :] = ref[:, k * width : (k + 1) * width]
            at += RANK
    table_ref[at:, :] = jnp.zeros((table_ref.shape[0] - at, width), F32)
    context = ctx_ref[...].astype(F32)
    for accs, factor, rank_ref, number, at in (
        (dk_refs, LN2, rk_ref, 9, 10),
        (dv_refs, 1.0, rv_ref, 10, 12),
    ):
        held = None
        for pair in range(PAIRS):
            whole = added([ref[pair] for ref in accs]) * factor
            out = whole[:PAD] * mask_ref[2 * pair : 2 * pair + 1, :].astype(F32)
            out = out + whole[PAD:] * mask_ref[2 * pair + 1 : 2 * pair + 2, :].astype(F32)
            low = out[:, :128]
            ctx_s[:, tile(pair)] = low if held is None else low + held
            held = out[:, 128:]
        ctx_s[:, tile(PAIRS)] = held
        grad_kv = ctx_s[...]
        grad_rank = lax.dot_general(
            grad_kv, ad_ref[2 * number + 1].astype(F32), (((1,), (1,)), ((), ())),
            precision=HIGHEST, preferred_element_type=F32,
        )
        table_ref[block_rows(at), :] = lax.dot_general(
            grad_rank, context, (((0,), (0,)), ((), ())),
            precision=HIGHEST, preferred_element_type=F32,
        )
        table_ref[block_rows(at + 1), :] = lax.dot_general(
            rank_ref[...].astype(F32), grad_kv, (((0,), (0,)), ((), ())),
            precision=HIGHEST, preferred_element_type=F32,
        )
    pack_columns(table_ref, packed_ref, clips)


def assemble(parts, seq_ref, *refs):
    early_refs, late_refs, refs = refs[:parts], refs[parts : 2 * parts], refs[2 * parts :]
    wide_ref, narrow_ref, early_ref, late_ref = refs
    for k in range(parts):
        source = lax.rem(seq_ref[0] + parts - k, parts)
        early_ref[source] = early_refs[k][...]
        late_ref[source] = late_refs[k][...]
    _, adapters, _, cols = wide_ref.shape
    times = narrow_ref.shape[3] // cols

    def block(ref, total, index, a):
        each = total // ref.shape[0]

        def get(k):
            return ref[index // each, a, block_rows(k), :].astype(F32)

        return get_block(get, index % each, each, cols)

    for a in range(adapters):
        for i in range(8):
            wide_ref[i, a] = block(late_ref, LATE_BLOCKS, i, a)
        for i in range(18):
            wide_ref[8 + i, a] = block(early_ref, EARLY_BLOCKS, i, a)
        for n in range(2):
            pieces = [block(early_ref, EARLY_BLOCKS, 18 + n * times + j, a) for j in range(times)]
            narrow_ref[n, a] = jnp.concatenate(pieces, 1)


def combine(index_ref, got_ref, out_ref, acc_ref):
    clips = index_ref.shape[0]
    parts = got_ref.shape[0] // clips
    acc_ref[...] = jnp.zeros_like(acc_ref)

    def step(f, carry):
        total = got_ref[f * parts].astype(F32)
        for s in range(1, parts):
            total = total + got_ref[f * parts + s].astype(F32)
        acc_ref[index_ref[f]] += total
        return carry

    lax.fori_loop(0, clips, step, 0)
    out_ref[...] = acc_ref[...].astype(BF16)


def pick(index_ref, wide_ref, narrow_ref, out_ref):
    count, _, _, cols = wide_ref.shape
    times = narrow_ref.shape[3] // cols

    def step(f, carry):
        a = index_ref[f]
        blocks = [wide_ref[k, a] for k in range(count)]
        for p in range(2):
            rows = narrow_ref[p, a]
            blocks += [rows[:, cols * j : cols * (j + 1)] for j in range(times)]

        def put(k, rows):
            out_ref[f, block_rows(k), :] = rows

        put_blocks(blocks, put)
        return carry

    lax.fori_loop(0, index_ref.shape[0], step, 0)


def unpick(count, cols, got_ref, out_ref):
    for k in range(count):
        pieces = []
        for f in range(got_ref.shape[0]):

            def get(index):
                return got_ref[f, block_rows(index), :]

            pieces.append(get_block(get, k, count, cols))
        out_ref[k] = jnp.concatenate(pieces, 1)


def whole_block(array):
    zeros = (0,) * array.ndim
    return pl.BlockSpec(array.shape, lambda i: zeros, pipeline_mode=pl.Buffered(1))


def anywhere():
    return pl.BlockSpec(memory_space=pl.ANY)


def like(shape, dtype):
    return jax.ShapeDtypeStruct(shape, dtype)


PARAMS = pltpu.CompilerParams(
    dimension_semantics=("arbitrary",), vmem_limit_bytes=VMEM_LIMIT
)


def cost(flops, read, part=4):
    return pl.CostEstimate(
        flops=flops // part, bytes_accessed=read // part, transcendentals=0
    )


def run_spatial_forward(seq, video, mods, masks, wide, w_s, parts):
    frames, rows, d = video.shape
    places = rows // parts
    by_frame = lambda i: (i, 0, 0)
    row_block = pl.BlockSpec((1, rows, d), by_frame)
    return pl.pallas_call(
        spatial_forward,
        grid=(frames,),
        in_specs=[in_smem(), row_block, whole_block(mods), whole_block(masks), whole_block(wide), anywhere()],
        out_specs=[pl.BlockSpec((1, places, d), by_frame)] * parts
        + [
            row_block,
            row_block,
            row_block,
            row_block,
            pl.BlockSpec((1, HEADS, rows), by_frame),
            pl.BlockSpec((1, rows, 3 * RANK), by_frame),
            pl.BlockSpec((1, rows, RANK), by_frame),
        ],
        out_shape=[like((frames, places, d), BF16)] * parts
        + [like(video.shape, BF16)] * 4
        + [
            like((frames, HEADS, rows), F32),
            like((frames, rows, 3 * RANK), BF16),
            like((frames, rows, RANK), BF16),
        ],
        scratch_shapes=[
            pltpu.VMEM((4, d + PAD, d), BF16),
            pltpu.VMEM((ROWS, d + PAD), BF16),
            pltpu.VMEM((ROWS, d), BF16),
            pltpu.SemaphoreType.DMA((4,)),
        ],
        compiler_params=PARAMS,
        cost_estimate=cost(10 * frames * rows * d * d, 30_000_000),
        name="spatial_forward",
    )(seq, video, mods, masks, wide, w_s)


def run_temporal_forward(x1, mods, masks, wide, w_t):
    parts = len(x1)
    own_frames, places, d = x1[0].shape
    frames = own_frames * parts
    groups = places * frames // ROWS
    each = ROWS // frames
    across = pl.BlockSpec((frames, each, d), lambda i: (0, i, 0))
    by_group = lambda i: (i, 0, 0)
    act = like((frames, places, d), BF16)

    def body(*refs):
        temporal_forward(parts, *refs)

    return pl.pallas_call(
        body,
        grid=(groups,),
        in_specs=[pl.BlockSpec((own_frames, each, d), lambda i: (0, i, 0))] * parts
        + [whole_block(mods), whole_block(masks), whole_block(wide), anywhere()],
        out_specs=[across] * 4
        + [
            pl.BlockSpec((1, HEADS, ROWS), by_group),
            pl.BlockSpec((1, ROWS, 3 * RANK), by_group),
            pl.BlockSpec((1, ROWS, RANK), by_group),
            across,
            across,
        ],
        out_shape=[act] * 4
        + [
            like((groups, HEADS, ROWS), F32),
            like((groups, ROWS, 3 * RANK), BF16),
            like((groups, ROWS, RANK), BF16),
            act,
            like((frames, places, d), F32),
        ],
        scratch_shapes=[pltpu.VMEM((4, d + PAD, d), BF16), pltpu.VMEM((ROWS, ROWS), F32)]
        + [pltpu.VMEM((ROWS, d + PAD), BF16)]
        + [pltpu.VMEM((ROWS, d), BF16)] * 3
        + [pltpu.SemaphoreType.DMA((4,))],
        compiler_params=PARAMS,
        cost_estimate=cost(10 * places * frames * d * d, 30_000_000),
        name="temporal_forward",
    )(*x1, mods, masks, wide, w_t)


def run_cross_forward(x2, context, masks, wide, w_c):
    frames, places, d = x2.shape
    groups = places * frames // ROWS
    across = pl.BlockSpec((frames, ROWS // frames, d), lambda i: (0, i, 0))
    by_group = lambda i: (i, 0, 0)
    full = lambda *shape: pl.BlockSpec(shape, lambda i: (0,) * len(shape))
    one = pl.BlockSpec((1, ROWS, RANK), by_group)
    one_shape = like((groups, ROWS, RANK), BF16)
    act = like((frames, places, d), BF16)
    return pl.pallas_call(
        cross_forward,
        grid=(groups,),
        in_specs=[across, whole_block(context), whole_block(masks), whole_block(wide), anywhere()],
        out_specs=[across] * 2 + [pl.BlockSpec((1, HEADS, ROWS), by_group), one, one]
        + [full(PAIRS, 2 * PAD, 256)] * 2 + [full(PAD, RANK)] * 2 + [across],
        out_shape=[act] * 2 + [like((groups, HEADS, ROWS), F32), one_shape, one_shape]
        + [like((PAIRS, 2 * PAD, 256), BF16)] * 2 + [like((PAD, RANK), BF16)] * 2
        + [like(x2.shape, F32)],
        scratch_shapes=[pltpu.VMEM((4, d + PAD, d), BF16), pltpu.VMEM((ROWS, d + PAD), BF16)]
        + [pltpu.VMEM((ROWS, d), BF16), pltpu.VMEM((PAD, d), BF16)]
        + [pltpu.SemaphoreType.DMA((4,))],
        compiler_params=PARAMS,
        cost_estimate=cost(8 * places * frames * d * d, 30_000_000),
        name="cross_forward",
    )(x2, context, masks, wide, w_c)


def in_smem():
    return pl.BlockSpec(memory_space=pltpu.SMEM)


def run_feed_forward_grad(cot, mods, maps, order, pieces):
    tokens, d = cot.shape
    chunks = len(pieces) // 2

    def body(*refs):
        feed_forward_grad(len(pieces), *refs)

    return pl.pallas_call(
        body,
        grid=(tokens // ROWS,),
        in_specs=[in_smem(), pl.BlockSpec((ROWS, d), lambda i: (i, 0)), whole_block(mods), whole_block(maps)]
        + [anywhere()] * len(pieces),
        out_specs=pl.BlockSpec((chunks, ROWS, d), lambda i: (0, i, 0)),
        out_shape=like((chunks, tokens, d), BF16),
        scratch_shapes=[
            pltpu.VMEM((chunks * d, d + PAD), BF16),
            pltpu.VMEM((ROWS, d + PAD), BF16),
            pltpu.SemaphoreType.DMA((len(pieces),)),
        ],
        compiler_params=PARAMS,
        cost_estimate=cost(2 * tokens * d * d * chunks, 20_000_000),
        name="feed_forward_grad",
    )(order, cot, mods, maps, *pieces)


def run_feed_forward(x3, cot, order, grad_active, pieces, mods, maps, up):
    tokens, d = x3.shape
    chunks = up.shape[0]
    late = len(pieces) // 2
    rows = pl.BlockSpec((ROWS, d), lambda i: (i, 0))
    wide_rows = pl.BlockSpec((ROWS, chunks * d), lambda i: (i, 0))
    more = [pltpu.VMEM((late * d, d + PAD), BF16), pltpu.VMEM((ROWS, d + PAD), BF16)] if late else []

    def body(*refs):
        feed_forward(len(grad_active), len(pieces), *refs)

    return pl.pallas_call(
        body,
        grid=(tokens // ROWS,),
        in_specs=[in_smem(), rows, rows]
        + [pl.BlockSpec((g.shape[0], ROWS, d), lambda i: (0, i, 0)) for g in grad_active]
        + [anywhere()] * len(pieces)
        + [whole_block(mods), whole_block(maps), anywhere()],
        out_specs=[
            wide_rows,
            rows,
            pl.BlockSpec((RANK, d), lambda i: (0, 0)),
            pl.BlockSpec((RANK, chunks * d), lambda i: (0, 0)),
        ],
        out_shape=[
            like((tokens, chunks * d), BF16),
            like((tokens, d), F32),
            like((RANK, d), F32),
            like((RANK, chunks * d), F32),
        ],
        scratch_shapes=[
            pltpu.VMEM((d + PAD, chunks * d), BF16),
            pltpu.VMEM((ROWS, d + PAD), BF16),
            pltpu.VMEM((ROWS, chunks * d), BF16),
            pltpu.SemaphoreType.DMA((chunks + len(pieces),)),
            *more,
        ],
        compiler_params=PARAMS,
        cost_estimate=cost(4 * tokens * d * d * chunks, 50_000_000),
        name="feed_forward",
    )(order, x3, cot, *grad_active, *pieces, mods, maps, up)


def run_feed_forward_out(active, x3, cot, mods, maps, down, parts, half, halves):
    tokens, d = x3.shape
    order, *pieces = down
    hidden = active.shape[1]
    share = tokens // parts
    parts = parts // halves
    steps = tokens // ROWS // halves
    start = half * steps

    def body(*refs):
        feed_forward_out(len(pieces), *refs)

    rows = pl.BlockSpec((ROWS, d), lambda i: (i + start, 0))
    return pl.pallas_call(
        body,
        grid=(steps,),
        in_specs=[
            in_smem(),
            pl.BlockSpec((ROWS, hidden), lambda i: (i + start, 0)),
            rows,
            rows,
            whole_block(mods),
            whole_block(maps),
        ]
        + [anywhere()] * len(pieces),
        out_specs=[pl.BlockSpec((share, d), lambda i: (0, 0))] * parts
        + [
            pl.BlockSpec((RANK, d), lambda i: (0, 0)),
            pl.BlockSpec((RANK, hidden), lambda i: (0, 0)),
        ],
        out_shape=[like((share, d), BF16)] * parts
        + [
            like((RANK, d), F32),
            like((RANK, hidden), F32),
        ],
        scratch_shapes=[
            pltpu.VMEM((hidden, d + PAD), BF16),
            pltpu.SemaphoreType.DMA((len(pieces),)),
        ],
        compiler_params=PARAMS,
        cost_estimate=cost(2 * steps * ROWS * d * hidden, 20_000_000, 64),
        name="feed_forward_out",
    )(order, active, x3, cot, mods, maps, *pieces)


def run_cross_temporal_backward(g3, u1, saved, mods, masks, wide, w_t, w_c, start, groups):
    parts = len(u1)
    own_frames, places, d = u1[0].shape
    frames = own_frames * parts
    each = ROWS // frames
    across = pl.BlockSpec((frames, ROWS // frames, d), lambda i: (0, i + start, 0))
    by_group = lambda i: (i + start, 0, 0)
    stat = pl.BlockSpec((1, HEADS, ROWS), by_group)
    three = pl.BlockSpec((1, ROWS, 3 * RANK), by_group)
    one = pl.BlockSpec((1, ROWS, RANK), by_group)
    kp, vp = saved[13:15]
    pair_sums = pl.BlockSpec((PAIRS, 2 * PAD, 256), lambda i: (0, 0, 0))

    def body(*refs):
        cross_temporal_backward(parts, *refs)

    return pl.pallas_call(
        body,
        grid=(groups,),
        in_specs=[pl.BlockSpec((own_frames, each, d), lambda i: (0, i + start, 0))] * parts
        + [across] + [across] * 4 + [stat, three, one] + [across] * 3 + [stat, one, one]
        + [whole_block(kp), whole_block(vp)]
        + [whole_block(mods), whole_block(masks), whole_block(wide), anywhere(), anywhere()],
        out_specs=[pl.BlockSpec((own_frames, each, d), lambda i: (0, i, 0))] * parts
        + [
            pl.BlockSpec((16 * RANK, d), lambda i: (0, 0)),
            pair_sums,
            pair_sums,
        ],
        out_shape=[like((own_frames, groups * each, d), BF16)] * parts
        + [like((16 * RANK, d), F32)]
        + [like((PAIRS, 2 * PAD, 256), F32)] * 2,
        scratch_shapes=[
            pltpu.VMEM((6, d + PAD, d), BF16),
            pltpu.VMEM((ROWS, ROWS), F32),
        ]
        + [pltpu.VMEM((ROWS, d), BF16)] * 7
        + [pltpu.SemaphoreType.DMA((6,))],
        compiler_params=PARAMS,
        cost_estimate=cost(14 * groups * ROWS * d * d, 30_000_000, 64),
        name="cross_temporal_backward",
    )(*u1, g3, *saved[:15], mods, masks, wide, w_t, w_c)


LATE_BLOCKS = 8
EARLY_BLOCKS = 28


def run_spatial_backward(seq, g1, halves, video, saved, mods, masks, wide, w_s, clips, start, count, before):
    frames, rows, d = video.shape
    parts = len(g1) // halves
    by_frame = lambda i: (i + start, 0, 0)
    row_block = pl.BlockSpec((1, rows, d), by_frame)
    last = start + count == frames
    sums = (8 * RANK, d)
    if last:
        sums = (clips * parts, *packed_rows(LATE_BLOCKS // parts, d // clips))
    zeros = (0,) * len(sums)

    def body(*refs):
        spatial_backward(len(g1), halves, clips, bool(before), last, *refs)

    extra = [anywhere(), whole_block(before[1])] if before else []
    return pl.pallas_call(
        body,
        grid=(count,),
        in_specs=[in_smem()] + [pl.BlockSpec((1, g.shape[1], d), by_frame) for g in g1]
        + extra
        + [row_block] * 5
        + [
            pl.BlockSpec((1, HEADS, rows), by_frame),
            pl.BlockSpec((1, rows, 3 * RANK), by_frame),
            pl.BlockSpec((1, rows, RANK), by_frame),
            whole_block(mods),
            whole_block(masks),
            whole_block(wide),
            anywhere(),
        ],
        out_specs=[
            pl.BlockSpec((1, rows, 3 * d + PAD), by_frame),
            pl.BlockSpec(sums, lambda i: zeros),
        ],
        out_shape=[like((frames, rows, 3 * d + PAD), BF16), like(sums, BF16 if last else F32)],
        input_output_aliases={1 + len(g1): 0} if before else {},
        scratch_shapes=[pltpu.VMEM((d + PAD, d), BF16), pltpu.VMEM((LATE_BLOCKS * RANK, d), F32)]
        + [pltpu.VMEM((ROWS, d), BF16), pltpu.SemaphoreType.DMA((1,))],
        compiler_params=PARAMS,
        cost_estimate=cost(6 * count * rows * d * d, 20_000_000, 64),
        name="spatial_backward",
    )(seq, *g1, *before, video, *saved, mods, masks, wide, w_s)


def run_spatial_input_grad(seq, g1, halves, video, grads, mods, wide, w_s):
    frames, rows, d = video.shape
    by_frame = lambda i: (i, 0, 0)
    row_block = pl.BlockSpec((1, rows, d), by_frame)

    def body(*refs):
        spatial_input_grad(len(g1), halves, *refs)

    return pl.pallas_call(
        body,
        grid=(frames,),
        in_specs=[in_smem()] + [pl.BlockSpec((1, g.shape[1], d), by_frame) for g in g1]
        + [
            row_block,
            pl.BlockSpec((1, rows, grads.shape[2]), by_frame),
            whole_block(mods),
            whole_block(wide),
            anywhere(),
        ],
        out_specs=row_block,
        out_shape=like(video.shape, BF16),
        scratch_shapes=[
            pltpu.VMEM((d, 3 * d + PAD), BF16),
            pltpu.VMEM((ROWS, d), BF16),
            pltpu.SemaphoreType.DMA((3,)),
        ],
        compiler_params=PARAMS,
        cost_estimate=cost(6 * frames * rows * d * d, 20_000_000, 64),
        name="spatial_input_grad",
    )(seq, *g1, video, grads, mods, wide, w_s)


def run_put_in_place(seq, pieces):
    frames, places, d = pieces[0].shape
    by_frame = lambda i: (i, 0, 0)
    rows = places * len(pieces)
    return pl.pallas_call(
        put_in_place,
        grid=(frames,),
        in_specs=[in_smem()] + [pl.BlockSpec((1, places, d), by_frame)] * len(pieces),
        out_specs=pl.BlockSpec((1, rows, d), by_frame),
        out_shape=like((frames, rows, d), BF16),
        compiler_params=PARAMS,
        cost_estimate=cost(0, 4 * frames * rows * d, 64),
        name="put_in_place",
    )(seq, *pieces)


PLAIN = pltpu.CompilerParams(vmem_limit_bytes=VMEM_LIMIT)


def in_vmem():
    return pl.BlockSpec(memory_space=pltpu.VMEM)


def run_pack_early(gw, dk, dv, sources, clips, parts):
    d = gw[0].shape[1]
    packed = (clips * parts, *packed_rows(EARLY_BLOCKS // parts, d // clips))

    def body(*refs):
        pack_early(clips, len(gw), *refs)

    return pl.pallas_call(
        body,
        out_shape=like(packed, BF16),
        scratch_shapes=[pltpu.VMEM((EARLY_BLOCKS * RANK, d), F32), pltpu.VMEM((PAD, d), F32)],
        compiler_params=PLAIN,
        cost_estimate=cost(50000000, 8000000, 64),
        name="pack_early",
    )(*gw, *dk, *dv, *sources)


def run_assemble(seq, early, late, wide_shape, narrow_shape):
    parts = len(early)

    def body(*refs):
        assemble(parts, *refs)

    return pl.pallas_call(
        body,
        in_specs=[in_smem()] + [in_vmem()] * (2 * parts),
        out_specs=[in_vmem()] * 2,
        out_shape=[like(wide_shape, F32), like(narrow_shape, F32)],
        scratch_shapes=[pltpu.VMEM((parts, *piece.shape), BF16) for piece in (early[0], late[0])],
        compiler_params=PLAIN,
        cost_estimate=cost(0, 6_000_000, 64),
        name="assemble",
    )(seq, *early, *late)


def run_pick(all_index, wide, narrow):
    count, _, _, cols = wide.shape
    shape = packed_rows(count + 2 * (narrow.shape[3] // cols), cols)
    return pl.pallas_call(
        pick,
        in_specs=[in_smem(), in_vmem(), in_vmem()],
        out_specs=in_vmem(),
        out_shape=like((all_index.shape[0], *shape), BF16),
        compiler_params=PLAIN,
        cost_estimate=cost(0, 3000000),
        name="pick",
    )(all_index, wide, narrow)


def run_unpick(got, blocks, cols):
    def body(*refs):
        unpick(blocks, cols, *refs)

    return pl.pallas_call(
        body,
        in_specs=[in_vmem()],
        out_specs=in_vmem(),
        out_shape=like((blocks, RANK, got.shape[0] * cols), BF16),
        compiler_params=PLAIN,
        cost_estimate=cost(0, 2500000),
        name="unpick",
    )(got)


def run_combine(all_index, got, adapters):
    _, share, cols = got.shape
    return pl.pallas_call(
        combine,
        in_specs=[pl.BlockSpec(memory_space=pltpu.SMEM), pl.BlockSpec(memory_space=pltpu.VMEM)],
        out_specs=pl.BlockSpec(memory_space=pltpu.VMEM),
        out_shape=like((adapters, share, cols), BF16),
        scratch_shapes=[pltpu.VMEM((adapters, share, cols), F32)],
        compiler_params=pltpu.CompilerParams(vmem_limit_bytes=VMEM_LIMIT),
        cost_estimate=cost(0, 1000000, 64),
        name="combine",
    )(all_index, got)


def exchange(array, axes="seq"):
    return lax.all_to_all(array, axes, split_axis=0, concat_axis=0, tiled=True)


def up_chunks(up, clips, times):
    rows, hidden = up.shape
    cols = hidden // (clips * times)
    return up.reshape(rows, clips, times, cols).transpose(2, 0, 1, 3).reshape(times, rows, -1)


def gather(array):
    return lax.all_gather(array, "fsdp", axis=1, tiled=True)


def send(array, axis, shift):
    size = lax.axis_size(axis)
    return lax.ppermute(array, axis, [(i, (i + shift) % size) for i in range(size)])


def to_places(pieces):
    return [pieces[0]] + [send(pieces[k], "seq", k) for k in range(1, len(pieces))]


def to_frames(pieces):
    return [pieces[0]] + [send(pieces[k], "seq", -k) for k in range(1, len(pieces))]


def gather_spatial_and_down(spatial, down, parts, times, clips, d):
    quarters = down.reshape(times, -1, d)
    if times != parts or clips % 2:
        return gather(spatial), None
    own = lax.dynamic_slice_in_dim(quarters, lax.axis_index("seq"), 1, 0)
    got = gather(jnp.concatenate([spatial, own], 0))
    half = d // 2
    core = lax.axis_index("fsdp") % 2
    first = lax.dynamic_slice(got, (times, core * half, 0), (1, half, d))[0]
    other = lax.dynamic_slice(got, (times, (1 - core) * half, 0), (1, half, d))[0]
    return got, (first, other, send(first, "seq", 1))


def swap_cores(piece, clips):
    return lax.ppermute(piece, "fsdp", [(i, i ^ 1) for i in range(clips)])


def to_all(piece):
    return [piece] + [send(piece, "seq", k) for k in range(1, lax.axis_size("seq"))]


def down_order(times, parts, clips):
    if times != parts or clips % 2:
        return jnp.arange(times, dtype=jnp.int32), jnp.zeros((1,), jnp.int32)
    seq = lax.axis_index("seq")
    core = lax.axis_index("fsdp") % 2
    return ((seq - jnp.arange(parts)) % parts).astype(jnp.int32), core.astype(jnp.int32)[None]


def on_device(
    video,
    context,
    modulation,
    adapter_index,
    cotangent,
    qkv_weights,
    out_weights,
    ffn_up,
    ffn_down,
    adapt_wide,
    adapt_ff,
):
    parts = lax.axis_size("seq")
    clips = lax.axis_size("fsdp")
    d = video.shape[-1]
    count, adapters, _, cols = adapt_wide.shape[1:]
    times = adapt_ff.shape[-1] // cols
    places = SPATIAL // parts
    frames = FRAMES // parts
    half_d = d // 2
    mods = modulation[0, 0]
    masks = head_masks()
    ctx = jnp.pad(context[0], ((0, PAD - context.shape[1]), (0, 0)))

    def attention_weights(j):
        return jnp.concatenate([qkv_weights[0, 3 * j : 3 * j + 3], out_weights[0, j : j + 1]], 0)

    seq = lax.axis_index("seq").astype(jnp.int32)[None]
    all_index = exchange(jnp.broadcast_to(adapter_index, (clips,)), "fsdp")
    w_s, started = gather_spatial_and_down(
        attention_weights(0), ffn_down[0], parts, times, clips, d
    )
    picked = run_pick(all_index, adapt_wide[0], adapt_ff[0])
    wide = run_unpick(exchange(picked, "fsdp"), count + 2 * times, cols)
    w_t = gather(attention_weights(1))
    w_c = gather(attention_weights(2))
    ffn_up, _ = lax.optimization_barrier((ffn_up, picked))
    up = gather(up_chunks(ffn_up[0], clips, times))
    maps_f = wide[24:]

    cot = cotangent.reshape(frames, SPATIAL, d)
    cot = to_places(
        [
            lax.dynamic_slice_in_dim(cot, (seq[0] + k) % parts * places, places, 1)
            for k in range(parts)
        ]
    )
    frames_in, *cot = lax.optimization_barrier((video.reshape(frames, SPATIAL, d), *cot))
    cot = jnp.concatenate(cot, 0).reshape(FRAMES * places, d)
    made = run_spatial_forward(seq, frames_in, mods, masks, wide, w_s, parts)
    u1, kept_s = to_places(made[:parts]), made[parts:]
    order, core = down_order(times, parts, clips)
    if started is None:
        whole_down = gather(ffn_down[0].reshape(times, -1, d))
        sides = [[whole_down[i, :half_d] for i in range(times)], [whole_down[i, half_d:] for i in range(times)]]
        *kept_t, x2 = run_temporal_forward(u1, mods, masks, wide, w_t)
        *kept_c, x3 = run_cross_forward(x2, ctx, masks, wide, w_c)
        late_pieces = []
        grad_active = [
            run_feed_forward_grad(cot, mods, maps_f, jnp.concatenate([order, core]), sides[0] + sides[1])
        ]
    else:
        first, other, second = started
        later, second, *u1 = lax.optimization_barrier((first, second, *u1))
        mine = [first, second] + [send(later, "seq", k) for k in range(3, parts)]
        last = send(later, "seq", 2)
        *kept_t, x2 = run_temporal_forward(u1, mods, masks, wide, w_t)
        x2, *mine = lax.optimization_barrier((x2, *mine))
        others = [other] + [swap_cores(piece, clips) for piece in mine[1:]]
        order = jnp.concatenate([order[:2], order[3:], order[2:3]])
        early_order = jnp.concatenate([order[:-1], core])
        *kept_c, x3 = run_cross_forward(x2, ctx, masks, wide, w_c)
        mine[0], x3 = lax.optimization_barrier((mine[0], x3))
        grad_early = run_feed_forward_grad(cot, mods, maps_f, early_order, mine + others)
        last, grad_early = lax.optimization_barrier((last, grad_early))
        last_other = swap_cores(last, clips)
        grad_active = [grad_early]
        late_pieces = [last, last_other]
        sides = [mine + [last], others + [last_other]]
    down = [jnp.concatenate([order, core]), *sides[0], *sides[1]]
    x3 = x3.reshape(FRAMES * places, d)
    active, g3, grad_a24, grad_b24 = run_feed_forward(
        x3, cot, jnp.concatenate([order, core]), grad_active, late_pieces, mods, maps_f, up
    )
    g3 = g3.reshape(FRAMES, places, d)
    groups = FRAMES * places // ROWS
    saved = kept_t + kept_c
    *x4, grad_b25, grad_down = run_feed_forward_out(
        active, x3, cot, mods, maps_f, down, parts, 0, 1
    )
    x4[0], g3 = lax.optimization_barrier((x4[0], g3))
    output = to_frames([piece.reshape(frames, places, d) for piece in x4])
    shares = [groups - 1, 1] if groups > 1 else [1]
    g1, gw, dk, dv = [], [], [], []
    for share, size in enumerate(shares):
        *pieces, gw_part, dk_part, dv_part = run_cross_temporal_backward(
            g3, u1, saved, mods, masks, wide, w_t, w_c, sum(shares[:share]), size
        )
        gw.append(gw_part)
        dk.append(dk_part)
        dv.append(dv_part)
        pieces[0], g3 = lax.optimization_barrier((pieces[0], g3))
        if share == 0:
            g3, *output = lax.optimization_barrier((g3, *output))
        g1.append(to_frames(pieces))
    sources = [grad_a24, grad_b25, grad_b24, grad_down, kept_c[7], kept_c[8], ctx, masks, wide]
    packed = run_pack_early(gw, dk, dv, sources, clips, parts)
    g1 = [piece for done in g1 for piece in done]
    packed, *g1 = lax.optimization_barrier((packed, *g1))
    got = exchange(packed, ("fsdp", "seq"))
    halves = len(shares)
    before = []
    spatial = [frames - frames // 2, frames // 2] if frames > 1 else [1]
    for turn, size in enumerate(spatial):
        grads, sums = before = run_spatial_backward(
            seq, g1, halves, frames_in, kept_s, mods, masks, wide, w_s, clips, sum(spatial[:turn]), size, before
        )
        if turn == 0:
            got, sums = lax.optimization_barrier((got, sums))
            table = run_combine(all_index, got, adapters)
            if len(spatial) > 1:
                table, sums = lax.optimization_barrier((table, sums))
            early = to_all(table)
        before = [grads, sums]
    packed, *early = lax.optimization_barrier((sums, *early))
    g0 = run_spatial_input_grad(seq, g1, halves, frames_in, grads, mods, wide, w_s)
    got, g0 = lax.optimization_barrier((exchange(packed, ("fsdp", "seq")), g0))
    late = run_combine(all_index, got, adapters)
    wide_out, narrow_out = run_assemble(
        seq, early, to_all(late), adapt_wide.shape[1:], adapt_ff.shape[1:]
    )
    output = run_put_in_place(seq, output).reshape(video.shape)
    return (output, g0.reshape(video.shape), wide_out[None], narrow_out[None])


def solution(mesh):
    return jax.shard_map(
        on_device,
        mesh=mesh,
        in_specs=(
            P("fsdp", "seq", None),
            P("fsdp", None, None),
            P("fsdp", None, None, None),
            P("fsdp"),
            P("fsdp", "seq", None),
            P(None, None, "fsdp", None),
            P(None, None, "fsdp", None),
            P(None, "fsdp", None),
            P(None, "fsdp", None),
            P(None, None, None, None, "fsdp"),
            P(None, None, None, None, "fsdp"),
        ),
        out_specs=(
            P("fsdp", "seq", None),
            P("fsdp", "seq", None),
            P(None, None, None, None, "fsdp"),
            P(None, None, None, None, "fsdp"),
        ),
        check_vma=False,
    )
```

```python
import math

import jax
import jax.numpy as jnp
from jax import lax
from jax.experimental import pallas as pl
from jax.experimental.pallas import tpu as pltpu
from jax.sharding import PartitionSpec as P

HEAD_DIM = 72
HEADS = 16
FRAMES = 16
SPATIAL = 256
RANK = 16
ROWS = 256
PAIRS = HEADS // 2
PAD = 128
SCALE = HEAD_DIM ** (-0.5)
EXP_SCALE = SCALE * math.log2(math.e)
LN2 = math.log(2.0)
HIGHEST = lax.Precision.HIGHEST
F32 = jnp.float32
BF16 = jnp.bfloat16
VMEM_LIMIT = 60 * 1024 * 1024


def nn(left, right):
    return lax.dot_general(left, right, (((1,), (0,)), ((), ())), preferred_element_type=F32)


def nt(left, right):
    return lax.dot_general(left, right, (((1,), (1,)), ((), ())), preferred_element_type=F32)


def tn(left, right):
    return lax.dot_general(left, right, (((0,), (0,)), ((), ())), preferred_element_type=F32)


def window(pair):
    return slice(128 * pair, 128 * pair + 256)


def normalize(stream):
    average = jnp.mean(stream, -1, keepdims=True)
    centred = stream - average
    inverse = lax.rsqrt(jnp.mean(centred * centred, -1, keepdims=True) + 1e-06)
    return centred * inverse, inverse


def normalize_back(normal, inverse, grad):
    mean_grad = jnp.mean(grad, -1, keepdims=True)
    mean_both = jnp.mean(grad * normal, -1, keepdims=True)
    return inverse * (grad - mean_grad - normal * mean_both)


def up_rows(ad_ref, number, slot, width):
    rows = ad_ref[2 * number + 1]
    before = jnp.zeros((RANK * slot, width), BF16)
    after = jnp.zeros((PAD - RANK * (slot + 1), width), BF16)
    return jnp.concatenate(([before] if slot else []) + [rows, after], 0)


def three_downs(ad_ref, number):
    return jnp.concatenate([ad_ref[2 * (number + i)] for i in range(3)], 0)


class Loads:
    def __init__(self, entries, sems):
        self.first = pl.program_id(0) == 0
        self.entries = entries
        self.sems = sems

    def copy(self, index):
        source, target = self.entries[index]
        return pltpu.make_async_copy(source, target, self.sems.at[index])

    def start(self):
        @pl.when(self.first)
        def _():
            for index in range(len(self.entries)):
                self.copy(index).start()

    def ready(self, index):
        @pl.when(self.first)
        def _():
            self.copy(index).wait()


def head_masks():
    lane = jnp.arange(256)[None, :]
    begin = jnp.array([16 * (h // 2) + HEAD_DIM * (h % 2) for h in range(HEADS)])[:, None]
    return ((lane >= begin) & (lane < begin + HEAD_DIM)).astype(BF16)


def same_place(shape):
    rows = lax.broadcasted_iota(jnp.int32, shape, 0)
    cols = lax.broadcasted_iota(jnp.int32, shape, 1)
    return jnp.where(rows % 16 == cols % 16, 0.0, -1e30).astype(F32)


def attend(q_ref, k_ref, v_ref, mask_ref, bias, put_out, stat_ref):
    carried = None
    for pair in range(PAIRS):
        win = window(pair)
        q_win, k_win, v_win = q_ref[:, win], k_ref[:, win], v_ref[:, win]
        all_weights, all_values = [], []
        for head in (2 * pair, 2 * pair + 1):
            mask = mask_ref[head : head + 1, :]
            scores = nt(k_win * mask, q_win)
            if bias is not None:
                scores = scores + bias[...]
            top = jnp.max(scores, 0, keepdims=True)
            grown = jnp.exp2(scores - top)
            total = jnp.sum(grown, 0, keepdims=True)
            stat_ref[head : head + 1, :] = top + jnp.log2(total)
            all_weights.append((grown * (1.0 / total)).astype(BF16))
            all_values.append(v_win * mask)
        out = tn(jnp.concatenate(all_weights, 0), jnp.concatenate(all_values, 0))
        low = out[:, :128]
        put_out(pair, low if carried is None else low + carried)
        carried = out[:, 128:]
    put_out(PAIRS, carried)


def attend_back(q_ref, k_ref, v_ref, do_ref, mask_ref, bias, stat_ref, put):
    carried = None
    for pair in range(PAIRS):
        win = window(pair)
        q_win, k_win, v_win, do_win = q_ref[:, win], k_ref[:, win], v_ref[:, win], do_ref[:, win]
        all_grads, all_probs, keys, queries, outs = [], [], [], [], []
        for head in (2 * pair, 2 * pair + 1):
            mask = mask_ref[head : head + 1, :]
            k_own = k_win * mask
            scores = nt(k_own, q_win)
            if bias is not None:
                scores = scores + bias[...]
            probs = jnp.exp2(scores - stat_ref[head : head + 1, :])
            grad_probs = nt(v_win * mask, do_win)
            inner = jnp.sum(probs * grad_probs, 0, keepdims=True)
            all_grads.append((probs * (grad_probs - inner)).astype(BF16))
            all_probs.append(probs.astype(BF16))
            keys.append(k_own)
            queries.append(q_win * mask)
            outs.append(do_win * mask)
        grads = (
            tn(jnp.concatenate(all_grads, 0), jnp.concatenate(keys, 0)),
            nn(jnp.concatenate(all_grads, 1), jnp.concatenate(queries, 0)),
            nn(jnp.concatenate(all_probs, 1), jnp.concatenate(outs, 0)),
        )
        lows = tuple(g[:, :128] for g in grads)
        if carried is not None:
            lows = tuple(a + b for a, b in zip(lows, carried))
        put(pair, lows)
        carried = tuple(g[:, 128:] for g in grads)
    put(PAIRS, carried)


def tile(index):
    return slice(128 * index, 128 * index + 128)


def three_projections(lhs_ref, ad_ref, number, weights, loads, first_load, outs, rank_ref):
    width = weights.shape[2]
    ranks = nt(lhs_ref[:, :width], three_downs(ad_ref, number)).astype(BF16)
    rank_ref[...] = ranks
    lhs_ref[:, width : width + 3 * RANK] = ranks
    for i in range(3):
        loads.ready(first_load + i)
        total = nn(lhs_ref[...], weights[first_load + i])
        outs[i][...] = (total * EXP_SCALE if i == 0 else total).astype(BF16)


def one_projection(lhs_ref, ad_ref, number, weight_ref, rank_ref):
    width = weight_ref.shape[1]
    ranks = nt(lhs_ref[:, :width], ad_ref[2 * number]).astype(BF16)
    rank_ref[...] = ranks
    lhs_ref[:, width : width + RANK] = ranks
    return nn(lhs_ref[...], weight_ref[...])


def block_rows(index):
    return slice(RANK * index, RANK * (index + 1))


def one_back(grad, kept, ranks, ad_ref, number, weight_ref, grad_ref, at):
    width = weight_ref.shape[1]
    both = nt(grad, weight_ref[...])
    grad_rank = both[:, width : width + RANK].astype(BF16)
    grad_ref[block_rows(at), :] += tn(grad_rank, kept)
    grad_ref[block_rows(at + 1), :] += tn(ranks, grad)
    return both[:, :width] + nn(grad_rank, ad_ref[2 * number])


def three_back(grads, inputs, ranks, ad_ref, number, weights, loads, first_load, grad_ref, at):
    width = weights.shape[2]
    both = None
    for i in range(3):
        grad = grads[i][...]
        ups = tn(ranks, grad)
        grad_ref[block_rows(at + 2 * i + 1), :] += ups[block_rows(i)]
        loads.ready(first_load + i)
        part = nt(grad, weights[first_load + i])
        both = part if both is None else both + part
    grad_ranks = both[:, width : width + 3 * RANK].astype(BF16)
    downs = tn(grad_ranks, inputs)
    for i in range(3):
        grad_ref[block_rows(at + 2 * i), :] += downs[block_rows(i)]
    return both[:, :width] + nn(grad_ranks, three_downs(ad_ref, number))


def place_of(seq_ref, k, parts, places):
    return pl.multiple_of(lax.rem(seq_ref[0] + k, parts) * places, 16)


def spatial_forward(seq_ref, x_ref, mod_ref, mask_ref, ad_ref, w_hbm, *refs):
    x1_refs = refs[:-11]
    q_ref, k_ref, v_ref, o_ref, stat_ref, rq_ref, ro_ref, w_ref, lhs_ref, x1_s, sems = refs[-11:]
    width = x_ref.shape[2]
    loads = Loads([(w_hbm.at[i], w_ref.at[i, pl.ds(0, width), :]) for i in range(4)], sems)
    loads.start()

    @pl.when(loads.first)
    def _():
        lhs_ref[:, width:] = jnp.zeros((ROWS, PAD), BF16)
        for i in range(4):
            w_ref[i, width:, :] = up_rows(ad_ref, i, i % 3, width)

    stream = x_ref[0].astype(F32)
    normal, _ = normalize(stream)
    lhs_ref[:, :width] = (normal * (1.0 + mod_ref[1:2, :]) + mod_ref[0:1, :]).astype(BF16)
    q, k, v = q_ref.at[0], k_ref.at[0], v_ref.at[0]
    three_projections(lhs_ref, ad_ref, 0, w_ref, loads, 0, (q, k, v), rq_ref.at[0])

    def put_out(index, value):
        value = value.astype(BF16)
        o_ref[0, :, tile(index)] = value
        lhs_ref[:, tile(index)] = value

    attend(q, k, v, mask_ref, None, put_out, stat_ref.at[0])
    loads.ready(3)
    branch = one_projection(lhs_ref, ad_ref, 3, w_ref.at[3], ro_ref.at[0])
    x1_s[...] = (stream + mod_ref[2:3, :] * branch).astype(BF16)
    places = x1_refs[0].shape[1]
    for k, ref in enumerate(x1_refs):
        ref[0] = x1_s[pl.ds(place_of(seq_ref, k, len(x1_refs), places), places), :]


def rows_of(refs):
    pieces = [ref[...].reshape(-1, ref.shape[2]) for ref in refs]
    return pieces[0] if len(pieces) == 1 else jnp.concatenate(pieces, 0)


def temporal_forward(parts, *refs):
    x_refs, refs = refs[:parts], refs[parts:]
    (
        mod_ref, mask_ref, ad_ref, w_hbm,
        q_ref, k_ref, v_ref, o_ref, stat_ref, rq_ref, ro_ref, u2_ref, x2_ref,
        w_ref, bias_ref, lhs_ref, q_s, k_s, v_s, sems,
    ) = refs
    width = x_refs[0].shape[2]
    loads = Loads([(w_hbm.at[i], w_ref.at[i, pl.ds(0, width), :]) for i in range(4)], sems)
    loads.start()

    @pl.when(loads.first)
    def _():
        bias_ref[...] = same_place(bias_ref.shape)
        lhs_ref[:, width:] = jnp.zeros((ROWS, PAD), BF16)
        for i in range(4):
            w_ref[i, width:, :] = up_rows(ad_ref, 4 + i, i % 3, width)

    loaded = rows_of(x_refs)
    lhs_ref[:, :width] = loaded
    three_projections(lhs_ref, ad_ref, 4, w_ref, loads, 0, (q_s, k_s, v_s), rq_ref.at[0])
    q_ref[...] = q_s[...].reshape(q_ref.shape)
    k_ref[...] = k_s[...].reshape(k_ref.shape)
    v_ref[...] = v_s[...].reshape(v_ref.shape)

    def put_out(index, value):
        lhs_ref[:, tile(index)] = value.astype(BF16)

    attend(q_s, k_s, v_s, mask_ref, bias_ref, put_out, stat_ref.at[0])
    o_ref[...] = lhs_ref[:, :width].reshape(o_ref.shape)
    loads.ready(3)
    branch = one_projection(lhs_ref, ad_ref, 7, w_ref.at[3], ro_ref.at[0])
    stream = loaded.astype(F32) + mod_ref[2:3, :] * branch
    u2_ref[...] = stream.astype(BF16).reshape(u2_ref.shape)
    x2_ref[...] = stream.reshape(x2_ref.shape)


def cross_forward(
    x_ref, ctx_ref, mask_ref, ad_ref, w_hbm,
    q_ref, o_ref, stat_ref, rq_ref, ro_ref, kp_ref, vp_ref, rk_ref, rv_ref, x3_ref,
    w_ref, lhs_ref, q_s, k_s, sems,
):
    width = x_ref.shape[2]
    loads = Loads([(w_hbm.at[4 + i], w_ref.at[i, pl.ds(0, width), :]) for i in range(4)], sems)
    loads.start()

    @pl.when(loads.first)
    def _():
        lhs_ref[:, width:] = jnp.zeros((ROWS, PAD), BF16)
        for i in (0, 3):
            w_ref[i, width:, :] = up_rows(ad_ref, 8 + i, 0, width)

    stream = x_ref[...].reshape(ROWS, width)
    lhs_ref[:, :width] = stream.astype(BF16)
    loads.ready(0)
    queries = one_projection(lhs_ref, ad_ref, 8, w_ref.at[0], rq_ref.at[0])
    q_s[...] = (queries * EXP_SCALE).astype(BF16)
    q_ref[...] = q_s[...].reshape(q_ref.shape)
    loads.ready(1)
    loads.ready(2)

    @pl.when(loads.first)
    def _():
        for number, at, rank_ref, pair_ref in ((9, 1, rk_ref, kp_ref), (10, 2, rv_ref, vp_ref)):
            ranks = nt(ctx_ref[...], ad_ref[2 * number]).astype(BF16)
            rank_ref[...] = ranks
            made = nn(ctx_ref[...], w_ref[at, :width, :]) + nn(ranks, ad_ref[2 * number + 1])
            k_s[...] = made.astype(BF16)
            for pair in range(PAIRS):
                piece = k_s[:, window(pair)]
                pair_ref[pair, :PAD, :] = piece * mask_ref[2 * pair : 2 * pair + 1, :]
                pair_ref[pair, PAD:, :] = piece * mask_ref[2 * pair + 1 : 2 * pair + 2, :]

    carried = None
    count = 120
    for pair in range(PAIRS):
        scores = nt(kp_ref[pair], q_s[:, window(pair)])
        pieces = []
        for sub in range(2):
            own = scores[PAD * sub : PAD * sub + count]
            top = jnp.max(own, 0, keepdims=True)
            grown = jnp.exp2(own - top)
            total = jnp.sum(grown, 0, keepdims=True)
            stat_ref[0, 2 * pair + sub : 2 * pair + sub + 1, :] = top + jnp.log2(total)
            pieces += [grown * (1.0 / total), jnp.zeros((PAD - count, ROWS), F32)]
        weights = jnp.concatenate(pieces, 0).astype(BF16)
        out = tn(weights, vp_ref[pair])
        low = out[:, :128]
        lhs_ref[:, tile(pair)] = (low if carried is None else low + carried).astype(BF16)
        carried = out[:, 128:]
    lhs_ref[:, tile(PAIRS)] = carried.astype(BF16)
    o_ref[...] = lhs_ref[:, :width].reshape(o_ref.shape)
    loads.ready(3)
    stream = stream + one_projection(lhs_ref, ad_ref, 11, w_ref.at[3], ro_ref.at[0])
    x3_ref[...] = stream.reshape(x3_ref.shape)


def gelu_both(hidden):
    root = math.sqrt(2.0 / math.pi)
    square = hidden * hidden
    inner = root * (hidden + 0.044715 * (square * hidden))
    bent = jnp.tanh(inner)
    half = 0.5 * (1.0 + bent)
    slope = half + 0.5 * hidden * (1.0 - bent * bent) * (root * (1.0 + 3.0 * 0.044715 * square))
    return hidden * half, slope


def transposed_map(rows):
    nothing = jnp.zeros((PAD - rows.shape[0], rows.shape[1]), F32)
    wide = jnp.concatenate([rows.astype(F32), nothing], 0)
    return wide.T.astype(BF16)


def down_loads(order_ref, pieces, down_ref, width):
    half = width // 2
    count = len(pieces) // 2
    core = order_ref[count]
    entries = []
    for k in range(count):
        for source, side in ((pieces[k], core), (pieces[count + k], 1 - core)):
            start = pl.multiple_of(order_ref[k] * width + side * half, 16)
            entries.append((source, down_ref.at[pl.ds(start, half), pl.ds(0, width)]))
    return entries


def fill_down_maps(ad_ref, down_ref, width):
    chunks = down_ref.shape[0] // width
    for c in range(chunks):
        rows = slice(c * width, (c + 1) * width)
        down_ref[rows, width:] = transposed_map(ad_ref[2 + chunks + c])


def feed_forward_grad(count, order_ref, cot_ref, mod_ref, ad_ref, *refs):
    pieces = refs[:count]
    grad_ref, down_ref, lhs_ref, sems = refs[count:]
    width = cot_ref.shape[1]
    half = width // 2
    chunks = count // 2
    core = order_ref[chunks]
    entries = []
    for k in range(chunks):
        for source, side in ((pieces[k], core), (pieces[chunks + k], 1 - core)):
            start = pl.multiple_of(k * width + side * half, 16)
            entries.append((source, down_ref.at[pl.ds(start, half), pl.ds(0, width)]))
    loads = Loads(entries, sems)
    loads.start()

    @pl.when(loads.first)
    def _():
        lhs_ref[:, width:] = jnp.zeros((ROWS, PAD), BF16)
        for k in range(chunks):
            rows = slice(k * width, (k + 1) * width)
            down_ref[rows, width:] = transposed_map(ad_ref[2 + (ad_ref.shape[0] - 2) // 2 + order_ref[k]])

    branch = (mod_ref[5:6, :] * cot_ref[...].astype(F32)).astype(BF16)
    lhs_ref[:, :width] = branch
    lhs_ref[:, width : width + RANK] = nt(branch, ad_ref[1]).astype(BF16)
    for i in range(len(entries)):
        loads.ready(i)
    for k in range(chunks):
        rows = slice(k * width, (k + 1) * width)
        grad_ref[k] = nt(lhs_ref[...], down_ref[rows, :]).astype(BF16)


def hidden_chunks(hidden):
    return [slice(at, at + 1536) for at in range(0, hidden, 1536)]


def feed_forward(groups, count, order_ref, x3_ref, cot_ref, *refs):
    grad_refs, pieces, refs = refs[:groups], refs[groups : groups + count], refs[groups + count :]
    (
        mod_ref, ad_ref, w_hbm, act_ref, g3_ref, gd_ref, gu_ref, up_ref, lhs_ref, dh_ref, sems, *rest
    ) = refs
    width = x3_ref.shape[1]
    hidden_size = up_ref.shape[1]
    chunks = hidden_size // width
    late = count // 2
    core = order_ref[chunks]
    entries = [
        (w_hbm.at[c], up_ref.at[pl.ds(0, width), pl.ds(c * width, width)]) for c in range(chunks)
    ]
    if late:
        down_ref, dlhs_ref = rest
        half = width // 2
        for k in range(late):
            for source, side in ((pieces[k], core), (pieces[late + k], 1 - core)):
                start = pl.multiple_of(k * width + side * half, 16)
                entries.append((source, down_ref.at[pl.ds(start, half), pl.ds(0, width)]))
    loads = Loads(entries, sems)
    loads.start()

    @pl.when(loads.first)
    def _():
        gd_ref[...] = jnp.zeros_like(gd_ref)
        gu_ref[...] = jnp.zeros_like(gu_ref)
        lhs_ref[:, width:] = jnp.zeros((ROWS, PAD), BF16)
        up_ref[width + RANK :, :] = jnp.zeros((PAD - RANK, hidden_size), BF16)
        for c in range(chunks):
            up_ref[width : width + RANK, c * width : (c + 1) * width] = ad_ref[2 + c]
        for k in range(late):
            rows = slice(k * width, (k + 1) * width)
            at = order_ref[chunks - late + k]
            down_ref[rows, width:] = transposed_map(ad_ref[2 + chunks + at])
        if late:
            dlhs_ref[:, width:] = jnp.zeros((ROWS, PAD), BF16)

    normal, inverse = normalize(x3_ref[...])
    inputs = (normal * (1.0 + mod_ref[4:5, :]) + mod_ref[3:4, :]).astype(BF16)
    rank_up = nt(inputs, ad_ref[0]).astype(BF16)
    lhs_ref[:, :width] = inputs
    lhs_ref[:, width : width + RANK] = rank_up
    at = 0
    for grad_ref in grad_refs:
        for k in range(grad_ref.shape[0]):
            start = pl.multiple_of(order_ref[at] * width, 128)
            dh_ref[:, pl.ds(start, width)] = grad_ref[k]
            at += 1
    if late:
        branch = (mod_ref[5:6, :] * cot_ref[...].astype(F32)).astype(BF16)
        dlhs_ref[:, :width] = branch
        dlhs_ref[:, width : width + RANK] = nt(branch, ad_ref[1]).astype(BF16)
    for i in range(len(entries)):
        loads.ready(i)
    for k in range(late):
        start = pl.multiple_of(order_ref[at + k] * width, 128)
        rows = slice(k * width, (k + 1) * width)
        dh_ref[:, pl.ds(start, width)] = nt(dlhs_ref[...], down_ref[rows, :]).astype(BF16)
    for cols in hidden_chunks(hidden_size):
        active, slope = gelu_both(nn(lhs_ref[...], up_ref[:, cols]))
        act_ref[:, cols] = active.astype(BF16)
        dh_ref[:, cols] = (slope * dh_ref[:, cols].astype(F32)).astype(BF16)
    both = nt(dh_ref[...], up_ref[...])
    gu_ref[...] += tn(rank_up, dh_ref[...])
    grad_rank = both[:, width : width + RANK].astype(BF16)
    grad_in = both[:, :width] + nn(grad_rank, ad_ref[0])
    gd_ref[...] += tn(grad_rank, lhs_ref[:, :width])
    grad_in = normalize_back(normal, inverse, grad_in * (1.0 + mod_ref[4:5, :]))
    g3_ref[...] = cot_ref[...].astype(F32) + grad_in


def feed_forward_out(count, order_ref, act_ref, x3_ref, cot_ref, mod_ref, ad_ref, *refs):
    pieces, refs = refs[:count], refs[count:]
    x4_refs = refs[:-4]
    gu_ref, gd_ref, down_ref, sems = refs[-4:]
    width = x3_ref.shape[1]
    step = pl.program_id(0)
    entries = down_loads(order_ref, pieces, down_ref, width)
    loads = Loads(entries, sems)
    loads.start()

    @pl.when(loads.first)
    def _():
        gu_ref[...] = jnp.zeros_like(gu_ref)
        gd_ref[...] = jnp.zeros_like(gd_ref)
        fill_down_maps(ad_ref, down_ref, width)

    share = x4_refs[0].shape[0]
    grad_branch = (mod_ref[5:6, :] * cot_ref[...].astype(F32)).astype(BF16)
    gd_ref[...] += tn(nt(grad_branch, ad_ref[1]).astype(BF16), act_ref[...])
    for i in range(len(entries)):
        loads.ready(i)
    both = nn(act_ref[...], down_ref[...])
    ranks = both[:, width : width + RANK].astype(BF16)
    branch = both[:, :width] + nn(ranks, ad_ref[1])
    gu_ref[...] += tn(ranks, grad_branch)
    result = (x3_ref[...] + mod_ref[5:6, :] * branch).astype(BF16)
    for k, ref in enumerate(x4_refs):
        at = k * share

        @pl.when(step == at // ROWS)
        def _():
            ref[...] = result[at % ROWS : at % ROWS + share]


def cross_temporal_backward(parts, *refs):
    outs = len(refs) - parts - 13
    _cross_temporal_backward(refs[:parts], refs[outs : outs + parts], *refs[parts:outs], *refs[outs + parts :])


def _cross_temporal_backward(
    u1_refs, g1_refs, g3_ref, q_ref, k_ref, v_ref, o_ref, stat_ref, rq_ref, ro_ref,
    u2_ref, qc_ref, oc_ref, statc_ref, rqc_ref, roc_ref, kp_ref, vp_ref,
    mod_ref, mask_ref, ad_ref, w_hbm,
    gw_ref, dk_acc, dv_acc, w_ref, bias_ref, q_s, k_s, v_s, do_s, dq_s, dk_s, dv_s, sems,
):
    width = u1_refs[0].shape[2]
    first = pl.program_id(0) == 0
    order = (7, 4, 3, 0, 1, 2)
    loads = Loads(
        [(w_hbm.at[n], w_ref.at[i, pl.ds(0, width), :]) for i, n in enumerate(order)], sems
    )
    loads.start()

    @pl.when(first)
    def _():
        bias_ref[...] = same_place(bias_ref.shape)
        gw_ref[...] = jnp.zeros_like(gw_ref)
        dk_acc[...] = jnp.zeros_like(dk_acc)
        dv_acc[...] = jnp.zeros_like(dv_acc)
        for i, n in enumerate(order):
            w_ref[i, width:, :] = up_rows(ad_ref, 4 + n, n if n < 3 else 0, width)

    def rows(ref):
        return ref[...].reshape(ROWS, ref.shape[2])

    grad = rows(g3_ref)
    loads.ready(0)
    do_s[...] = one_back(
        grad.astype(BF16), rows(oc_ref), roc_ref[0], ad_ref, 11, w_ref.at[0], gw_ref, 14
    ).astype(BF16)
    q_s[...] = rows(qc_ref)
    count = 120
    carried = None
    for pair in range(PAIRS):
        win = window(pair)
        q_win, do_win = q_s[:, win], do_s[:, win]
        scores = nt(kp_ref[pair], q_win)
        grad_probs = nt(vp_ref[pair], do_win)
        all_probs, all_grads = [], []
        nothing = jnp.zeros((PAD - count, ROWS), F32)
        for sub in range(2):
            span = slice(PAD * sub, PAD * sub + count)
            row = 2 * pair + sub
            probs = jnp.exp2(scores[span] - statc_ref[0, row : row + 1, :])
            own = grad_probs[span]
            inner = jnp.sum(probs * own, 0, keepdims=True)
            all_probs += [probs, nothing]
            all_grads += [probs * (own - inner), nothing]
        probs = jnp.concatenate(all_probs, 0).astype(BF16)
        grad_scores = jnp.concatenate(all_grads, 0).astype(BF16)
        dk_acc[pair] += nn(grad_scores, q_win)
        dv_acc[pair] += nn(probs, do_win)
        out = tn(grad_scores, kp_ref[pair])
        low = out[:, :128]
        dq_s[:, tile(pair)] = ((low if carried is None else low + carried) * SCALE).astype(BF16)
        carried = out[:, 128:]
    dq_s[:, tile(PAIRS)] = (carried * SCALE).astype(BF16)
    loads.ready(1)
    grad = grad + one_back(
        dq_s[...], rows(u2_ref), rqc_ref[0], ad_ref, 8, w_ref.at[1], gw_ref, 8
    )
    loads.ready(2)
    do_s[...] = one_back(
        (mod_ref[2:3, :] * grad).astype(BF16), rows(o_ref), ro_ref[0], ad_ref, 7, w_ref.at[2], gw_ref, 6
    ).astype(BF16)
    q_s[...] = rows(q_ref)
    k_s[...] = rows(k_ref)
    v_s[...] = rows(v_ref)

    def put(index, values):
        dq_s[:, tile(index)] = (values[0] * SCALE).astype(BF16)
        dk_s[:, tile(index)] = (values[1] * LN2).astype(BF16)
        dv_s[:, tile(index)] = values[2].astype(BF16)

    attend_back(q_s, k_s, v_s, do_s, mask_ref, bias_ref, stat_ref.at[0], put)
    grad = grad + three_back(
        (dq_s, dk_s, dv_s), rows_of(u1_refs), rq_ref[0], ad_ref, 4, w_ref, loads, 3, gw_ref, 0
    )
    grad = grad.astype(BF16)
    share = ROWS // len(g1_refs)
    for k, ref in enumerate(g1_refs):
        ref[...] = grad[share * k : share * (k + 1)].reshape(ref.shape)


def tail_groups(cols):
    tail = cols - PAD
    return PAD // tail if 0 < tail < PAD and PAD % tail == 0 else 0


def packed_rows(blocks, cols):
    group = tail_groups(cols)
    if not group:
        return blocks * RANK, cols
    return (blocks + -(-blocks // group)) * RANK, PAD


def put_blocks(blocks, put):
    cols = blocks[0].shape[1]
    group = tail_groups(cols)
    for k, rows in enumerate(blocks):
        put(k, rows[:, :PAD] if group else rows)
    for k in range(0, len(blocks), group) if group else ():
        tails = [rows[:, PAD:] for rows in blocks[k : k + group]]
        missing = group - len(tails)
        if missing:
            tails.append(jnp.zeros((RANK, missing * (cols - PAD)), blocks[0].dtype))
        put(len(blocks) + k // group, jnp.concatenate(tails, 1))


def get_block(get, index, count, cols):
    group = tail_groups(cols)
    if not group:
        return get(index)
    at = (index % group) * (cols - PAD)
    return jnp.concatenate([get(index), get(count + index // group)[:, at : at + cols - PAD]], 1)


def pack_columns(table_ref, packed_ref, clips):
    parts = packed_ref.shape[0] // clips
    share = table_ref.shape[0] // parts
    cols = table_ref.shape[1] // clips
    for f in range(clips):
        for s in range(parts):
            piece = table_ref[share * s : share * (s + 1), cols * f : cols * (f + 1)].astype(BF16)
            blocks = [piece[block_rows(k)] for k in range(share // RANK)]

            def put(k, rows):
                packed_ref[f * parts + s, block_rows(k), :] = rows

            put_blocks(blocks, put)


def stacked(seq_ref, g1_refs, shares, whole_ref):
    parts = len(g1_refs) // shares
    places = whole_ref.shape[0] // parts
    at = 0
    for share in range(shares):
        refs = g1_refs[share * parts : (share + 1) * parts]
        size = refs[0].shape[1]
        for k, ref in enumerate(refs):
            start = pl.multiple_of(place_of(seq_ref, k, parts, places) + at, 16)
            whole_ref[pl.ds(start, size), :] = ref[0]
        at += size
    return whole_ref[...].astype(F32)


def spatial_backward(pieces, halves, clips, continued, last, seq_ref, *refs):
    g1_refs, refs = refs[:pieces], refs[pieces:]
    if continued:
        (_, before_ref), refs = refs[:2], refs[2:]
    (
        x_ref, q_ref, k_ref, v_ref, o_ref, stat_ref, rq_ref, ro_ref, mod_ref, mask_ref, ad_ref, w_hbm,
        d_ref, sums_ref, w_ref, gw_ref, do_s, sems,
    ) = refs
    width = x_ref.shape[2]
    loads = Loads([(w_hbm.at[3], w_ref.at[pl.ds(0, width), :])], sems)
    loads.start()

    @pl.when(loads.first)
    def _():
        gw_ref[...] = before_ref[...] if continued else jnp.zeros_like(gw_ref)
        w_ref[width:, :] = up_rows(ad_ref, 3, 0, width)

    grad = stacked(seq_ref, g1_refs, halves, do_s)
    loads.ready(0)
    do_s[...] = one_back(
        (mod_ref[2:3, :] * grad).astype(BF16), o_ref[0], ro_ref[0], ad_ref, 3, w_ref, gw_ref, 6
    ).astype(BF16)

    def put(index, values):
        for i, factor in enumerate((SCALE, LN2, 1.0)):
            value = values[i] if factor == 1.0 else values[i] * factor
            d_ref[0, :, width * i + 128 * index : width * i + 128 * index + 128] = value.astype(BF16)

    attend_back(
        q_ref.at[0], k_ref.at[0], v_ref.at[0], do_s, mask_ref, None, stat_ref.at[0], put
    )
    ranks = rq_ref[0]
    grad_ranks = None
    for i in range(3):
        grad = d_ref[0, :, width * i : width * (i + 1)]
        gw_ref[block_rows(2 * i + 1), :] += tn(ranks, grad)[block_rows(i)]
        part = nt(grad, up_rows(ad_ref, i, i, width))
        grad_ranks = part if grad_ranks is None else grad_ranks + part
    d_ref[0, :, 3 * width :] = grad_ranks.astype(BF16)
    normal, _ = normalize(x_ref[0].astype(F32))
    inputs = (normal * (1.0 + mod_ref[1:2, :]) + mod_ref[0:1, :]).astype(BF16)
    downs = tn(d_ref[0, :, 3 * width :], inputs)
    for i in range(3):
        gw_ref[block_rows(2 * i), :] += downs[block_rows(i)]

    @pl.when(pl.program_id(0) == pl.num_programs(0) - 1)
    def _():
        if last:
            pack_columns(gw_ref, sums_ref, clips)
        else:
            sums_ref[...] = gw_ref[...]


def spatial_input_grad(pieces, halves, seq_ref, *refs):
    g1_refs, refs = refs[:pieces], refs[pieces:]
    x_ref, d_ref, mod_ref, ad_ref, w_hbm, g0_ref, w_ref, whole_s, sems = refs
    width = x_ref.shape[2]
    loads = Loads(
        [(w_hbm.at[i], w_ref.at[:, pl.ds(i * width, width)]) for i in range(3)], sems
    )
    loads.start()

    @pl.when(loads.first)
    def _():
        w_ref[:, 3 * width :] = transposed_map(three_downs(ad_ref, 0))

    normal, inverse = normalize(x_ref[0].astype(F32))
    grad = stacked(seq_ref, g1_refs, halves, whole_s)
    for i in range(3):
        loads.ready(i)
    grad_in = nt(d_ref[0], w_ref[...])
    grad = grad + normalize_back(normal, inverse, grad_in * (1.0 + mod_ref[1:2, :]))
    g0_ref[0] = grad.astype(BF16)


def put_in_place(seq_ref, *refs):
    *pieces, out_ref = refs
    places = pieces[0].shape[1]
    for k, ref in enumerate(pieces):
        out_ref[0, pl.ds(place_of(seq_ref, k, len(pieces), places), places), :] = ref[0]


def pack_early(clips, shares, *refs):
    gw_refs, refs = refs[:shares], refs[shares:]
    dk_refs, refs = refs[:shares], refs[shares:]
    dv_refs, refs = refs[:shares], refs[shares:]
    *others, rk_ref, rv_ref, ctx_ref, mask_ref, ad_ref, packed_ref, table_ref, ctx_s = refs

    def added(each):
        total = each[0]
        for value in each[1:]:
            total = total + value
        return total

    at = gw_refs[0].shape[0]
    table_ref[:at, :] = added([ref[...] for ref in gw_refs])
    width = table_ref.shape[1]
    for ref in others:
        for k in range(ref.shape[1] // width):
            table_ref[at : at + RANK, :] = ref[:, k * width : (k + 1) * width]
            at += RANK
    table_ref[at:, :] = jnp.zeros((table_ref.shape[0] - at, width), F32)
    context = ctx_ref[...].astype(F32)
    for accs, factor, rank_ref, number, at in (
        (dk_refs, LN2, rk_ref, 9, 10),
        (dv_refs, 1.0, rv_ref, 10, 12),
    ):
        held = None
        for pair in range(PAIRS):
            whole = added([ref[pair] for ref in accs]) * factor
            out = whole[:PAD] * mask_ref[2 * pair : 2 * pair + 1, :].astype(F32)
            out = out + whole[PAD:] * mask_ref[2 * pair + 1 : 2 * pair + 2, :].astype(F32)
            low = out[:, :128]
            ctx_s[:, tile(pair)] = low if held is None else low + held
            held = out[:, 128:]
        ctx_s[:, tile(PAIRS)] = held
        grad_kv = ctx_s[...]
        grad_rank = lax.dot_general(
            grad_kv, ad_ref[2 * number + 1].astype(F32), (((1,), (1,)), ((), ())),
            precision=HIGHEST, preferred_element_type=F32,
        )
        table_ref[block_rows(at), :] = lax.dot_general(
            grad_rank, context, (((0,), (0,)), ((), ())),
            precision=HIGHEST, preferred_element_type=F32,
        )
        table_ref[block_rows(at + 1), :] = lax.dot_general(
            rank_ref[...].astype(F32), grad_kv, (((0,), (0,)), ((), ())),
            precision=HIGHEST, preferred_element_type=F32,
        )
    pack_columns(table_ref, packed_ref, clips)


def assemble(parts, seq_ref, *refs):
    early_refs, late_refs, refs = refs[:parts], refs[parts : 2 * parts], refs[2 * parts :]
    wide_ref, narrow_ref, early_ref, late_ref = refs
    for k in range(parts):
        source = lax.rem(seq_ref[0] + parts - k, parts)
        early_ref[source] = early_refs[k][...]
        late_ref[source] = late_refs[k][...]
    _, adapters, _, cols = wide_ref.shape
    times = narrow_ref.shape[3] // cols

    def block(ref, total, index, a):
        each = total // ref.shape[0]

        def get(k):
            return ref[index // each, a, block_rows(k), :].astype(F32)

        return get_block(get, index % each, each, cols)

    for a in range(adapters):
        for i in range(8):
            wide_ref[i, a] = block(late_ref, LATE_BLOCKS, i, a)
        for i in range(18):
            wide_ref[8 + i, a] = block(early_ref, EARLY_BLOCKS, i, a)
        for n in range(2):
            pieces = [block(early_ref, EARLY_BLOCKS, 18 + n * times + j, a) for j in range(times)]
            narrow_ref[n, a] = jnp.concatenate(pieces, 1)


def combine(index_ref, got_ref, out_ref, acc_ref):
    clips = index_ref.shape[0]
    parts = got_ref.shape[0] // clips
    acc_ref[...] = jnp.zeros_like(acc_ref)

    def step(f, carry):
        total = got_ref[f * parts].astype(F32)
        for s in range(1, parts):
            total = total + got_ref[f * parts + s].astype(F32)
        acc_ref[index_ref[f]] += total
        return carry

    lax.fori_loop(0, clips, step, 0)
    out_ref[...] = acc_ref[...].astype(BF16)


def pick(index_ref, wide_ref, narrow_ref, out_ref):
    count, _, _, cols = wide_ref.shape
    times = narrow_ref.shape[3] // cols

    def step(f, carry):
        a = index_ref[f]
        blocks = [wide_ref[k, a] for k in range(count)]
        for p in range(2):
            rows = narrow_ref[p, a]
            blocks += [rows[:, cols * j : cols * (j + 1)] for j in range(times)]

        def put(k, rows):
            out_ref[f, block_rows(k), :] = rows

        put_blocks(blocks, put)
        return carry

    lax.fori_loop(0, index_ref.shape[0], step, 0)


def unpick(count, cols, got_ref, out_ref):
    for k in range(count):
        pieces = []
        for f in range(got_ref.shape[0]):

            def get(index):
                return got_ref[f, block_rows(index), :]

            pieces.append(get_block(get, k, count, cols))
        out_ref[k] = jnp.concatenate(pieces, 1)


def whole_block(array):
    zeros = (0,) * array.ndim
    return pl.BlockSpec(array.shape, lambda i: zeros, pipeline_mode=pl.Buffered(1))


def anywhere():
    return pl.BlockSpec(memory_space=pl.ANY)


def like(shape, dtype):
    return jax.ShapeDtypeStruct(shape, dtype)


PARAMS = pltpu.CompilerParams(
    dimension_semantics=("arbitrary",), vmem_limit_bytes=VMEM_LIMIT
)


def cost(flops, read, part=4):
    return pl.CostEstimate(
        flops=flops // part, bytes_accessed=read // part, transcendentals=0
    )


def run_spatial_forward(seq, video, mods, masks, wide, w_s, parts):
    frames, rows, d = video.shape
    places = rows // parts
    by_frame = lambda i: (i, 0, 0)
    row_block = pl.BlockSpec((1, rows, d), by_frame)
    return pl.pallas_call(
        spatial_forward,
        grid=(frames,),
        in_specs=[in_smem(), row_block, whole_block(mods), whole_block(masks), whole_block(wide), anywhere()],
        out_specs=[pl.BlockSpec((1, places, d), by_frame)] * parts
        + [
            row_block,
            row_block,
            row_block,
            row_block,
            pl.BlockSpec((1, HEADS, rows), by_frame),
            pl.BlockSpec((1, rows, 3 * RANK), by_frame),
            pl.BlockSpec((1, rows, RANK), by_frame),
        ],
        out_shape=[like((frames, places, d), BF16)] * parts
        + [like(video.shape, BF16)] * 4
        + [
            like((frames, HEADS, rows), F32),
            like((frames, rows, 3 * RANK), BF16),
            like((frames, rows, RANK), BF16),
        ],
        scratch_shapes=[
            pltpu.VMEM((4, d + PAD, d), BF16),
            pltpu.VMEM((ROWS, d + PAD), BF16),
            pltpu.VMEM((ROWS, d), BF16),
            pltpu.SemaphoreType.DMA((4,)),
        ],
        compiler_params=PARAMS,
        cost_estimate=cost(10 * frames * rows * d * d, 30_000_000),
        name="spatial_forward",
    )(seq, video, mods, masks, wide, w_s)


def run_temporal_forward(x1, mods, masks, wide, w_t):
    parts = len(x1)
    own_frames, places, d = x1[0].shape
    frames = own_frames * parts
    groups = places * frames // ROWS
    each = ROWS // frames
    across = pl.BlockSpec((frames, each, d), lambda i: (0, i, 0))
    by_group = lambda i: (i, 0, 0)
    act = like((frames, places, d), BF16)

    def body(*refs):
        temporal_forward(parts, *refs)

    return pl.pallas_call(
        body,
        grid=(groups,),
        in_specs=[pl.BlockSpec((own_frames, each, d), lambda i: (0, i, 0))] * parts
        + [whole_block(mods), whole_block(masks), whole_block(wide), anywhere()],
        out_specs=[across] * 4
        + [
            pl.BlockSpec((1, HEADS, ROWS), by_group),
            pl.BlockSpec((1, ROWS, 3 * RANK), by_group),
            pl.BlockSpec((1, ROWS, RANK), by_group),
            across,
            across,
        ],
        out_shape=[act] * 4
        + [
            like((groups, HEADS, ROWS), F32),
            like((groups, ROWS, 3 * RANK), BF16),
            like((groups, ROWS, RANK), BF16),
            act,
            like((frames, places, d), F32),
        ],
        scratch_shapes=[pltpu.VMEM((4, d + PAD, d), BF16), pltpu.VMEM((ROWS, ROWS), F32)]
        + [pltpu.VMEM((ROWS, d + PAD), BF16)]
        + [pltpu.VMEM((ROWS, d), BF16)] * 3
        + [pltpu.SemaphoreType.DMA((4,))],
        compiler_params=PARAMS,
        cost_estimate=cost(10 * places * frames * d * d, 30_000_000),
        name="temporal_forward",
    )(*x1, mods, masks, wide, w_t)


def run_cross_forward(x2, context, masks, wide, w_c):
    frames, places, d = x2.shape
    groups = places * frames // ROWS
    across = pl.BlockSpec((frames, ROWS // frames, d), lambda i: (0, i, 0))
    by_group = lambda i: (i, 0, 0)
    full = lambda *shape: pl.BlockSpec(shape, lambda i: (0,) * len(shape))
    one = pl.BlockSpec((1, ROWS, RANK), by_group)
    one_shape = like((groups, ROWS, RANK), BF16)
    act = like((frames, places, d), BF16)
    return pl.pallas_call(
        cross_forward,
        grid=(groups,),
        in_specs=[across, whole_block(context), whole_block(masks), whole_block(wide), anywhere()],
        out_specs=[across] * 2 + [pl.BlockSpec((1, HEADS, ROWS), by_group), one, one]
        + [full(PAIRS, 2 * PAD, 256)] * 2 + [full(PAD, RANK)] * 2 + [across],
        out_shape=[act] * 2 + [like((groups, HEADS, ROWS), F32), one_shape, one_shape]
        + [like((PAIRS, 2 * PAD, 256), BF16)] * 2 + [like((PAD, RANK), BF16)] * 2
        + [like(x2.shape, F32)],
        scratch_shapes=[pltpu.VMEM((4, d + PAD, d), BF16), pltpu.VMEM((ROWS, d + PAD), BF16)]
        + [pltpu.VMEM((ROWS, d), BF16), pltpu.VMEM((PAD, d), BF16)]
        + [pltpu.SemaphoreType.DMA((4,))],
        compiler_params=PARAMS,
        cost_estimate=cost(8 * places * frames * d * d, 30_000_000),
        name="cross_forward",
    )(x2, context, masks, wide, w_c)


def in_smem():
    return pl.BlockSpec(memory_space=pltpu.SMEM)


def run_feed_forward_grad(cot, mods, maps, order, pieces):
    tokens, d = cot.shape
    chunks = len(pieces) // 2

    def body(*refs):
        feed_forward_grad(len(pieces), *refs)

    return pl.pallas_call(
        body,
        grid=(tokens // ROWS,),
        in_specs=[in_smem(), pl.BlockSpec((ROWS, d), lambda i: (i, 0)), whole_block(mods), whole_block(maps)]
        + [anywhere()] * len(pieces),
        out_specs=pl.BlockSpec((chunks, ROWS, d), lambda i: (0, i, 0)),
        out_shape=like((chunks, tokens, d), BF16),
        scratch_shapes=[
            pltpu.VMEM((chunks * d, d + PAD), BF16),
            pltpu.VMEM((ROWS, d + PAD), BF16),
            pltpu.SemaphoreType.DMA((len(pieces),)),
        ],
        compiler_params=PARAMS,
        cost_estimate=cost(2 * tokens * d * d * chunks, 20_000_000),
        name="feed_forward_grad",
    )(order, cot, mods, maps, *pieces)


def run_feed_forward(x3, cot, order, grad_active, pieces, mods, maps, up):
    tokens, d = x3.shape
    chunks = up.shape[0]
    late = len(pieces) // 2
    rows = pl.BlockSpec((ROWS, d), lambda i: (i, 0))
    wide_rows = pl.BlockSpec((ROWS, chunks * d), lambda i: (i, 0))
    more = [pltpu.VMEM((late * d, d + PAD), BF16), pltpu.VMEM((ROWS, d + PAD), BF16)] if late else []

    def body(*refs):
        feed_forward(len(grad_active), len(pieces), *refs)

    return pl.pallas_call(
        body,
        grid=(tokens // ROWS,),
        in_specs=[in_smem(), rows, rows]
        + [pl.BlockSpec((g.shape[0], ROWS, d), lambda i: (0, i, 0)) for g in grad_active]
        + [anywhere()] * len(pieces)
        + [whole_block(mods), whole_block(maps), anywhere()],
        out_specs=[
            wide_rows,
            rows,
            pl.BlockSpec((RANK, d), lambda i: (0, 0)),
            pl.BlockSpec((RANK, chunks * d), lambda i: (0, 0)),
        ],
        out_shape=[
            like((tokens, chunks * d), BF16),
            like((tokens, d), F32),
            like((RANK, d), F32),
            like((RANK, chunks * d), F32),
        ],
        scratch_shapes=[
            pltpu.VMEM((d + PAD, chunks * d), BF16),
            pltpu.VMEM((ROWS, d + PAD), BF16),
            pltpu.VMEM((ROWS, chunks * d), BF16),
            pltpu.SemaphoreType.DMA((chunks + len(pieces),)),
            *more,
        ],
        compiler_params=PARAMS,
        cost_estimate=cost(4 * tokens * d * d * chunks, 50_000_000),
        name="feed_forward",
    )(order, x3, cot, *grad_active, *pieces, mods, maps, up)


def run_feed_forward_out(active, x3, cot, mods, maps, down, parts, half, halves):
    tokens, d = x3.shape
    order, *pieces = down
    hidden = active.shape[1]
    share = tokens // parts
    parts = parts // halves
    steps = tokens // ROWS // halves
    start = half * steps

    def body(*refs):
        feed_forward_out(len(pieces), *refs)

    rows = pl.BlockSpec((ROWS, d), lambda i: (i + start, 0))
    return pl.pallas_call(
        body,
        grid=(steps,),
        in_specs=[
            in_smem(),
            pl.BlockSpec((ROWS, hidden), lambda i: (i + start, 0)),
            rows,
            rows,
            whole_block(mods),
            whole_block(maps),
        ]
        + [anywhere()] * len(pieces),
        out_specs=[pl.BlockSpec((share, d), lambda i: (0, 0))] * parts
        + [
            pl.BlockSpec((RANK, d), lambda i: (0, 0)),
            pl.BlockSpec((RANK, hidden), lambda i: (0, 0)),
        ],
        out_shape=[like((share, d), BF16)] * parts
        + [
            like((RANK, d), F32),
            like((RANK, hidden), F32),
        ],
        scratch_shapes=[
            pltpu.VMEM((hidden, d + PAD), BF16),
            pltpu.SemaphoreType.DMA((len(pieces),)),
        ],
        compiler_params=PARAMS,
        cost_estimate=cost(2 * steps * ROWS * d * hidden, 20_000_000, 64),
        name="feed_forward_out",
    )(order, active, x3, cot, mods, maps, *pieces)


def run_cross_temporal_backward(g3, u1, saved, mods, masks, wide, w_tc, start, groups):
    parts = len(u1)
    own_frames, places, d = u1[0].shape
    frames = own_frames * parts
    each = ROWS // frames
    across = pl.BlockSpec((frames, ROWS // frames, d), lambda i: (0, i + start, 0))
    by_group = lambda i: (i + start, 0, 0)
    stat = pl.BlockSpec((1, HEADS, ROWS), by_group)
    three = pl.BlockSpec((1, ROWS, 3 * RANK), by_group)
    one = pl.BlockSpec((1, ROWS, RANK), by_group)
    kp, vp = saved[13:15]
    pair_sums = pl.BlockSpec((PAIRS, 2 * PAD, 256), lambda i: (0, 0, 0))

    def body(*refs):
        cross_temporal_backward(parts, *refs)

    return pl.pallas_call(
        body,
        grid=(groups,),
        in_specs=[pl.BlockSpec((own_frames, each, d), lambda i: (0, i + start, 0))] * parts
        + [across] + [across] * 4 + [stat, three, one] + [across] * 3 + [stat, one, one]
        + [whole_block(kp), whole_block(vp)]
        + [whole_block(mods), whole_block(masks), whole_block(wide), anywhere()],
        out_specs=[pl.BlockSpec((own_frames, each, d), lambda i: (0, i, 0))] * parts
        + [
            pl.BlockSpec((16 * RANK, d), lambda i: (0, 0)),
            pair_sums,
            pair_sums,
        ],
        out_shape=[like((own_frames, groups * each, d), BF16)] * parts
        + [like((16 * RANK, d), F32)]
        + [like((PAIRS, 2 * PAD, 256), F32)] * 2,
        scratch_shapes=[
            pltpu.VMEM((6, d + PAD, d), BF16),
            pltpu.VMEM((ROWS, ROWS), F32),
        ]
        + [pltpu.VMEM((ROWS, d), BF16)] * 7
        + [pltpu.SemaphoreType.DMA((6,))],
        compiler_params=PARAMS,
        cost_estimate=cost(14 * groups * ROWS * d * d, 30_000_000, 64),
        name="cross_temporal_backward",
    )(*u1, g3, *saved[:15], mods, masks, wide, w_tc)


LATE_BLOCKS = 8
EARLY_BLOCKS = 28


def run_spatial_backward(seq, g1, halves, video, saved, mods, masks, wide, w_s, clips, start, count, before):
    frames, rows, d = video.shape
    parts = len(g1) // halves
    by_frame = lambda i: (i + start, 0, 0)
    row_block = pl.BlockSpec((1, rows, d), by_frame)
    last = start + count == frames
    sums = (8 * RANK, d)
    if last:
        sums = (clips * parts, *packed_rows(LATE_BLOCKS // parts, d // clips))
    zeros = (0,) * len(sums)

    def body(*refs):
        spatial_backward(len(g1), halves, clips, bool(before), last, *refs)

    extra = [anywhere(), whole_block(before[1])] if before else []
    return pl.pallas_call(
        body,
        grid=(count,),
        in_specs=[in_smem()] + [pl.BlockSpec((1, g.shape[1], d), by_frame) for g in g1]
        + extra
        + [row_block] * 5
        + [
            pl.BlockSpec((1, HEADS, rows), by_frame),
            pl.BlockSpec((1, rows, 3 * RANK), by_frame),
            pl.BlockSpec((1, rows, RANK), by_frame),
            whole_block(mods),
            whole_block(masks),
            whole_block(wide),
            anywhere(),
        ],
        out_specs=[
            pl.BlockSpec((1, rows, 3 * d + PAD), by_frame),
            pl.BlockSpec(sums, lambda i: zeros),
        ],
        out_shape=[like((frames, rows, 3 * d + PAD), BF16), like(sums, BF16 if last else F32)],
        input_output_aliases={1 + len(g1): 0} if before else {},
        scratch_shapes=[pltpu.VMEM((d + PAD, d), BF16), pltpu.VMEM((LATE_BLOCKS * RANK, d), F32)]
        + [pltpu.VMEM((ROWS, d), BF16), pltpu.SemaphoreType.DMA((1,))],
        compiler_params=PARAMS,
        cost_estimate=cost(6 * count * rows * d * d, 20_000_000, 64),
        name="spatial_backward",
    )(seq, *g1, *before, video, *saved, mods, masks, wide, w_s)


def run_spatial_input_grad(seq, g1, halves, video, grads, mods, wide, w_s):
    frames, rows, d = video.shape
    by_frame = lambda i: (i, 0, 0)
    row_block = pl.BlockSpec((1, rows, d), by_frame)

    def body(*refs):
        spatial_input_grad(len(g1), halves, *refs)

    return pl.pallas_call(
        body,
        grid=(frames,),
        in_specs=[in_smem()] + [pl.BlockSpec((1, g.shape[1], d), by_frame) for g in g1]
        + [
            row_block,
            pl.BlockSpec((1, rows, grads.shape[2]), by_frame),
            whole_block(mods),
            whole_block(wide),
            anywhere(),
        ],
        out_specs=row_block,
        out_shape=like(video.shape, BF16),
        scratch_shapes=[
            pltpu.VMEM((d, 3 * d + PAD), BF16),
            pltpu.VMEM((ROWS, d), BF16),
            pltpu.SemaphoreType.DMA((3,)),
        ],
        compiler_params=PARAMS,
        cost_estimate=cost(6 * frames * rows * d * d, 20_000_000, 64),
        name="spatial_input_grad",
    )(seq, *g1, video, grads, mods, wide, w_s)


def run_put_in_place(seq, pieces):
    frames, places, d = pieces[0].shape
    by_frame = lambda i: (i, 0, 0)
    rows = places * len(pieces)
    return pl.pallas_call(
        put_in_place,
        grid=(frames,),
        in_specs=[in_smem()] + [pl.BlockSpec((1, places, d), by_frame)] * len(pieces),
        out_specs=pl.BlockSpec((1, rows, d), by_frame),
        out_shape=like((frames, rows, d), BF16),
        compiler_params=PARAMS,
        cost_estimate=cost(0, 4 * frames * rows * d, 64),
        name="put_in_place",
    )(seq, *pieces)


PLAIN = pltpu.CompilerParams(vmem_limit_bytes=VMEM_LIMIT)


def in_vmem():
    return pl.BlockSpec(memory_space=pltpu.VMEM)


def run_pack_early(gw, dk, dv, sources, clips, parts):
    d = gw[0].shape[1]
    packed = (clips * parts, *packed_rows(EARLY_BLOCKS // parts, d // clips))

    def body(*refs):
        pack_early(clips, len(gw), *refs)

    return pl.pallas_call(
        body,
        out_shape=like(packed, BF16),
        scratch_shapes=[pltpu.VMEM((EARLY_BLOCKS * RANK, d), F32), pltpu.VMEM((PAD, d), F32)],
        compiler_params=PLAIN,
        cost_estimate=cost(50000000, 8000000, 64),
        name="pack_early",
    )(*gw, *dk, *dv, *sources)


def run_assemble(seq, early, late, wide_shape, narrow_shape):
    parts = len(early)

    def body(*refs):
        assemble(parts, *refs)

    return pl.pallas_call(
        body,
        in_specs=[in_smem()] + [in_vmem()] * (2 * parts),
        out_specs=[in_vmem()] * 2,
        out_shape=[like(wide_shape, F32), like(narrow_shape, F32)],
        scratch_shapes=[pltpu.VMEM((parts, *piece.shape), BF16) for piece in (early[0], late[0])],
        compiler_params=PLAIN,
        cost_estimate=cost(0, 6_000_000, 64),
        name="assemble",
    )(seq, *early, *late)


def run_pick(all_index, wide, narrow):
    count, _, _, cols = wide.shape
    shape = packed_rows(count + 2 * (narrow.shape[3] // cols), cols)
    return pl.pallas_call(
        pick,
        in_specs=[in_smem(), in_vmem(), in_vmem()],
        out_specs=in_vmem(),
        out_shape=like((all_index.shape[0], *shape), BF16),
        compiler_params=PLAIN,
        cost_estimate=cost(0, 3000000),
        name="pick",
    )(all_index, wide, narrow)


def run_unpick(got, blocks, cols):
    def body(*refs):
        unpick(blocks, cols, *refs)

    return pl.pallas_call(
        body,
        in_specs=[in_vmem()],
        out_specs=in_vmem(),
        out_shape=like((blocks, RANK, got.shape[0] * cols), BF16),
        compiler_params=PLAIN,
        cost_estimate=cost(0, 2500000),
        name="unpick",
    )(got)


def run_combine(all_index, got, adapters):
    _, share, cols = got.shape
    return pl.pallas_call(
        combine,
        in_specs=[pl.BlockSpec(memory_space=pltpu.SMEM), pl.BlockSpec(memory_space=pltpu.VMEM)],
        out_specs=pl.BlockSpec(memory_space=pltpu.VMEM),
        out_shape=like((adapters, share, cols), BF16),
        scratch_shapes=[pltpu.VMEM((adapters, share, cols), F32)],
        compiler_params=pltpu.CompilerParams(vmem_limit_bytes=VMEM_LIMIT),
        cost_estimate=cost(0, 1000000, 64),
        name="combine",
    )(all_index, got)


def exchange(array, axes="seq"):
    return lax.all_to_all(array, axes, split_axis=0, concat_axis=0, tiled=True)


def up_chunks(up, clips, times):
    rows, hidden = up.shape
    cols = hidden // (clips * times)
    return up.reshape(rows, clips, times, cols).transpose(2, 0, 1, 3).reshape(times, rows, -1)


def gather(array):
    return lax.all_gather(array, "fsdp", axis=1, tiled=True)


def send(array, axis, shift):
    size = lax.axis_size(axis)
    return lax.ppermute(array, axis, [(i, (i + shift) % size) for i in range(size)])


def to_places(pieces):
    return [pieces[0]] + [send(pieces[k], "seq", k) for k in range(1, len(pieces))]


def to_frames(pieces):
    return [pieces[0]] + [send(pieces[k], "seq", -k) for k in range(1, len(pieces))]


def gather_spatial_and_down(spatial, down, parts, times, clips, d):
    if times != parts or clips % 2:
        return gather(spatial)
    own = lax.dynamic_slice_in_dim(down.reshape(times, -1, d), lax.axis_index("seq"), 1, 0)
    return gather(jnp.concatenate([spatial, own], 0))


def start_down(got, parts, times, clips, d):
    if times != parts or clips % 2:
        return None
    half = d // 2
    core = lax.axis_index("fsdp") % 2
    first = lax.dynamic_slice(got, (times, core * half, 0), (1, half, d))[0]
    other = lax.dynamic_slice(got, (times, (1 - core) * half, 0), (1, half, d))[0]
    return first, other, send(first, "seq", 1), send(first, "seq", -1)


def swap_cores(piece, clips):
    return lax.ppermute(piece, "fsdp", [(i, i ^ 1) for i in range(clips)])


def to_all(piece):
    return [piece] + [send(piece, "seq", k) for k in range(1, lax.axis_size("seq"))]


def down_order(times, parts, clips):
    if times != parts or clips % 2:
        return jnp.arange(times, dtype=jnp.int32), jnp.zeros((1,), jnp.int32)
    seq = lax.axis_index("seq")
    core = lax.axis_index("fsdp") % 2
    return ((seq - jnp.arange(parts)) % parts).astype(jnp.int32), core.astype(jnp.int32)[None]


def on_device(
    video,
    context,
    modulation,
    adapter_index,
    cotangent,
    qkv_weights,
    out_weights,
    ffn_up,
    ffn_down,
    adapt_wide,
    adapt_ff,
):
    parts = lax.axis_size("seq")
    clips = lax.axis_size("fsdp")
    d = video.shape[-1]
    count, adapters, _, cols = adapt_wide.shape[1:]
    times = adapt_ff.shape[-1] // cols
    places = SPATIAL // parts
    frames = FRAMES // parts
    half_d = d // 2
    mods = modulation[0, 0]
    masks = head_masks()
    ctx = jnp.pad(context[0], ((0, PAD - context.shape[1]), (0, 0)))

    def attention_weights(j):
        return jnp.concatenate([qkv_weights[0, 3 * j : 3 * j + 3], out_weights[0, j : j + 1]], 0)

    seq = lax.axis_index("seq").astype(jnp.int32)[None]
    all_index = exchange(jnp.broadcast_to(adapter_index, (clips,)), "fsdp")
    w_s = gather_spatial_and_down(attention_weights(0), ffn_down[0], parts, times, clips, d)
    picked = run_pick(all_index, adapt_wide[0], adapt_ff[0])
    wide = run_unpick(exchange(picked, "fsdp"), count + 2 * times, cols)
    w_tc = gather(jnp.concatenate([attention_weights(1), attention_weights(2)], 0))
    ffn_up, _ = lax.optimization_barrier((ffn_up, picked))
    up = gather(up_chunks(ffn_up[0], clips, times))
    cot = cotangent.reshape(frames, SPATIAL, d)
    cot = to_places(
        [
            lax.dynamic_slice_in_dim(cot, (seq[0] + k) % parts * places, places, 1)
            for k in range(parts)
        ]
    )
    frames_in = video.reshape(frames, SPATIAL, d)
    maps_f = wide[24:]
    order, core = down_order(times, parts, clips)
    packed_order = jnp.concatenate([order, core])
    if times == parts and clips % 2 == 0:
        packed_order = jnp.concatenate([order[:2], order[parts - 1 :], order[2 : parts - 1], core])
    w_s, wide, maps_f, packed_order, *cot = lax.optimization_barrier((w_s, wide, maps_f, packed_order, *cot))
    started = start_down(w_s, parts, times, clips, d)
    cot = jnp.concatenate(cot, 0).reshape(FRAMES * places, d)
    made = run_spatial_forward(seq, frames_in, mods, masks, wide, w_s, parts)
    u1, kept_s = to_places(made[:parts]), made[parts:]
    if started is None:
        whole_down = gather(ffn_down[0].reshape(times, -1, d))
        sides = [[whole_down[i, :half_d] for i in range(times)], [whole_down[i, half_d:] for i in range(times)]]
        *kept_t, x2 = run_temporal_forward(u1, mods, masks, wide, w_tc)
        *kept_c, x3 = run_cross_forward(x2, ctx, masks, wide, w_tc)
        late_pieces = []
        grad_active = [run_feed_forward_grad(cot, mods, maps_f, packed_order, sides[0] + sides[1])]
    else:
        first, other, second, third = started
        second, third, cot, x1_own = lax.optimization_barrier((second, third, cot, u1[0]))
        mine = [first, second, third]
        others = [other] + [swap_cores(piece, clips) for piece in mine[1:]]
        early_order = jnp.concatenate([packed_order[:3], core])
        grad_active = run_feed_forward_grad(cot, mods, maps_f, early_order, mine + others)
        second, grad_active, *u1 = lax.optimization_barrier((second, grad_active, x1_own, *u1[1:]))
        rest = [send(second, "seq", 1)] + [send(first, "seq", k) for k in range(3, parts - 1)]
        *kept_t, x2 = run_temporal_forward(u1, mods, masks, wide, w_tc)
        x2, *rest = lax.optimization_barrier((x2, *rest))
        rest_others = [swap_cores(piece, clips) for piece in rest]
        *kept_c, x3 = run_cross_forward(x2, ctx, masks, wide, w_tc)
        grad_active = [grad_active]
        late_pieces = rest + rest_others
        sides = [mine + rest, others + rest_others]
    down = [packed_order, *sides[0], *sides[1]]
    x3 = x3.reshape(FRAMES * places, d)
    active, g3, grad_a24, grad_b24 = run_feed_forward(
        x3, cot, packed_order, grad_active, late_pieces, mods, maps_f, up
    )
    g3 = g3.reshape(FRAMES, places, d)
    groups = FRAMES * places // ROWS
    saved = kept_t + kept_c
    *x4, grad_b25, grad_down = run_feed_forward_out(
        active, x3, cot, mods, maps_f, down, parts, 0, 1
    )
    x4[0], g3 = lax.optimization_barrier((x4[0], g3))
    output = to_frames([piece.reshape(frames, places, d) for piece in x4])
    shares = [groups - 1, 1] if groups > 1 else [1]
    g1, gw, dk, dv = [], [], [], []
    for share, size in enumerate(shares):
        *pieces, gw_part, dk_part, dv_part = run_cross_temporal_backward(
            g3, u1, saved, mods, masks, wide, w_tc, sum(shares[:share]), size
        )
        gw.append(gw_part)
        dk.append(dk_part)
        dv.append(dv_part)
        pieces[0], g3 = lax.optimization_barrier((pieces[0], g3))
        if share == 0:
            g3, *output = lax.optimization_barrier((g3, *output))
        g1.append(to_frames(pieces))
    sources = [grad_a24, grad_b25, grad_b24, grad_down, kept_c[7], kept_c[8], ctx, masks, wide]
    packed = run_pack_early(gw, dk, dv, sources, clips, parts)
    g1 = [piece for done in g1 for piece in done]
    packed, *g1 = lax.optimization_barrier((packed, *g1))
    got = exchange(packed, ("fsdp", "seq"))
    halves = len(shares)
    before = []
    spatial = [frames - frames // 2, frames // 2] if frames > 1 else [1]
    for turn, size in enumerate(spatial):
        grads, sums = before = run_spatial_backward(
            seq, g1, halves, frames_in, kept_s, mods, masks, wide, w_s, clips, sum(spatial[:turn]), size, before
        )
        if turn == 0:
            got, sums = lax.optimization_barrier((got, sums))
            table = run_combine(all_index, got, adapters)
            if len(spatial) > 1:
                table, sums = lax.optimization_barrier((table, sums))
            early = to_all(table)
        before = [grads, sums]
    packed, *early = lax.optimization_barrier((sums, *early))
    g0 = run_spatial_input_grad(seq, g1, halves, frames_in, grads, mods, wide, w_s)
    got, g0 = lax.optimization_barrier((exchange(packed, ("fsdp", "seq")), g0))
    late = run_combine(all_index, got, adapters)
    wide_out, narrow_out = run_assemble(
        seq, early, to_all(late), adapt_wide.shape[1:], adapt_ff.shape[1:]
    )
    output = run_put_in_place(seq, output).reshape(video.shape)
    return (output, g0.reshape(video.shape), wide_out[None], narrow_out[None])


def solution(mesh):
    return jax.shard_map(
        on_device,
        mesh=mesh,
        in_specs=(
            P("fsdp", "seq", None),
            P("fsdp", None, None),
            P("fsdp", None, None, None),
            P("fsdp"),
            P("fsdp", "seq", None),
            P(None, None, "fsdp", None),
            P(None, None, "fsdp", None),
            P(None, "fsdp", None),
            P(None, "fsdp", None),
            P(None, None, None, None, "fsdp"),
            P(None, None, None, None, "fsdp"),
        ),
        out_specs=(
            P("fsdp", "seq", None),
            P("fsdp", "seq", None),
            P(None, None, None, None, "fsdp"),
            P(None, None, None, None, "fsdp"),
        ),
        check_vma=False,
    )
```

```python
import math

import jax
import jax.numpy as jnp
from jax import lax
from jax.experimental import pallas as pl
from jax.experimental.pallas import tpu as pltpu
from jax.sharding import PartitionSpec as P

HEAD_DIM = 72
HEADS = 16
FRAMES = 16
SPATIAL = 256
RANK = 16
ROWS = 256
PAIRS = HEADS // 2
PAD = 128
SCALE = HEAD_DIM ** (-0.5)
EXP_SCALE = SCALE * math.log2(math.e)
LN2 = math.log(2.0)
HIGHEST = lax.Precision.HIGHEST
F32 = jnp.float32
BF16 = jnp.bfloat16
VMEM_LIMIT = 60 * 1024 * 1024


def nn(left, right):
    return lax.dot_general(left, right, (((1,), (0,)), ((), ())), preferred_element_type=F32)


def nt(left, right):
    return lax.dot_general(left, right, (((1,), (1,)), ((), ())), preferred_element_type=F32)


def tn(left, right):
    return lax.dot_general(left, right, (((0,), (0,)), ((), ())), preferred_element_type=F32)


def window(pair):
    return slice(128 * pair, 128 * pair + 256)


def normalize(stream):
    average = jnp.mean(stream, -1, keepdims=True)
    centred = stream - average
    inverse = lax.rsqrt(jnp.mean(centred * centred, -1, keepdims=True) + 1e-06)
    return centred * inverse, inverse


def normalize_back(normal, inverse, grad):
    mean_grad = jnp.mean(grad, -1, keepdims=True)
    mean_both = jnp.mean(grad * normal, -1, keepdims=True)
    return inverse * (grad - mean_grad - normal * mean_both)


def up_rows(ad_ref, number, slot, width):
    rows = ad_ref[2 * number + 1]
    before = jnp.zeros((RANK * slot, width), BF16)
    after = jnp.zeros((PAD - RANK * (slot + 1), width), BF16)
    return jnp.concatenate(([before] if slot else []) + [rows, after], 0)


def three_downs(ad_ref, number):
    return jnp.concatenate([ad_ref[2 * (number + i)] for i in range(3)], 0)


class Loads:
    def __init__(self, entries, sems):
        self.first = pl.program_id(0) == 0
        self.entries = entries
        self.sems = sems

    def copy(self, index):
        source, target = self.entries[index]
        return pltpu.make_async_copy(source, target, self.sems.at[index])

    def start(self):
        @pl.when(self.first)
        def _():
            for index in range(len(self.entries)):
                self.copy(index).start()

    def ready(self, index):
        @pl.when(self.first)
        def _():
            self.copy(index).wait()


def head_masks():
    lane = jnp.arange(256)[None, :]
    begin = jnp.array([16 * (h // 2) + HEAD_DIM * (h % 2) for h in range(HEADS)])[:, None]
    return ((lane >= begin) & (lane < begin + HEAD_DIM)).astype(BF16)


def same_place(shape):
    rows = lax.broadcasted_iota(jnp.int32, shape, 0)
    cols = lax.broadcasted_iota(jnp.int32, shape, 1)
    return jnp.where(rows % 16 == cols % 16, 0.0, -1e30).astype(F32)


def attend(q_ref, k_ref, v_ref, mask_ref, bias, put_out, stat_ref):
    carried = None
    for pair in range(PAIRS):
        win = window(pair)
        q_win, k_win, v_win = q_ref[:, win], k_ref[:, win], v_ref[:, win]
        all_weights, all_values = [], []
        for head in (2 * pair, 2 * pair + 1):
            mask = mask_ref[head : head + 1, :]
            scores = nt(k_win * mask, q_win)
            if bias is not None:
                scores = scores + bias[...]
            top = jnp.max(scores, 0, keepdims=True)
            grown = jnp.exp2(scores - top)
            total = jnp.sum(grown, 0, keepdims=True)
            stat_ref[head : head + 1, :] = top + jnp.log2(total)
            all_weights.append((grown * (1.0 / total)).astype(BF16))
            all_values.append(v_win * mask)
        out = tn(jnp.concatenate(all_weights, 0), jnp.concatenate(all_values, 0))
        low = out[:, :128]
        put_out(pair, low if carried is None else low + carried)
        carried = out[:, 128:]
    put_out(PAIRS, carried)


def attend_back(q_ref, k_ref, v_ref, do_ref, mask_ref, bias, stat_ref, put):
    carried = None
    for pair in range(PAIRS):
        win = window(pair)
        q_win, k_win, v_win, do_win = q_ref[:, win], k_ref[:, win], v_ref[:, win], do_ref[:, win]
        all_grads, all_probs, keys, queries, outs = [], [], [], [], []
        for head in (2 * pair, 2 * pair + 1):
            mask = mask_ref[head : head + 1, :]
            k_own = k_win * mask
            scores = nt(k_own, q_win)
            if bias is not None:
                scores = scores + bias[...]
            probs = jnp.exp2(scores - stat_ref[head : head + 1, :])
            grad_probs = nt(v_win * mask, do_win)
            inner = jnp.sum(probs * grad_probs, 0, keepdims=True)
            all_grads.append((probs * (grad_probs - inner)).astype(BF16))
            all_probs.append(probs.astype(BF16))
            keys.append(k_own)
            queries.append(q_win * mask)
            outs.append(do_win * mask)
        grads = (
            tn(jnp.concatenate(all_grads, 0), jnp.concatenate(keys, 0)),
            nn(jnp.concatenate(all_grads, 1), jnp.concatenate(queries, 0)),
            nn(jnp.concatenate(all_probs, 1), jnp.concatenate(outs, 0)),
        )
        lows = tuple(g[:, :128] for g in grads)
        if carried is not None:
            lows = tuple(a + b for a, b in zip(lows, carried))
        put(pair, lows)
        carried = tuple(g[:, 128:] for g in grads)
    put(PAIRS, carried)


def tile(index):
    return slice(128 * index, 128 * index + 128)


def three_projections(lhs_ref, ad_ref, number, weights, loads, first_load, outs, rank_ref):
    width = weights.shape[2]
    ranks = nt(lhs_ref[:, :width], three_downs(ad_ref, number)).astype(BF16)
    rank_ref[...] = ranks
    lhs_ref[:, width : width + 3 * RANK] = ranks
    for i in range(3):
        loads.ready(first_load + i)
        total = nn(lhs_ref[...], weights[first_load + i])
        outs[i][...] = (total * EXP_SCALE if i == 0 else total).astype(BF16)


def one_projection(lhs_ref, ad_ref, number, weight_ref, rank_ref):
    width = weight_ref.shape[1]
    ranks = nt(lhs_ref[:, :width], ad_ref[2 * number]).astype(BF16)
    rank_ref[...] = ranks
    lhs_ref[:, width : width + RANK] = ranks
    return nn(lhs_ref[...], weight_ref[...])


def block_rows(index):
    return slice(RANK * index, RANK * (index + 1))


def one_back(grad, kept, ranks, ad_ref, number, weight_ref, grad_ref, at):
    width = weight_ref.shape[1]
    both = nt(grad, weight_ref[...])
    grad_rank = both[:, width : width + RANK].astype(BF16)
    grad_ref[block_rows(at), :] += tn(grad_rank, kept)
    grad_ref[block_rows(at + 1), :] += tn(ranks, grad)
    return both[:, :width] + nn(grad_rank, ad_ref[2 * number])


def three_back(grads, inputs, ranks, ad_ref, number, weights, loads, first_load, grad_ref, at):
    width = weights.shape[2]
    both = None
    for i in range(3):
        grad = grads[i][...]
        ups = tn(ranks, grad)
        grad_ref[block_rows(at + 2 * i + 1), :] += ups[block_rows(i)]
        loads.ready(first_load + i)
        part = nt(grad, weights[first_load + i])
        both = part if both is None else both + part
    grad_ranks = both[:, width : width + 3 * RANK].astype(BF16)
    downs = tn(grad_ranks, inputs)
    for i in range(3):
        grad_ref[block_rows(at + 2 * i), :] += downs[block_rows(i)]
    return both[:, :width] + nn(grad_ranks, three_downs(ad_ref, number))


def place_of(seq_ref, k, parts, places):
    return pl.multiple_of(lax.rem(seq_ref[0] + k, parts) * places, 16)


def spatial_forward(seq_ref, x_ref, mod_ref, mask_ref, ad_ref, w_hbm, *refs):
    x1_refs = refs[:-11]
    q_ref, k_ref, v_ref, o_ref, stat_ref, rq_ref, ro_ref, w_ref, lhs_ref, x1_s, sems = refs[-11:]
    width = x_ref.shape[2]
    loads = Loads([(w_hbm.at[i], w_ref.at[i, pl.ds(0, width), :]) for i in range(4)], sems)
    loads.start()

    @pl.when(loads.first)
    def _():
        lhs_ref[:, width:] = jnp.zeros((ROWS, PAD), BF16)
        for i in range(4):
            w_ref[i, width:, :] = up_rows(ad_ref, i, i % 3, width)

    stream = x_ref[0].astype(F32)
    normal, _ = normalize(stream)
    lhs_ref[:, :width] = (normal * (1.0 + mod_ref[1:2, :]) + mod_ref[0:1, :]).astype(BF16)
    q, k, v = q_ref.at[0], k_ref.at[0], v_ref.at[0]
    three_projections(lhs_ref, ad_ref, 0, w_ref, loads, 0, (q, k, v), rq_ref.at[0])

    def put_out(index, value):
        value = value.astype(BF16)
        o_ref[0, :, tile(index)] = value
        lhs_ref[:, tile(index)] = value

    attend(q, k, v, mask_ref, None, put_out, stat_ref.at[0])
    loads.ready(3)
    branch = one_projection(lhs_ref, ad_ref, 3, w_ref.at[3], ro_ref.at[0])
    x1_s[...] = (stream + mod_ref[2:3, :] * branch).astype(BF16)
    places = x1_refs[0].shape[1]
    for k, ref in enumerate(x1_refs):
        ref[0] = x1_s[pl.ds(place_of(seq_ref, k, len(x1_refs), places), places), :]


def rows_of(refs):
    pieces = [ref[...].reshape(-1, ref.shape[2]) for ref in refs]
    return pieces[0] if len(pieces) == 1 else jnp.concatenate(pieces, 0)


def temporal_forward(parts, *refs):
    x_refs, refs = refs[:parts], refs[parts:]
    (
        mod_ref, mask_ref, ad_ref, w_hbm,
        q_ref, k_ref, v_ref, o_ref, stat_ref, rq_ref, ro_ref, u2_ref, x2_ref,
        w_ref, bias_ref, lhs_ref, q_s, k_s, v_s, sems,
    ) = refs
    width = x_refs[0].shape[2]
    loads = Loads([(w_hbm.at[i], w_ref.at[i, pl.ds(0, width), :]) for i in range(4)], sems)
    loads.start()

    @pl.when(loads.first)
    def _():
        bias_ref[...] = same_place(bias_ref.shape)
        lhs_ref[:, width:] = jnp.zeros((ROWS, PAD), BF16)
        for i in range(4):
            w_ref[i, width:, :] = up_rows(ad_ref, 4 + i, i % 3, width)

    loaded = rows_of(x_refs)
    lhs_ref[:, :width] = loaded
    three_projections(lhs_ref, ad_ref, 4, w_ref, loads, 0, (q_s, k_s, v_s), rq_ref.at[0])
    q_ref[...] = q_s[...].reshape(q_ref.shape)
    k_ref[...] = k_s[...].reshape(k_ref.shape)
    v_ref[...] = v_s[...].reshape(v_ref.shape)

    def put_out(index, value):
        lhs_ref[:, tile(index)] = value.astype(BF16)

    attend(q_s, k_s, v_s, mask_ref, bias_ref, put_out, stat_ref.at[0])
    o_ref[...] = lhs_ref[:, :width].reshape(o_ref.shape)
    loads.ready(3)
    branch = one_projection(lhs_ref, ad_ref, 7, w_ref.at[3], ro_ref.at[0])
    stream = loaded.astype(F32) + mod_ref[2:3, :] * branch
    u2_ref[...] = stream.astype(BF16).reshape(u2_ref.shape)
    x2_ref[...] = stream.reshape(x2_ref.shape)


def cross_forward(
    x_ref, ctx_ref, mask_ref, ad_ref, w_hbm,
    q_ref, o_ref, stat_ref, rq_ref, ro_ref, kp_ref, vp_ref, rk_ref, rv_ref, x3_ref,
    w_ref, lhs_ref, q_s, k_s, sems,
):
    width = x_ref.shape[2]
    loads = Loads([(w_hbm.at[4 + i], w_ref.at[i, pl.ds(0, width), :]) for i in range(4)], sems)
    loads.start()

    @pl.when(loads.first)
    def _():
        lhs_ref[:, width:] = jnp.zeros((ROWS, PAD), BF16)
        for i in (0, 3):
            w_ref[i, width:, :] = up_rows(ad_ref, 8 + i, 0, width)

    stream = x_ref[...].reshape(ROWS, width)
    lhs_ref[:, :width] = stream.astype(BF16)
    loads.ready(0)
    queries = one_projection(lhs_ref, ad_ref, 8, w_ref.at[0], rq_ref.at[0])
    q_s[...] = (queries * EXP_SCALE).astype(BF16)
    q_ref[...] = q_s[...].reshape(q_ref.shape)
    loads.ready(1)
    loads.ready(2)

    @pl.when(loads.first)
    def _():
        for number, at, rank_ref, pair_ref in ((9, 1, rk_ref, kp_ref), (10, 2, rv_ref, vp_ref)):
            ranks = nt(ctx_ref[...], ad_ref[2 * number]).astype(BF16)
            rank_ref[...] = ranks
            made = nn(ctx_ref[...], w_ref[at, :width, :]) + nn(ranks, ad_ref[2 * number + 1])
            k_s[...] = made.astype(BF16)
            for pair in range(PAIRS):
                piece = k_s[:, window(pair)]
                pair_ref[pair, :PAD, :] = piece * mask_ref[2 * pair : 2 * pair + 1, :]
                pair_ref[pair, PAD:, :] = piece * mask_ref[2 * pair + 1 : 2 * pair + 2, :]

    carried = None
    count = 120
    for pair in range(PAIRS):
        scores = nt(kp_ref[pair], q_s[:, window(pair)])
        pieces = []
        for sub in range(2):
            own = scores[PAD * sub : PAD * sub + count]
            top = jnp.max(own, 0, keepdims=True)
            grown = jnp.exp2(own - top)
            total = jnp.sum(grown, 0, keepdims=True)
            stat_ref[0, 2 * pair + sub : 2 * pair + sub + 1, :] = top + jnp.log2(total)
            pieces += [grown * (1.0 / total), jnp.zeros((PAD - count, ROWS), F32)]
        weights = jnp.concatenate(pieces, 0).astype(BF16)
        out = tn(weights, vp_ref[pair])
        low = out[:, :128]
        lhs_ref[:, tile(pair)] = (low if carried is None else low + carried).astype(BF16)
        carried = out[:, 128:]
    lhs_ref[:, tile(PAIRS)] = carried.astype(BF16)
    o_ref[...] = lhs_ref[:, :width].reshape(o_ref.shape)
    loads.ready(3)
    stream = stream + one_projection(lhs_ref, ad_ref, 11, w_ref.at[3], ro_ref.at[0])
    x3_ref[...] = stream.reshape(x3_ref.shape)


def gelu_both(hidden):
    root = math.sqrt(2.0 / math.pi)
    square = hidden * hidden
    inner = root * (hidden + 0.044715 * (square * hidden))
    bent = jnp.tanh(inner)
    half = 0.5 * (1.0 + bent)
    slope = half + 0.5 * hidden * (1.0 - bent * bent) * (root * (1.0 + 3.0 * 0.044715 * square))
    return hidden * half, slope


def transposed_map(rows):
    nothing = jnp.zeros((PAD - rows.shape[0], rows.shape[1]), F32)
    wide = jnp.concatenate([rows.astype(F32), nothing], 0)
    return wide.T.astype(BF16)


def down_loads(order_ref, pieces, down_ref, width):
    half = width // 2
    count = len(pieces) // 2
    core = order_ref[count]
    entries = []
    for k in range(count):
        for source, side in ((pieces[k], core), (pieces[count + k], 1 - core)):
            start = pl.multiple_of(order_ref[k] * width + side * half, 16)
            entries.append((source, down_ref.at[pl.ds(start, half), pl.ds(0, width)]))
    return entries


def fill_down_maps(ad_ref, down_ref, width):
    chunks = down_ref.shape[0] // width
    for c in range(chunks):
        rows = slice(c * width, (c + 1) * width)
        down_ref[rows, width:] = transposed_map(ad_ref[2 + chunks + c])


def feed_forward_grad(count, order_ref, cot_ref, mod_ref, ad_ref, *refs):
    pieces = refs[:count]
    grad_ref, down_ref, lhs_ref, sems = refs[count:]
    width = cot_ref.shape[1]
    half = width // 2
    chunks = count // 2
    core = order_ref[chunks]
    entries = []
    for k in range(chunks):
        for source, side in ((pieces[k], core), (pieces[chunks + k], 1 - core)):
            start = pl.multiple_of(k * width + side * half, 16)
            entries.append((source, down_ref.at[pl.ds(start, half), pl.ds(0, width)]))
    loads = Loads(entries, sems)
    loads.start()

    @pl.when(loads.first)
    def _():
        lhs_ref[:, width:] = jnp.zeros((ROWS, PAD), BF16)
        for k in range(chunks):
            rows = slice(k * width, (k + 1) * width)
            down_ref[rows, width:] = transposed_map(ad_ref[2 + (ad_ref.shape[0] - 2) // 2 + order_ref[k]])

    branch = (mod_ref[5:6, :] * cot_ref[...].astype(F32)).astype(BF16)
    lhs_ref[:, :width] = branch
    lhs_ref[:, width : width + RANK] = nt(branch, ad_ref[1]).astype(BF16)
    for i in range(len(entries)):
        loads.ready(i)
    for k in range(chunks):
        rows = slice(k * width, (k + 1) * width)
        grad_ref[k] = nt(lhs_ref[...], down_ref[rows, :]).astype(BF16)


def hidden_chunks(hidden):
    return [slice(at, at + 1536) for at in range(0, hidden, 1536)]


def feed_forward(groups, count, order_ref, x3_ref, cot_ref, *refs):
    grad_refs, pieces, refs = refs[:groups], refs[groups : groups + count], refs[groups + count :]
    (
        mod_ref, ad_ref, w_hbm, act_ref, g3_ref, gd_ref, gu_ref, up_ref, lhs_ref, dh_ref, sems, *rest
    ) = refs
    width = x3_ref.shape[1]
    hidden_size = up_ref.shape[1]
    chunks = hidden_size // width
    late = count // 2
    core = order_ref[chunks]
    entries = [
        (w_hbm.at[c], up_ref.at[pl.ds(0, width), pl.ds(c * width, width)]) for c in range(chunks)
    ]
    if late:
        down_ref, dlhs_ref = rest
        half = width // 2
        for k in range(late):
            for source, side in ((pieces[k], core), (pieces[late + k], 1 - core)):
                start = pl.multiple_of(k * width + side * half, 16)
                entries.append((source, down_ref.at[pl.ds(start, half), pl.ds(0, width)]))
    loads = Loads(entries, sems)
    loads.start()

    @pl.when(loads.first)
    def _():
        gd_ref[...] = jnp.zeros_like(gd_ref)
        gu_ref[...] = jnp.zeros_like(gu_ref)
        lhs_ref[:, width:] = jnp.zeros((ROWS, PAD), BF16)
        up_ref[width + RANK :, :] = jnp.zeros((PAD - RANK, hidden_size), BF16)
        for c in range(chunks):
            up_ref[width : width + RANK, c * width : (c + 1) * width] = ad_ref[2 + c]
        for k in range(late):
            rows = slice(k * width, (k + 1) * width)
            at = order_ref[chunks - late + k]
            down_ref[rows, width:] = transposed_map(ad_ref[2 + chunks + at])
        if late:
            dlhs_ref[:, width:] = jnp.zeros((ROWS, PAD), BF16)

    normal, inverse = normalize(x3_ref[...])
    inputs = (normal * (1.0 + mod_ref[4:5, :]) + mod_ref[3:4, :]).astype(BF16)
    rank_up = nt(inputs, ad_ref[0]).astype(BF16)
    lhs_ref[:, :width] = inputs
    lhs_ref[:, width : width + RANK] = rank_up
    at = 0
    for grad_ref in grad_refs:
        for k in range(grad_ref.shape[0]):
            start = pl.multiple_of(order_ref[at] * width, 128)
            dh_ref[:, pl.ds(start, width)] = grad_ref[k]
            at += 1
    if late:
        branch = (mod_ref[5:6, :] * cot_ref[...].astype(F32)).astype(BF16)
        dlhs_ref[:, :width] = branch
        dlhs_ref[:, width : width + RANK] = nt(branch, ad_ref[1]).astype(BF16)
    for i in range(len(entries)):
        loads.ready(i)
    for k in range(late):
        start = pl.multiple_of(order_ref[at + k] * width, 128)
        rows = slice(k * width, (k + 1) * width)
        dh_ref[:, pl.ds(start, width)] = nt(dlhs_ref[...], down_ref[rows, :]).astype(BF16)
    for cols in hidden_chunks(hidden_size):
        active, slope = gelu_both(nn(lhs_ref[...], up_ref[:, cols]))
        act_ref[:, cols] = active.astype(BF16)
        dh_ref[:, cols] = (slope * dh_ref[:, cols].astype(F32)).astype(BF16)
    both = nt(dh_ref[...], up_ref[...])
    gu_ref[...] += tn(rank_up, dh_ref[...])
    grad_rank = both[:, width : width + RANK].astype(BF16)
    grad_in = both[:, :width] + nn(grad_rank, ad_ref[0])
    gd_ref[...] += tn(grad_rank, lhs_ref[:, :width])
    grad_in = normalize_back(normal, inverse, grad_in * (1.0 + mod_ref[4:5, :]))
    g3_ref[...] = cot_ref[...].astype(F32) + grad_in


def feed_forward_out(count, order_ref, act_ref, x3_ref, cot_ref, mod_ref, ad_ref, *refs):
    pieces, refs = refs[:count], refs[count:]
    x4_refs = refs[:-4]
    gu_ref, gd_ref, down_ref, sems = refs[-4:]
    width = x3_ref.shape[1]
    step = pl.program_id(0)
    entries = down_loads(order_ref, pieces, down_ref, width)
    loads = Loads(entries, sems)
    loads.start()

    @pl.when(loads.first)
    def _():
        gu_ref[...] = jnp.zeros_like(gu_ref)
        gd_ref[...] = jnp.zeros_like(gd_ref)
        fill_down_maps(ad_ref, down_ref, width)

    share = x4_refs[0].shape[0]
    grad_branch = (mod_ref[5:6, :] * cot_ref[...].astype(F32)).astype(BF16)
    gd_ref[...] += tn(nt(grad_branch, ad_ref[1]).astype(BF16), act_ref[...])
    for i in range(len(entries)):
        loads.ready(i)
    both = nn(act_ref[...], down_ref[...])
    ranks = both[:, width : width + RANK].astype(BF16)
    branch = both[:, :width] + nn(ranks, ad_ref[1])
    gu_ref[...] += tn(ranks, grad_branch)
    result = (x3_ref[...] + mod_ref[5:6, :] * branch).astype(BF16)
    for k, ref in enumerate(x4_refs):
        at = k * share

        @pl.when(step == at // ROWS)
        def _():
            ref[...] = result[at % ROWS : at % ROWS + share]


def cross_temporal_backward(parts, *refs):
    outs = len(refs) - parts - 13
    _cross_temporal_backward(refs[:parts], refs[outs : outs + parts], *refs[parts:outs], *refs[outs + parts :])


def _cross_temporal_backward(
    u1_refs, g1_refs, g3_ref, q_ref, k_ref, v_ref, o_ref, stat_ref, rq_ref, ro_ref,
    u2_ref, qc_ref, oc_ref, statc_ref, rqc_ref, roc_ref, kp_ref, vp_ref,
    mod_ref, mask_ref, ad_ref, w_hbm,
    gw_ref, dk_acc, dv_acc, w_ref, bias_ref, q_s, k_s, v_s, do_s, dq_s, dk_s, dv_s, sems,
):
    width = u1_refs[0].shape[2]
    first = pl.program_id(0) == 0
    order = (7, 4, 3, 0, 1, 2)
    loads = Loads(
        [(w_hbm.at[n], w_ref.at[i, pl.ds(0, width), :]) for i, n in enumerate(order)], sems
    )
    loads.start()

    @pl.when(first)
    def _():
        bias_ref[...] = same_place(bias_ref.shape)
        gw_ref[...] = jnp.zeros_like(gw_ref)
        dk_acc[...] = jnp.zeros_like(dk_acc)
        dv_acc[...] = jnp.zeros_like(dv_acc)
        for i, n in enumerate(order):
            w_ref[i, width:, :] = up_rows(ad_ref, 4 + n, n if n < 3 else 0, width)

    def rows(ref):
        return ref[...].reshape(ROWS, ref.shape[2])

    grad = rows(g3_ref)
    loads.ready(0)
    do_s[...] = one_back(
        grad.astype(BF16), rows(oc_ref), roc_ref[0], ad_ref, 11, w_ref.at[0], gw_ref, 14
    ).astype(BF16)
    q_s[...] = rows(qc_ref)
    count = 120
    carried = None
    for pair in range(PAIRS):
        win = window(pair)
        q_win, do_win = q_s[:, win], do_s[:, win]
        scores = nt(kp_ref[pair], q_win)
        grad_probs = nt(vp_ref[pair], do_win)
        all_probs, all_grads = [], []
        nothing = jnp.zeros((PAD - count, ROWS), F32)
        for sub in range(2):
            span = slice(PAD * sub, PAD * sub + count)
            row = 2 * pair + sub
            probs = jnp.exp2(scores[span] - statc_ref[0, row : row + 1, :])
            own = grad_probs[span]
            inner = jnp.sum(probs * own, 0, keepdims=True)
            all_probs += [probs, nothing]
            all_grads += [probs * (own - inner), nothing]
        probs = jnp.concatenate(all_probs, 0).astype(BF16)
        grad_scores = jnp.concatenate(all_grads, 0).astype(BF16)
        dk_acc[pair] += nn(grad_scores, q_win)
        dv_acc[pair] += nn(probs, do_win)
        out = tn(grad_scores, kp_ref[pair])
        low = out[:, :128]
        dq_s[:, tile(pair)] = ((low if carried is None else low + carried) * SCALE).astype(BF16)
        carried = out[:, 128:]
    dq_s[:, tile(PAIRS)] = (carried * SCALE).astype(BF16)
    loads.ready(1)
    grad = grad + one_back(
        dq_s[...], rows(u2_ref), rqc_ref[0], ad_ref, 8, w_ref.at[1], gw_ref, 8
    )
    loads.ready(2)
    do_s[...] = one_back(
        (mod_ref[2:3, :] * grad).astype(BF16), rows(o_ref), ro_ref[0], ad_ref, 7, w_ref.at[2], gw_ref, 6
    ).astype(BF16)
    q_s[...] = rows(q_ref)
    k_s[...] = rows(k_ref)
    v_s[...] = rows(v_ref)

    def put(index, values):
        dq_s[:, tile(index)] = (values[0] * SCALE).astype(BF16)
        dk_s[:, tile(index)] = (values[1] * LN2).astype(BF16)
        dv_s[:, tile(index)] = values[2].astype(BF16)

    attend_back(q_s, k_s, v_s, do_s, mask_ref, bias_ref, stat_ref.at[0], put)
    grad = grad + three_back(
        (dq_s, dk_s, dv_s), rows_of(u1_refs), rq_ref[0], ad_ref, 4, w_ref, loads, 3, gw_ref, 0
    )
    grad = grad.astype(BF16)
    share = ROWS // len(g1_refs)
    for k, ref in enumerate(g1_refs):
        ref[...] = grad[share * k : share * (k + 1)].reshape(ref.shape)


def tail_groups(cols):
    tail = cols - PAD
    return PAD // tail if 0 < tail < PAD and PAD % tail == 0 else 0


def packed_rows(blocks, cols):
    group = tail_groups(cols)
    if not group:
        return blocks * RANK, cols
    return (blocks + -(-blocks // group)) * RANK, PAD


def put_blocks(blocks, put):
    cols = blocks[0].shape[1]
    group = tail_groups(cols)
    for k, rows in enumerate(blocks):
        put(k, rows[:, :PAD] if group else rows)
    for k in range(0, len(blocks), group) if group else ():
        tails = [rows[:, PAD:] for rows in blocks[k : k + group]]
        missing = group - len(tails)
        if missing:
            tails.append(jnp.zeros((RANK, missing * (cols - PAD)), blocks[0].dtype))
        put(len(blocks) + k // group, jnp.concatenate(tails, 1))


def get_block(get, index, count, cols):
    group = tail_groups(cols)
    if not group:
        return get(index)
    at = (index % group) * (cols - PAD)
    return jnp.concatenate([get(index), get(count + index // group)[:, at : at + cols - PAD]], 1)


def pack_columns(table_ref, packed_ref, clips):
    parts = packed_ref.shape[0] // clips
    share = table_ref.shape[0] // parts
    cols = table_ref.shape[1] // clips
    for f in range(clips):
        for s in range(parts):
            piece = table_ref[share * s : share * (s + 1), cols * f : cols * (f + 1)].astype(BF16)
            blocks = [piece[block_rows(k)] for k in range(share // RANK)]

            def put(k, rows):
                packed_ref[f * parts + s, block_rows(k), :] = rows

            put_blocks(blocks, put)


def stacked(seq_ref, g1_refs, shares, whole_ref):
    parts = len(g1_refs) // shares
    places = whole_ref.shape[0] // parts
    at = 0
    for share in range(shares):
        refs = g1_refs[share * parts : (share + 1) * parts]
        size = refs[0].shape[1]
        for k, ref in enumerate(refs):
            start = pl.multiple_of(place_of(seq_ref, k, parts, places) + at, 16)
            whole_ref[pl.ds(start, size), :] = ref[0]
        at += size
    return whole_ref[...].astype(F32)


def spatial_backward(pieces, halves, clips, continued, last, seq_ref, *refs):
    g1_refs, refs = refs[:pieces], refs[pieces:]
    if continued:
        (_, before_ref), refs = refs[:2], refs[2:]
    (
        x_ref, q_ref, k_ref, v_ref, o_ref, stat_ref, rq_ref, ro_ref, mod_ref, mask_ref, ad_ref, w_hbm,
        d_ref, sums_ref, w_ref, gw_ref, do_s, sems,
    ) = refs
    width = x_ref.shape[2]
    loads = Loads([(w_hbm.at[3], w_ref.at[pl.ds(0, width), :])], sems)
    loads.start()

    @pl.when(loads.first)
    def _():
        gw_ref[...] = before_ref[...] if continued else jnp.zeros_like(gw_ref)
        w_ref[width:, :] = up_rows(ad_ref, 3, 0, width)

    grad = stacked(seq_ref, g1_refs, halves, do_s)
    loads.ready(0)
    do_s[...] = one_back(
        (mod_ref[2:3, :] * grad).astype(BF16), o_ref[0], ro_ref[0], ad_ref, 3, w_ref, gw_ref, 6
    ).astype(BF16)

    def put(index, values):
        for i, factor in enumerate((SCALE, LN2, 1.0)):
            value = values[i] if factor == 1.0 else values[i] * factor
            d_ref[0, :, width * i + 128 * index : width * i + 128 * index + 128] = value.astype(BF16)

    attend_back(
        q_ref.at[0], k_ref.at[0], v_ref.at[0], do_s, mask_ref, None, stat_ref.at[0], put
    )
    ranks = rq_ref[0]
    grad_ranks = None
    for i in range(3):
        grad = d_ref[0, :, width * i : width * (i + 1)]
        gw_ref[block_rows(2 * i + 1), :] += tn(ranks, grad)[block_rows(i)]
        part = nt(grad, up_rows(ad_ref, i, i, width))
        grad_ranks = part if grad_ranks is None else grad_ranks + part
    d_ref[0, :, 3 * width :] = grad_ranks.astype(BF16)
    normal, _ = normalize(x_ref[0].astype(F32))
    inputs = (normal * (1.0 + mod_ref[1:2, :]) + mod_ref[0:1, :]).astype(BF16)
    downs = tn(d_ref[0, :, 3 * width :], inputs)
    for i in range(3):
        gw_ref[block_rows(2 * i), :] += downs[block_rows(i)]

    @pl.when(pl.program_id(0) == pl.num_programs(0) - 1)
    def _():
        if last:
            pack_columns(gw_ref, sums_ref, clips)
        else:
            sums_ref[...] = gw_ref[...]


def spatial_input_grad(pieces, halves, seq_ref, *refs):
    g1_refs, refs = refs[:pieces], refs[pieces:]
    x_ref, d_ref, mod_ref, ad_ref, w_hbm, g0_ref, w_ref, whole_s, sems = refs
    width = x_ref.shape[2]
    loads = Loads(
        [(w_hbm.at[i], w_ref.at[:, pl.ds(i * width, width)]) for i in range(3)], sems
    )
    loads.start()

    @pl.when(loads.first)
    def _():
        w_ref[:, 3 * width :] = transposed_map(three_downs(ad_ref, 0))

    normal, inverse = normalize(x_ref[0].astype(F32))
    grad = stacked(seq_ref, g1_refs, halves, whole_s)
    for i in range(3):
        loads.ready(i)
    grad_in = nt(d_ref[0], w_ref[...])
    grad = grad + normalize_back(normal, inverse, grad_in * (1.0 + mod_ref[1:2, :]))
    g0_ref[0] = grad.astype(BF16)


def put_in_place(seq_ref, *refs):
    *pieces, out_ref = refs
    places = pieces[0].shape[1]
    for k, ref in enumerate(pieces):
        out_ref[0, pl.ds(place_of(seq_ref, k, len(pieces), places), places), :] = ref[0]


def pack_early(clips, shares, counts, *refs):
    gw_refs, refs = refs[:shares], refs[shares:]
    dk_refs, refs = refs[:shares], refs[shares:]
    dv_refs, refs = refs[:shares], refs[shares:]
    *others, rk_ref, rv_ref, ctx_ref, mask_ref, ad_ref, packed_ref, table_ref, ctx_s = refs

    def added(each):
        total = each[0]
        for value in each[1:]:
            total = total + value
        return total

    at = gw_refs[0].shape[0]
    table_ref[:at, :] = added([ref[...] for ref in gw_refs])
    width = table_ref.shape[1]
    for count in counts:
        each, others = others[:count], others[count:]
        for k in range(each[0].shape[1] // width):
            cols = slice(k * width, (k + 1) * width)
            table_ref[at : at + RANK, :] = added([ref[:, cols] for ref in each])
            at += RANK
    table_ref[at:, :] = jnp.zeros((table_ref.shape[0] - at, width), F32)
    context = ctx_ref[...].astype(F32)
    for accs, factor, rank_ref, number, at in (
        (dk_refs, LN2, rk_ref, 9, 10),
        (dv_refs, 1.0, rv_ref, 10, 12),
    ):
        held = None
        for pair in range(PAIRS):
            whole = added([ref[pair] for ref in accs]) * factor
            out = whole[:PAD] * mask_ref[2 * pair : 2 * pair + 1, :].astype(F32)
            out = out + whole[PAD:] * mask_ref[2 * pair + 1 : 2 * pair + 2, :].astype(F32)
            low = out[:, :128]
            ctx_s[:, tile(pair)] = low if held is None else low + held
            held = out[:, 128:]
        ctx_s[:, tile(PAIRS)] = held
        grad_kv = ctx_s[...]
        grad_rank = lax.dot_general(
            grad_kv, ad_ref[2 * number + 1].astype(F32), (((1,), (1,)), ((), ())),
            precision=HIGHEST, preferred_element_type=F32,
        )
        table_ref[block_rows(at), :] = lax.dot_general(
            grad_rank, context, (((0,), (0,)), ((), ())),
            precision=HIGHEST, preferred_element_type=F32,
        )
        table_ref[block_rows(at + 1), :] = lax.dot_general(
            rank_ref[...].astype(F32), grad_kv, (((0,), (0,)), ((), ())),
            precision=HIGHEST, preferred_element_type=F32,
        )
    pack_columns(table_ref, packed_ref, clips)


def assemble(parts, seq_ref, *refs):
    early_refs, late_refs, refs = refs[:parts], refs[parts : 2 * parts], refs[2 * parts :]
    wide_ref, narrow_ref, early_ref, late_ref = refs
    for k in range(parts):
        source = lax.rem(seq_ref[0] + parts - k, parts)
        early_ref[source] = early_refs[k][...]
        late_ref[source] = late_refs[k][...]
    _, adapters, _, cols = wide_ref.shape
    times = narrow_ref.shape[3] // cols

    def block(ref, total, index, a):
        each = total // ref.shape[0]

        def get(k):
            return ref[index // each, a, block_rows(k), :].astype(F32)

        return get_block(get, index % each, each, cols)

    for a in range(adapters):
        for i in range(8):
            wide_ref[i, a] = block(late_ref, LATE_BLOCKS, i, a)
        for i in range(18):
            wide_ref[8 + i, a] = block(early_ref, EARLY_BLOCKS, i, a)
        for n in range(2):
            pieces = [block(early_ref, EARLY_BLOCKS, 18 + n * times + j, a) for j in range(times)]
            narrow_ref[n, a] = jnp.concatenate(pieces, 1)


def combine(index_ref, got_ref, out_ref, acc_ref):
    clips = index_ref.shape[0]
    parts = got_ref.shape[0] // clips
    acc_ref[...] = jnp.zeros_like(acc_ref)

    def step(f, carry):
        total = got_ref[f * parts].astype(F32)
        for s in range(1, parts):
            total = total + got_ref[f * parts + s].astype(F32)
        acc_ref[index_ref[f]] += total
        return carry

    lax.fori_loop(0, clips, step, 0)
    out_ref[...] = acc_ref[...].astype(BF16)


def pick(index_ref, wide_ref, narrow_ref, out_ref):
    count, _, _, cols = wide_ref.shape
    times = narrow_ref.shape[3] // cols

    def step(f, carry):
        a = index_ref[f]
        blocks = [wide_ref[k, a] for k in range(count)]
        for p in range(2):
            rows = narrow_ref[p, a]
            blocks += [rows[:, cols * j : cols * (j + 1)] for j in range(times)]

        def put(k, rows):
            out_ref[f, block_rows(k), :] = rows

        put_blocks(blocks, put)
        return carry

    lax.fori_loop(0, index_ref.shape[0], step, 0)


def unpick(count, cols, got_ref, out_ref):
    for k in range(count):
        pieces = []
        for f in range(got_ref.shape[0]):

            def get(index):
                return got_ref[f, block_rows(index), :]

            pieces.append(get_block(get, k, count, cols))
        out_ref[k] = jnp.concatenate(pieces, 1)


def whole_block(array):
    zeros = (0,) * array.ndim
    return pl.BlockSpec(array.shape, lambda i: zeros, pipeline_mode=pl.Buffered(1))


def anywhere():
    return pl.BlockSpec(memory_space=pl.ANY)


def like(shape, dtype):
    return jax.ShapeDtypeStruct(shape, dtype)


PARAMS = pltpu.CompilerParams(
    dimension_semantics=("arbitrary",), vmem_limit_bytes=VMEM_LIMIT
)


def cost(flops, read, part=4):
    return pl.CostEstimate(
        flops=flops // part, bytes_accessed=read // part, transcendentals=0
    )


def run_spatial_forward(seq, video, mods, masks, wide, w_s, parts):
    frames, rows, d = video.shape
    places = rows // parts
    by_frame = lambda i: (i, 0, 0)
    row_block = pl.BlockSpec((1, rows, d), by_frame)
    return pl.pallas_call(
        spatial_forward,
        grid=(frames,),
        in_specs=[in_smem(), row_block, whole_block(mods), whole_block(masks), whole_block(wide), anywhere()],
        out_specs=[pl.BlockSpec((1, places, d), by_frame)] * parts
        + [
            row_block,
            row_block,
            row_block,
            row_block,
            pl.BlockSpec((1, HEADS, rows), by_frame),
            pl.BlockSpec((1, rows, 3 * RANK), by_frame),
            pl.BlockSpec((1, rows, RANK), by_frame),
        ],
        out_shape=[like((frames, places, d), BF16)] * parts
        + [like(video.shape, BF16)] * 4
        + [
            like((frames, HEADS, rows), F32),
            like((frames, rows, 3 * RANK), BF16),
            like((frames, rows, RANK), BF16),
        ],
        scratch_shapes=[
            pltpu.VMEM((4, d + PAD, d), BF16),
            pltpu.VMEM((ROWS, d + PAD), BF16),
            pltpu.VMEM((ROWS, d), BF16),
            pltpu.SemaphoreType.DMA((4,)),
        ],
        compiler_params=PARAMS,
        cost_estimate=cost(10 * frames * rows * d * d, 30_000_000),
        name="spatial_forward",
    )(seq, video, mods, masks, wide, w_s)


def run_temporal_forward(x1, mods, masks, wide, w_t):
    parts = len(x1)
    own_frames, places, d = x1[0].shape
    frames = own_frames * parts
    groups = places * frames // ROWS
    each = ROWS // frames
    across = pl.BlockSpec((frames, each, d), lambda i: (0, i, 0))
    by_group = lambda i: (i, 0, 0)
    act = like((frames, places, d), BF16)

    def body(*refs):
        temporal_forward(parts, *refs)

    return pl.pallas_call(
        body,
        grid=(groups,),
        in_specs=[pl.BlockSpec((own_frames, each, d), lambda i: (0, i, 0))] * parts
        + [whole_block(mods), whole_block(masks), whole_block(wide), anywhere()],
        out_specs=[across] * 4
        + [
            pl.BlockSpec((1, HEADS, ROWS), by_group),
            pl.BlockSpec((1, ROWS, 3 * RANK), by_group),
            pl.BlockSpec((1, ROWS, RANK), by_group),
            across,
            across,
        ],
        out_shape=[act] * 4
        + [
            like((groups, HEADS, ROWS), F32),
            like((groups, ROWS, 3 * RANK), BF16),
            like((groups, ROWS, RANK), BF16),
            act,
            like((frames, places, d), F32),
        ],
        scratch_shapes=[pltpu.VMEM((4, d + PAD, d), BF16), pltpu.VMEM((ROWS, ROWS), F32)]
        + [pltpu.VMEM((ROWS, d + PAD), BF16)]
        + [pltpu.VMEM((ROWS, d), BF16)] * 3
        + [pltpu.SemaphoreType.DMA((4,))],
        compiler_params=PARAMS,
        cost_estimate=cost(10 * places * frames * d * d, 30_000_000),
        name="temporal_forward",
    )(*x1, mods, masks, wide, w_t)


def run_cross_forward(x2, context, masks, wide, w_c):
    frames, places, d = x2.shape
    groups = places * frames // ROWS
    across = pl.BlockSpec((frames, ROWS // frames, d), lambda i: (0, i, 0))
    by_group = lambda i: (i, 0, 0)
    full = lambda *shape: pl.BlockSpec(shape, lambda i: (0,) * len(shape))
    one = pl.BlockSpec((1, ROWS, RANK), by_group)
    one_shape = like((groups, ROWS, RANK), BF16)
    act = like((frames, places, d), BF16)
    return pl.pallas_call(
        cross_forward,
        grid=(groups,),
        in_specs=[across, whole_block(context), whole_block(masks), whole_block(wide), anywhere()],
        out_specs=[across] * 2 + [pl.BlockSpec((1, HEADS, ROWS), by_group), one, one]
        + [full(PAIRS, 2 * PAD, 256)] * 2 + [full(PAD, RANK)] * 2 + [across],
        out_shape=[act] * 2 + [like((groups, HEADS, ROWS), F32), one_shape, one_shape]
        + [like((PAIRS, 2 * PAD, 256), BF16)] * 2 + [like((PAD, RANK), BF16)] * 2
        + [like(x2.shape, F32)],
        scratch_shapes=[pltpu.VMEM((4, d + PAD, d), BF16), pltpu.VMEM((ROWS, d + PAD), BF16)]
        + [pltpu.VMEM((ROWS, d), BF16), pltpu.VMEM((PAD, d), BF16)]
        + [pltpu.SemaphoreType.DMA((4,))],
        compiler_params=PARAMS,
        cost_estimate=cost(8 * places * frames * d * d, 30_000_000),
        name="cross_forward",
    )(x2, context, masks, wide, w_c)


def in_smem():
    return pl.BlockSpec(memory_space=pltpu.SMEM)


def run_feed_forward_grad(cot, mods, maps, order, pieces):
    tokens, d = cot.shape
    chunks = len(pieces) // 2

    def body(*refs):
        feed_forward_grad(len(pieces), *refs)

    return pl.pallas_call(
        body,
        grid=(tokens // ROWS,),
        in_specs=[in_smem(), pl.BlockSpec((ROWS, d), lambda i: (i, 0)), whole_block(mods), whole_block(maps)]
        + [anywhere()] * len(pieces),
        out_specs=pl.BlockSpec((chunks, ROWS, d), lambda i: (0, i, 0)),
        out_shape=like((chunks, tokens, d), BF16),
        scratch_shapes=[
            pltpu.VMEM((chunks * d, d + PAD), BF16),
            pltpu.VMEM((ROWS, d + PAD), BF16),
            pltpu.SemaphoreType.DMA((len(pieces),)),
        ],
        compiler_params=PARAMS,
        cost_estimate=cost(2 * tokens * d * d * chunks, 20_000_000),
        name="feed_forward_grad",
    )(order, cot, mods, maps, *pieces)


def run_feed_forward(x3, cot, order, grad_active, pieces, mods, maps, up):
    tokens, d = x3.shape
    chunks = up.shape[0]
    late = len(pieces) // 2
    rows = pl.BlockSpec((ROWS, d), lambda i: (i, 0))
    wide_rows = pl.BlockSpec((ROWS, chunks * d), lambda i: (i, 0))
    more = [pltpu.VMEM((late * d, d + PAD), BF16), pltpu.VMEM((ROWS, d + PAD), BF16)] if late else []

    def body(*refs):
        feed_forward(len(grad_active), len(pieces), *refs)

    return pl.pallas_call(
        body,
        grid=(tokens // ROWS,),
        in_specs=[in_smem(), rows, rows]
        + [pl.BlockSpec((g.shape[0], ROWS, d), lambda i: (0, i, 0)) for g in grad_active]
        + [anywhere()] * len(pieces)
        + [whole_block(mods), whole_block(maps), anywhere()],
        out_specs=[
            wide_rows,
            rows,
            pl.BlockSpec((RANK, d), lambda i: (0, 0)),
            pl.BlockSpec((RANK, chunks * d), lambda i: (0, 0)),
        ],
        out_shape=[
            like((tokens, chunks * d), BF16),
            like((tokens, d), F32),
            like((RANK, d), F32),
            like((RANK, chunks * d), F32),
        ],
        scratch_shapes=[
            pltpu.VMEM((d + PAD, chunks * d), BF16),
            pltpu.VMEM((ROWS, d + PAD), BF16),
            pltpu.VMEM((ROWS, chunks * d), BF16),
            pltpu.SemaphoreType.DMA((chunks + len(pieces),)),
            *more,
        ],
        compiler_params=PARAMS,
        cost_estimate=cost(4 * tokens * d * d * chunks, 50_000_000),
        name="feed_forward",
    )(order, x3, cot, *grad_active, *pieces, mods, maps, up)


def run_feed_forward_out(active, x3, cot, mods, maps, down, parts, half, halves):
    tokens, d = x3.shape
    order, *pieces = down
    hidden = active.shape[1]
    share = tokens // parts
    parts = parts // halves
    steps = tokens // ROWS // halves
    start = half * steps

    def body(*refs):
        feed_forward_out(len(pieces), *refs)

    rows = pl.BlockSpec((ROWS, d), lambda i: (i + start, 0))
    return pl.pallas_call(
        body,
        grid=(steps,),
        in_specs=[
            in_smem(),
            pl.BlockSpec((ROWS, hidden), lambda i: (i + start, 0)),
            rows,
            rows,
            whole_block(mods),
            whole_block(maps),
        ]
        + [anywhere()] * len(pieces),
        out_specs=[pl.BlockSpec((share, d), lambda i: (0, 0))] * parts
        + [
            pl.BlockSpec((RANK, d), lambda i: (0, 0)),
            pl.BlockSpec((RANK, hidden), lambda i: (0, 0)),
        ],
        out_shape=[like((share, d), BF16)] * parts
        + [
            like((RANK, d), F32),
            like((RANK, hidden), F32),
        ],
        scratch_shapes=[
            pltpu.VMEM((hidden, d + PAD), BF16),
            pltpu.SemaphoreType.DMA((len(pieces),)),
        ],
        compiler_params=PARAMS,
        cost_estimate=cost(2 * steps * ROWS * d * hidden, 20_000_000, 64),
        name="feed_forward_out",
    )(order, active, x3, cot, mods, maps, *pieces)


def run_cross_temporal_backward(g3, u1, saved, mods, masks, wide, w_tc, start, groups):
    parts = len(u1)
    own_frames, places, d = u1[0].shape
    frames = own_frames * parts
    each = ROWS // frames
    across = pl.BlockSpec((frames, ROWS // frames, d), lambda i: (0, i + start, 0))
    by_group = lambda i: (i + start, 0, 0)
    stat = pl.BlockSpec((1, HEADS, ROWS), by_group)
    three = pl.BlockSpec((1, ROWS, 3 * RANK), by_group)
    one = pl.BlockSpec((1, ROWS, RANK), by_group)
    kp, vp = saved[13:15]
    pair_sums = pl.BlockSpec((PAIRS, 2 * PAD, 256), lambda i: (0, 0, 0))

    def body(*refs):
        cross_temporal_backward(parts, *refs)

    return pl.pallas_call(
        body,
        grid=(groups,),
        in_specs=[pl.BlockSpec((own_frames, each, d), lambda i: (0, i + start, 0))] * parts
        + [across] + [across] * 4 + [stat, three, one] + [across] * 3 + [stat, one, one]
        + [whole_block(kp), whole_block(vp)]
        + [whole_block(mods), whole_block(masks), whole_block(wide), anywhere()],
        out_specs=[pl.BlockSpec((own_frames, each, d), lambda i: (0, i, 0))] * parts
        + [
            pl.BlockSpec((16 * RANK, d), lambda i: (0, 0)),
            pair_sums,
            pair_sums,
        ],
        out_shape=[like((own_frames, groups * each, d), BF16)] * parts
        + [like((16 * RANK, d), F32)]
        + [like((PAIRS, 2 * PAD, 256), F32)] * 2,
        scratch_shapes=[
            pltpu.VMEM((6, d + PAD, d), BF16),
            pltpu.VMEM((ROWS, ROWS), F32),
        ]
        + [pltpu.VMEM((ROWS, d), BF16)] * 7
        + [pltpu.SemaphoreType.DMA((6,))],
        compiler_params=PARAMS,
        cost_estimate=cost(14 * groups * ROWS * d * d, 30_000_000, 64),
        name="cross_temporal_backward",
    )(*u1, g3, *saved[:15], mods, masks, wide, w_tc)


LATE_BLOCKS = 8
EARLY_BLOCKS = 28


def run_spatial_backward(seq, g1, halves, video, saved, mods, masks, wide, w_s, clips, start, count, before):
    frames, rows, d = video.shape
    parts = len(g1) // halves
    by_frame = lambda i: (i + start, 0, 0)
    row_block = pl.BlockSpec((1, rows, d), by_frame)
    last = start + count == frames
    sums = (8 * RANK, d)
    if last:
        sums = (clips * parts, *packed_rows(LATE_BLOCKS // parts, d // clips))
    zeros = (0,) * len(sums)

    def body(*refs):
        spatial_backward(len(g1), halves, clips, bool(before), last, *refs)

    extra = [anywhere(), whole_block(before[1])] if before else []
    return pl.pallas_call(
        body,
        grid=(count,),
        in_specs=[in_smem()] + [pl.BlockSpec((1, g.shape[1], d), by_frame) for g in g1]
        + extra
        + [row_block] * 5
        + [
            pl.BlockSpec((1, HEADS, rows), by_frame),
            pl.BlockSpec((1, rows, 3 * RANK), by_frame),
            pl.BlockSpec((1, rows, RANK), by_frame),
            whole_block(mods),
            whole_block(masks),
            whole_block(wide),
            anywhere(),
        ],
        out_specs=[
            pl.BlockSpec((1, rows, 3 * d + PAD), by_frame),
            pl.BlockSpec(sums, lambda i: zeros),
        ],
        out_shape=[like((frames, rows, 3 * d + PAD), BF16), like(sums, BF16 if last else F32)],
        input_output_aliases={1 + len(g1): 0} if before else {},
        scratch_shapes=[pltpu.VMEM((d + PAD, d), BF16), pltpu.VMEM((LATE_BLOCKS * RANK, d), F32)]
        + [pltpu.VMEM((ROWS, d), BF16), pltpu.SemaphoreType.DMA((1,))],
        compiler_params=PARAMS,
        cost_estimate=cost(6 * count * rows * d * d, 20_000_000, 64),
        name="spatial_backward",
    )(seq, *g1, *before, video, *saved, mods, masks, wide, w_s)


def run_spatial_input_grad(seq, g1, halves, video, grads, mods, wide, w_s):
    frames, rows, d = video.shape
    by_frame = lambda i: (i, 0, 0)
    row_block = pl.BlockSpec((1, rows, d), by_frame)

    def body(*refs):
        spatial_input_grad(len(g1), halves, *refs)

    return pl.pallas_call(
        body,
        grid=(frames,),
        in_specs=[in_smem()] + [pl.BlockSpec((1, g.shape[1], d), by_frame) for g in g1]
        + [
            row_block,
            pl.BlockSpec((1, rows, grads.shape[2]), by_frame),
            whole_block(mods),
            whole_block(wide),
            anywhere(),
        ],
        out_specs=row_block,
        out_shape=like(video.shape, BF16),
        scratch_shapes=[
            pltpu.VMEM((d, 3 * d + PAD), BF16),
            pltpu.VMEM((ROWS, d), BF16),
            pltpu.SemaphoreType.DMA((3,)),
        ],
        compiler_params=PARAMS,
        cost_estimate=cost(6 * frames * rows * d * d, 20_000_000, 64),
        name="spatial_input_grad",
    )(seq, *g1, video, grads, mods, wide, w_s)


def run_put_in_place(seq, pieces):
    frames, places, d = pieces[0].shape
    by_frame = lambda i: (i, 0, 0)
    rows = places * len(pieces)
    return pl.pallas_call(
        put_in_place,
        grid=(frames,),
        in_specs=[in_smem()] + [pl.BlockSpec((1, places, d), by_frame)] * len(pieces),
        out_specs=pl.BlockSpec((1, rows, d), by_frame),
        out_shape=like((frames, rows, d), BF16),
        compiler_params=PARAMS,
        cost_estimate=cost(0, 4 * frames * rows * d, 64),
        name="put_in_place",
    )(seq, *pieces)


PLAIN = pltpu.CompilerParams(vmem_limit_bytes=VMEM_LIMIT)


def in_vmem():
    return pl.BlockSpec(memory_space=pltpu.VMEM)


def run_pack_early(gw, dk, dv, others, sources, clips, parts):
    d = gw[0].shape[1]
    packed = (clips * parts, *packed_rows(EARLY_BLOCKS // parts, d // clips))

    def body(*refs):
        pack_early(clips, len(gw), [len(each) for each in others], *refs)

    return pl.pallas_call(
        body,
        out_shape=like(packed, BF16),
        scratch_shapes=[pltpu.VMEM((EARLY_BLOCKS * RANK, d), F32), pltpu.VMEM((PAD, d), F32)],
        compiler_params=PLAIN,
        cost_estimate=cost(50000000, 8000000, 64),
        name="pack_early",
    )(*gw, *dk, *dv, *[array for each in others for array in each], *sources)


def run_assemble(seq, early, late, wide_shape, narrow_shape):
    parts = len(early)

    def body(*refs):
        assemble(parts, *refs)

    return pl.pallas_call(
        body,
        in_specs=[in_smem()] + [in_vmem()] * (2 * parts),
        out_specs=[in_vmem()] * 2,
        out_shape=[like(wide_shape, F32), like(narrow_shape, F32)],
        scratch_shapes=[pltpu.VMEM((parts, *piece.shape), BF16) for piece in (early[0], late[0])],
        compiler_params=PLAIN,
        cost_estimate=cost(0, 6_000_000, 64),
        name="assemble",
    )(seq, *early, *late)


def run_pick(all_index, wide, narrow):
    count, _, _, cols = wide.shape
    shape = packed_rows(count + 2 * (narrow.shape[3] // cols), cols)
    return pl.pallas_call(
        pick,
        in_specs=[in_smem(), in_vmem(), in_vmem()],
        out_specs=in_vmem(),
        out_shape=like((all_index.shape[0], *shape), BF16),
        compiler_params=PLAIN,
        cost_estimate=cost(0, 3000000),
        name="pick",
    )(all_index, wide, narrow)


def run_unpick(got, blocks, cols):
    def body(*refs):
        unpick(blocks, cols, *refs)

    return pl.pallas_call(
        body,
        in_specs=[in_vmem()],
        out_specs=in_vmem(),
        out_shape=like((blocks, RANK, got.shape[0] * cols), BF16),
        compiler_params=PLAIN,
        cost_estimate=cost(0, 2500000),
        name="unpick",
    )(got)


def run_combine(all_index, got, adapters):
    _, share, cols = got.shape
    return pl.pallas_call(
        combine,
        in_specs=[pl.BlockSpec(memory_space=pltpu.SMEM), pl.BlockSpec(memory_space=pltpu.VMEM)],
        out_specs=pl.BlockSpec(memory_space=pltpu.VMEM),
        out_shape=like((adapters, share, cols), BF16),
        scratch_shapes=[pltpu.VMEM((adapters, share, cols), F32)],
        compiler_params=pltpu.CompilerParams(vmem_limit_bytes=VMEM_LIMIT),
        cost_estimate=cost(0, 1000000, 64),
        name="combine",
    )(all_index, got)


def exchange(array, axes="seq"):
    return lax.all_to_all(array, axes, split_axis=0, concat_axis=0, tiled=True)


def up_chunks(up, clips, times):
    rows, hidden = up.shape
    cols = hidden // (clips * times)
    return up.reshape(rows, clips, times, cols).transpose(2, 0, 1, 3).reshape(times, rows, -1)


def gather(array):
    return lax.all_gather(array, "fsdp", axis=1, tiled=True)


def send(array, axis, shift):
    size = lax.axis_size(axis)
    return lax.ppermute(array, axis, [(i, (i + shift) % size) for i in range(size)])


def to_places(pieces):
    return [pieces[0]] + [send(pieces[k], "seq", k) for k in range(1, len(pieces))]


def to_frames(pieces):
    return [pieces[0]] + [send(pieces[k], "seq", -k) for k in range(1, len(pieces))]


def gather_spatial_and_down(spatial, down, parts, times, clips, d):
    if times != parts or clips % 2:
        return gather(spatial)
    own = lax.dynamic_slice_in_dim(down.reshape(times, -1, d), lax.axis_index("seq"), 1, 0)
    return gather(jnp.concatenate([spatial, own], 0))


def start_down(got, parts, times, clips, d):
    if times != parts or clips % 2:
        return None
    half = d // 2
    core = lax.axis_index("fsdp") % 2
    first = lax.dynamic_slice(got, (times, core * half, 0), (1, half, d))[0]
    other = lax.dynamic_slice(got, (times, (1 - core) * half, 0), (1, half, d))[0]
    return first, other, send(first, "seq", 1), send(first, "seq", -1)


def swap_cores(piece, clips):
    return lax.ppermute(piece, "fsdp", [(i, i ^ 1) for i in range(clips)])


def to_all(piece):
    return [piece] + [send(piece, "seq", k) for k in range(1, lax.axis_size("seq"))]


def down_order(times, parts, clips):
    if times != parts or clips % 2:
        return jnp.arange(times, dtype=jnp.int32), jnp.zeros((1,), jnp.int32)
    seq = lax.axis_index("seq")
    core = lax.axis_index("fsdp") % 2
    return ((seq - jnp.arange(parts)) % parts).astype(jnp.int32), core.astype(jnp.int32)[None]


def on_device(
    video,
    context,
    modulation,
    adapter_index,
    cotangent,
    qkv_weights,
    out_weights,
    ffn_up,
    ffn_down,
    adapt_wide,
    adapt_ff,
):
    parts = lax.axis_size("seq")
    clips = lax.axis_size("fsdp")
    d = video.shape[-1]
    count, adapters, _, cols = adapt_wide.shape[1:]
    times = adapt_ff.shape[-1] // cols
    places = SPATIAL // parts
    frames = FRAMES // parts
    half_d = d // 2
    mods = modulation[0, 0]
    masks = head_masks()
    ctx = jnp.pad(context[0], ((0, PAD - context.shape[1]), (0, 0)))

    def attention_weights(j):
        return jnp.concatenate([qkv_weights[0, 3 * j : 3 * j + 3], out_weights[0, j : j + 1]], 0)

    seq = lax.axis_index("seq").astype(jnp.int32)[None]
    all_index = exchange(jnp.broadcast_to(adapter_index, (clips,)), "fsdp")
    w_s = gather_spatial_and_down(attention_weights(0), ffn_down[0], parts, times, clips, d)
    picked = run_pick(all_index, adapt_wide[0], adapt_ff[0])
    wide = run_unpick(exchange(picked, "fsdp"), count + 2 * times, cols)
    w_tc = gather(jnp.concatenate([attention_weights(1), attention_weights(2)], 0))
    ffn_up, _ = lax.optimization_barrier((ffn_up, picked))
    up = gather(up_chunks(ffn_up[0], clips, times))
    cot = cotangent.reshape(frames, SPATIAL, d)
    cot = to_places(
        [
            lax.dynamic_slice_in_dim(cot, (seq[0] + k) % parts * places, places, 1)
            for k in range(parts)
        ]
    )
    frames_in = video.reshape(frames, SPATIAL, d)
    maps_f = wide[24:]
    order, core = down_order(times, parts, clips)
    packed_order = jnp.concatenate([order, core])
    if times == parts and clips % 2 == 0:
        packed_order = jnp.concatenate([order[:2], order[parts - 1 :], order[2 : parts - 1], core])
    w_s, wide, maps_f, packed_order, *cot = lax.optimization_barrier((w_s, wide, maps_f, packed_order, *cot))
    started = start_down(w_s, parts, times, clips, d)
    cot = jnp.concatenate(cot, 0).reshape(FRAMES * places, d)
    made = run_spatial_forward(seq, frames_in, mods, masks, wide, w_s, parts)
    u1, kept_s = to_places(made[:parts]), made[parts:]
    if started is None:
        whole_down = gather(ffn_down[0].reshape(times, -1, d))
        sides = [[whole_down[i, :half_d] for i in range(times)], [whole_down[i, half_d:] for i in range(times)]]
        *kept_t, x2 = run_temporal_forward(u1, mods, masks, wide, w_tc)
        *kept_c, x3 = run_cross_forward(x2, ctx, masks, wide, w_tc)
        late_pieces = []
        grad_active = [run_feed_forward_grad(cot, mods, maps_f, packed_order, sides[0] + sides[1])]
    else:
        first, other, second, third = started
        second, third, cot, x1_own = lax.optimization_barrier((second, third, cot, u1[0]))
        mine = [first, second, third]
        others = [other] + [swap_cores(piece, clips) for piece in mine[1:]]
        early_order = jnp.concatenate([packed_order[:3], core])
        grad_active = run_feed_forward_grad(cot, mods, maps_f, early_order, mine + others)
        second, grad_active, *u1 = lax.optimization_barrier((second, grad_active, x1_own, *u1[1:]))
        rest = [send(second, "seq", 1)] + [send(first, "seq", k) for k in range(3, parts - 1)]
        *kept_t, x2 = run_temporal_forward(u1, mods, masks, wide, w_tc)
        x2, *rest = lax.optimization_barrier((x2, *rest))
        rest_others = [swap_cores(piece, clips) for piece in rest]
        *kept_c, x3 = run_cross_forward(x2, ctx, masks, wide, w_tc)
        grad_active = [grad_active]
        late_pieces = rest + rest_others
        sides = [mine + rest, others + rest_others]
    down = [packed_order, *sides[0], *sides[1]]
    x3 = x3.reshape(FRAMES * places, d)
    active, g3, grad_a24, grad_b24 = run_feed_forward(
        x3, cot, packed_order, grad_active, late_pieces, mods, maps_f, up
    )
    g3 = g3.reshape(FRAMES, places, d)
    groups = FRAMES * places // ROWS
    saved = kept_t + kept_c
    turns = 2 if groups % 2 == 0 and parts % 2 == 0 else 1
    output, grad_b25, grad_down = [None] * parts, [], []

    def finish_tokens(turn, active):
        *x4, b25, rows = run_feed_forward_out(active, x3, cot, mods, maps_f, down, parts, turn, turns)
        grad_b25.append(b25)
        grad_down.append(rows)
        for k, piece in enumerate(x4, turn * parts // turns):
            output[k] = piece.reshape(frames, places, d)

    def send_tokens(turn):
        for k in range(turn * parts // turns, (turn + 1) * parts // turns):
            output[k] = send(output[k], "seq", -k) if k else output[k]

    finish_tokens(turns - 1, active)
    output[-1], g3 = lax.optimization_barrier((output[-1], g3))
    send_tokens(turns - 1)
    shares = [groups - groups // 2, groups // 2] if groups > 1 else [1]
    g1, gw, dk, dv = [], [], [], []
    for share, size in enumerate(shares):
        *pieces, gw_part, dk_part, dv_part = run_cross_temporal_backward(
            g3, u1, saved, mods, masks, wide, w_tc, sum(shares[:share]), size
        )
        gw.append(gw_part)
        dk.append(dk_part)
        dv.append(dv_part)
        if share == 0 and turns > 1:
            half = parts // turns
            pieces[0], g3, *output[half:] = lax.optimization_barrier((pieces[0], g3, *output[half:]))
        else:
            pieces[0], g3 = lax.optimization_barrier((pieces[0], g3))
        g1.append(to_frames(pieces))
    if len(shares) > 1:
        active, gw[-1], *g1[0] = lax.optimization_barrier((active, gw[-1], *g1[0]))
    if turns > 1:
        finish_tokens(0, active)
        send_tokens(0)
    others = [[grad_a24], grad_b25, [grad_b24], grad_down]
    sources = [kept_c[7], kept_c[8], ctx, masks, wide]
    packed = run_pack_early(gw, dk, dv, others, sources, clips, parts)
    g1 = [piece for done in g1 for piece in done]
    packed, *g1 = lax.optimization_barrier((packed, *g1))
    got = exchange(packed, ("fsdp", "seq"))
    halves = len(shares)
    grads, packed = run_spatial_backward(
        seq, g1, halves, frames_in, kept_s, mods, masks, wide, w_s, clips, 0, frames, []
    )
    packed, got, *output = lax.optimization_barrier((packed, got, *output))
    early = to_all(run_combine(all_index, got, adapters))
    g0 = run_spatial_input_grad(seq, g1, halves, frames_in, grads, mods, wide, w_s)
    got, g0 = lax.optimization_barrier((exchange(packed, ("fsdp", "seq")), g0))
    late = run_combine(all_index, got, adapters)
    wide_out, narrow_out = run_assemble(
        seq, early, to_all(late), adapt_wide.shape[1:], adapt_ff.shape[1:]
    )
    output = run_put_in_place(seq, output).reshape(video.shape)
    return (output, g0.reshape(video.shape), wide_out[None], narrow_out[None])


def solution(mesh):
    return jax.shard_map(
        on_device,
        mesh=mesh,
        in_specs=(
            P("fsdp", "seq", None),
            P("fsdp", None, None),
            P("fsdp", None, None, None),
            P("fsdp"),
            P("fsdp", "seq", None),
            P(None, None, "fsdp", None),
            P(None, None, "fsdp", None),
            P(None, "fsdp", None),
            P(None, "fsdp", None),
            P(None, None, None, None, "fsdp"),
            P(None, None, None, None, "fsdp"),
        ),
        out_specs=(
            P("fsdp", "seq", None),
            P("fsdp", "seq", None),
            P(None, None, None, None, "fsdp"),
            P(None, None, None, None, "fsdp"),
        ),
        check_vma=False,
    )
```

```python
import math

import jax
import jax.numpy as jnp
from jax import lax
from jax.experimental import pallas as pl
from jax.experimental.pallas import tpu as pltpu
from jax.sharding import PartitionSpec as P

HEAD_DIM = 72
HEADS = 16
FRAMES = 16
SPATIAL = 256
RANK = 16
ROWS = 256
PAIRS = HEADS // 2
PAD = 128
SCALE = HEAD_DIM ** (-0.5)
EXP_SCALE = SCALE * math.log2(math.e)
LN2 = math.log(2.0)
HIGHEST = lax.Precision.HIGHEST
F32 = jnp.float32
BF16 = jnp.bfloat16
VMEM_LIMIT = 60 * 1024 * 1024


def nn(left, right):
    return lax.dot_general(left, right, (((1,), (0,)), ((), ())), preferred_element_type=F32)


def nt(left, right):
    return lax.dot_general(left, right, (((1,), (1,)), ((), ())), preferred_element_type=F32)


def tn(left, right):
    return lax.dot_general(left, right, (((0,), (0,)), ((), ())), preferred_element_type=F32)


def window(pair):
    return slice(128 * pair, 128 * pair + 256)


def normalize(stream):
    average = jnp.mean(stream, -1, keepdims=True)
    centred = stream - average
    inverse = lax.rsqrt(jnp.mean(centred * centred, -1, keepdims=True) + 1e-06)
    return centred * inverse, inverse


def normalize_back(normal, inverse, grad):
    mean_grad = jnp.mean(grad, -1, keepdims=True)
    mean_both = jnp.mean(grad * normal, -1, keepdims=True)
    return inverse * (grad - mean_grad - normal * mean_both)


def up_rows(ad_ref, number, slot, width):
    rows = ad_ref[2 * number + 1]
    before = jnp.zeros((RANK * slot, width), BF16)
    after = jnp.zeros((PAD - RANK * (slot + 1), width), BF16)
    return jnp.concatenate(([before] if slot else []) + [rows, after], 0)


def three_downs(ad_ref, number):
    return jnp.concatenate([ad_ref[2 * (number + i)] for i in range(3)], 0)


class Loads:
    def __init__(self, entries, sems):
        self.first = pl.program_id(0) == 0
        self.entries = entries
        self.sems = sems

    def copy(self, index):
        source, target = self.entries[index]
        return pltpu.make_async_copy(source, target, self.sems.at[index])

    def start(self):
        @pl.when(self.first)
        def _():
            for index in range(len(self.entries)):
                self.copy(index).start()

    def ready(self, index):
        @pl.when(self.first)
        def _():
            self.copy(index).wait()


def head_masks():
    lane = jnp.arange(256)[None, :]
    begin = jnp.array([16 * (h // 2) + HEAD_DIM * (h % 2) for h in range(HEADS)])[:, None]
    return ((lane >= begin) & (lane < begin + HEAD_DIM)).astype(BF16)


def same_place(shape):
    rows = lax.broadcasted_iota(jnp.int32, shape, 0)
    cols = lax.broadcasted_iota(jnp.int32, shape, 1)
    return jnp.where(rows % 16 == cols % 16, 0.0, -1e30).astype(F32)


def attend(q_ref, k_ref, v_ref, mask_ref, bias, put_out, stat_ref):
    carried = None
    for pair in range(PAIRS):
        win = window(pair)
        q_win, k_win, v_win = q_ref[:, win], k_ref[:, win], v_ref[:, win]
        all_weights, all_values = [], []
        for head in (2 * pair, 2 * pair + 1):
            mask = mask_ref[head : head + 1, :]
            scores = nt(k_win * mask, q_win)
            if bias is not None:
                scores = scores + bias[...]
            top = jnp.max(scores, 0, keepdims=True)
            grown = jnp.exp2(scores - top)
            total = jnp.sum(grown, 0, keepdims=True)
            stat_ref[head : head + 1, :] = top + jnp.log2(total)
            all_weights.append((grown * (1.0 / total)).astype(BF16))
            all_values.append(v_win * mask)
        out = tn(jnp.concatenate(all_weights, 0), jnp.concatenate(all_values, 0))
        low = out[:, :128]
        put_out(pair, low if carried is None else low + carried)
        carried = out[:, 128:]
    put_out(PAIRS, carried)


def attend_back(q_ref, k_ref, v_ref, do_ref, mask_ref, bias, stat_ref, put):
    carried = None
    for pair in range(PAIRS):
        win = window(pair)
        q_win, k_win, v_win, do_win = q_ref[:, win], k_ref[:, win], v_ref[:, win], do_ref[:, win]
        all_grads, all_probs, keys, queries, outs = [], [], [], [], []
        for head in (2 * pair, 2 * pair + 1):
            mask = mask_ref[head : head + 1, :]
            k_own = k_win * mask
            scores = nt(k_own, q_win)
            if bias is not None:
                scores = scores + bias[...]
            probs = jnp.exp2(scores - stat_ref[head : head + 1, :])
            grad_probs = nt(v_win * mask, do_win)
            inner = jnp.sum(probs * grad_probs, 0, keepdims=True)
            all_grads.append((probs * (grad_probs - inner)).astype(BF16))
            all_probs.append(probs.astype(BF16))
            keys.append(k_own)
            queries.append(q_win * mask)
            outs.append(do_win * mask)
        grads = (
            tn(jnp.concatenate(all_grads, 0), jnp.concatenate(keys, 0)),
            nn(jnp.concatenate(all_grads, 1), jnp.concatenate(queries, 0)),
            nn(jnp.concatenate(all_probs, 1), jnp.concatenate(outs, 0)),
        )
        lows = tuple(g[:, :128] for g in grads)
        if carried is not None:
            lows = tuple(a + b for a, b in zip(lows, carried))
        put(pair, lows)
        carried = tuple(g[:, 128:] for g in grads)
    put(PAIRS, carried)


def tile(index):
    return slice(128 * index, 128 * index + 128)


def three_projections(lhs_ref, ad_ref, number, weights, loads, first_load, outs, rank_ref):
    width = weights.shape[2]
    ranks = nt(lhs_ref[:, :width], three_downs(ad_ref, number)).astype(BF16)
    rank_ref[...] = ranks
    lhs_ref[:, width : width + 3 * RANK] = ranks
    for i in range(3):
        loads.ready(first_load + i)
        total = nn(lhs_ref[...], weights[first_load + i])
        outs[i][...] = (total * EXP_SCALE if i == 0 else total).astype(BF16)


def one_projection(lhs_ref, ad_ref, number, weight_ref, rank_ref):
    width = weight_ref.shape[1]
    ranks = nt(lhs_ref[:, :width], ad_ref[2 * number]).astype(BF16)
    rank_ref[...] = ranks
    lhs_ref[:, width : width + RANK] = ranks
    return nn(lhs_ref[...], weight_ref[...])


def block_rows(index):
    return slice(RANK * index, RANK * (index + 1))


def one_back(grad, kept, ranks, ad_ref, number, weight_ref, grad_ref, at):
    width = weight_ref.shape[1]
    both = nt(grad, weight_ref[...])
    grad_rank = both[:, width : width + RANK].astype(BF16)
    grad_ref[block_rows(at), :] += tn(grad_rank, kept)
    grad_ref[block_rows(at + 1), :] += tn(ranks, grad)
    return both[:, :width] + nn(grad_rank, ad_ref[2 * number])


def three_back(grads, inputs, ranks, ad_ref, number, weights, loads, first_load, grad_ref, at):
    width = weights.shape[2]
    both = None
    for i in range(3):
        grad = grads[i][...]
        ups = tn(ranks, grad)
        grad_ref[block_rows(at + 2 * i + 1), :] += ups[block_rows(i)]
        loads.ready(first_load + i)
        part = nt(grad, weights[first_load + i])
        both = part if both is None else both + part
    grad_ranks = both[:, width : width + 3 * RANK].astype(BF16)
    downs = tn(grad_ranks, inputs)
    for i in range(3):
        grad_ref[block_rows(at + 2 * i), :] += downs[block_rows(i)]
    return both[:, :width] + nn(grad_ranks, three_downs(ad_ref, number))


def place_of(seq_ref, k, parts, places):
    return pl.multiple_of(lax.rem(seq_ref[0] + k, parts) * places, 16)


def spatial_forward(seq_ref, x_ref, mod_ref, mask_ref, ad_ref, w_hbm, *refs):
    x1_refs = refs[:-11]
    q_ref, k_ref, v_ref, o_ref, stat_ref, rq_ref, ro_ref, w_ref, lhs_ref, x1_s, sems = refs[-11:]
    width = x_ref.shape[2]
    loads = Loads([(w_hbm.at[i], w_ref.at[i, pl.ds(0, width), :]) for i in range(4)], sems)
    loads.start()

    @pl.when(loads.first)
    def _():
        lhs_ref[:, width:] = jnp.zeros((ROWS, PAD), BF16)
        for i in range(4):
            w_ref[i, width:, :] = up_rows(ad_ref, i, i % 3, width)

    stream = x_ref[0].astype(F32)
    normal, _ = normalize(stream)
    lhs_ref[:, :width] = (normal * (1.0 + mod_ref[1:2, :]) + mod_ref[0:1, :]).astype(BF16)
    q, k, v = q_ref.at[0], k_ref.at[0], v_ref.at[0]
    three_projections(lhs_ref, ad_ref, 0, w_ref, loads, 0, (q, k, v), rq_ref.at[0])

    def put_out(index, value):
        value = value.astype(BF16)
        o_ref[0, :, tile(index)] = value
        lhs_ref[:, tile(index)] = value

    attend(q, k, v, mask_ref, None, put_out, stat_ref.at[0])
    loads.ready(3)
    branch = one_projection(lhs_ref, ad_ref, 3, w_ref.at[3], ro_ref.at[0])
    x1_s[...] = (stream + mod_ref[2:3, :] * branch).astype(BF16)
    places = x1_refs[0].shape[1]
    for k, ref in enumerate(x1_refs):
        ref[0] = x1_s[pl.ds(place_of(seq_ref, k, len(x1_refs), places), places), :]


def rows_of(refs):
    pieces = [ref[...].reshape(-1, ref.shape[2]) for ref in refs]
    return pieces[0] if len(pieces) == 1 else jnp.concatenate(pieces, 0)


def temporal_forward(parts, *refs):
    x_refs, refs = refs[:parts], refs[parts:]
    (
        mod_ref, mask_ref, ad_ref, w_hbm,
        q_ref, k_ref, v_ref, o_ref, stat_ref, rq_ref, ro_ref, u2_ref, x2_ref,
        w_ref, bias_ref, lhs_ref, q_s, k_s, v_s, sems,
    ) = refs
    width = x_refs[0].shape[2]
    loads = Loads([(w_hbm.at[i], w_ref.at[i, pl.ds(0, width), :]) for i in range(4)], sems)
    loads.start()

    @pl.when(loads.first)
    def _():
        bias_ref[...] = same_place(bias_ref.shape)
        lhs_ref[:, width:] = jnp.zeros((ROWS, PAD), BF16)
        for i in range(4):
            w_ref[i, width:, :] = up_rows(ad_ref, 4 + i, i % 3, width)

    loaded = rows_of(x_refs)
    lhs_ref[:, :width] = loaded
    three_projections(lhs_ref, ad_ref, 4, w_ref, loads, 0, (q_s, k_s, v_s), rq_ref.at[0])
    q_ref[...] = q_s[...].reshape(q_ref.shape)
    k_ref[...] = k_s[...].reshape(k_ref.shape)
    v_ref[...] = v_s[...].reshape(v_ref.shape)

    def put_out(index, value):
        lhs_ref[:, tile(index)] = value.astype(BF16)

    attend(q_s, k_s, v_s, mask_ref, bias_ref, put_out, stat_ref.at[0])
    o_ref[...] = lhs_ref[:, :width].reshape(o_ref.shape)
    loads.ready(3)
    branch = one_projection(lhs_ref, ad_ref, 7, w_ref.at[3], ro_ref.at[0])
    stream = loaded.astype(F32) + mod_ref[2:3, :] * branch
    u2_ref[...] = stream.astype(BF16).reshape(u2_ref.shape)
    x2_ref[...] = stream.reshape(x2_ref.shape)


def cross_forward(
    x_ref, ctx_ref, mask_ref, ad_ref, w_hbm,
    q_ref, o_ref, stat_ref, rq_ref, ro_ref, kp_ref, vp_ref, rk_ref, rv_ref, x3_ref,
    w_ref, lhs_ref, q_s, k_s, sems,
):
    width = x_ref.shape[2]
    loads = Loads([(w_hbm.at[4 + i], w_ref.at[i, pl.ds(0, width), :]) for i in range(4)], sems)
    loads.start()

    @pl.when(loads.first)
    def _():
        lhs_ref[:, width:] = jnp.zeros((ROWS, PAD), BF16)
        for i in (0, 3):
            w_ref[i, width:, :] = up_rows(ad_ref, 8 + i, 0, width)

    stream = x_ref[...].reshape(ROWS, width)
    lhs_ref[:, :width] = stream.astype(BF16)
    loads.ready(0)
    queries = one_projection(lhs_ref, ad_ref, 8, w_ref.at[0], rq_ref.at[0])
    q_s[...] = (queries * EXP_SCALE).astype(BF16)
    q_ref[...] = q_s[...].reshape(q_ref.shape)
    loads.ready(1)
    loads.ready(2)

    @pl.when(loads.first)
    def _():
        for number, at, rank_ref, pair_ref in ((9, 1, rk_ref, kp_ref), (10, 2, rv_ref, vp_ref)):
            ranks = nt(ctx_ref[...], ad_ref[2 * number]).astype(BF16)
            rank_ref[...] = ranks
            made = nn(ctx_ref[...], w_ref[at, :width, :]) + nn(ranks, ad_ref[2 * number + 1])
            k_s[...] = made.astype(BF16)
            for pair in range(PAIRS):
                piece = k_s[:, window(pair)]
                pair_ref[pair, :PAD, :] = piece * mask_ref[2 * pair : 2 * pair + 1, :]
                pair_ref[pair, PAD:, :] = piece * mask_ref[2 * pair + 1 : 2 * pair + 2, :]

    carried = None
    count = 120
    for pair in range(PAIRS):
        scores = nt(kp_ref[pair], q_s[:, window(pair)])
        pieces = []
        for sub in range(2):
            own = scores[PAD * sub : PAD * sub + count]
            top = jnp.max(own, 0, keepdims=True)
            grown = jnp.exp2(own - top)
            total = jnp.sum(grown, 0, keepdims=True)
            stat_ref[0, 2 * pair + sub : 2 * pair + sub + 1, :] = top + jnp.log2(total)
            pieces += [grown * (1.0 / total), jnp.zeros((PAD - count, ROWS), F32)]
        weights = jnp.concatenate(pieces, 0).astype(BF16)
        out = tn(weights, vp_ref[pair])
        low = out[:, :128]
        lhs_ref[:, tile(pair)] = (low if carried is None else low + carried).astype(BF16)
        carried = out[:, 128:]
    lhs_ref[:, tile(PAIRS)] = carried.astype(BF16)
    o_ref[...] = lhs_ref[:, :width].reshape(o_ref.shape)
    loads.ready(3)
    stream = stream + one_projection(lhs_ref, ad_ref, 11, w_ref.at[3], ro_ref.at[0])
    x3_ref[...] = stream.reshape(x3_ref.shape)


def gelu_both(hidden):
    root = math.sqrt(2.0 / math.pi)
    square = hidden * hidden
    inner = root * (hidden + 0.044715 * (square * hidden))
    bent = jnp.tanh(inner)
    half = 0.5 * (1.0 + bent)
    slope = half + 0.5 * hidden * (1.0 - bent * bent) * (root * (1.0 + 3.0 * 0.044715 * square))
    return hidden * half, slope


def transposed_map(rows):
    nothing = jnp.zeros((PAD - rows.shape[0], rows.shape[1]), F32)
    wide = jnp.concatenate([rows.astype(F32), nothing], 0)
    return wide.T.astype(BF16)


def down_loads(order_ref, pieces, down_ref, width):
    half = width // 2
    count = len(pieces) // 2
    core = order_ref[count]
    entries = []
    for k in range(count):
        for source, side in ((pieces[k], core), (pieces[count + k], 1 - core)):
            start = pl.multiple_of(order_ref[k] * width + side * half, 16)
            entries.append((source, down_ref.at[pl.ds(start, half), pl.ds(0, width)]))
    return entries


def fill_down_maps(ad_ref, down_ref, width):
    chunks = down_ref.shape[0] // width
    for c in range(chunks):
        rows = slice(c * width, (c + 1) * width)
        down_ref[rows, width:] = transposed_map(ad_ref[2 + chunks + c])


def feed_forward_grad(count, order_ref, cot_ref, mod_ref, ad_ref, *refs):
    pieces = refs[:count]
    grad_ref, down_ref, lhs_ref, sems = refs[count:]
    width = cot_ref.shape[1]
    half = width // 2
    chunks = count // 2
    core = order_ref[chunks]
    entries = []
    for k in range(chunks):
        for source, side in ((pieces[k], core), (pieces[chunks + k], 1 - core)):
            start = pl.multiple_of(k * width + side * half, 16)
            entries.append((source, down_ref.at[pl.ds(start, half), pl.ds(0, width)]))
    loads = Loads(entries, sems)
    loads.start()

    @pl.when(loads.first)
    def _():
        lhs_ref[:, width:] = jnp.zeros((ROWS, PAD), BF16)
        for k in range(chunks):
            rows = slice(k * width, (k + 1) * width)
            down_ref[rows, width:] = transposed_map(ad_ref[2 + (ad_ref.shape[0] - 2) // 2 + order_ref[k]])

    branch = (mod_ref[5:6, :] * cot_ref[...].astype(F32)).astype(BF16)
    lhs_ref[:, :width] = branch
    lhs_ref[:, width : width + RANK] = nt(branch, ad_ref[1]).astype(BF16)
    for i in range(len(entries)):
        loads.ready(i)
    for k in range(chunks):
        rows = slice(k * width, (k + 1) * width)
        grad_ref[k] = nt(lhs_ref[...], down_ref[rows, :]).astype(BF16)


def hidden_chunks(hidden):
    return [slice(at, at + 1536) for at in range(0, hidden, 1536)]


def feed_forward(groups, count, order_ref, x3_ref, cot_ref, *refs):
    grad_refs, pieces, refs = refs[:groups], refs[groups : groups + count], refs[groups + count :]
    (
        mod_ref, ad_ref, w_hbm, act_ref, g3_ref, gd_ref, gu_ref, up_ref, lhs_ref, dh_ref, sems, *rest
    ) = refs
    width = x3_ref.shape[1]
    hidden_size = up_ref.shape[1]
    chunks = hidden_size // width
    late = count // 2
    core = order_ref[chunks]
    entries = [
        (w_hbm.at[c], up_ref.at[pl.ds(0, width), pl.ds(c * width, width)]) for c in range(chunks)
    ]
    if late:
        down_ref, dlhs_ref = rest
        half = width // 2
        for k in range(late):
            for source, side in ((pieces[k], core), (pieces[late + k], 1 - core)):
                start = pl.multiple_of(k * width + side * half, 16)
                entries.append((source, down_ref.at[pl.ds(start, half), pl.ds(0, width)]))
    loads = Loads(entries, sems)
    loads.start()

    @pl.when(loads.first)
    def _():
        gd_ref[...] = jnp.zeros_like(gd_ref)
        gu_ref[...] = jnp.zeros_like(gu_ref)
        lhs_ref[:, width:] = jnp.zeros((ROWS, PAD), BF16)
        up_ref[width + RANK :, :] = jnp.zeros((PAD - RANK, hidden_size), BF16)
        for c in range(chunks):
            up_ref[width : width + RANK, c * width : (c + 1) * width] = ad_ref[2 + c]
        for k in range(late):
            rows = slice(k * width, (k + 1) * width)
            at = order_ref[chunks - late + k]
            down_ref[rows, width:] = transposed_map(ad_ref[2 + chunks + at])
        if late:
            dlhs_ref[:, width:] = jnp.zeros((ROWS, PAD), BF16)

    normal, inverse = normalize(x3_ref[...])
    inputs = (normal * (1.0 + mod_ref[4:5, :]) + mod_ref[3:4, :]).astype(BF16)
    rank_up = nt(inputs, ad_ref[0]).astype(BF16)
    lhs_ref[:, :width] = inputs
    lhs_ref[:, width : width + RANK] = rank_up
    at = 0
    for grad_ref in grad_refs:
        for k in range(grad_ref.shape[0]):
            start = pl.multiple_of(order_ref[at] * width, 128)
            dh_ref[:, pl.ds(start, width)] = grad_ref[k]
            at += 1
    if late:
        branch = (mod_ref[5:6, :] * cot_ref[...].astype(F32)).astype(BF16)
        dlhs_ref[:, :width] = branch
        dlhs_ref[:, width : width + RANK] = nt(branch, ad_ref[1]).astype(BF16)
    for i in range(len(entries)):
        loads.ready(i)
    for k in range(late):
        start = pl.multiple_of(order_ref[at + k] * width, 128)
        rows = slice(k * width, (k + 1) * width)
        dh_ref[:, pl.ds(start, width)] = nt(dlhs_ref[...], down_ref[rows, :]).astype(BF16)
    for cols in hidden_chunks(hidden_size):
        active, slope = gelu_both(nn(lhs_ref[...], up_ref[:, cols]))
        act_ref[:, cols] = active.astype(BF16)
        dh_ref[:, cols] = (slope * dh_ref[:, cols].astype(F32)).astype(BF16)
    both = nt(dh_ref[...], up_ref[...])
    gu_ref[...] += tn(rank_up, dh_ref[...])
    grad_rank = both[:, width : width + RANK].astype(BF16)
    grad_in = both[:, :width] + nn(grad_rank, ad_ref[0])
    gd_ref[...] += tn(grad_rank, lhs_ref[:, :width])
    grad_in = normalize_back(normal, inverse, grad_in * (1.0 + mod_ref[4:5, :]))
    g3_ref[...] = cot_ref[...].astype(F32) + grad_in


def feed_forward_out(count, order_ref, act_ref, x3_ref, cot_ref, mod_ref, ad_ref, *refs):
    pieces, refs = refs[:count], refs[count:]
    x4_refs = refs[:-4]
    gu_ref, gd_ref, down_ref, sems = refs[-4:]
    width = x3_ref.shape[1]
    step = pl.program_id(0)
    entries = down_loads(order_ref, pieces, down_ref, width)
    loads = Loads(entries, sems)
    loads.start()

    @pl.when(loads.first)
    def _():
        gu_ref[...] = jnp.zeros_like(gu_ref)
        gd_ref[...] = jnp.zeros_like(gd_ref)
        fill_down_maps(ad_ref, down_ref, width)

    share = x4_refs[0].shape[0]
    grad_branch = (mod_ref[5:6, :] * cot_ref[...].astype(F32)).astype(BF16)
    gd_ref[...] += tn(nt(grad_branch, ad_ref[1]).astype(BF16), act_ref[...])
    for i in range(len(entries)):
        loads.ready(i)
    both = nn(act_ref[...], down_ref[...])
    ranks = both[:, width : width + RANK].astype(BF16)
    branch = both[:, :width] + nn(ranks, ad_ref[1])
    gu_ref[...] += tn(ranks, grad_branch)
    result = (x3_ref[...] + mod_ref[5:6, :] * branch).astype(BF16)
    for k, ref in enumerate(x4_refs):
        at = k * share

        @pl.when(step == at // ROWS)
        def _():
            ref[...] = result[at % ROWS : at % ROWS + share]


def cross_temporal_backward(parts, *refs):
    outs = len(refs) - parts - 13
    _cross_temporal_backward(refs[:parts], refs[outs : outs + parts], *refs[parts:outs], *refs[outs + parts :])


def _cross_temporal_backward(
    u1_refs, g1_refs, g3_ref, q_ref, k_ref, v_ref, o_ref, stat_ref, rq_ref, ro_ref,
    u2_ref, qc_ref, oc_ref, statc_ref, rqc_ref, roc_ref, kp_ref, vp_ref,
    mod_ref, mask_ref, ad_ref, w_hbm,
    gw_ref, dk_acc, dv_acc, w_ref, bias_ref, q_s, k_s, v_s, do_s, dq_s, dk_s, dv_s, sems,
):
    width = u1_refs[0].shape[2]
    first = pl.program_id(0) == 0
    order = (7, 4, 3, 0, 1, 2)
    loads = Loads(
        [(w_hbm.at[n], w_ref.at[i, pl.ds(0, width), :]) for i, n in enumerate(order)], sems
    )
    loads.start()

    @pl.when(first)
    def _():
        bias_ref[...] = same_place(bias_ref.shape)
        gw_ref[...] = jnp.zeros_like(gw_ref)
        dk_acc[...] = jnp.zeros_like(dk_acc)
        dv_acc[...] = jnp.zeros_like(dv_acc)
        for i, n in enumerate(order):
            w_ref[i, width:, :] = up_rows(ad_ref, 4 + n, n if n < 3 else 0, width)

    def rows(ref):
        return ref[...].reshape(ROWS, ref.shape[2])

    grad = rows(g3_ref)
    loads.ready(0)
    do_s[...] = one_back(
        grad.astype(BF16), rows(oc_ref), roc_ref[0], ad_ref, 11, w_ref.at[0], gw_ref, 14
    ).astype(BF16)
    q_s[...] = rows(qc_ref)
    count = 120
    carried = None
    for pair in range(PAIRS):
        win = window(pair)
        q_win, do_win = q_s[:, win], do_s[:, win]
        scores = nt(kp_ref[pair], q_win)
        grad_probs = nt(vp_ref[pair], do_win)
        all_probs, all_grads = [], []
        nothing = jnp.zeros((PAD - count, ROWS), F32)
        for sub in range(2):
            span = slice(PAD * sub, PAD * sub + count)
            row = 2 * pair + sub
            probs = jnp.exp2(scores[span] - statc_ref[0, row : row + 1, :])
            own = grad_probs[span]
            inner = jnp.sum(probs * own, 0, keepdims=True)
            all_probs += [probs, nothing]
            all_grads += [probs * (own - inner), nothing]
        probs = jnp.concatenate(all_probs, 0).astype(BF16)
        grad_scores = jnp.concatenate(all_grads, 0).astype(BF16)
        dk_acc[pair] += nn(grad_scores, q_win)
        dv_acc[pair] += nn(probs, do_win)
        out = tn(grad_scores, kp_ref[pair])
        low = out[:, :128]
        dq_s[:, tile(pair)] = ((low if carried is None else low + carried) * SCALE).astype(BF16)
        carried = out[:, 128:]
    dq_s[:, tile(PAIRS)] = (carried * SCALE).astype(BF16)
    loads.ready(1)
    grad = grad + one_back(
        dq_s[...], rows(u2_ref), rqc_ref[0], ad_ref, 8, w_ref.at[1], gw_ref, 8
    )
    loads.ready(2)
    do_s[...] = one_back(
        (mod_ref[2:3, :] * grad).astype(BF16), rows(o_ref), ro_ref[0], ad_ref, 7, w_ref.at[2], gw_ref, 6
    ).astype(BF16)
    q_s[...] = rows(q_ref)
    k_s[...] = rows(k_ref)
    v_s[...] = rows(v_ref)

    def put(index, values):
        dq_s[:, tile(index)] = (values[0] * SCALE).astype(BF16)
        dk_s[:, tile(index)] = (values[1] * LN2).astype(BF16)
        dv_s[:, tile(index)] = values[2].astype(BF16)

    attend_back(q_s, k_s, v_s, do_s, mask_ref, bias_ref, stat_ref.at[0], put)
    grad = grad + three_back(
        (dq_s, dk_s, dv_s), rows_of(u1_refs), rq_ref[0], ad_ref, 4, w_ref, loads, 3, gw_ref, 0
    )
    grad = grad.astype(BF16)
    share = ROWS // len(g1_refs)
    for k, ref in enumerate(g1_refs):
        ref[...] = grad[share * k : share * (k + 1)].reshape(ref.shape)


def tail_groups(cols):
    tail = cols - PAD
    return PAD // tail if 0 < tail < PAD and PAD % tail == 0 else 0


def packed_rows(blocks, cols):
    group = tail_groups(cols)
    if not group:
        return blocks * RANK, cols
    return (blocks + -(-blocks // group)) * RANK, PAD


def put_blocks(blocks, put):
    cols = blocks[0].shape[1]
    group = tail_groups(cols)
    for k, rows in enumerate(blocks):
        put(k, rows[:, :PAD] if group else rows)
    for k in range(0, len(blocks), group) if group else ():
        tails = [rows[:, PAD:] for rows in blocks[k : k + group]]
        missing = group - len(tails)
        if missing:
            tails.append(jnp.zeros((RANK, missing * (cols - PAD)), blocks[0].dtype))
        put(len(blocks) + k // group, jnp.concatenate(tails, 1))


def get_block(get, index, count, cols):
    group = tail_groups(cols)
    if not group:
        return get(index)
    at = (index % group) * (cols - PAD)
    return jnp.concatenate([get(index), get(count + index // group)[:, at : at + cols - PAD]], 1)


def pack_columns(table_ref, packed_ref, clips):
    parts = packed_ref.shape[0] // clips
    share = table_ref.shape[0] // parts
    cols = table_ref.shape[1] // clips
    for f in range(clips):
        for s in range(parts):
            piece = table_ref[share * s : share * (s + 1), cols * f : cols * (f + 1)].astype(BF16)
            blocks = [piece[block_rows(k)] for k in range(share // RANK)]

            def put(k, rows):
                packed_ref[f * parts + s, block_rows(k), :] = rows

            put_blocks(blocks, put)


def stacked(seq_ref, g1_refs, shares, whole_ref):
    parts = len(g1_refs) // shares
    places = whole_ref.shape[0] // parts
    at = 0
    for share in range(shares):
        refs = g1_refs[share * parts : (share + 1) * parts]
        size = refs[0].shape[1]
        for k, ref in enumerate(refs):
            start = pl.multiple_of(place_of(seq_ref, k, parts, places) + at, 16)
            whole_ref[pl.ds(start, size), :] = ref[0]
        at += size
    return whole_ref[...].astype(F32)


def spatial_backward(pieces, halves, clips, continued, last, seq_ref, *refs):
    g1_refs, refs = refs[:pieces], refs[pieces:]
    if continued:
        (_, before_ref), refs = refs[:2], refs[2:]
    (
        x_ref, q_ref, k_ref, v_ref, o_ref, stat_ref, rq_ref, ro_ref, mod_ref, mask_ref, ad_ref, w_hbm,
        d_ref, sums_ref, w_ref, gw_ref, do_s, sems,
    ) = refs
    width = x_ref.shape[2]
    loads = Loads([(w_hbm.at[3], w_ref.at[pl.ds(0, width), :])], sems)
    loads.start()

    @pl.when(loads.first)
    def _():
        gw_ref[...] = before_ref[...] if continued else jnp.zeros_like(gw_ref)
        w_ref[width:, :] = up_rows(ad_ref, 3, 0, width)

    grad = stacked(seq_ref, g1_refs, halves, do_s)
    loads.ready(0)
    do_s[...] = one_back(
        (mod_ref[2:3, :] * grad).astype(BF16), o_ref[0], ro_ref[0], ad_ref, 3, w_ref, gw_ref, 6
    ).astype(BF16)

    def put(index, values):
        for i, factor in enumerate((SCALE, LN2, 1.0)):
            value = values[i] if factor == 1.0 else values[i] * factor
            d_ref[0, :, width * i + 128 * index : width * i + 128 * index + 128] = value.astype(BF16)

    attend_back(
        q_ref.at[0], k_ref.at[0], v_ref.at[0], do_s, mask_ref, None, stat_ref.at[0], put
    )
    ranks = rq_ref[0]
    grad_ranks = None
    for i in range(3):
        grad = d_ref[0, :, width * i : width * (i + 1)]
        gw_ref[block_rows(2 * i + 1), :] += tn(ranks, grad)[block_rows(i)]
        part = nt(grad, up_rows(ad_ref, i, i, width))
        grad_ranks = part if grad_ranks is None else grad_ranks + part
    d_ref[0, :, 3 * width :] = grad_ranks.astype(BF16)
    normal, _ = normalize(x_ref[0].astype(F32))
    inputs = (normal * (1.0 + mod_ref[1:2, :]) + mod_ref[0:1, :]).astype(BF16)
    downs = tn(d_ref[0, :, 3 * width :], inputs)
    for i in range(3):
        gw_ref[block_rows(2 * i), :] += downs[block_rows(i)]

    @pl.when(pl.program_id(0) == pl.num_programs(0) - 1)
    def _():
        if last:
            pack_columns(gw_ref, sums_ref, clips)
        else:
            sums_ref[...] = gw_ref[...]


def spatial_input_grad(pieces, halves, seq_ref, *refs):
    g1_refs, refs = refs[:pieces], refs[pieces:]
    x_ref, d_ref, mod_ref, ad_ref, w_hbm, g0_ref, w_ref, whole_s, sems = refs
    width = x_ref.shape[2]
    loads = Loads(
        [(w_hbm.at[i], w_ref.at[:, pl.ds(i * width, width)]) for i in range(3)], sems
    )
    loads.start()

    @pl.when(loads.first)
    def _():
        w_ref[:, 3 * width :] = transposed_map(three_downs(ad_ref, 0))

    normal, inverse = normalize(x_ref[0].astype(F32))
    grad = stacked(seq_ref, g1_refs, halves, whole_s)
    for i in range(3):
        loads.ready(i)
    grad_in = nt(d_ref[0], w_ref[...])
    grad = grad + normalize_back(normal, inverse, grad_in * (1.0 + mod_ref[1:2, :]))
    g0_ref[0] = grad.astype(BF16)


def put_in_place(seq_ref, *refs):
    *pieces, out_ref = refs
    places = pieces[0].shape[1]
    for k, ref in enumerate(pieces):
        out_ref[0, pl.ds(place_of(seq_ref, k, len(pieces), places), places), :] = ref[0]


def pack_early(clips, shares, counts, *refs):
    gw_refs, refs = refs[:shares], refs[shares:]
    dk_refs, refs = refs[:shares], refs[shares:]
    dv_refs, refs = refs[:shares], refs[shares:]
    *others, rk_ref, rv_ref, ctx_ref, mask_ref, ad_ref, packed_ref, table_ref, ctx_s = refs

    def added(each):
        total = each[0]
        for value in each[1:]:
            total = total + value
        return total

    at = gw_refs[0].shape[0]
    table_ref[:at, :] = added([ref[...] for ref in gw_refs])
    width = table_ref.shape[1]
    for count in counts:
        each, others = others[:count], others[count:]
        for k in range(each[0].shape[1] // width):
            cols = slice(k * width, (k + 1) * width)
            table_ref[at : at + RANK, :] = added([ref[:, cols] for ref in each])
            at += RANK
    table_ref[at:, :] = jnp.zeros((table_ref.shape[0] - at, width), F32)
    context = ctx_ref[...].astype(F32)
    for accs, factor, rank_ref, number, at in (
        (dk_refs, LN2, rk_ref, 9, 10),
        (dv_refs, 1.0, rv_ref, 10, 12),
    ):
        held = None
        for pair in range(PAIRS):
            whole = added([ref[pair] for ref in accs]) * factor
            out = whole[:PAD] * mask_ref[2 * pair : 2 * pair + 1, :].astype(F32)
            out = out + whole[PAD:] * mask_ref[2 * pair + 1 : 2 * pair + 2, :].astype(F32)
            low = out[:, :128]
            ctx_s[:, tile(pair)] = low if held is None else low + held
            held = out[:, 128:]
        ctx_s[:, tile(PAIRS)] = held
        grad_kv = ctx_s[...]
        grad_rank = lax.dot_general(
            grad_kv, ad_ref[2 * number + 1].astype(F32), (((1,), (1,)), ((), ())),
            precision=HIGHEST, preferred_element_type=F32,
        )
        table_ref[block_rows(at), :] = lax.dot_general(
            grad_rank, context, (((0,), (0,)), ((), ())),
            precision=HIGHEST, preferred_element_type=F32,
        )
        table_ref[block_rows(at + 1), :] = lax.dot_general(
            rank_ref[...].astype(F32), grad_kv, (((0,), (0,)), ((), ())),
            precision=HIGHEST, preferred_element_type=F32,
        )
    pack_columns(table_ref, packed_ref, clips)


def assemble(parts, seq_ref, *refs):
    early_refs, late_refs, refs = refs[:parts], refs[parts : 2 * parts], refs[2 * parts :]
    wide_ref, narrow_ref, early_ref, late_ref = refs
    for k in range(parts):
        source = lax.rem(seq_ref[0] + parts - k, parts)
        early_ref[source] = early_refs[k][...]
        late_ref[source] = late_refs[k][...]
    _, adapters, _, cols = wide_ref.shape
    times = narrow_ref.shape[3] // cols

    def block(ref, total, index, a):
        each = total // ref.shape[0]

        def get(k):
            return ref[index // each, a, block_rows(k), :].astype(F32)

        return get_block(get, index % each, each, cols)

    for a in range(adapters):
        for i in range(8):
            wide_ref[i, a] = block(late_ref, LATE_BLOCKS, i, a)
        for i in range(18):
            wide_ref[8 + i, a] = block(early_ref, EARLY_BLOCKS, i, a)
        for n in range(2):
            pieces = [block(early_ref, EARLY_BLOCKS, 18 + n * times + j, a) for j in range(times)]
            narrow_ref[n, a] = jnp.concatenate(pieces, 1)


def combine(index_ref, got_ref, out_ref, acc_ref):
    clips = index_ref.shape[0]
    parts = got_ref.shape[0] // clips
    acc_ref[...] = jnp.zeros_like(acc_ref)

    def step(f, carry):
        total = got_ref[f * parts].astype(F32)
        for s in range(1, parts):
            total = total + got_ref[f * parts + s].astype(F32)
        acc_ref[index_ref[f]] += total
        return carry

    lax.fori_loop(0, clips, step, 0)
    out_ref[...] = acc_ref[...].astype(BF16)


def pick(index_ref, wide_ref, narrow_ref, out_ref):
    count, _, _, cols = wide_ref.shape
    times = narrow_ref.shape[3] // cols

    def step(f, carry):
        a = index_ref[f]
        blocks = [wide_ref[k, a] for k in range(count)]
        for p in range(2):
            rows = narrow_ref[p, a]
            blocks += [rows[:, cols * j : cols * (j + 1)] for j in range(times)]

        def put(k, rows):
            out_ref[f, block_rows(k), :] = rows

        put_blocks(blocks, put)
        return carry

    lax.fori_loop(0, index_ref.shape[0], step, 0)


def unpick(count, cols, got_ref, out_ref):
    for k in range(count):
        pieces = []
        for f in range(got_ref.shape[0]):

            def get(index):
                return got_ref[f, block_rows(index), :]

            pieces.append(get_block(get, k, count, cols))
        out_ref[k] = jnp.concatenate(pieces, 1)


def whole_block(array):
    zeros = (0,) * array.ndim
    return pl.BlockSpec(array.shape, lambda i: zeros, pipeline_mode=pl.Buffered(1))


def anywhere():
    return pl.BlockSpec(memory_space=pl.ANY)


def like(shape, dtype):
    return jax.ShapeDtypeStruct(shape, dtype)


PARAMS = pltpu.CompilerParams(
    dimension_semantics=("arbitrary",), vmem_limit_bytes=VMEM_LIMIT
)


def cost(flops, read, part=4):
    return pl.CostEstimate(
        flops=flops // part, bytes_accessed=read // part, transcendentals=0
    )


def run_spatial_forward(seq, video, mods, masks, wide, w_s, parts):
    frames, rows, d = video.shape
    places = rows // parts
    by_frame = lambda i: (i, 0, 0)
    row_block = pl.BlockSpec((1, rows, d), by_frame)
    return pl.pallas_call(
        spatial_forward,
        grid=(frames,),
        in_specs=[in_smem(), row_block, whole_block(mods), whole_block(masks), whole_block(wide), anywhere()],
        out_specs=[pl.BlockSpec((1, places, d), by_frame)] * parts
        + [
            row_block,
            row_block,
            row_block,
            row_block,
            pl.BlockSpec((1, HEADS, rows), by_frame),
            pl.BlockSpec((1, rows, 3 * RANK), by_frame),
            pl.BlockSpec((1, rows, RANK), by_frame),
        ],
        out_shape=[like((frames, places, d), BF16)] * parts
        + [like(video.shape, BF16)] * 4
        + [
            like((frames, HEADS, rows), F32),
            like((frames, rows, 3 * RANK), BF16),
            like((frames, rows, RANK), BF16),
        ],
        scratch_shapes=[
            pltpu.VMEM((4, d + PAD, d), BF16),
            pltpu.VMEM((ROWS, d + PAD), BF16),
            pltpu.VMEM((ROWS, d), BF16),
            pltpu.SemaphoreType.DMA((4,)),
        ],
        compiler_params=PARAMS,
        cost_estimate=cost(10 * frames * rows * d * d, 30_000_000),
        name="spatial_forward",
    )(seq, video, mods, masks, wide, w_s)


def run_temporal_forward(x1, mods, masks, wide, w_t):
    parts = len(x1)
    own_frames, places, d = x1[0].shape
    frames = own_frames * parts
    groups = places * frames // ROWS
    each = ROWS // frames
    across = pl.BlockSpec((frames, each, d), lambda i: (0, i, 0))
    by_group = lambda i: (i, 0, 0)
    act = like((frames, places, d), BF16)

    def body(*refs):
        temporal_forward(parts, *refs)

    return pl.pallas_call(
        body,
        grid=(groups,),
        in_specs=[pl.BlockSpec((own_frames, each, d), lambda i: (0, i, 0))] * parts
        + [whole_block(mods), whole_block(masks), whole_block(wide), anywhere()],
        out_specs=[across] * 4
        + [
            pl.BlockSpec((1, HEADS, ROWS), by_group),
            pl.BlockSpec((1, ROWS, 3 * RANK), by_group),
            pl.BlockSpec((1, ROWS, RANK), by_group),
            across,
            across,
        ],
        out_shape=[act] * 4
        + [
            like((groups, HEADS, ROWS), F32),
            like((groups, ROWS, 3 * RANK), BF16),
            like((groups, ROWS, RANK), BF16),
            act,
            like((frames, places, d), F32),
        ],
        scratch_shapes=[pltpu.VMEM((4, d + PAD, d), BF16), pltpu.VMEM((ROWS, ROWS), F32)]
        + [pltpu.VMEM((ROWS, d + PAD), BF16)]
        + [pltpu.VMEM((ROWS, d), BF16)] * 3
        + [pltpu.SemaphoreType.DMA((4,))],
        compiler_params=PARAMS,
        cost_estimate=cost(10 * places * frames * d * d, 30_000_000, 64),
        name="temporal_forward",
    )(*x1, mods, masks, wide, w_t)


def run_cross_forward(x2, context, masks, wide, w_c):
    frames, places, d = x2.shape
    groups = places * frames // ROWS
    across = pl.BlockSpec((frames, ROWS // frames, d), lambda i: (0, i, 0))
    by_group = lambda i: (i, 0, 0)
    full = lambda *shape: pl.BlockSpec(shape, lambda i: (0,) * len(shape))
    one = pl.BlockSpec((1, ROWS, RANK), by_group)
    one_shape = like((groups, ROWS, RANK), BF16)
    act = like((frames, places, d), BF16)
    return pl.pallas_call(
        cross_forward,
        grid=(groups,),
        in_specs=[across, whole_block(context), whole_block(masks), whole_block(wide), anywhere()],
        out_specs=[across] * 2 + [pl.BlockSpec((1, HEADS, ROWS), by_group), one, one]
        + [full(PAIRS, 2 * PAD, 256)] * 2 + [full(PAD, RANK)] * 2 + [across],
        out_shape=[act] * 2 + [like((groups, HEADS, ROWS), F32), one_shape, one_shape]
        + [like((PAIRS, 2 * PAD, 256), BF16)] * 2 + [like((PAD, RANK), BF16)] * 2
        + [like(x2.shape, F32)],
        scratch_shapes=[pltpu.VMEM((4, d + PAD, d), BF16), pltpu.VMEM((ROWS, d + PAD), BF16)]
        + [pltpu.VMEM((ROWS, d), BF16), pltpu.VMEM((PAD, d), BF16)]
        + [pltpu.SemaphoreType.DMA((4,))],
        compiler_params=PARAMS,
        cost_estimate=cost(8 * places * frames * d * d, 30_000_000, 64),
        name="cross_forward",
    )(x2, context, masks, wide, w_c)


def in_smem():
    return pl.BlockSpec(memory_space=pltpu.SMEM)


def run_feed_forward_grad(cot, mods, maps, order, pieces):
    tokens, d = cot.shape
    chunks = len(pieces) // 2

    def body(*refs):
        feed_forward_grad(len(pieces), *refs)

    return pl.pallas_call(
        body,
        grid=(tokens // ROWS,),
        in_specs=[in_smem(), pl.BlockSpec((ROWS, d), lambda i: (i, 0)), whole_block(mods), whole_block(maps)]
        + [anywhere()] * len(pieces),
        out_specs=pl.BlockSpec((chunks, ROWS, d), lambda i: (0, i, 0)),
        out_shape=like((chunks, tokens, d), BF16),
        scratch_shapes=[
            pltpu.VMEM((chunks * d, d + PAD), BF16),
            pltpu.VMEM((ROWS, d + PAD), BF16),
            pltpu.SemaphoreType.DMA((len(pieces),)),
        ],
        compiler_params=PARAMS,
        cost_estimate=cost(2 * tokens * d * d * chunks, 20_000_000),
        name="feed_forward_grad",
    )(order, cot, mods, maps, *pieces)


def run_feed_forward(x3, cot, order, grad_active, pieces, mods, maps, up):
    tokens, d = x3.shape
    chunks = up.shape[0]
    late = len(pieces) // 2
    rows = pl.BlockSpec((ROWS, d), lambda i: (i, 0))
    wide_rows = pl.BlockSpec((ROWS, chunks * d), lambda i: (i, 0))
    more = [pltpu.VMEM((late * d, d + PAD), BF16), pltpu.VMEM((ROWS, d + PAD), BF16)] if late else []

    def body(*refs):
        feed_forward(len(grad_active), len(pieces), *refs)

    return pl.pallas_call(
        body,
        grid=(tokens // ROWS,),
        in_specs=[in_smem(), rows, rows]
        + [pl.BlockSpec((g.shape[0], ROWS, d), lambda i: (0, i, 0)) for g in grad_active]
        + [anywhere()] * len(pieces)
        + [whole_block(mods), whole_block(maps), anywhere()],
        out_specs=[
            wide_rows,
            rows,
            pl.BlockSpec((RANK, d), lambda i: (0, 0)),
            pl.BlockSpec((RANK, chunks * d), lambda i: (0, 0)),
        ],
        out_shape=[
            like((tokens, chunks * d), BF16),
            like((tokens, d), F32),
            like((RANK, d), F32),
            like((RANK, chunks * d), F32),
        ],
        scratch_shapes=[
            pltpu.VMEM((d + PAD, chunks * d), BF16),
            pltpu.VMEM((ROWS, d + PAD), BF16),
            pltpu.VMEM((ROWS, chunks * d), BF16),
            pltpu.SemaphoreType.DMA((chunks + len(pieces),)),
            *more,
        ],
        compiler_params=PARAMS,
        cost_estimate=cost(4 * tokens * d * d * chunks, 50_000_000),
        name="feed_forward",
    )(order, x3, cot, *grad_active, *pieces, mods, maps, up)


def run_feed_forward_out(active, x3, cot, mods, maps, down, parts, half, halves):
    tokens, d = x3.shape
    order, *pieces = down
    hidden = active.shape[1]
    share = tokens // parts
    parts = parts // halves
    steps = tokens // ROWS // halves
    start = half * steps

    def body(*refs):
        feed_forward_out(len(pieces), *refs)

    rows = pl.BlockSpec((ROWS, d), lambda i: (i + start, 0))
    return pl.pallas_call(
        body,
        grid=(steps,),
        in_specs=[
            in_smem(),
            pl.BlockSpec((ROWS, hidden), lambda i: (i + start, 0)),
            rows,
            rows,
            whole_block(mods),
            whole_block(maps),
        ]
        + [anywhere()] * len(pieces),
        out_specs=[pl.BlockSpec((share, d), lambda i: (0, 0))] * parts
        + [
            pl.BlockSpec((RANK, d), lambda i: (0, 0)),
            pl.BlockSpec((RANK, hidden), lambda i: (0, 0)),
        ],
        out_shape=[like((share, d), BF16)] * parts
        + [
            like((RANK, d), F32),
            like((RANK, hidden), F32),
        ],
        scratch_shapes=[
            pltpu.VMEM((hidden, d + PAD), BF16),
            pltpu.SemaphoreType.DMA((len(pieces),)),
        ],
        compiler_params=PARAMS,
        cost_estimate=cost(2 * steps * ROWS * d * hidden, 20_000_000, 64),
        name="feed_forward_out",
    )(order, active, x3, cot, mods, maps, *pieces)


def run_cross_temporal_backward(g3, u1, saved, mods, masks, wide, w_tc, start, groups):
    parts = len(u1)
    own_frames, places, d = u1[0].shape
    frames = own_frames * parts
    each = ROWS // frames
    across = pl.BlockSpec((frames, ROWS // frames, d), lambda i: (0, i + start, 0))
    by_group = lambda i: (i + start, 0, 0)
    stat = pl.BlockSpec((1, HEADS, ROWS), by_group)
    three = pl.BlockSpec((1, ROWS, 3 * RANK), by_group)
    one = pl.BlockSpec((1, ROWS, RANK), by_group)
    kp, vp = saved[13:15]
    pair_sums = pl.BlockSpec((PAIRS, 2 * PAD, 256), lambda i: (0, 0, 0))

    def body(*refs):
        cross_temporal_backward(parts, *refs)

    return pl.pallas_call(
        body,
        grid=(groups,),
        in_specs=[pl.BlockSpec((own_frames, each, d), lambda i: (0, i + start, 0))] * parts
        + [across] + [across] * 4 + [stat, three, one] + [across] * 3 + [stat, one, one]
        + [whole_block(kp), whole_block(vp)]
        + [whole_block(mods), whole_block(masks), whole_block(wide), anywhere()],
        out_specs=[pl.BlockSpec((own_frames, each, d), lambda i: (0, i, 0))] * parts
        + [
            pl.BlockSpec((16 * RANK, d), lambda i: (0, 0)),
            pair_sums,
            pair_sums,
        ],
        out_shape=[like((own_frames, groups * each, d), BF16)] * parts
        + [like((16 * RANK, d), F32)]
        + [like((PAIRS, 2 * PAD, 256), F32)] * 2,
        scratch_shapes=[
            pltpu.VMEM((6, d + PAD, d), BF16),
            pltpu.VMEM((ROWS, ROWS), F32),
        ]
        + [pltpu.VMEM((ROWS, d), BF16)] * 7
        + [pltpu.SemaphoreType.DMA((6,))],
        compiler_params=PARAMS,
        cost_estimate=cost(14 * groups * ROWS * d * d, 30_000_000, 64),
        name="cross_temporal_backward",
    )(*u1, g3, *saved[:15], mods, masks, wide, w_tc)


LATE_BLOCKS = 8
EARLY_BLOCKS = 28


def run_spatial_backward(seq, g1, halves, video, saved, mods, masks, wide, w_s, clips, start, count, before):
    frames, rows, d = video.shape
    parts = len(g1) // halves
    by_frame = lambda i: (i + start, 0, 0)
    row_block = pl.BlockSpec((1, rows, d), by_frame)
    last = start + count == frames
    sums = (8 * RANK, d)
    if last:
        sums = (clips * parts, *packed_rows(LATE_BLOCKS // parts, d // clips))
    zeros = (0,) * len(sums)

    def body(*refs):
        spatial_backward(len(g1), halves, clips, bool(before), last, *refs)

    extra = [anywhere(), whole_block(before[1])] if before else []
    return pl.pallas_call(
        body,
        grid=(count,),
        in_specs=[in_smem()] + [pl.BlockSpec((1, g.shape[1], d), by_frame) for g in g1]
        + extra
        + [row_block] * 5
        + [
            pl.BlockSpec((1, HEADS, rows), by_frame),
            pl.BlockSpec((1, rows, 3 * RANK), by_frame),
            pl.BlockSpec((1, rows, RANK), by_frame),
            whole_block(mods),
            whole_block(masks),
            whole_block(wide),
            anywhere(),
        ],
        out_specs=[
            pl.BlockSpec((1, rows, 3 * d + PAD), by_frame),
            pl.BlockSpec(sums, lambda i: zeros),
        ],
        out_shape=[like((frames, rows, 3 * d + PAD), BF16), like(sums, BF16 if last else F32)],
        input_output_aliases={1 + len(g1): 0} if before else {},
        scratch_shapes=[pltpu.VMEM((d + PAD, d), BF16), pltpu.VMEM((LATE_BLOCKS * RANK, d), F32)]
        + [pltpu.VMEM((ROWS, d), BF16), pltpu.SemaphoreType.DMA((1,))],
        compiler_params=PARAMS,
        cost_estimate=cost(6 * count * rows * d * d, 20_000_000, 64),
        name="spatial_backward",
    )(seq, *g1, *before, video, *saved, mods, masks, wide, w_s)


def run_spatial_input_grad(seq, g1, halves, video, grads, mods, wide, w_s):
    frames, rows, d = video.shape
    by_frame = lambda i: (i, 0, 0)
    row_block = pl.BlockSpec((1, rows, d), by_frame)

    def body(*refs):
        spatial_input_grad(len(g1), halves, *refs)

    return pl.pallas_call(
        body,
        grid=(frames,),
        in_specs=[in_smem()] + [pl.BlockSpec((1, g.shape[1], d), by_frame) for g in g1]
        + [
            row_block,
            pl.BlockSpec((1, rows, grads.shape[2]), by_frame),
            whole_block(mods),
            whole_block(wide),
            anywhere(),
        ],
        out_specs=row_block,
        out_shape=like(video.shape, BF16),
        scratch_shapes=[
            pltpu.VMEM((d, 3 * d + PAD), BF16),
            pltpu.VMEM((ROWS, d), BF16),
            pltpu.SemaphoreType.DMA((3,)),
        ],
        compiler_params=PARAMS,
        cost_estimate=cost(6 * frames * rows * d * d, 20_000_000, 64),
        name="spatial_input_grad",
    )(seq, *g1, video, grads, mods, wide, w_s)


def run_put_in_place(seq, pieces):
    frames, places, d = pieces[0].shape
    by_frame = lambda i: (i, 0, 0)
    rows = places * len(pieces)
    return pl.pallas_call(
        put_in_place,
        grid=(frames,),
        in_specs=[in_smem()] + [pl.BlockSpec((1, places, d), by_frame)] * len(pieces),
        out_specs=pl.BlockSpec((1, rows, d), by_frame),
        out_shape=like((frames, rows, d), BF16),
        compiler_params=PARAMS,
        cost_estimate=cost(0, 4 * frames * rows * d, 64),
        name="put_in_place",
    )(seq, *pieces)


PLAIN = pltpu.CompilerParams(vmem_limit_bytes=VMEM_LIMIT)


def in_vmem():
    return pl.BlockSpec(memory_space=pltpu.VMEM)


def run_pack_early(gw, dk, dv, others, sources, clips, parts):
    d = gw[0].shape[1]
    packed = (clips * parts, *packed_rows(EARLY_BLOCKS // parts, d // clips))

    def body(*refs):
        pack_early(clips, len(gw), [len(each) for each in others], *refs)

    return pl.pallas_call(
        body,
        out_shape=like(packed, BF16),
        scratch_shapes=[pltpu.VMEM((EARLY_BLOCKS * RANK, d), F32), pltpu.VMEM((PAD, d), F32)],
        compiler_params=PLAIN,
        cost_estimate=cost(50000000, 8000000, 64),
        name="pack_early",
    )(*gw, *dk, *dv, *[array for each in others for array in each], *sources)


def run_assemble(seq, early, late, wide_shape, narrow_shape):
    parts = len(early)

    def body(*refs):
        assemble(parts, *refs)

    return pl.pallas_call(
        body,
        in_specs=[in_smem()] + [in_vmem()] * (2 * parts),
        out_specs=[in_vmem()] * 2,
        out_shape=[like(wide_shape, F32), like(narrow_shape, F32)],
        scratch_shapes=[pltpu.VMEM((parts, *piece.shape), BF16) for piece in (early[0], late[0])],
        compiler_params=PLAIN,
        cost_estimate=cost(0, 6_000_000, 64),
        name="assemble",
    )(seq, *early, *late)


def run_pick(all_index, wide, narrow):
    count, _, _, cols = wide.shape
    shape = packed_rows(count + 2 * (narrow.shape[3] // cols), cols)
    return pl.pallas_call(
        pick,
        in_specs=[in_smem(), in_vmem(), in_vmem()],
        out_specs=in_vmem(),
        out_shape=like((all_index.shape[0], *shape), BF16),
        compiler_params=PLAIN,
        cost_estimate=cost(0, 3000000),
        name="pick",
    )(all_index, wide, narrow)


def run_unpick(got, blocks, cols):
    def body(*refs):
        unpick(blocks, cols, *refs)

    return pl.pallas_call(
        body,
        in_specs=[in_vmem()],
        out_specs=in_vmem(),
        out_shape=like((blocks, RANK, got.shape[0] * cols), BF16),
        compiler_params=PLAIN,
        cost_estimate=cost(0, 2500000),
        name="unpick",
    )(got)


def run_combine(all_index, got, adapters):
    _, share, cols = got.shape
    return pl.pallas_call(
        combine,
        in_specs=[pl.BlockSpec(memory_space=pltpu.SMEM), pl.BlockSpec(memory_space=pltpu.VMEM)],
        out_specs=pl.BlockSpec(memory_space=pltpu.VMEM),
        out_shape=like((adapters, share, cols), BF16),
        scratch_shapes=[pltpu.VMEM((adapters, share, cols), F32)],
        compiler_params=pltpu.CompilerParams(vmem_limit_bytes=VMEM_LIMIT),
        cost_estimate=cost(0, 1000000, 64),
        name="combine",
    )(all_index, got)


def exchange(array, axes="seq"):
    return lax.all_to_all(array, axes, split_axis=0, concat_axis=0, tiled=True)


def up_chunks(up, clips, times):
    rows, hidden = up.shape
    cols = hidden // (clips * times)
    return up.reshape(rows, clips, times, cols).transpose(2, 0, 1, 3).reshape(times, rows, -1)


def gather(array):
    return lax.all_gather(array, "fsdp", axis=1, tiled=True)


def send(array, axis, shift):
    size = lax.axis_size(axis)
    return lax.ppermute(array, axis, [(i, (i + shift) % size) for i in range(size)])


def to_places(pieces):
    return [pieces[0]] + [send(pieces[k], "seq", k) for k in range(1, len(pieces))]


def to_frames(pieces):
    return [pieces[0]] + [send(pieces[k], "seq", -k) for k in range(1, len(pieces))]


def gather_spatial_and_down(spatial, down, parts, times, clips, d):
    if times != parts or clips % 2:
        return gather(spatial)
    own = lax.dynamic_slice_in_dim(down.reshape(times, -1, d), lax.axis_index("seq"), 1, 0)
    return gather(jnp.concatenate([spatial, own], 0))


def start_down(got, parts, times, clips, d):
    if times != parts or clips % 2:
        return None
    half = d // 2
    core = lax.axis_index("fsdp") % 2
    first = lax.dynamic_slice(got, (times, core * half, 0), (1, half, d))[0]
    other = lax.dynamic_slice(got, (times, (1 - core) * half, 0), (1, half, d))[0]
    return first, other, send(first, "seq", 1)


def swap_cores(piece, clips):
    return lax.ppermute(piece, "fsdp", [(i, i ^ 1) for i in range(clips)])


def to_all(piece):
    return [piece] + [send(piece, "seq", k) for k in range(1, lax.axis_size("seq"))]


def down_order(times, parts, clips):
    if times != parts or clips % 2:
        return jnp.arange(times, dtype=jnp.int32), jnp.zeros((1,), jnp.int32)
    seq = lax.axis_index("seq")
    core = lax.axis_index("fsdp") % 2
    return ((seq - jnp.arange(parts)) % parts).astype(jnp.int32), core.astype(jnp.int32)[None]


def on_device(
    video,
    context,
    modulation,
    adapter_index,
    cotangent,
    qkv_weights,
    out_weights,
    ffn_up,
    ffn_down,
    adapt_wide,
    adapt_ff,
):
    parts = lax.axis_size("seq")
    clips = lax.axis_size("fsdp")
    d = video.shape[-1]
    count, adapters, _, cols = adapt_wide.shape[1:]
    times = adapt_ff.shape[-1] // cols
    places = SPATIAL // parts
    frames = FRAMES // parts
    half_d = d // 2
    mods = modulation[0, 0]
    masks = head_masks()
    ctx = jnp.pad(context[0], ((0, PAD - context.shape[1]), (0, 0)))

    def attention_weights(j):
        return jnp.concatenate([qkv_weights[0, 3 * j : 3 * j + 3], out_weights[0, j : j + 1]], 0)

    seq = lax.axis_index("seq").astype(jnp.int32)[None]
    all_index = exchange(jnp.broadcast_to(adapter_index, (clips,)), "fsdp")
    w_s = gather_spatial_and_down(attention_weights(0), ffn_down[0], parts, times, clips, d)
    picked = run_pick(all_index, adapt_wide[0], adapt_ff[0])
    wide = run_unpick(exchange(picked, "fsdp"), count + 2 * times, cols)
    w_tc = gather(jnp.concatenate([attention_weights(1), attention_weights(2)], 0))
    ffn_up, _ = lax.optimization_barrier((ffn_up, picked))
    up = gather(up_chunks(ffn_up[0], clips, times))
    cot = cotangent.reshape(frames, SPATIAL, d)
    cot = to_places(
        [
            lax.dynamic_slice_in_dim(cot, (seq[0] + k) % parts * places, places, 1)
            for k in range(parts)
        ]
    )
    frames_in = video.reshape(frames, SPATIAL, d)
    maps_f = wide[24:]
    order, core = down_order(times, parts, clips)
    packed_order = jnp.concatenate([order, core])
    if times == parts and clips % 2 == 0:
        packed_order = jnp.concatenate([order[:2], order[parts - 1 :], order[2 : parts - 1], core])
    w_s, wide, maps_f, packed_order, *cot = lax.optimization_barrier((w_s, wide, maps_f, packed_order, *cot))
    started = start_down(w_s, parts, times, clips, d)
    cot = jnp.concatenate(cot, 0).reshape(FRAMES * places, d)
    made = run_spatial_forward(seq, frames_in, mods, masks, wide, w_s, parts)
    u1, kept_s = to_places(made[:parts]), made[parts:]
    if started is None:
        whole_down = gather(ffn_down[0].reshape(times, -1, d))
        sides = [[whole_down[i, :half_d] for i in range(times)], [whole_down[i, half_d:] for i in range(times)]]
        *kept_t, x2 = run_temporal_forward(u1, mods, masks, wide, w_tc)
        *kept_c, x3 = run_cross_forward(x2, ctx, masks, wide, w_tc)
        late_pieces = []
        grad_active = [run_feed_forward_grad(cot, mods, maps_f, packed_order, sides[0] + sides[1])]
    else:
        first, other, second = started
        second, cot, x1_own = lax.optimization_barrier((second, cot, u1[0]))
        mine = [first, second]
        others = [other, swap_cores(second, clips)]
        early_order = jnp.concatenate([packed_order[:2], core])
        grad_early = run_feed_forward_grad(cot, mods, maps_f, early_order, mine + others)
        first, second, grad_early, *u1 = lax.optimization_barrier(
            (first, second, grad_early, x1_own, *u1[1:])
        )
        third = send(first, "seq", -1)
        rest = [send(second, "seq", 1)] + [send(first, "seq", k) for k in range(3, parts - 1)]
        *kept_t, x2 = run_temporal_forward(u1, mods, masks, wide, w_tc)
        *kept_c, x3 = run_cross_forward(x2, ctx, masks, wide, w_tc)
        x3, third, *rest = lax.optimization_barrier((x3, third, *rest))
        rest = [third] + rest
        rest_others = [swap_cores(piece, clips) for piece in rest]
        late_order = jnp.concatenate([packed_order[2:parts], core])
        grad_late = run_feed_forward_grad(cot, mods, maps_f, late_order, rest + rest_others)
        grad_active = [grad_early, grad_late]
        late_pieces = []
        sides = [mine + rest, others + rest_others]
    down = [packed_order, *sides[0], *sides[1]]
    x3 = x3.reshape(FRAMES * places, d)
    active, g3, grad_a24, grad_b24 = run_feed_forward(
        x3, cot, packed_order, grad_active, late_pieces, mods, maps_f, up
    )
    g3 = g3.reshape(FRAMES, places, d)
    groups = FRAMES * places // ROWS
    saved = kept_t + kept_c
    turns = 2 if groups % 2 == 0 and parts % 2 == 0 else 1
    output, grad_b25, grad_down = [None] * parts, [], []

    def finish_tokens(turn, active):
        *x4, b25, rows = run_feed_forward_out(active, x3, cot, mods, maps_f, down, parts, turn, turns)
        grad_b25.append(b25)
        grad_down.append(rows)
        for k, piece in enumerate(x4, turn * parts // turns):
            output[k] = piece.reshape(frames, places, d)

    def send_tokens(turn):
        for k in range(turn * parts // turns, (turn + 1) * parts // turns):
            output[k] = send(output[k], "seq", -k) if k else output[k]

    finish_tokens(turns - 1, active)
    output[-1], g3 = lax.optimization_barrier((output[-1], g3))
    send_tokens(turns - 1)
    shares = [groups - groups // 2, groups // 2] if groups > 1 else [1]
    g1, gw, dk, dv = [], [], [], []
    for share, size in enumerate(shares):
        *pieces, gw_part, dk_part, dv_part = run_cross_temporal_backward(
            g3, u1, saved, mods, masks, wide, w_tc, sum(shares[:share]), size
        )
        gw.append(gw_part)
        dk.append(dk_part)
        dv.append(dv_part)
        if share == 0 and turns > 1:
            half = parts // turns
            pieces[0], g3, *output[half:] = lax.optimization_barrier((pieces[0], g3, *output[half:]))
        else:
            pieces[0], g3 = lax.optimization_barrier((pieces[0], g3))
        g1.append(to_frames(pieces))
    if len(shares) > 1:
        active, gw[-1], *g1[0] = lax.optimization_barrier((active, gw[-1], *g1[0]))
    if turns > 1:
        finish_tokens(0, active)
        send_tokens(0)
    others = [[grad_a24], grad_b25, [grad_b24], grad_down]
    sources = [kept_c[7], kept_c[8], ctx, masks, wide]
    packed = run_pack_early(gw, dk, dv, others, sources, clips, parts)
    g1 = [piece for done in g1 for piece in done]
    packed, *g1 = lax.optimization_barrier((packed, *g1))
    got = exchange(packed, ("fsdp", "seq"))
    halves = len(shares)
    grads, packed = run_spatial_backward(
        seq, g1, halves, frames_in, kept_s, mods, masks, wide, w_s, clips, 0, frames, []
    )
    packed, got, *output = lax.optimization_barrier((packed, got, *output))
    early = to_all(run_combine(all_index, got, adapters))
    g0 = run_spatial_input_grad(seq, g1, halves, frames_in, grads, mods, wide, w_s)
    got, g0 = lax.optimization_barrier((exchange(packed, ("fsdp", "seq")), g0))
    late = run_combine(all_index, got, adapters)
    wide_out, narrow_out = run_assemble(
        seq, early, to_all(late), adapt_wide.shape[1:], adapt_ff.shape[1:]
    )
    output = run_put_in_place(seq, output).reshape(video.shape)
    return (output, g0.reshape(video.shape), wide_out[None], narrow_out[None])


def solution(mesh):
    return jax.shard_map(
        on_device,
        mesh=mesh,
        in_specs=(
            P("fsdp", "seq", None),
            P("fsdp", None, None),
            P("fsdp", None, None, None),
            P("fsdp"),
            P("fsdp", "seq", None),
            P(None, None, "fsdp", None),
            P(None, None, "fsdp", None),
            P(None, "fsdp", None),
            P(None, "fsdp", None),
            P(None, None, None, None, "fsdp"),
            P(None, None, None, None, "fsdp"),
        ),
        out_specs=(
            P("fsdp", "seq", None),
            P("fsdp", "seq", None),
            P(None, None, None, None, "fsdp"),
            P(None, None, None, None, "fsdp"),
        ),
        check_vma=False,
    )
```

```python
import math

import jax
import jax.numpy as jnp
from jax import lax
from jax.experimental import pallas as pl
from jax.experimental.pallas import tpu as pltpu
from jax.sharding import PartitionSpec as P

HEAD_DIM = 72
HEADS = 16
FRAMES = 16
SPATIAL = 256
RANK = 16
ROWS = 256
PAIRS = HEADS // 2
PAD = 128
SCALE = HEAD_DIM ** (-0.5)
EXP_SCALE = SCALE * math.log2(math.e)
LN2 = math.log(2.0)
F32 = jnp.float32
BF16 = jnp.bfloat16
VMEM_LIMIT = 60 * 1024 * 1024


def nn(left, right):
    return lax.dot_general(left, right, (((1,), (0,)), ((), ())), preferred_element_type=F32)


def nt(left, right):
    return lax.dot_general(left, right, (((1,), (1,)), ((), ())), preferred_element_type=F32)


def tn(left, right):
    return lax.dot_general(left, right, (((0,), (0,)), ((), ())), preferred_element_type=F32)


def window(pair):
    return slice(128 * pair, 128 * pair + 256)


def normalize(stream):
    average = jnp.mean(stream, -1, keepdims=True)
    centred = stream - average
    inverse = lax.rsqrt(jnp.mean(centred * centred, -1, keepdims=True) + 1e-06)
    return centred * inverse, inverse


def normalize_back(normal, inverse, grad):
    mean_grad = jnp.mean(grad, -1, keepdims=True)
    mean_both = jnp.mean(grad * normal, -1, keepdims=True)
    return inverse * (grad - mean_grad - normal * mean_both)


def up_rows(ad_ref, number, slot, width):
    rows = ad_ref[2 * number + 1]
    before = jnp.zeros((RANK * slot, width), BF16)
    after = jnp.zeros((PAD - RANK * (slot + 1), width), BF16)
    return jnp.concatenate(([before] if slot else []) + [rows, after], 0)


def three_downs(ad_ref, number):
    return jnp.concatenate([ad_ref[2 * (number + i)] for i in range(3)], 0)


class Loads:
    def __init__(self, entries, sems):
        self.first = pl.program_id(0) == 0
        self.entries = entries
        self.sems = sems

    def copy(self, index):
        source, target = self.entries[index]
        return pltpu.make_async_copy(source, target, self.sems.at[index])

    def start(self):
        @pl.when(self.first)
        def _():
            for index in range(len(self.entries)):
                self.copy(index).start()

    def ready(self, index):
        @pl.when(self.first)
        def _():
            self.copy(index).wait()


def head_masks():
    lane = jnp.arange(256)[None, :]
    begin = jnp.array([16 * (h // 2) + HEAD_DIM * (h % 2) for h in range(HEADS)])[:, None]
    return ((lane >= begin) & (lane < begin + HEAD_DIM)).astype(BF16)


def same_place(shape):
    rows = lax.broadcasted_iota(jnp.int32, shape, 0)
    cols = lax.broadcasted_iota(jnp.int32, shape, 1)
    return jnp.where(rows % 16 == cols % 16, 0.0, -1e30).astype(F32)


def attend(q_ref, k_ref, v_ref, mask_ref, bias, put_out, stat_ref):
    carried = None
    for pair in range(PAIRS):
        win = window(pair)
        q_win, k_win, v_win = q_ref[:, win], k_ref[:, win], v_ref[:, win]
        all_weights, all_values = [], []
        for head in (2 * pair, 2 * pair + 1):
            mask = mask_ref[head : head + 1, :]
            scores = nt(k_win * mask, q_win)
            if bias is not None:
                scores = scores + bias[...]
            top = jnp.max(scores, 0, keepdims=True)
            grown = jnp.exp2(scores - top)
            total = jnp.sum(grown, 0, keepdims=True)
            stat_ref[head : head + 1, :] = top + jnp.log2(total)
            all_weights.append((grown * (1.0 / total)).astype(BF16))
            all_values.append(v_win * mask)
        out = tn(jnp.concatenate(all_weights, 0), jnp.concatenate(all_values, 0))
        low = out[:, :128]
        put_out(pair, low if carried is None else low + carried)
        carried = out[:, 128:]
    put_out(PAIRS, carried)


def attend_back(q_ref, k_ref, v_ref, do_ref, mask_ref, bias, stat_ref, put):
    carried = None
    for pair in range(PAIRS):
        win = window(pair)
        q_win, k_win, v_win, do_win = q_ref[:, win], k_ref[:, win], v_ref[:, win], do_ref[:, win]
        all_grads, all_probs, keys, queries, outs = [], [], [], [], []
        for head in (2 * pair, 2 * pair + 1):
            mask = mask_ref[head : head + 1, :]
            k_own = k_win * mask
            scores = nt(k_own, q_win)
            if bias is not None:
                scores = scores + bias[...]
            probs = jnp.exp2(scores - stat_ref[head : head + 1, :])
            grad_probs = nt(v_win * mask, do_win)
            inner = jnp.sum(probs * grad_probs, 0, keepdims=True)
            all_grads.append((probs * (grad_probs - inner)).astype(BF16))
            all_probs.append(probs.astype(BF16))
            keys.append(k_own)
            queries.append(q_win * mask)
            outs.append(do_win * mask)
        grads = (
            tn(jnp.concatenate(all_grads, 0), jnp.concatenate(keys, 0)),
            nn(jnp.concatenate(all_grads, 1), jnp.concatenate(queries, 0)),
            nn(jnp.concatenate(all_probs, 1), jnp.concatenate(outs, 0)),
        )
        lows = tuple(g[:, :128] for g in grads)
        if carried is not None:
            lows = tuple(a + b for a, b in zip(lows, carried))
        put(pair, lows)
        carried = tuple(g[:, 128:] for g in grads)
    put(PAIRS, carried)


def tile(index):
    return slice(128 * index, 128 * index + 128)


def three_projections(lhs_ref, ad_ref, number, weights, loads, first_load, outs, rank_ref):
    width = weights.shape[2]
    ranks = nt(lhs_ref[:, :width], three_downs(ad_ref, number)).astype(BF16)
    rank_ref[...] = ranks
    lhs_ref[:, width : width + 3 * RANK] = ranks
    for i in range(3):
        loads.ready(first_load + i)
        total = nn(lhs_ref[...], weights[first_load + i])
        outs[i][...] = (total * EXP_SCALE if i == 0 else total).astype(BF16)


def one_projection(lhs_ref, ad_ref, number, weight_ref, rank_ref):
    width = weight_ref.shape[1]
    ranks = nt(lhs_ref[:, :width], ad_ref[2 * number]).astype(BF16)
    rank_ref[...] = ranks
    lhs_ref[:, width : width + RANK] = ranks
    return nn(lhs_ref[...], weight_ref[...])


def block_rows(index):
    return slice(RANK * index, RANK * (index + 1))


def one_back(grad, kept, ranks, ad_ref, number, weight_ref, grad_ref, at):
    width = weight_ref.shape[1]
    both = nt(grad, weight_ref[...])
    grad_rank = both[:, width : width + RANK].astype(BF16)
    grad_ref[block_rows(at), :] += tn(grad_rank, kept)
    grad_ref[block_rows(at + 1), :] += tn(ranks, grad)
    return both[:, :width] + nn(grad_rank, ad_ref[2 * number])


def three_back(grads, inputs, ranks, ad_ref, number, weights, loads, first_load, grad_ref, at):
    width = weights.shape[2]
    both = None
    for i in range(3):
        grad = grads[i][...]
        ups = tn(ranks, grad)
        grad_ref[block_rows(at + 2 * i + 1), :] += ups[block_rows(i)]
        loads.ready(first_load + i)
        part = nt(grad, weights[first_load + i])
        both = part if both is None else both + part
    grad_ranks = both[:, width : width + 3 * RANK].astype(BF16)
    downs = tn(grad_ranks, inputs)
    for i in range(3):
        grad_ref[block_rows(at + 2 * i), :] += downs[block_rows(i)]
    return both[:, :width] + nn(grad_ranks, three_downs(ad_ref, number))


def place_of(seq_ref, k, parts, places):
    return pl.multiple_of(lax.rem(seq_ref[0] + k, parts) * places, 16)


def spatial_forward(seq_ref, x_ref, mod_ref, mask_ref, ad_ref, w_hbm, *refs):
    x1_refs = refs[:-11]
    q_ref, k_ref, v_ref, o_ref, stat_ref, rq_ref, ro_ref, w_ref, lhs_ref, x1_s, sems = refs[-11:]
    width = x_ref.shape[2]
    loads = Loads([(w_hbm.at[i], w_ref.at[i, pl.ds(0, width), :]) for i in range(4)], sems)
    loads.start()

    @pl.when(loads.first)
    def _():
        lhs_ref[:, width:] = jnp.zeros((ROWS, PAD), BF16)
        for i in range(4):
            w_ref[i, width:, :] = up_rows(ad_ref, i, i % 3, width)

    stream = x_ref[0].astype(F32)
    normal, _ = normalize(stream)
    lhs_ref[:, :width] = (normal * (1.0 + mod_ref[1:2, :]) + mod_ref[0:1, :]).astype(BF16)
    q, k, v = q_ref.at[0], k_ref.at[0], v_ref.at[0]
    three_projections(lhs_ref, ad_ref, 0, w_ref, loads, 0, (q, k, v), rq_ref.at[0])

    def put_out(index, value):
        value = value.astype(BF16)
        o_ref[0, :, tile(index)] = value
        lhs_ref[:, tile(index)] = value

    attend(q, k, v, mask_ref, None, put_out, stat_ref.at[0])
    loads.ready(3)
    branch = one_projection(lhs_ref, ad_ref, 3, w_ref.at[3], ro_ref.at[0])
    x1_s[...] = (stream + mod_ref[2:3, :] * branch).astype(BF16)
    places = x1_refs[0].shape[1]
    for k, ref in enumerate(x1_refs):
        ref[0] = x1_s[pl.ds(place_of(seq_ref, k, len(x1_refs), places), places), :]


def rows_of(refs):
    pieces = [ref[...].reshape(-1, ref.shape[2]) for ref in refs]
    return pieces[0] if len(pieces) == 1 else jnp.concatenate(pieces, 0)


def temporal_forward(parts, *refs):
    x_refs, refs = refs[:parts], refs[parts:]
    (
        mod_ref, mask_ref, ad_ref, w_hbm,
        q_ref, k_ref, v_ref, o_ref, stat_ref, rq_ref, ro_ref, u2_ref, x2_ref,
        w_ref, bias_ref, lhs_ref, q_s, k_s, v_s, sems,
    ) = refs
    width = x_refs[0].shape[2]
    loads = Loads([(w_hbm.at[i], w_ref.at[i, pl.ds(0, width), :]) for i in range(4)], sems)
    loads.start()

    @pl.when(loads.first)
    def _():
        bias_ref[...] = same_place(bias_ref.shape)
        lhs_ref[:, width:] = jnp.zeros((ROWS, PAD), BF16)
        for i in range(4):
            w_ref[i, width:, :] = up_rows(ad_ref, 4 + i, i % 3, width)

    loaded = rows_of(x_refs)
    lhs_ref[:, :width] = loaded
    three_projections(lhs_ref, ad_ref, 4, w_ref, loads, 0, (q_s, k_s, v_s), rq_ref.at[0])
    q_ref[...] = q_s[...].reshape(q_ref.shape)
    k_ref[...] = k_s[...].reshape(k_ref.shape)
    v_ref[...] = v_s[...].reshape(v_ref.shape)

    def put_out(index, value):
        lhs_ref[:, tile(index)] = value.astype(BF16)

    attend(q_s, k_s, v_s, mask_ref, bias_ref, put_out, stat_ref.at[0])
    o_ref[...] = lhs_ref[:, :width].reshape(o_ref.shape)
    loads.ready(3)
    branch = one_projection(lhs_ref, ad_ref, 7, w_ref.at[3], ro_ref.at[0])
    stream = loaded.astype(F32) + mod_ref[2:3, :] * branch
    u2_ref[...] = stream.astype(BF16).reshape(u2_ref.shape)
    x2_ref[...] = stream.reshape(x2_ref.shape)


def cross_forward(
    x_ref, ctx_ref, mask_ref, ad_ref, w_hbm,
    q_ref, o_ref, stat_ref, rq_ref, ro_ref, kp_ref, vp_ref, rk_ref, rv_ref, x3_ref,
    w_ref, lhs_ref, q_s, k_s, sems,
):
    width = x_ref.shape[2]
    loads = Loads([(w_hbm.at[4 + i], w_ref.at[i, pl.ds(0, width), :]) for i in range(4)], sems)
    loads.start()

    @pl.when(loads.first)
    def _():
        lhs_ref[:, width:] = jnp.zeros((ROWS, PAD), BF16)
        for i in (0, 3):
            w_ref[i, width:, :] = up_rows(ad_ref, 8 + i, 0, width)

    stream = x_ref[...].reshape(ROWS, width)
    lhs_ref[:, :width] = stream.astype(BF16)
    loads.ready(0)
    queries = one_projection(lhs_ref, ad_ref, 8, w_ref.at[0], rq_ref.at[0])
    q_s[...] = (queries * EXP_SCALE).astype(BF16)
    q_ref[...] = q_s[...].reshape(q_ref.shape)
    loads.ready(1)
    loads.ready(2)

    @pl.when(loads.first)
    def _():
        for number, at, rank_ref, pair_ref in ((9, 1, rk_ref, kp_ref), (10, 2, rv_ref, vp_ref)):
            ranks = nt(ctx_ref[...], ad_ref[2 * number]).astype(BF16)
            rank_ref[...] = ranks
            made = nn(ctx_ref[...], w_ref[at, :width, :]) + nn(ranks, ad_ref[2 * number + 1])
            k_s[...] = made.astype(BF16)
            for pair in range(PAIRS):
                piece = k_s[:, window(pair)]
                pair_ref[pair, :PAD, :] = piece * mask_ref[2 * pair : 2 * pair + 1, :]
                pair_ref[pair, PAD:, :] = piece * mask_ref[2 * pair + 1 : 2 * pair + 2, :]

    carried = None
    count = 120
    for pair in range(PAIRS):
        scores = nt(kp_ref[pair], q_s[:, window(pair)])
        pieces = []
        for sub in range(2):
            own = scores[PAD * sub : PAD * sub + count]
            top = jnp.max(own, 0, keepdims=True)
            grown = jnp.exp2(own - top)
            total = jnp.sum(grown, 0, keepdims=True)
            stat_ref[0, 2 * pair + sub : 2 * pair + sub + 1, :] = top + jnp.log2(total)
            pieces += [grown * (1.0 / total), jnp.zeros((PAD - count, ROWS), F32)]
        weights = jnp.concatenate(pieces, 0).astype(BF16)
        out = tn(weights, vp_ref[pair])
        low = out[:, :128]
        lhs_ref[:, tile(pair)] = (low if carried is None else low + carried).astype(BF16)
        carried = out[:, 128:]
    lhs_ref[:, tile(PAIRS)] = carried.astype(BF16)
    o_ref[...] = lhs_ref[:, :width].reshape(o_ref.shape)
    loads.ready(3)
    stream = stream + one_projection(lhs_ref, ad_ref, 11, w_ref.at[3], ro_ref.at[0])
    x3_ref[...] = stream.reshape(x3_ref.shape)


def gelu_both(hidden):
    root = math.sqrt(2.0 / math.pi)
    square = hidden * hidden
    inner = root * (hidden + 0.044715 * (square * hidden))
    bent = jnp.tanh(inner)
    half = 0.5 * (1.0 + bent)
    slope = half + 0.5 * hidden * (1.0 - bent * bent) * (root * (1.0 + 3.0 * 0.044715 * square))
    return hidden * half, slope


def transposed_map(rows):
    nothing = jnp.zeros((PAD - rows.shape[0], rows.shape[1]), F32)
    wide = jnp.concatenate([rows.astype(F32), nothing], 0)
    return wide.T.astype(BF16)


def down_loads(order_ref, pieces, down_ref, width):
    half = width // 2
    count = len(pieces) // 2
    core = order_ref[count]
    entries = []
    for k in range(count):
        for source, side in ((pieces[k], core), (pieces[count + k], 1 - core)):
            start = pl.multiple_of(order_ref[k] * width + side * half, 16)
            entries.append((source, down_ref.at[pl.ds(start, half), pl.ds(0, width)]))
    return entries


def fill_down_maps(ad_ref, down_ref, width):
    chunks = down_ref.shape[0] // width
    for c in range(chunks):
        rows = slice(c * width, (c + 1) * width)
        down_ref[rows, width:] = transposed_map(ad_ref[2 + chunks + c])


def feed_forward_grad(count, order_ref, cot_ref, mod_ref, ad_ref, *refs):
    pieces = refs[:count]
    grad_ref, down_ref, lhs_ref, sems = refs[count:]
    width = cot_ref.shape[1]
    half = width // 2
    chunks = count // 2
    core = order_ref[chunks]
    entries = []
    for k in range(chunks):
        for source, side in ((pieces[k], core), (pieces[chunks + k], 1 - core)):
            start = pl.multiple_of(k * width + side * half, 16)
            entries.append((source, down_ref.at[pl.ds(start, half), pl.ds(0, width)]))
    loads = Loads(entries, sems)
    loads.start()

    @pl.when(loads.first)
    def _():
        lhs_ref[:, width:] = jnp.zeros((ROWS, PAD), BF16)
        for k in range(chunks):
            rows = slice(k * width, (k + 1) * width)
            down_ref[rows, width:] = transposed_map(ad_ref[2 + (ad_ref.shape[0] - 2) // 2 + order_ref[k]])

    branch = (mod_ref[5:6, :] * cot_ref[...].astype(F32)).astype(BF16)
    lhs_ref[:, :width] = branch
    lhs_ref[:, width : width + RANK] = nt(branch, ad_ref[1]).astype(BF16)
    for i in range(len(entries)):
        loads.ready(i)
    for k in range(chunks):
        rows = slice(k * width, (k + 1) * width)
        grad_ref[k] = nt(lhs_ref[...], down_ref[rows, :]).astype(BF16)


def hidden_chunks(hidden):
    return [slice(at, at + 1536) for at in range(0, hidden, 1536)]


def feed_forward(groups, count, order_ref, x3_ref, cot_ref, *refs):
    grad_refs, pieces, refs = refs[:groups], refs[groups : groups + count], refs[groups + count :]
    (
        mod_ref, ad_ref, w_hbm, act_ref, g3_ref, gd_ref, gu_ref, up_ref, lhs_ref, dh_ref, sems, *rest
    ) = refs
    width = x3_ref.shape[1]
    hidden_size = up_ref.shape[1]
    chunks = hidden_size // width
    late = count // 2
    core = order_ref[chunks]
    entries = [
        (w_hbm.at[c], up_ref.at[pl.ds(0, width), pl.ds(c * width, width)]) for c in range(chunks)
    ]
    if late:
        down_ref, dlhs_ref = rest
        half = width // 2
        for k in range(late):
            for source, side in ((pieces[k], core), (pieces[late + k], 1 - core)):
                start = pl.multiple_of(k * width + side * half, 16)
                entries.append((source, down_ref.at[pl.ds(start, half), pl.ds(0, width)]))
    loads = Loads(entries, sems)
    loads.start()

    @pl.when(loads.first)
    def _():
        gd_ref[...] = jnp.zeros_like(gd_ref)
        gu_ref[...] = jnp.zeros_like(gu_ref)
        lhs_ref[:, width:] = jnp.zeros((ROWS, PAD), BF16)
        up_ref[width + RANK :, :] = jnp.zeros((PAD - RANK, hidden_size), BF16)
        for c in range(chunks):
            up_ref[width : width + RANK, c * width : (c + 1) * width] = ad_ref[2 + c]
        for k in range(late):
            rows = slice(k * width, (k + 1) * width)
            at = order_ref[chunks - late + k]
            down_ref[rows, width:] = transposed_map(ad_ref[2 + chunks + at])
        if late:
            dlhs_ref[:, width:] = jnp.zeros((ROWS, PAD), BF16)

    normal, inverse = normalize(x3_ref[...])
    inputs = (normal * (1.0 + mod_ref[4:5, :]) + mod_ref[3:4, :]).astype(BF16)
    rank_up = nt(inputs, ad_ref[0]).astype(BF16)
    lhs_ref[:, :width] = inputs
    lhs_ref[:, width : width + RANK] = rank_up
    at = 0
    for grad_ref in grad_refs:
        for k in range(grad_ref.shape[0]):
            start = pl.multiple_of(order_ref[at] * width, 128)
            dh_ref[:, pl.ds(start, width)] = grad_ref[k]
            at += 1
    if late:
        branch = (mod_ref[5:6, :] * cot_ref[...].astype(F32)).astype(BF16)
        dlhs_ref[:, :width] = branch
        dlhs_ref[:, width : width + RANK] = nt(branch, ad_ref[1]).astype(BF16)
    for i in range(len(entries)):
        loads.ready(i)
    for k in range(late):
        start = pl.multiple_of(order_ref[at + k] * width, 128)
        rows = slice(k * width, (k + 1) * width)
        dh_ref[:, pl.ds(start, width)] = nt(dlhs_ref[...], down_ref[rows, :]).astype(BF16)
    for cols in hidden_chunks(hidden_size):
        active, slope = gelu_both(nn(lhs_ref[...], up_ref[:, cols]))
        act_ref[:, cols] = active.astype(BF16)
        dh_ref[:, cols] = (slope * dh_ref[:, cols].astype(F32)).astype(BF16)
    both = nt(dh_ref[...], up_ref[...])
    gu_ref[...] += tn(rank_up, dh_ref[...])
    grad_rank = both[:, width : width + RANK].astype(BF16)
    grad_in = both[:, :width] + nn(grad_rank, ad_ref[0])
    gd_ref[...] += tn(grad_rank, lhs_ref[:, :width])
    grad_in = normalize_back(normal, inverse, grad_in * (1.0 + mod_ref[4:5, :]))
    g3_ref[...] = cot_ref[...].astype(F32) + grad_in


def feed_forward_out(count, order_ref, act_ref, x3_ref, cot_ref, mod_ref, ad_ref, *refs):
    pieces, refs = refs[:count], refs[count:]
    x4_refs = refs[:-4]
    gu_ref, gd_ref, down_ref, sems = refs[-4:]
    width = x3_ref.shape[1]
    step = pl.program_id(0)
    entries = down_loads(order_ref, pieces, down_ref, width)
    loads = Loads(entries, sems)
    loads.start()

    @pl.when(loads.first)
    def _():
        gu_ref[...] = jnp.zeros_like(gu_ref)
        gd_ref[...] = jnp.zeros_like(gd_ref)
        fill_down_maps(ad_ref, down_ref, width)

    share = x4_refs[0].shape[0]
    grad_branch = (mod_ref[5:6, :] * cot_ref[...].astype(F32)).astype(BF16)
    gd_ref[...] += tn(nt(grad_branch, ad_ref[1]).astype(BF16), act_ref[...])
    for i in range(len(entries)):
        loads.ready(i)
    both = nn(act_ref[...], down_ref[...])
    ranks = both[:, width : width + RANK].astype(BF16)
    branch = both[:, :width] + nn(ranks, ad_ref[1])
    gu_ref[...] += tn(ranks, grad_branch)
    result = (x3_ref[...] + mod_ref[5:6, :] * branch).astype(BF16)
    for k, ref in enumerate(x4_refs):
        at = k * share

        @pl.when(step == at // ROWS)
        def _():
            ref[...] = result[at % ROWS : at % ROWS + share]


def cross_temporal_backward(parts, *refs):
    outs = len(refs) - parts - 13
    _cross_temporal_backward(refs[:parts], refs[outs : outs + parts], *refs[parts:outs], *refs[outs + parts :])


def _cross_temporal_backward(
    u1_refs, g1_refs, g3_ref, q_ref, k_ref, v_ref, o_ref, stat_ref, rq_ref, ro_ref,
    u2_ref, qc_ref, oc_ref, statc_ref, rqc_ref, roc_ref, kp_ref, vp_ref,
    mod_ref, mask_ref, ad_ref, w_hbm,
    gw_ref, dk_acc, dv_acc, w_ref, bias_ref, q_s, k_s, v_s, do_s, dq_s, dk_s, dv_s, sems,
):
    width = u1_refs[0].shape[2]
    first = pl.program_id(0) == 0
    order = (7, 4, 3, 0, 1, 2)
    loads = Loads(
        [(w_hbm.at[n], w_ref.at[i, pl.ds(0, width), :]) for i, n in enumerate(order)], sems
    )
    loads.start()

    @pl.when(first)
    def _():
        bias_ref[...] = same_place(bias_ref.shape)
        gw_ref[...] = jnp.zeros_like(gw_ref)
        dk_acc[...] = jnp.zeros_like(dk_acc)
        dv_acc[...] = jnp.zeros_like(dv_acc)
        for i, n in enumerate(order):
            w_ref[i, width:, :] = up_rows(ad_ref, 4 + n, n if n < 3 else 0, width)

    def rows(ref):
        return ref[...].reshape(ROWS, ref.shape[2])

    grad = rows(g3_ref)
    loads.ready(0)
    do_s[...] = one_back(
        grad.astype(BF16), rows(oc_ref), roc_ref[0], ad_ref, 11, w_ref.at[0], gw_ref, 14
    ).astype(BF16)
    q_s[...] = rows(qc_ref)
    count = 120
    carried = None
    for pair in range(PAIRS):
        win = window(pair)
        q_win, do_win = q_s[:, win], do_s[:, win]
        scores = nt(kp_ref[pair], q_win)
        grad_probs = nt(vp_ref[pair], do_win)
        all_probs, all_grads = [], []
        nothing = jnp.zeros((PAD - count, ROWS), F32)
        for sub in range(2):
            span = slice(PAD * sub, PAD * sub + count)
            row = 2 * pair + sub
            probs = jnp.exp2(scores[span] - statc_ref[0, row : row + 1, :])
            own = grad_probs[span]
            inner = jnp.sum(probs * own, 0, keepdims=True)
            all_probs += [probs, nothing]
            all_grads += [probs * (own - inner), nothing]
        probs = jnp.concatenate(all_probs, 0).astype(BF16)
        grad_scores = jnp.concatenate(all_grads, 0).astype(BF16)
        dk_acc[pair] += nn(grad_scores, q_win)
        dv_acc[pair] += nn(probs, do_win)
        out = tn(grad_scores, kp_ref[pair])
        low = out[:, :128]
        dq_s[:, tile(pair)] = ((low if carried is None else low + carried) * SCALE).astype(BF16)
        carried = out[:, 128:]
    dq_s[:, tile(PAIRS)] = (carried * SCALE).astype(BF16)
    loads.ready(1)
    grad = grad + one_back(
        dq_s[...], rows(u2_ref), rqc_ref[0], ad_ref, 8, w_ref.at[1], gw_ref, 8
    )
    loads.ready(2)
    do_s[...] = one_back(
        (mod_ref[2:3, :] * grad).astype(BF16), rows(o_ref), ro_ref[0], ad_ref, 7, w_ref.at[2], gw_ref, 6
    ).astype(BF16)
    q_s[...] = rows(q_ref)
    k_s[...] = rows(k_ref)
    v_s[...] = rows(v_ref)

    def put(index, values):
        dq_s[:, tile(index)] = (values[0] * SCALE).astype(BF16)
        dk_s[:, tile(index)] = (values[1] * LN2).astype(BF16)
        dv_s[:, tile(index)] = values[2].astype(BF16)

    attend_back(q_s, k_s, v_s, do_s, mask_ref, bias_ref, stat_ref.at[0], put)
    grad = grad + three_back(
        (dq_s, dk_s, dv_s), rows_of(u1_refs), rq_ref[0], ad_ref, 4, w_ref, loads, 3, gw_ref, 0
    )
    grad = grad.astype(BF16)
    share = ROWS // len(g1_refs)
    for k, ref in enumerate(g1_refs):
        ref[...] = grad[share * k : share * (k + 1)].reshape(ref.shape)


def tail_groups(cols):
    tail = cols - PAD
    return PAD // tail if 0 < tail < PAD and PAD % tail == 0 else 0


def packed_rows(blocks, cols):
    group = tail_groups(cols)
    if not group:
        return blocks * RANK, cols
    return (blocks + -(-blocks // group)) * RANK, PAD


def put_blocks(blocks, put):
    cols = blocks[0].shape[1]
    group = tail_groups(cols)
    for k, rows in enumerate(blocks):
        put(k, rows[:, :PAD] if group else rows)
    for k in range(0, len(blocks), group) if group else ():
        tails = [rows[:, PAD:] for rows in blocks[k : k + group]]
        missing = group - len(tails)
        if missing:
            tails.append(jnp.zeros((RANK, missing * (cols - PAD)), blocks[0].dtype))
        put(len(blocks) + k // group, jnp.concatenate(tails, 1))


def get_block(get, index, count, cols):
    group = tail_groups(cols)
    if not group:
        return get(index)
    at = (index % group) * (cols - PAD)
    return jnp.concatenate([get(index), get(count + index // group)[:, at : at + cols - PAD]], 1)


def pack_columns(table_ref, packed_ref, clips):
    parts = packed_ref.shape[0] // clips
    share = table_ref.shape[0] // parts
    cols = table_ref.shape[1] // clips
    for f in range(clips):
        for s in range(parts):
            piece = table_ref[share * s : share * (s + 1), cols * f : cols * (f + 1)].astype(BF16)
            blocks = [piece[block_rows(k)] for k in range(share // RANK)]

            def put(k, rows):
                packed_ref[f * parts + s, block_rows(k), :] = rows

            put_blocks(blocks, put)


def stacked(seq_ref, g1_refs, shares, whole_ref):
    parts = len(g1_refs) // shares
    places = whole_ref.shape[0] // parts
    at = 0
    for share in range(shares):
        refs = g1_refs[share * parts : (share + 1) * parts]
        size = refs[0].shape[1]
        for k, ref in enumerate(refs):
            start = pl.multiple_of(place_of(seq_ref, k, parts, places) + at, 16)
            whole_ref[pl.ds(start, size), :] = ref[0]
        at += size
    return whole_ref[...].astype(F32)


def spatial_backward(pieces, halves, clips, continued, last, seq_ref, *refs):
    g1_refs, refs = refs[:pieces], refs[pieces:]
    if continued:
        (_, before_ref), refs = refs[:2], refs[2:]
    (
        x_ref, q_ref, k_ref, v_ref, o_ref, stat_ref, rq_ref, ro_ref, mod_ref, mask_ref, ad_ref, w_hbm,
        d_ref, sums_ref, w_ref, gw_ref, do_s, sems,
    ) = refs
    width = x_ref.shape[2]
    loads = Loads([(w_hbm.at[3], w_ref.at[pl.ds(0, width), :])], sems)
    loads.start()

    @pl.when(loads.first)
    def _():
        gw_ref[...] = before_ref[...] if continued else jnp.zeros_like(gw_ref)
        w_ref[width:, :] = up_rows(ad_ref, 3, 0, width)

    grad = stacked(seq_ref, g1_refs, halves, do_s)
    loads.ready(0)
    do_s[...] = one_back(
        (mod_ref[2:3, :] * grad).astype(BF16), o_ref[0], ro_ref[0], ad_ref, 3, w_ref, gw_ref, 6
    ).astype(BF16)

    def put(index, values):
        for i, factor in enumerate((SCALE, LN2, 1.0)):
            value = values[i] if factor == 1.0 else values[i] * factor
            d_ref[0, :, width * i + 128 * index : width * i + 128 * index + 128] = value.astype(BF16)

    attend_back(
        q_ref.at[0], k_ref.at[0], v_ref.at[0], do_s, mask_ref, None, stat_ref.at[0], put
    )
    ranks = rq_ref[0]
    grad_ranks = None
    for i in range(3):
        grad = d_ref[0, :, width * i : width * (i + 1)]
        gw_ref[block_rows(2 * i + 1), :] += tn(ranks, grad)[block_rows(i)]
        part = nt(grad, up_rows(ad_ref, i, i, width))
        grad_ranks = part if grad_ranks is None else grad_ranks + part
    d_ref[0, :, 3 * width :] = grad_ranks.astype(BF16)
    normal, _ = normalize(x_ref[0].astype(F32))
    inputs = (normal * (1.0 + mod_ref[1:2, :]) + mod_ref[0:1, :]).astype(BF16)
    downs = tn(d_ref[0, :, 3 * width :], inputs)
    for i in range(3):
        gw_ref[block_rows(2 * i), :] += downs[block_rows(i)]

    @pl.when(pl.program_id(0) == pl.num_programs(0) - 1)
    def _():
        if last:
            pack_columns(gw_ref, sums_ref, clips)
        else:
            sums_ref[...] = gw_ref[...]


def spatial_input_grad(pieces, halves, seq_ref, *refs):
    g1_refs, refs = refs[:pieces], refs[pieces:]
    x_ref, d_ref, mod_ref, ad_ref, w_hbm, g0_ref, w_ref, whole_s, sems = refs
    width = x_ref.shape[2]
    loads = Loads(
        [(w_hbm.at[i], w_ref.at[:, pl.ds(i * width, width)]) for i in range(3)], sems
    )
    loads.start()

    @pl.when(loads.first)
    def _():
        w_ref[:, 3 * width :] = transposed_map(three_downs(ad_ref, 0))

    normal, inverse = normalize(x_ref[0].astype(F32))
    grad = stacked(seq_ref, g1_refs, halves, whole_s)
    for i in range(3):
        loads.ready(i)
    grad_in = nt(d_ref[0], w_ref[...])
    grad = grad + normalize_back(normal, inverse, grad_in * (1.0 + mod_ref[1:2, :]))
    g0_ref[0] = grad.astype(BF16)


def put_in_place(seq_ref, *refs):
    *pieces, out_ref = refs
    places = pieces[0].shape[1]
    for k, ref in enumerate(pieces):
        out_ref[0, pl.ds(place_of(seq_ref, k, len(pieces), places), places), :] = ref[0]


def pack_early(clips, shares, counts, *refs):
    gw_refs, refs = refs[:shares], refs[shares:]
    dk_refs, refs = refs[:shares], refs[shares:]
    dv_refs, refs = refs[:shares], refs[shares:]
    *others, rk_ref, rv_ref, ctx_ref, mask_ref, ad_ref, packed_ref, table_ref, ctx_s = refs

    def added(each):
        total = each[0]
        for value in each[1:]:
            total = total + value
        return total

    at = gw_refs[0].shape[0]
    table_ref[:at, :] = added([ref[...] for ref in gw_refs])
    width = table_ref.shape[1]
    for count in counts:
        each, others = others[:count], others[count:]
        for k in range(each[0].shape[1] // width):
            cols = slice(k * width, (k + 1) * width)
            table_ref[at : at + RANK, :] = added([ref[:, cols] for ref in each])
            at += RANK
    table_ref[at:, :] = jnp.zeros((table_ref.shape[0] - at, width), F32)
    for accs, factor, rank_ref, number, at in (
        (dk_refs, LN2, rk_ref, 9, 10),
        (dv_refs, 1.0, rv_ref, 10, 12),
    ):
        held = None
        for pair in range(PAIRS):
            whole = added([ref[pair] for ref in accs]) * factor
            out = whole[:PAD] * mask_ref[2 * pair : 2 * pair + 1, :].astype(F32)
            out = out + whole[PAD:] * mask_ref[2 * pair + 1 : 2 * pair + 2, :].astype(F32)
            low = out[:, :128]
            ctx_s[:, tile(pair)] = low if held is None else low + held
            held = out[:, 128:]
        ctx_s[:, tile(PAIRS)] = held
        grad_kv = ctx_s[...].astype(BF16)
        grad_rank = nt(grad_kv, ad_ref[2 * number + 1]).astype(BF16)
        table_ref[block_rows(at), :] = tn(grad_rank, ctx_ref[...])
        table_ref[block_rows(at + 1), :] = tn(rank_ref[...], grad_kv)
    pack_columns(table_ref, packed_ref, clips)


def assemble(parts, seq_ref, *refs):
    early_refs, late_refs, refs = refs[:parts], refs[parts : 2 * parts], refs[2 * parts :]
    wide_ref, narrow_ref, early_ref, late_ref = refs
    for k in range(parts):
        source = lax.rem(seq_ref[0] + parts - k, parts)
        early_ref[source] = early_refs[k][...]
        late_ref[source] = late_refs[k][...]
    _, adapters, _, cols = wide_ref.shape
    times = narrow_ref.shape[3] // cols

    def block(ref, total, index, a):
        each = total // ref.shape[0]

        def get(k):
            return ref[index // each, a, block_rows(k), :].astype(F32)

        return get_block(get, index % each, each, cols)

    for a in range(adapters):
        for i in range(8):
            wide_ref[i, a] = block(late_ref, LATE_BLOCKS, i, a)
        for i in range(18):
            wide_ref[8 + i, a] = block(early_ref, EARLY_BLOCKS, i, a)
        for n in range(2):
            pieces = [block(early_ref, EARLY_BLOCKS, 18 + n * times + j, a) for j in range(times)]
            narrow_ref[n, a] = jnp.concatenate(pieces, 1)


def combine(index_ref, got_ref, out_ref, acc_ref):
    clips = index_ref.shape[0]
    parts = got_ref.shape[0] // clips
    acc_ref[...] = jnp.zeros_like(acc_ref)

    def step(f, carry):
        total = got_ref[f * parts].astype(F32)
        for s in range(1, parts):
            total = total + got_ref[f * parts + s].astype(F32)
        acc_ref[index_ref[f]] += total
        return carry

    lax.fori_loop(0, clips, step, 0)
    out_ref[...] = acc_ref[...].astype(BF16)


def pick(index_ref, wide_ref, narrow_ref, out_ref):
    count, _, _, cols = wide_ref.shape
    times = narrow_ref.shape[3] // cols

    def step(f, carry):
        a = index_ref[f]
        blocks = [wide_ref[k, a] for k in range(count)]
        for p in range(2):
            rows = narrow_ref[p, a]
            blocks += [rows[:, cols * j : cols * (j + 1)] for j in range(times)]

        def put(k, rows):
            out_ref[f, block_rows(k), :] = rows

        put_blocks(blocks, put)
        return carry

    lax.fori_loop(0, index_ref.shape[0], step, 0)


def unpick(count, cols, got_ref, out_ref):
    for k in range(count):
        pieces = []
        for f in range(got_ref.shape[0]):

            def get(index):
                return got_ref[f, block_rows(index), :]

            pieces.append(get_block(get, k, count, cols))
        out_ref[k] = jnp.concatenate(pieces, 1)


def whole_block(array):
    zeros = (0,) * array.ndim
    return pl.BlockSpec(array.shape, lambda i: zeros, pipeline_mode=pl.Buffered(1))


def anywhere():
    return pl.BlockSpec(memory_space=pl.ANY)


def like(shape, dtype):
    return jax.ShapeDtypeStruct(shape, dtype)


PARAMS = pltpu.CompilerParams(
    dimension_semantics=("arbitrary",), vmem_limit_bytes=VMEM_LIMIT
)


def cost(flops, read, part=4):
    return pl.CostEstimate(
        flops=flops // part, bytes_accessed=read // part, transcendentals=0
    )


def run_spatial_forward(seq, video, mods, masks, wide, w_s, parts):
    frames, rows, d = video.shape
    places = rows // parts
    by_frame = lambda i: (i, 0, 0)
    row_block = pl.BlockSpec((1, rows, d), by_frame)
    return pl.pallas_call(
        spatial_forward,
        grid=(frames,),
        in_specs=[in_smem(), row_block, whole_block(mods), whole_block(masks), whole_block(wide), anywhere()],
        out_specs=[pl.BlockSpec((1, places, d), by_frame)] * parts
        + [
            row_block,
            row_block,
            row_block,
            row_block,
            pl.BlockSpec((1, HEADS, rows), by_frame),
            pl.BlockSpec((1, rows, 3 * RANK), by_frame),
            pl.BlockSpec((1, rows, RANK), by_frame),
        ],
        out_shape=[like((frames, places, d), BF16)] * parts
        + [like(video.shape, BF16)] * 4
        + [
            like((frames, HEADS, rows), F32),
            like((frames, rows, 3 * RANK), BF16),
            like((frames, rows, RANK), BF16),
        ],
        scratch_shapes=[
            pltpu.VMEM((4, d + PAD, d), BF16),
            pltpu.VMEM((ROWS, d + PAD), BF16),
            pltpu.VMEM((ROWS, d), BF16),
            pltpu.SemaphoreType.DMA((4,)),
        ],
        compiler_params=PARAMS,
        cost_estimate=cost(10 * frames * rows * d * d, 30_000_000),
        name="spatial_forward",
    )(seq, video, mods, masks, wide, w_s)


def run_temporal_forward(x1, mods, masks, wide, w_t):
    parts = len(x1)
    own_frames, places, d = x1[0].shape
    frames = own_frames * parts
    groups = places * frames // ROWS
    each = ROWS // frames
    across = pl.BlockSpec((frames, each, d), lambda i: (0, i, 0))
    by_group = lambda i: (i, 0, 0)
    act = like((frames, places, d), BF16)

    def body(*refs):
        temporal_forward(parts, *refs)

    return pl.pallas_call(
        body,
        grid=(groups,),
        in_specs=[pl.BlockSpec((own_frames, each, d), lambda i: (0, i, 0))] * parts
        + [whole_block(mods), whole_block(masks), whole_block(wide), anywhere()],
        out_specs=[across] * 4
        + [
            pl.BlockSpec((1, HEADS, ROWS), by_group),
            pl.BlockSpec((1, ROWS, 3 * RANK), by_group),
            pl.BlockSpec((1, ROWS, RANK), by_group),
            across,
            across,
        ],
        out_shape=[act] * 4
        + [
            like((groups, HEADS, ROWS), F32),
            like((groups, ROWS, 3 * RANK), BF16),
            like((groups, ROWS, RANK), BF16),
            act,
            like((frames, places, d), F32),
        ],
        scratch_shapes=[pltpu.VMEM((4, d + PAD, d), BF16), pltpu.VMEM((ROWS, ROWS), F32)]
        + [pltpu.VMEM((ROWS, d + PAD), BF16)]
        + [pltpu.VMEM((ROWS, d), BF16)] * 3
        + [pltpu.SemaphoreType.DMA((4,))],
        compiler_params=PARAMS,
        cost_estimate=cost(10 * places * frames * d * d, 30_000_000, 64),
        name="temporal_forward",
    )(*x1, mods, masks, wide, w_t)


def run_cross_forward(x2, context, masks, wide, w_c):
    frames, places, d = x2.shape
    groups = places * frames // ROWS
    across = pl.BlockSpec((frames, ROWS // frames, d), lambda i: (0, i, 0))
    by_group = lambda i: (i, 0, 0)
    full = lambda *shape: pl.BlockSpec(shape, lambda i: (0,) * len(shape))
    one = pl.BlockSpec((1, ROWS, RANK), by_group)
    one_shape = like((groups, ROWS, RANK), BF16)
    act = like((frames, places, d), BF16)
    return pl.pallas_call(
        cross_forward,
        grid=(groups,),
        in_specs=[across, whole_block(context), whole_block(masks), whole_block(wide), anywhere()],
        out_specs=[across] * 2 + [pl.BlockSpec((1, HEADS, ROWS), by_group), one, one]
        + [full(PAIRS, 2 * PAD, 256)] * 2 + [full(PAD, RANK)] * 2 + [across],
        out_shape=[act] * 2 + [like((groups, HEADS, ROWS), F32), one_shape, one_shape]
        + [like((PAIRS, 2 * PAD, 256), BF16)] * 2 + [like((PAD, RANK), BF16)] * 2
        + [like(x2.shape, F32)],
        scratch_shapes=[pltpu.VMEM((4, d + PAD, d), BF16), pltpu.VMEM((ROWS, d + PAD), BF16)]
        + [pltpu.VMEM((ROWS, d), BF16), pltpu.VMEM((PAD, d), BF16)]
        + [pltpu.SemaphoreType.DMA((4,))],
        compiler_params=PARAMS,
        cost_estimate=cost(8 * places * frames * d * d, 30_000_000, 64),
        name="cross_forward",
    )(x2, context, masks, wide, w_c)


def in_smem():
    return pl.BlockSpec(memory_space=pltpu.SMEM)


def run_feed_forward_grad(cot, mods, maps, order, pieces):
    tokens, d = cot.shape
    chunks = len(pieces) // 2

    def body(*refs):
        feed_forward_grad(len(pieces), *refs)

    return pl.pallas_call(
        body,
        grid=(tokens // ROWS,),
        in_specs=[in_smem(), pl.BlockSpec((ROWS, d), lambda i: (i, 0)), whole_block(mods), whole_block(maps)]
        + [anywhere()] * len(pieces),
        out_specs=pl.BlockSpec((chunks, ROWS, d), lambda i: (0, i, 0)),
        out_shape=like((chunks, tokens, d), BF16),
        scratch_shapes=[
            pltpu.VMEM((chunks * d, d + PAD), BF16),
            pltpu.VMEM((ROWS, d + PAD), BF16),
            pltpu.SemaphoreType.DMA((len(pieces),)),
        ],
        compiler_params=PARAMS,
        cost_estimate=cost(2 * tokens * d * d * chunks, 20_000_000),
        name="feed_forward_grad",
    )(order, cot, mods, maps, *pieces)


def run_feed_forward(x3, cot, order, grad_active, pieces, mods, maps, up):
    tokens, d = x3.shape
    chunks = up.shape[0]
    late = len(pieces) // 2
    rows = pl.BlockSpec((ROWS, d), lambda i: (i, 0))
    wide_rows = pl.BlockSpec((ROWS, chunks * d), lambda i: (i, 0))
    more = [pltpu.VMEM((late * d, d + PAD), BF16), pltpu.VMEM((ROWS, d + PAD), BF16)] if late else []

    def body(*refs):
        feed_forward(len(grad_active), len(pieces), *refs)

    return pl.pallas_call(
        body,
        grid=(tokens // ROWS,),
        in_specs=[in_smem(), rows, rows]
        + [pl.BlockSpec((g.shape[0], ROWS, d), lambda i: (0, i, 0)) for g in grad_active]
        + [anywhere()] * len(pieces)
        + [whole_block(mods), whole_block(maps), anywhere()],
        out_specs=[
            wide_rows,
            rows,
            pl.BlockSpec((RANK, d), lambda i: (0, 0)),
            pl.BlockSpec((RANK, chunks * d), lambda i: (0, 0)),
        ],
        out_shape=[
            like((tokens, chunks * d), BF16),
            like((tokens, d), F32),
            like((RANK, d), F32),
            like((RANK, chunks * d), F32),
        ],
        scratch_shapes=[
            pltpu.VMEM((d + PAD, chunks * d), BF16),
            pltpu.VMEM((ROWS, d + PAD), BF16),
            pltpu.VMEM((ROWS, chunks * d), BF16),
            pltpu.SemaphoreType.DMA((chunks + len(pieces),)),
            *more,
        ],
        compiler_params=PARAMS,
        cost_estimate=cost(4 * tokens * d * d * chunks, 50_000_000),
        name="feed_forward",
    )(order, x3, cot, *grad_active, *pieces, mods, maps, up)


def run_feed_forward_out(active, x3, cot, mods, maps, down, parts, half, halves):
    tokens, d = x3.shape
    order, *pieces = down
    hidden = active.shape[1]
    share = tokens // parts
    parts = parts // halves
    steps = tokens // ROWS // halves
    start = half * steps

    def body(*refs):
        feed_forward_out(len(pieces), *refs)

    rows = pl.BlockSpec((ROWS, d), lambda i: (i + start, 0))
    return pl.pallas_call(
        body,
        grid=(steps,),
        in_specs=[
            in_smem(),
            pl.BlockSpec((ROWS, hidden), lambda i: (i + start, 0)),
            rows,
            rows,
            whole_block(mods),
            whole_block(maps),
        ]
        + [anywhere()] * len(pieces),
        out_specs=[pl.BlockSpec((share, d), lambda i: (0, 0))] * parts
        + [
            pl.BlockSpec((RANK, d), lambda i: (0, 0)),
            pl.BlockSpec((RANK, hidden), lambda i: (0, 0)),
        ],
        out_shape=[like((share, d), BF16)] * parts
        + [
            like((RANK, d), F32),
            like((RANK, hidden), F32),
        ],
        scratch_shapes=[
            pltpu.VMEM((hidden, d + PAD), BF16),
            pltpu.SemaphoreType.DMA((len(pieces),)),
        ],
        compiler_params=PARAMS,
        cost_estimate=cost(2 * steps * ROWS * d * hidden, 20_000_000, 64),
        name="feed_forward_out",
    )(order, active, x3, cot, mods, maps, *pieces)


def run_cross_temporal_backward(g3, u1, saved, mods, masks, wide, w_tc, start, groups):
    parts = len(u1)
    own_frames, places, d = u1[0].shape
    frames = own_frames * parts
    each = ROWS // frames
    across = pl.BlockSpec((frames, ROWS // frames, d), lambda i: (0, i + start, 0))
    by_group = lambda i: (i + start, 0, 0)
    stat = pl.BlockSpec((1, HEADS, ROWS), by_group)
    three = pl.BlockSpec((1, ROWS, 3 * RANK), by_group)
    one = pl.BlockSpec((1, ROWS, RANK), by_group)
    kp, vp = saved[13:15]
    pair_sums = pl.BlockSpec((PAIRS, 2 * PAD, 256), lambda i: (0, 0, 0))

    def body(*refs):
        cross_temporal_backward(parts, *refs)

    return pl.pallas_call(
        body,
        grid=(groups,),
        in_specs=[pl.BlockSpec((own_frames, each, d), lambda i: (0, i + start, 0))] * parts
        + [across] + [across] * 4 + [stat, three, one] + [across] * 3 + [stat, one, one]
        + [whole_block(kp), whole_block(vp)]
        + [whole_block(mods), whole_block(masks), whole_block(wide), anywhere()],
        out_specs=[pl.BlockSpec((own_frames, each, d), lambda i: (0, i, 0))] * parts
        + [
            pl.BlockSpec((16 * RANK, d), lambda i: (0, 0)),
            pair_sums,
            pair_sums,
        ],
        out_shape=[like((own_frames, groups * each, d), BF16)] * parts
        + [like((16 * RANK, d), F32)]
        + [like((PAIRS, 2 * PAD, 256), F32)] * 2,
        scratch_shapes=[
            pltpu.VMEM((6, d + PAD, d), BF16),
            pltpu.VMEM((ROWS, ROWS), F32),
        ]
        + [pltpu.VMEM((ROWS, d), BF16)] * 7
        + [pltpu.SemaphoreType.DMA((6,))],
        compiler_params=PARAMS,
        cost_estimate=cost(14 * groups * ROWS * d * d, 30_000_000, 64),
        name="cross_temporal_backward",
    )(*u1, g3, *saved[:15], mods, masks, wide, w_tc)


LATE_BLOCKS = 8
EARLY_BLOCKS = 28


def run_spatial_backward(seq, g1, halves, video, saved, mods, masks, wide, w_s, clips, start, count, before):
    frames, rows, d = video.shape
    parts = len(g1) // halves
    by_frame = lambda i: (i + start, 0, 0)
    row_block = pl.BlockSpec((1, rows, d), by_frame)
    last = start + count == frames
    sums = (8 * RANK, d)
    if last:
        sums = (clips * parts, *packed_rows(LATE_BLOCKS // parts, d // clips))
    zeros = (0,) * len(sums)

    def body(*refs):
        spatial_backward(len(g1), halves, clips, bool(before), last, *refs)

    extra = [anywhere(), whole_block(before[1])] if before else []
    return pl.pallas_call(
        body,
        grid=(count,),
        in_specs=[in_smem()] + [pl.BlockSpec((1, g.shape[1], d), by_frame) for g in g1]
        + extra
        + [row_block] * 5
        + [
            pl.BlockSpec((1, HEADS, rows), by_frame),
            pl.BlockSpec((1, rows, 3 * RANK), by_frame),
            pl.BlockSpec((1, rows, RANK), by_frame),
            whole_block(mods),
            whole_block(masks),
            whole_block(wide),
            anywhere(),
        ],
        out_specs=[
            pl.BlockSpec((1, rows, 3 * d + PAD), by_frame),
            pl.BlockSpec(sums, lambda i: zeros),
        ],
        out_shape=[like((frames, rows, 3 * d + PAD), BF16), like(sums, BF16 if last else F32)],
        input_output_aliases={1 + len(g1): 0} if before else {},
        scratch_shapes=[pltpu.VMEM((d + PAD, d), BF16), pltpu.VMEM((LATE_BLOCKS * RANK, d), F32)]
        + [pltpu.VMEM((ROWS, d), BF16), pltpu.SemaphoreType.DMA((1,))],
        compiler_params=PARAMS,
        cost_estimate=cost(6 * count * rows * d * d, 20_000_000, 64),
        name="spatial_backward",
    )(seq, *g1, *before, video, *saved, mods, masks, wide, w_s)


def run_spatial_input_grad(seq, g1, halves, video, grads, mods, wide, w_s):
    frames, rows, d = video.shape
    by_frame = lambda i: (i, 0, 0)
    row_block = pl.BlockSpec((1, rows, d), by_frame)

    def body(*refs):
        spatial_input_grad(len(g1), halves, *refs)

    return pl.pallas_call(
        body,
        grid=(frames,),
        in_specs=[in_smem()] + [pl.BlockSpec((1, g.shape[1], d), by_frame) for g in g1]
        + [
            row_block,
            pl.BlockSpec((1, rows, grads.shape[2]), by_frame),
            whole_block(mods),
            whole_block(wide),
            anywhere(),
        ],
        out_specs=row_block,
        out_shape=like(video.shape, BF16),
        scratch_shapes=[
            pltpu.VMEM((d, 3 * d + PAD), BF16),
            pltpu.VMEM((ROWS, d), BF16),
            pltpu.SemaphoreType.DMA((3,)),
        ],
        compiler_params=PARAMS,
        cost_estimate=cost(6 * frames * rows * d * d, 20_000_000, 64),
        name="spatial_input_grad",
    )(seq, *g1, video, grads, mods, wide, w_s)


def run_put_in_place(seq, pieces):
    frames, places, d = pieces[0].shape
    by_frame = lambda i: (i, 0, 0)
    rows = places * len(pieces)
    return pl.pallas_call(
        put_in_place,
        grid=(frames,),
        in_specs=[in_smem()] + [pl.BlockSpec((1, places, d), by_frame)] * len(pieces),
        out_specs=pl.BlockSpec((1, rows, d), by_frame),
        out_shape=like((frames, rows, d), BF16),
        compiler_params=PARAMS,
        cost_estimate=cost(0, 4 * frames * rows * d, 64),
        name="put_in_place",
    )(seq, *pieces)


PLAIN = pltpu.CompilerParams(vmem_limit_bytes=VMEM_LIMIT)


def in_vmem():
    return pl.BlockSpec(memory_space=pltpu.VMEM)


def run_pack_early(gw, dk, dv, others, sources, clips, parts):
    d = gw[0].shape[1]
    packed = (clips * parts, *packed_rows(EARLY_BLOCKS // parts, d // clips))

    def body(*refs):
        pack_early(clips, len(gw), [len(each) for each in others], *refs)

    return pl.pallas_call(
        body,
        out_shape=like(packed, BF16),
        scratch_shapes=[pltpu.VMEM((EARLY_BLOCKS * RANK, d), F32), pltpu.VMEM((PAD, d), F32)],
        compiler_params=PLAIN,
        cost_estimate=cost(50000000, 8000000, 64),
        name="pack_early",
    )(*gw, *dk, *dv, *[array for each in others for array in each], *sources)


def run_assemble(seq, early, late, wide_shape, narrow_shape):
    parts = len(early)

    def body(*refs):
        assemble(parts, *refs)

    return pl.pallas_call(
        body,
        in_specs=[in_smem()] + [in_vmem()] * (2 * parts),
        out_specs=[in_vmem()] * 2,
        out_shape=[like(wide_shape, F32), like(narrow_shape, F32)],
        scratch_shapes=[pltpu.VMEM((parts, *piece.shape), BF16) for piece in (early[0], late[0])],
        compiler_params=PLAIN,
        cost_estimate=cost(0, 6_000_000, 64),
        name="assemble",
    )(seq, *early, *late)


def run_pick(all_index, wide, narrow):
    count, _, _, cols = wide.shape
    shape = packed_rows(count + 2 * (narrow.shape[3] // cols), cols)
    return pl.pallas_call(
        pick,
        in_specs=[in_smem(), in_vmem(), in_vmem()],
        out_specs=in_vmem(),
        out_shape=like((all_index.shape[0], *shape), BF16),
        compiler_params=PLAIN,
        cost_estimate=cost(0, 3000000),
        name="pick",
    )(all_index, wide, narrow)


def run_unpick(got, blocks, cols):
    def body(*refs):
        unpick(blocks, cols, *refs)

    return pl.pallas_call(
        body,
        in_specs=[in_vmem()],
        out_specs=in_vmem(),
        out_shape=like((blocks, RANK, got.shape[0] * cols), BF16),
        compiler_params=PLAIN,
        cost_estimate=cost(0, 2500000),
        name="unpick",
    )(got)


def run_combine(all_index, got, adapters):
    _, share, cols = got.shape
    return pl.pallas_call(
        combine,
        in_specs=[pl.BlockSpec(memory_space=pltpu.SMEM), pl.BlockSpec(memory_space=pltpu.VMEM)],
        out_specs=pl.BlockSpec(memory_space=pltpu.VMEM),
        out_shape=like((adapters, share, cols), BF16),
        scratch_shapes=[pltpu.VMEM((adapters, share, cols), F32)],
        compiler_params=pltpu.CompilerParams(vmem_limit_bytes=VMEM_LIMIT),
        cost_estimate=cost(0, 1000000, 64),
        name="combine",
    )(all_index, got)


def exchange(array, axes="seq"):
    return lax.all_to_all(array, axes, split_axis=0, concat_axis=0, tiled=True)


def up_chunks(up, clips, times):
    rows, hidden = up.shape
    cols = hidden // (clips * times)
    return up.reshape(rows, clips, times, cols).transpose(2, 0, 1, 3).reshape(times, rows, -1)


def gather(array):
    return lax.all_gather(array, "fsdp", axis=1, tiled=True)


def send(array, axis, shift):
    size = lax.axis_size(axis)
    return lax.ppermute(array, axis, [(i, (i + shift) % size) for i in range(size)])


def to_places(pieces):
    return [pieces[0]] + [send(pieces[k], "seq", k) for k in range(1, len(pieces))]


def to_frames(pieces):
    return [pieces[0]] + [send(pieces[k], "seq", -k) for k in range(1, len(pieces))]


def gather_spatial_and_down(spatial, down, parts, times, clips, d):
    if times != parts or clips % 2:
        return gather(spatial)
    own = lax.dynamic_slice_in_dim(down.reshape(times, -1, d), lax.axis_index("seq"), 1, 0)
    return gather(jnp.concatenate([spatial, own], 0))


def start_down(got, parts, times, clips, d):
    if times != parts or clips % 2:
        return None
    half = d // 2
    core = lax.axis_index("fsdp") % 2
    first = lax.dynamic_slice(got, (times, core * half, 0), (1, half, d))[0]
    other = lax.dynamic_slice(got, (times, (1 - core) * half, 0), (1, half, d))[0]
    return first, other, send(first, "seq", 1)


def swap_cores(piece, clips):
    return lax.ppermute(piece, "fsdp", [(i, i ^ 1) for i in range(clips)])


def to_all(piece):
    return [piece] + [send(piece, "seq", k) for k in range(1, lax.axis_size("seq"))]


def down_order(times, parts, clips):
    if times != parts or clips % 2:
        return jnp.arange(times, dtype=jnp.int32), jnp.zeros((1,), jnp.int32)
    seq = lax.axis_index("seq")
    core = lax.axis_index("fsdp") % 2
    return ((seq - jnp.arange(parts)) % parts).astype(jnp.int32), core.astype(jnp.int32)[None]


def on_device(
    video,
    context,
    modulation,
    adapter_index,
    cotangent,
    qkv_weights,
    out_weights,
    ffn_up,
    ffn_down,
    adapt_wide,
    adapt_ff,
):
    parts = lax.axis_size("seq")
    clips = lax.axis_size("fsdp")
    d = video.shape[-1]
    count, adapters, _, cols = adapt_wide.shape[1:]
    times = adapt_ff.shape[-1] // cols
    places = SPATIAL // parts
    frames = FRAMES // parts
    half_d = d // 2
    mods = modulation[0, 0]
    masks = head_masks()
    ctx = jnp.pad(context[0], ((0, PAD - context.shape[1]), (0, 0)))

    def attention_weights(j):
        return jnp.concatenate([qkv_weights[0, 3 * j : 3 * j + 3], out_weights[0, j : j + 1]], 0)

    seq = lax.axis_index("seq").astype(jnp.int32)[None]
    all_index = exchange(jnp.broadcast_to(adapter_index, (clips,)), "fsdp")
    w_s = gather_spatial_and_down(attention_weights(0), ffn_down[0], parts, times, clips, d)
    picked = run_pick(all_index, adapt_wide[0], adapt_ff[0])
    wide = run_unpick(exchange(picked, "fsdp"), count + 2 * times, cols)
    w_tc = gather(jnp.concatenate([attention_weights(1), attention_weights(2)], 0))
    ffn_up, _ = lax.optimization_barrier((ffn_up, picked))
    up = gather(up_chunks(ffn_up[0], clips, times))
    cot = cotangent.reshape(frames, SPATIAL, d)
    cot = to_places(
        [
            lax.dynamic_slice_in_dim(cot, (seq[0] + k) % parts * places, places, 1)
            for k in range(parts)
        ]
    )
    frames_in = video.reshape(frames, SPATIAL, d)
    maps_f = wide[24:]
    order, core = down_order(times, parts, clips)
    packed_order = jnp.concatenate([order, core])
    if times == parts and clips % 2 == 0:
        packed_order = jnp.concatenate([order[:2], order[parts - 1 :], order[2 : parts - 1], core])
    w_s, wide, maps_f, packed_order, *cot = lax.optimization_barrier((w_s, wide, maps_f, packed_order, *cot))
    started = start_down(w_s, parts, times, clips, d)
    cot = jnp.concatenate(cot, 0).reshape(FRAMES * places, d)
    made = run_spatial_forward(seq, frames_in, mods, masks, wide, w_s, parts)
    u1, kept_s = to_places(made[:parts]), made[parts:]
    if started is None:
        whole_down = gather(ffn_down[0].reshape(times, -1, d))
        sides = [[whole_down[i, :half_d] for i in range(times)], [whole_down[i, half_d:] for i in range(times)]]
        *kept_t, x2 = run_temporal_forward(u1, mods, masks, wide, w_tc)
        *kept_c, x3 = run_cross_forward(x2, ctx, masks, wide, w_tc)
        late_pieces = []
        grad_active = [run_feed_forward_grad(cot, mods, maps_f, packed_order, sides[0] + sides[1])]
    else:
        first, other, second = started
        second, cot, x1_own = lax.optimization_barrier((second, cot, u1[0]))
        mine = [first, second]
        others = [other, swap_cores(second, clips)]
        early_order = jnp.concatenate([packed_order[:2], core])
        grad_early = run_feed_forward_grad(cot, mods, maps_f, early_order, mine + others)
        first, second, grad_early, *u1 = lax.optimization_barrier(
            (first, second, grad_early, x1_own, *u1[1:])
        )
        third = send(first, "seq", -1)
        rest = [send(second, "seq", 1)] + [send(first, "seq", k) for k in range(3, parts - 1)]
        *kept_t, x2 = run_temporal_forward(u1, mods, masks, wide, w_tc)
        *kept_c, x3 = run_cross_forward(x2, ctx, masks, wide, w_tc)
        x3, third, *rest = lax.optimization_barrier((x3, third, *rest))
        rest = [third] + rest
        rest_others = [swap_cores(piece, clips) for piece in rest]
        late_order = jnp.concatenate([packed_order[2:parts], core])
        grad_late = run_feed_forward_grad(cot, mods, maps_f, late_order, rest + rest_others)
        grad_active = [grad_early, grad_late]
        late_pieces = []
        sides = [mine + rest, others + rest_others]
    down = [packed_order, *sides[0], *sides[1]]
    x3 = x3.reshape(FRAMES * places, d)
    active, g3, grad_a24, grad_b24 = run_feed_forward(
        x3, cot, packed_order, grad_active, late_pieces, mods, maps_f, up
    )
    g3 = g3.reshape(FRAMES, places, d)
    groups = FRAMES * places // ROWS
    saved = kept_t + kept_c
    turns = 2 if groups % 2 == 0 and parts % 2 == 0 else 1
    output, grad_b25, grad_down = [None] * parts, [], []

    def finish_tokens(turn, active):
        *x4, b25, rows = run_feed_forward_out(active, x3, cot, mods, maps_f, down, parts, turn, turns)
        grad_b25.append(b25)
        grad_down.append(rows)
        for k, piece in enumerate(x4, turn * parts // turns):
            output[k] = piece.reshape(frames, places, d)

    def send_tokens(turn):
        for k in range(turn * parts // turns, (turn + 1) * parts // turns):
            output[k] = send(output[k], "seq", -k) if k else output[k]

    finish_tokens(turns - 1, active)
    output[-1], g3 = lax.optimization_barrier((output[-1], g3))
    send_tokens(turns - 1)
    shares = [groups - groups // 2, groups // 2] if groups > 1 else [1]
    g1, gw, dk, dv = [], [], [], []
    for share, size in enumerate(shares):
        *pieces, gw_part, dk_part, dv_part = run_cross_temporal_backward(
            g3, u1, saved, mods, masks, wide, w_tc, sum(shares[:share]), size
        )
        gw.append(gw_part)
        dk.append(dk_part)
        dv.append(dv_part)
        if share == 0 and turns > 1:
            half = parts // turns
            pieces[0], g3, *output[half:] = lax.optimization_barrier((pieces[0], g3, *output[half:]))
        else:
            pieces[0], g3 = lax.optimization_barrier((pieces[0], g3))
        g1.append(to_frames(pieces))
    if len(shares) > 1:
        active, gw[-1], *g1[0] = lax.optimization_barrier((active, gw[-1], *g1[0]))
    if turns > 1:
        finish_tokens(0, active)
        send_tokens(0)
    others = [[grad_a24], grad_b25, [grad_b24], grad_down]
    sources = [kept_c[7], kept_c[8], ctx, masks, wide]
    packed = run_pack_early(gw, dk, dv, others, sources, clips, parts)
    g1 = [piece for done in g1 for piece in done]
    packed, *g1 = lax.optimization_barrier((packed, *g1))
    got = exchange(packed, ("fsdp", "seq"))
    halves = len(shares)
    grads, packed = run_spatial_backward(
        seq, g1, halves, frames_in, kept_s, mods, masks, wide, w_s, clips, 0, frames, []
    )
    packed, got, *output = lax.optimization_barrier((packed, got, *output))
    early = to_all(run_combine(all_index, got, adapters))
    g0 = run_spatial_input_grad(seq, g1, halves, frames_in, grads, mods, wide, w_s)
    got, g0 = lax.optimization_barrier((exchange(packed, ("fsdp", "seq")), g0))
    late = run_combine(all_index, got, adapters)
    wide_out, narrow_out = run_assemble(
        seq, early, to_all(late), adapt_wide.shape[1:], adapt_ff.shape[1:]
    )
    output = run_put_in_place(seq, output).reshape(video.shape)
    return (output, g0.reshape(video.shape), wide_out[None], narrow_out[None])


def solution(mesh):
    return jax.shard_map(
        on_device,
        mesh=mesh,
        in_specs=(
            P("fsdp", "seq", None),
            P("fsdp", None, None),
            P("fsdp", None, None, None),
            P("fsdp"),
            P("fsdp", "seq", None),
            P(None, None, "fsdp", None),
            P(None, None, "fsdp", None),
            P(None, "fsdp", None),
            P(None, "fsdp", None),
            P(None, None, None, None, "fsdp"),
            P(None, None, None, None, "fsdp"),
        ),
        out_specs=(
            P("fsdp", "seq", None),
            P("fsdp", "seq", None),
            P(None, None, None, None, "fsdp"),
            P(None, None, None, None, "fsdp"),
        ),
        check_vma=False,
    )
```
